32 devices in a mesh: dp: 8 (over z, y), var: 4 (over x, core).
Axes of the slice: x: 2, y: 2, z: 4, core: 2. Of those that a mesh axis runs over, the one named last changes fastest.
Arguments:
- img_lo: bfloat16 [320, 128, 320], P('dp', None, 'var'), may hold values from -6 to 6
- img_hi: bfloat16 [160, 512, 320], P('dp', None, 'var'), may hold values from -6 to 6
- keep_lo: int32 [320, 32], P('dp'), may hold values from 0 to 127, as said below
- keep_hi: int32 [160, 128], P('dp'), may hold values from 0 to 511, as said below
- mask_lo: int32 [320, 32], P('dp'), may hold values 0 or 1
- mask_hi: int32 [160, 128], P('dp'), may hold values 0 or 1
- w_embed: bfloat16 [320, 768], P('var'), may hold values from -0.3125 to 0.3125
- pos_lo: bfloat16 [128, 768], replicated, may hold values from -3 to 3
- pos_hi: bfloat16 [512, 768], replicated, may hold values from -3 to 3
- ln1_gain: float32 [768], replicated, may hold values from 0.25 to 1.75
- w_qkv: bfloat16 [768, 2304], replicated, may hold values from -0.21875 to 0.21875
- w_out: bfloat16 [768, 768], replicated, may hold values from -0.625 to 0.625
- ln2_gain: float32 [768], replicated, may hold values from 0.25 to 1.75
- w_fc1: bfloat16 [768, 3072], replicated, may hold values from -0.21875 to 0.21875
- b_fc1: float32 [3072], replicated, may hold values from -3 to 3
- w_fc2: bfloat16 [3072, 768], replicated, may hold values from -0.109375 to 0.109375
- b_fc2: float32 [768], replicated, may hold values from -3 to 3
- w_head: bfloat16 [768, 320], P(None, 'var'), may hold values from -0.21875 to 0.21875
- cot_lo: bfloat16 [320, 32, 320], P('dp', None, 'var'), may hold values from -6 to 6
- cot_hi: bfloat16 [160, 128, 320], P('dp', None, 'var'), may hold values from -6 to 6
Outputs:
- pred_lo: bfloat16 [320, 32, 320], P('dp', None, 'var')
- pred_hi: bfloat16 [160, 128, 320], P('dp', None, 'var')
- grad_img_lo: bfloat16 [320, 128, 320], P('dp', None, 'var')
- grad_img_hi: bfloat16 [160, 512, 320], P('dp', None, 'var')
- grad_embed: float32 [320, 768], P('var')
- grad_pos_lo: float32 [128, 768], P(('dp', 'var'))
- grad_pos_hi: float32 [512, 768], P(('dp', 'var'))
- grad_ln1: float32 [768], P(('dp', 'var'))
- grad_qkv: float32 [768, 2304], P(('dp', 'var'))
- grad_out: float32 [768, 768], P(('dp', 'var'))
- grad_ln2: float32 [768], P(('dp', 'var'))
- grad_fc1: float32 [768, 3072], P(('dp', 'var'))
- grad_b1: float32 [3072], P(('dp', 'var'))
- grad_fc2: float32 [3072, 768], P(('dp', 'var'))
- grad_b2: float32 [768], P(('dp', 'var'))
- grad_head: float32 [768, 320], P(None, 'var')
The draws below stay inside these ranges and needn't reach their ends.
Inputs may be any that keep to these rules, and one draw needn't show every extreme that they name: `keep_lo`: each row names 32 different patches of its sample. `keep_hi`: each row names 128 different patches of its sample. `mask_lo`: slot 0 counts as visible whatever its entry. `mask_hi`: slot 0 counts as visible whatever its entry.
All inputs are finite; a program needn't handle non-finite values. No bound on the sum of `mask_lo` or of `mask_hi` on one device may be relied on, other than what follows from the above.
Results may differ from the reference program's by a relative error of at most 0.02.
Values may be sent and summed in bfloat16 or wider, within the bound.
No kernel may reach another device: no remote copies, remote signals or barrier semaphores. Data moves between devices by JAX's collectives and lax.ppermute only.
A program may use at most 256 MiB of HBM per device.

```python
import math
import jax
import jax.numpy as jnp
from jax import lax

D = 768
HEADS = 12
HD = 64
FF = 3072
NP_LO = 128
NP_HI = 512
C = 320
KEEP_LO = 32
KEEP_HI = 128
LO_SAMPLES = 320
HI_SAMPLES = 160


def draw_keep_lo(key, part):
    keys = jax.random.split(jax.random.fold_in(key, 11), LO_SAMPLES)
    return jax.vmap(lambda single: jax.random.permutation(single, NP_LO)[:KEEP_LO])(keys).astype(jnp.int32)


def draw_keep_hi(key, part):
    keys = jax.random.split(jax.random.fold_in(key, 23), HI_SAMPLES)
    return jax.vmap(lambda single: jax.random.permutation(single, NP_HI)[:KEEP_HI])(keys).astype(jnp.int32)


def touch_ends(values, stream_key, smallest, high):
    index_at = [jax.random.randint(jax.random.fold_in(stream_key, axis), (), 0, length) for axis, length in enumerate(values.shape)]
    longest = values.shape.index(max(values.shape))
    neighbour = index_at[:longest] + [(index_at[longest] + 1) % values.shape[longest]] + index_at[longest + 1:]
    return values.at[tuple(index_at)].set(smallest).at[tuple(neighbour)].set(high)


def steps_of(key, shape, shards, least, high):
    factor_of, own = 1.0, jax.random.fold_in(key, 6)
    for dim, parts in shards:
        draws = jnp.exp(jax.random.uniform(jax.random.fold_in(own, dim), (parts,), jnp.float32, least / len(shards), high / len(shards)))
        factor_of = factor_of * jnp.repeat(draws, shape[dim] // parts).reshape([-1 if axis == dim else 1 for axis in range(len(shape))])
    return factor_of


def normal_values(key, dims, deviation, limit, cuts=(), held_as=jnp.bfloat16):
    level = steps_of(key, dims, cuts, -0.22, 0.18) if cuts else 1.0
    drawn = jax.random.normal(key, dims, jnp.float32) * deviation * level
    return jnp.minimum(jnp.maximum(drawn, -limit), limit).astype(held_as)


def setup_inputs(seed: int = 0) -> dict:
    streams_of = jax.random.split(jax.random.key(seed), 21)
    img_lo = normal_values(streams_of[0], (LO_SAMPLES, NP_LO, C), 1.0, 6.0, ((0, 8), (2, 4)))
    img_hi = normal_values(streams_of[1], (HI_SAMPLES, NP_HI, C), 1.0, 6.0, ((0, 8), (2, 4)))
    keep_lo = draw_keep_lo(jax.random.fold_in(streams_of[20], 71), 0)
    keep_hi = draw_keep_hi(jax.random.fold_in(streams_of[20], 71), 0)
    mask_lo = touch_ends((jax.random.randint(streams_of[4], (LO_SAMPLES, KEEP_LO), 0, 4) < 3).astype(jnp.int32), jax.random.fold_in(streams_of[4], 1), 0, 1)
    mask_hi = touch_ends((jax.random.randint(streams_of[5], (HI_SAMPLES, KEEP_HI), 0, 4) < 3).astype(jnp.int32), jax.random.fold_in(streams_of[5], 1), 0, 1)
    w_embed = normal_values(streams_of[6], (C, D), C ** -0.5, 0.3125, ((0, 4),))
    pos_lo = normal_values(streams_of[7], (NP_LO, D), 0.5, 3.0)
    pos_hi = normal_values(streams_of[8], (NP_HI, D), 0.5, 3.0)
    ln1_gain = jnp.clip(1.0 + 0.15 * jax.random.normal(streams_of[9], (D,), jnp.float32), 0.25, 1.75)
    w_qkv = normal_values(streams_of[10], (D, 3 * D), D ** -0.5, 0.21875)
    w_out = normal_values(streams_of[11], (D, D), (D // 8) ** -0.5, 0.625)
    ln2_gain = jnp.clip(1.0 + 0.15 * jax.random.normal(streams_of[12], (D,), jnp.float32), 0.25, 1.75)
    w_fc1 = normal_values(streams_of[13], (D, FF), D ** -0.5, 0.21875)
    b_fc1 = normal_values(streams_of[14], (FF,), 0.5, 3.0, (), jnp.float32)
    w_fc2 = normal_values(streams_of[15], (FF, D), FF ** -0.5, 0.109375)
    b_fc2 = normal_values(streams_of[16], (D,), 0.5, 3.0, (), jnp.float32)
    w_head = normal_values(streams_of[17], (D, C), D ** -0.5, 0.21875, ((1, 4),))
    cot_lo = normal_values(streams_of[18], (LO_SAMPLES, KEEP_LO, C), 1.0, 6.0, ((0, 8), (2, 4)))
    cot_hi = normal_values(streams_of[19], (HI_SAMPLES, KEEP_HI, C), 1.0, 6.0, ((0, 8), (2, 4)))
    return dict(img_lo=img_lo, img_hi=img_hi, keep_lo=keep_lo, keep_hi=keep_hi, mask_lo=mask_lo, mask_hi=mask_hi, w_embed=w_embed, pos_lo=pos_lo, pos_hi=pos_hi, ln1_gain=ln1_gain, w_qkv=w_qkv, w_out=w_out, ln2_gain=ln2_gain, w_fc1=w_fc1, b_fc1=b_fc1, w_fc2=w_fc2, b_fc2=b_fc2, w_head=w_head, cot_lo=cot_lo, cot_hi=cot_hi)


@jax.custom_vjp
def low(v):
    return lax.optimization_barrier(v.astype(jnp.bfloat16)).astype(jnp.float32)

@jax.custom_vjp
def low_back(v):
    return v

def low_keep(v):
    return (low(v), None)

def low_pass(kept, grad):
    return (grad,)

def back_keep(v):
    return (v, None)

def back_low(kept, grad):
    return (low(grad),)
low.defvjp(low_keep, low_pass)
low_back.defvjp(back_keep, back_low)
epsilon = 1e-06
highest = lax.Precision.HIGHEST

def product(left, right):
    return jnp.dot(left, right, precision=highest, preferred_element_type=jnp.float32)

def normalize(values, gains):
    center = values - lax.optimization_barrier(jnp.mean(values, axis=-1, keepdims=True))
    spread = lax.optimization_barrier(jnp.mean(center * center, axis=-1, keepdims=True))
    return center * lax.rsqrt(spread + epsilon) * gains

def encoder(weights, images, indices, visible, positions):
    w_embed, gain_one, w_qkv, w_out, gain_two, w_fc1, b_fc1, w_fc2, b_fc2, w_head = weights
    samples, length = indices.shape
    patches = jnp.take_along_axis(images, indices[:, :, None], axis=1).reshape(samples * length, -1)
    places = jnp.take(positions, indices.reshape(-1), axis=0)
    embedded = low_back(product(patches, w_embed) + places)
    normed = low(normalize(embedded, gain_one))
    triple = low(low_back(product(normed, w_qkv))).reshape(samples, length, 3, HEADS, HD)
    scores = low_back(jnp.einsum('bqhd,bkhd->bhqk', triple[:, :, 0], triple[:, :, 1], precision=highest) * (1.0 / math.sqrt(HD)))
    scores = jnp.where(visible[:, None, None, :] > 0, scores, -1000000000.0)
    chances = jax.nn.softmax(scores, axis=-1)
    mixed = jnp.einsum('bhqk,bkhd->bqhd', low(chances), triple[:, :, 2], precision=highest)
    mixed = low(low_back(mixed)).reshape(samples * length, HEADS * HD)
    middle = embedded + low_back(product(mixed, w_out))
    second = low(normalize(middle, gain_two))
    hidden = low_back(product(second, w_fc1) + b_fc1)
    activated = low(jax.nn.gelu(hidden, approximate=False))
    result_rows = middle + low_back(product(activated, w_fc2) + b_fc2)
    outputs = product(low(result_rows), w_head).reshape(samples, length, -1)
    return outputs * visible[:, :, None].astype(jnp.float32)

def blockwise(weights, images, indices, visible, positions, block):
    samples = indices.shape[0]
    group_size = math.gcd(samples, block)

    def shaped(array):
        return array.reshape((samples // group_size, group_size) + array.shape[1:])
    checked = jax.checkpoint(encoder)
    result = lax.map(lambda pieces: checked(weights, pieces[0], pieces[1], pieces[2], positions), (shaped(images), shaped(indices), shaped(visible)))
    return result.reshape((samples,) + result.shape[2:])

def visible_of(mask):
    first = (lax.broadcasted_iota(jnp.int32, mask.shape, 1) == 0).astype(jnp.int32)
    return jnp.maximum(mask, first)

def reference(img_lo, img_hi, keep_lo, keep_hi, mask_lo, mask_hi, w_embed, pos_lo, pos_hi, ln1_gain, w_qkv, w_out, ln2_gain, w_fc1, b_fc1, w_fc2, b_fc2, w_head, cot_lo, cot_hi):
    visible_lo = visible_of(mask_lo)
    visible_hi = visible_of(mask_hi)

    def forward(images_lo, images_hi, embed, table_lo, table_hi, gain_one, project_qkv, project_out, gain_two, first_fc, bias_one, second_fc, bias_two, project_head):
        weights = (embed, gain_one, project_qkv, project_out, gain_two, first_fc, bias_one, second_fc, bias_two, project_head)
        return (blockwise(weights, images_lo, keep_lo, visible_lo, table_lo, 128), blockwise(weights, images_hi, keep_hi, visible_hi, table_hi, 32))
    floats = tuple((array.astype(jnp.float32) for array in (img_lo, img_hi, w_embed, pos_lo, pos_hi, ln1_gain, w_qkv, w_out, ln2_gain, w_fc1, b_fc1, w_fc2, b_fc2, w_head)))
    preds, pull = jax.vjp(forward, *floats)
    grads = pull((cot_lo.astype(jnp.float32), cot_hi.astype(jnp.float32)))
    return (preds[0].astype(jnp.bfloat16), preds[1].astype(jnp.bfloat16), grads[0].astype(jnp.bfloat16), grads[1].astype(jnp.bfloat16), grads[2], grads[3], grads[4], grads[5], grads[6], grads[7], grads[8], grads[9], grads[10], grads[11], grads[12], grads[13])
```

```python
import math

import jax
import jax.numpy as jnp
from jax import lax
from jax.sharding import PartitionSpec as P

HEADS = 12
EPSILON = 1e-06
AXES = ("dp", "var")
BF16 = jnp.bfloat16
F32 = jnp.float32


def dot(left, right, dims):
    return lax.dot_general(left, right, (dims, ((), ())), preferred_element_type=F32)


def nn(left, right):
    return dot(left, right, ((1,), (0,)))


def nt(left, right):
    return dot(left, right, ((1,), (1,)))


def tn(left, right):
    return dot(left, right, ((0,), (0,)))


def swap(value, data_bit, var_bit):
    dp, var = lax.axis_size("dp"), lax.axis_size("var")
    pairs = [
        (d * var + v, (d ^ data_bit) * var + (v ^ var_bit)) for d in range(dp) for v in range(var)
    ]
    return lax.ppermute(value, AXES, pairs)


def add_rounded(left, right):
    return (left.astype(F32) + right.astype(F32)).astype(BF16)


def stages(order):
    dp, var = lax.axis_size("dp"), lax.axis_size("var")
    data = [("d", 1 << i) for i in range(dp.bit_length() - 1)]
    core = [("v", 1 << i) for i in range(var.bit_length() - 1)]
    if order == 0:
        return core + data
    return core[:1] + data[:1] + core[1:] + data[1:]


def reduce_scatter(full, order):
    dp, var = lax.axis_size("dp"), lax.axis_size("var")
    places = [("d", 1 << i) for i in reversed(range(dp.bit_length() - 1))]
    places += [("v", 1 << i) for i in reversed(range(var.bit_length() - 1))]
    rows = full.shape[0] // (dp * var)
    value = full.astype(BF16).reshape((2,) * len(places) + (rows,) + full.shape[1:])
    d, v = lax.axis_index("dp"), lax.axis_index("var")
    for stage in stages(order):
        axis = places.index(stage)
        kind, bit = stage
        mine = ((d if kind == "d" else v) // bit) % 2
        keep = lax.dynamic_index_in_dim(value, mine, axis, keepdims=False)
        send = lax.dynamic_index_in_dim(value, 1 - mine, axis, keepdims=False)
        got = swap(send, bit if kind == "d" else 0, bit if kind == "v" else 0)
        value = add_rounded(keep, got)
        places.remove(stage)
    return value.astype(F32)


def reduce_relative(blocks):
    var, dp = lax.axis_size("var"), lax.axis_size("dp")
    value = blocks
    bit = 1
    while bit < var:
        value = value.reshape((value.shape[0] // 2, 2) + value.shape[1:])
        value = add_rounded(value[:, 0], swap(value[:, 1], 0, bit))
        bit *= 2
    value = value[0]
    bit = 1
    while bit < dp:
        value = add_rounded(value, swap(value, bit, 0))
        bit *= 2
    return value.astype(F32)


def gather_relative(value):
    value = value[None]
    bit = 1
    while bit < lax.axis_size("var"):
        value = jnp.concatenate([value, swap(value, 0, bit)], axis=0)
        bit *= 2
    return value


def exchange_relative(blocks):
    return [blocks[0]] + [swap(blocks[k], 0, k) for k in range(1, len(blocks))]


def normalize(values, gains):
    center = values - jnp.mean(values, axis=-1, keepdims=True)
    inverse = lax.rsqrt(jnp.mean(center * center, axis=-1, keepdims=True) + EPSILON)
    normed = center * inverse
    return (normed * gains, normed, inverse)


def normalize_back(upstream, normed, inverse, gains):
    scaled = upstream * gains
    mean_plain = jnp.mean(scaled, axis=-1, keepdims=True)
    mean_mixed = jnp.mean(scaled * normed, axis=-1, keepdims=True)
    return (
        inverse * (scaled - mean_plain - normed * mean_mixed),
        jnp.sum(upstream * normed, axis=0),
    )


def score_table(queries, keys_in, visible, scale):
    scores = (
        jnp.einsum("bqhd,bkhd->bhqk", queries, keys_in, preferred_element_type=F32) * scale
    )
    return jnp.where(visible[:, None, None, :] > 0, scores, -1000000000.0)


def attention(queries, keys_in, values_in, visible, scale):
    scores = score_table(queries, keys_in, visible, scale)
    topmost = jnp.max(scores, axis=-1, keepdims=True)
    raised = jnp.exp(scores - topmost)
    summed = jnp.sum(raised, axis=-1, keepdims=True)
    chances = (raised / summed).astype(BF16)
    mixed = jnp.einsum("bhqk,bkhd->bqhd", chances, values_in, preferred_element_type=F32)
    return (mixed, topmost + jnp.log(summed))


def attention_back(queries, keys_in, values_in, visible, scale, logsum, upstream):
    chances = jnp.exp(score_table(queries, keys_in, visible, scale) - logsum)
    grad_values = jnp.einsum(
        "bhqk,bqhd->bkhd", chances.astype(BF16), upstream, preferred_element_type=F32
    )
    grad_chances = jnp.einsum("bqhd,bkhd->bhqk", upstream, values_in, preferred_element_type=F32)
    centred = grad_chances - jnp.sum(chances * grad_chances, axis=-1, keepdims=True)
    grad_scores = (chances * centred).astype(BF16)
    grad_queries = (
        jnp.einsum("bhqk,bkhd->bqhd", grad_scores, keys_in, preferred_element_type=F32) * scale
    )
    grad_keys = (
        jnp.einsum("bhqk,bqhd->bkhd", grad_scores, queries, preferred_element_type=F32) * scale
    )
    return jnp.stack([grad_queries, grad_keys, grad_values], axis=2)


def visible_of(mask):
    first = (lax.broadcasted_iota(jnp.int32, mask.shape, 1) == 0).astype(jnp.int32)
    return jnp.maximum(mask, first)


def one_hot(indices, size):
    places = lax.broadcasted_iota(jnp.int32, indices.shape + (size,), indices.ndim)
    return (indices[..., None] == places).astype(BF16)


def body(
    img_lo,
    img_hi,
    keep_lo,
    keep_hi,
    mask_lo,
    mask_hi,
    w_embed,
    pos_lo,
    pos_hi,
    ln1_gain,
    w_qkv,
    w_out,
    ln2_gain,
    w_fc1,
    b_fc1,
    w_fc2,
    b_fc2,
    w_head,
    cot_lo,
    cot_hi,
):
    groups = lax.axis_size("var")
    member = lax.axis_index("var")
    lo_group, lo_length = keep_lo.shape
    hi_group, hi_length = keep_hi.shape
    lo_each = lo_group // groups
    hi_each = hi_group // groups
    lo_rows = lo_each * lo_length
    hi_rows = hi_each * hi_length
    features = w_embed.shape[0]
    model_width = w_qkv.shape[0]
    head_dim = model_width // HEADS
    scale = 1.0 / math.sqrt(head_dim)
    visible_lo = visible_of(mask_lo)
    visible_hi = visible_of(mask_hi)
    kept_lo = one_hot(keep_lo, img_lo.shape[1])
    kept_hi = one_hot(keep_hi, img_hi.shape[1])

    def to_rows(lower, upper):
        return jnp.concatenate(
            [
                lower.transpose(1, 0, 2).reshape(features, -1),
                upper.transpose(1, 0, 2).reshape(features, -1),
            ],
            axis=1,
        )

    def for_member(lower, upper, k):
        other = member ^ k
        return to_rows(
            lax.dynamic_slice_in_dim(lower, other * lo_each, lo_each, 0),
            lax.dynamic_slice_in_dim(upper, other * hi_each, hi_each, 0),
        )

    def from_members(pieces):
        stacked = jnp.stack(pieces)
        ordered = jnp.concatenate(
            [lax.dynamic_index_in_dim(stacked, member ^ v, 0) for v in range(groups)], axis=0
        )
        lower = ordered[:, :, :lo_rows].reshape(groups, features, lo_each, lo_length)
        upper = ordered[:, :, lo_rows:].reshape(groups, features, hi_each, hi_length)
        return (
            lower.transpose(0, 2, 1, 3).reshape(lo_group, features, lo_length),
            upper.transpose(0, 2, 1, 3).reshape(hi_group, features, hi_length),
        )

    picked_lo = jnp.einsum(
        "scp,sjp->scj", img_lo.transpose(0, 2, 1), kept_lo, preferred_element_type=F32
    ).astype(BF16)
    picked_hi = jnp.einsum(
        "scp,sjp->scj", img_hi.transpose(0, 2, 1), kept_hi, preferred_element_type=F32
    ).astype(BF16)
    patches = jnp.concatenate(
        exchange_relative([for_member(picked_lo, picked_hi, k) for k in range(groups)]), axis=0
    )
    embed_all = gather_relative(w_embed).reshape(groups * features, model_width)
    head_all = gather_relative(w_head.T).reshape(groups * features, model_width)
    cots = exchange_relative(
        [
            for_member(
                cot_lo.transpose(0, 2, 1) * visible_lo[:, None, :].astype(BF16),
                cot_hi.transpose(0, 2, 1) * visible_hi[:, None, :].astype(BF16),
                k,
            )
            for k in range(groups)
        ]
    )
    grad_pred = jnp.concatenate(cots, axis=0)

    own_keep_lo = lax.dynamic_slice_in_dim(kept_lo, member * lo_each, lo_each, 0)
    own_keep_hi = lax.dynamic_slice_in_dim(kept_hi, member * hi_each, hi_each, 0)
    onehot_lo = own_keep_lo.reshape(lo_rows, -1)
    onehot_hi = own_keep_hi.reshape(hi_rows, -1)
    own_visible_lo = lax.dynamic_slice_in_dim(visible_lo, member * lo_each, lo_each, 0)
    own_visible_hi = lax.dynamic_slice_in_dim(visible_hi, member * hi_each, hi_each, 0)
    own_visible = jnp.concatenate([own_visible_lo.reshape(-1), own_visible_hi.reshape(-1)])

    places = jnp.concatenate([nn(onehot_lo, pos_lo), nn(onehot_hi, pos_hi)], axis=0)
    start_rows = tn(patches, embed_all) + places
    normed_one, plain_one, inverse_one = normalize(start_rows, ln1_gain)
    normed_one = normed_one.astype(BF16)
    triple = nn(normed_one, w_qkv).astype(BF16)
    triple_lo = triple[:lo_rows].reshape(lo_each, lo_length, 3, HEADS, head_dim)
    triple_hi = triple[lo_rows:].reshape(hi_each, hi_length, 3, HEADS, head_dim)
    mixed_lo, logsum_lo = attention(
        triple_lo[:, :, 0], triple_lo[:, :, 1], triple_lo[:, :, 2], own_visible_lo, scale
    )
    mixed_hi, logsum_hi = attention(
        triple_hi[:, :, 0], triple_hi[:, :, 1], triple_hi[:, :, 2], own_visible_hi, scale
    )
    mixed = jnp.concatenate(
        [mixed_lo.reshape(lo_rows, model_width), mixed_hi.reshape(hi_rows, model_width)], axis=0
    ).astype(BF16)
    middle = start_rows + nn(mixed, w_out)
    normed_two, plain_two, inverse_two = normalize(middle, ln2_gain)
    normed_two = normed_two.astype(BF16)
    hidden = nn(normed_two, w_fc1) + b_fc1
    activated, gelu_pull = jax.vjp(lambda values: jax.nn.gelu(values, approximate=False), hidden)
    activated = activated.astype(BF16)

    grad_final = tn(grad_pred, head_all)
    grad_branch = grad_final.astype(BF16)
    grad_b2 = jnp.sum(grad_branch.astype(F32), axis=0)
    grad_fc2 = reduce_scatter(tn(activated, grad_branch), 0)
    grad_hidden = gelu_pull(nt(grad_branch, w_fc2))[0].astype(BF16)
    grad_b1 = jnp.sum(grad_hidden.astype(F32), axis=0)
    grad_fc1 = reduce_scatter(tn(normed_two, grad_hidden), 1)

    final_rows = (middle + (nn(activated, w_fc2) + b_fc2)).astype(BF16)
    outputs = (nt(head_all, final_rows) * own_visible.astype(F32)).astype(BF16)
    pred_lo, pred_hi = from_members(
        exchange_relative([outputs[k * features : (k + 1) * features] for k in range(groups)])
    )
    grad_head = nn(grad_pred, final_rows)

    grad_norm_two, grad_ln2 = normalize_back(
        nt(grad_hidden, w_fc1), plain_two, inverse_two, ln2_gain
    )
    grad_middle = grad_final + grad_norm_two
    grad_attn = grad_middle.astype(BF16)
    grad_out = tn(mixed, grad_attn)
    grad_mixed = nt(grad_attn, w_out).astype(BF16)
    grad_triple_lo = attention_back(
        triple_lo[:, :, 0],
        triple_lo[:, :, 1],
        triple_lo[:, :, 2],
        own_visible_lo,
        scale,
        logsum_lo,
        grad_mixed[:lo_rows].reshape(lo_each, lo_length, HEADS, head_dim),
    )
    grad_triple_hi = attention_back(
        triple_hi[:, :, 0],
        triple_hi[:, :, 1],
        triple_hi[:, :, 2],
        own_visible_hi,
        scale,
        logsum_hi,
        grad_mixed[lo_rows:].reshape(hi_each, hi_length, HEADS, head_dim),
    )
    grad_triple = jnp.concatenate(
        [
            grad_triple_lo.reshape(lo_rows, 3 * model_width),
            grad_triple_hi.reshape(hi_rows, 3 * model_width),
        ],
        axis=0,
    ).astype(BF16)
    grad_qkv = reduce_scatter(tn(normed_one, grad_triple), 0)
    grad_norm_one, grad_ln1 = normalize_back(
        nt(grad_triple, w_qkv), plain_one, inverse_one, ln1_gain
    )
    grad_start = (grad_middle + grad_norm_one).astype(BF16)
    grad_pos_lo = tn(onehot_lo, grad_start[:lo_rows])
    grad_pos_hi = tn(onehot_hi, grad_start[lo_rows:])

    devices = lax.axis_size("dp") * groups
    pieces = [
        value.reshape((devices, -1, model_width)) for value in (grad_out, grad_pos_lo, grad_pos_hi)
    ]
    sides = [value.reshape(devices, -1) for value in (grad_ln1, grad_ln2, grad_b1, grad_b2)]
    width = sum(side.shape[1] for side in sides)
    side_rows = -(-width // model_width)
    sides = jnp.pad(jnp.concatenate(sides, axis=1), ((0, 0), (0, side_rows * model_width - width)))
    pieces.append(sides.reshape(devices, side_rows, model_width))
    counts = [piece.shape[1] for piece in pieces]
    total = sum(counts)
    rest = reduce_scatter(
        jnp.concatenate([p.astype(BF16) for p in pieces], axis=1).reshape(-1, model_width), 1
    )
    grad_out = rest[: counts[0]]
    grad_pos_lo = rest[counts[0] : counts[0] + counts[1]]
    grad_pos_hi = rest[counts[0] + counts[1] : counts[0] + counts[1] + counts[2]]
    sides = rest[total - side_rows :].reshape(-1)
    n1 = model_width // devices
    nf = w_fc1.shape[1] // devices
    grad_ln1 = sides[:n1]
    grad_ln2 = sides[n1 : 2 * n1]
    grad_b1 = sides[2 * n1 : 2 * n1 + nf]
    grad_b2 = sides[2 * n1 + nf : 3 * n1 + nf]

    grad_embed = nn(patches, grad_start)
    both = reduce_relative(
        jnp.concatenate(
            [
                grad_embed.astype(BF16).reshape(groups, features, model_width),
                grad_head.astype(BF16).reshape(groups, features, model_width),
            ],
            axis=1,
        )
    )
    grad_embed = both[:features]
    grad_head = both[features:].T

    rows_grad = nt(embed_all, grad_start).astype(BF16)
    back_lo, back_hi = from_members(
        exchange_relative([rows_grad[k * features : (k + 1) * features] for k in range(groups)])
    )
    grad_img_lo = jnp.einsum("scj,sjp->scp", back_lo, kept_lo, preferred_element_type=F32)
    grad_img_hi = jnp.einsum("scj,sjp->scp", back_hi, kept_hi, preferred_element_type=F32)
    return (
        pred_lo.transpose(0, 2, 1),
        pred_hi.transpose(0, 2, 1),
        grad_img_lo.astype(BF16).transpose(0, 2, 1),
        grad_img_hi.astype(BF16).transpose(0, 2, 1),
        grad_embed,
        grad_pos_lo,
        grad_pos_hi,
        grad_ln1,
        grad_qkv,
        grad_out,
        grad_ln2,
        grad_fc1,
        grad_b1,
        grad_fc2,
        grad_b2,
        grad_head,
    )


def solution(mesh):
    placed = (
        P("dp", None, "var"),
        P("dp", None, "var"),
        P("dp", None),
        P("dp", None),
        P("dp", None),
        P("dp", None),
        P("var", None),
        P(),
        P(),
        P(),
        P(),
        P(),
        P(),
        P(),
        P(),
        P(),
        P(),
        P(None, "var"),
        P("dp", None, "var"),
        P("dp", None, "var"),
    )
    return jax.shard_map(
        body,
        mesh=mesh,
        in_specs=placed,
        out_specs=(
            P("dp", None, "var"),
            P("dp", None, "var"),
            P("dp", None, "var"),
            P("dp", None, "var"),
            P("var", None),
            P(("dp", "var"), None),
            P(("dp", "var"), None),
            P(("dp", "var")),
            P(("dp", "var"), None),
            P(("dp", "var"), None),
            P(("dp", "var")),
            P(("dp", "var"), None),
            P(("dp", "var")),
            P(("dp", "var"), None),
            P(("dp", "var")),
            P(None, "var"),
        ),
        check_vma=False,
    )
```

```python
import functools
import math

import jax
import jax.numpy as jnp
from jax import lax
from jax.experimental import pallas as pl
from jax.experimental.pallas import tpu as pltpu
from jax.sharding import PartitionSpec as P

HEADS = 12
EPSILON = 1e-06
AXES = ("dp", "var")
BF16 = jnp.bfloat16
F32 = jnp.float32
LANES = 128
ROWS = 256
MASKED = -1000000000.0


def dot(left, right, dims):
    return lax.dot_general(left, right, (dims, ((), ())), preferred_element_type=F32)


def nn(left, right):
    return dot(left, right, ((1,), (0,)))


def nt(left, right):
    return dot(left, right, ((1,), (1,)))


def tn(left, right):
    return dot(left, right, ((0,), (0,)))


def shape(dims, dtype):
    return jax.ShapeDtypeStruct(dims, dtype)


def whole(array):
    zeros = (0,) * array.ndim
    return pl.BlockSpec(array.shape, lambda *_: zeros, pipeline_mode=pl.Buffered(1))


def across(rows, width):
    return pl.BlockSpec((rows, width), lambda i, *_: (i, 0))


def along(height, columns):
    return pl.BlockSpec((height, columns), lambda i, *_: (0, i))


def fixed(*dims):
    zeros = (0,) * len(dims)
    return pl.BlockSpec(dims, lambda *_: zeros)


def params(mebibytes):
    return pltpu.CompilerParams(vmem_limit_bytes=mebibytes << 20)


def cost(flops, nbytes):
    return pl.CostEstimate(flops=int(flops), bytes_accessed=int(nbytes), transcendentals=0)


def iota(dims, axis):
    return lax.broadcasted_iota(jnp.int32, dims, axis)


def accumulate(ref, first, value):
    @pl.when(first)
    def _():
        ref[...] = value

    @pl.when(jnp.logical_not(first))
    def _():
        ref[...] += value


def normalize(values):
    center = values - jnp.mean(values, axis=-1, keepdims=True)
    inverse = lax.rsqrt(jnp.mean(center * center, axis=-1, keepdims=True) + EPSILON)
    return center * inverse, inverse


def normalize_back(upstream, normed, inverse, gains):
    scaled = upstream * gains
    mean_plain = jnp.mean(scaled, axis=-1, keepdims=True)
    mean_mixed = jnp.mean(scaled * normed, axis=-1, keepdims=True)
    return inverse * (scaled - mean_plain - normed * mean_mixed)


def gelu_parts(u):
    ratio = 1.0 / (1.0 + (0.3275911 * math.sqrt(0.5)) * jnp.abs(u))
    bell = jnp.exp(-0.5 * u * u)
    series = 0.5 * 1.061405429
    for factor in (-1.453152027, 1.421413741, -0.284496736, 0.254829592):
        series = series * ratio + 0.5 * factor
    tail = series * ratio * bell
    below = jnp.where(u < 0, tail, 1.0 - tail)
    return u * below, below + u * (bell * (1.0 / math.sqrt(2.0 * math.pi)))


class Sizes:
    def __init__(self, keep_lo, keep_hi, w_embed, img_lo, img_hi, groups):
        self.lo_each, self.hi_each = keep_lo[0] // groups, keep_hi[0] // groups
        self.lo_length, self.hi_length = keep_lo[1], keep_hi[1]
        self.features, self.width = w_embed
        self.lo_patches, self.hi_patches = img_lo[1], img_hi[1]
        self.groups = groups
        self.pack = LANES // self.lo_length
        self.lo_tiles = -(-self.lo_each // self.pack)
        self.hi_rows = self.hi_each * self.hi_length
        tiles = self.hi_each + self.lo_tiles
        self.tiles = tiles + tiles % 2
        self.rows = self.tiles * LANES


def sample_tiles(s):
    out = []
    for t in range(s.tiles - s.hi_each):
        first = t * s.pack
        out.append((s.hi_each + t, first, max(0, min(s.pack, s.lo_each - first))))
    return out


def slots(rows, fill, s):
    missing = s.pack - len(rows)
    if missing:
        rows = rows + [jnp.full((1, missing * s.lo_length), fill, rows[0].dtype if rows else jnp.int32)]
    return rows[0] if len(rows) == 1 else jnp.concatenate(rows, axis=1)


def pick_kernel(s, members, member_ref, keep_lo_ref, keep_hi_ref, img_lo_ref, img_hi_ref, *out_refs):
    for k, out_ref in zip(members, out_refs):
        other = member_ref[0] ^ k
        for i in range(s.hi_each):
            at = other * s.hi_each + i
            chosen = iota((s.hi_patches, LANES), 0) == keep_hi_ref[pl.ds(at, 1), :]
            got = nn(img_hi_ref[at], jnp.where(chosen, 1.0, 0.0).astype(BF16))
            out_ref[:, i * LANES : (i + 1) * LANES] = got.astype(BF16)
        for tile, first, count in sample_tiles(s):
            parts = []
            for j in range(count):
                at = other * s.lo_each + first + j
                chosen = iota((s.lo_patches, s.lo_length), 0) == keep_lo_ref[pl.ds(at, 1), :]
                parts.append(nn(img_lo_ref[at], jnp.where(chosen, 1.0, 0.0).astype(BF16)))
            if count < s.pack:
                parts.append(jnp.zeros((s.features, (s.pack - count) * s.lo_length), F32))
            joined = jnp.concatenate(parts, axis=1) if len(parts) > 1 else parts[0]
            out_ref[:, tile * LANES : (tile + 1) * LANES] = joined.astype(BF16)


def pick(s, members, member, keep_lo, keep_hi, img_lo, img_hi):
    args = (keep_lo, keep_hi, img_lo, img_hi)
    return pl.pallas_call(
        functools.partial(pick_kernel, s, members),
        grid_spec=pltpu.PrefetchScalarGridSpec(
            num_scalar_prefetch=1,
            grid=(1,),
            in_specs=[whole(a) for a in args],
            out_specs=[fixed(s.features, s.rows)] * len(members),
        ),
        out_shape=[shape((s.features, s.rows), BF16)] * len(members),
        compiler_params=params(24),
        cost_estimate=cost(2e9, 4e6),
    )(member, *args)


def stage_kernel(s, member_ref, keep_lo_ref, keep_hi_ref, mask_lo_ref, mask_hi_ref, cot_lo_ref, cot_hi_ref, keep_ref, seen_ref, *out_refs):
    eye = jnp.where(iota((s.features, s.features), 0) == iota((s.features, s.features), 1), 1.0, 0.0).astype(BF16)
    first_hi = (iota((1, s.hi_length), 1) == 0).astype(jnp.int32)
    first_lo = (iota((1, s.lo_length), 1) == 0).astype(jnp.int32)
    for k, out_ref in enumerate(out_refs):
        other = member_ref[0] ^ k
        for i in range(s.hi_each):
            at = other * s.hi_each + i
            keep_ref[k, i : i + 1, :] = keep_hi_ref[pl.ds(at, 1), :]
            out_ref[:, i * LANES : (i + 1) * LANES] = cot_hi_ref[at]
            if k == 0:
                seen_ref[i : i + 1, :] = jnp.maximum(mask_hi_ref[pl.ds(at, 1), :], first_hi).astype(F32)
        for tile, first, count in sample_tiles(s):
            begin = other * s.lo_each + first
            keep_ref[k, tile : tile + 1, :] = slots([keep_lo_ref[pl.ds(begin + j, 1), :] for j in range(count)], -1, s)
            if k == 0:
                seen = [jnp.maximum(mask_lo_ref[pl.ds(begin + j, 1), :], first_lo) for j in range(count)]
                seen_ref[tile : tile + 1, :] = slots(seen, 0, s).astype(F32)
            where = slice(tile * LANES, (tile + 1) * LANES)
            if count < s.pack:
                out_ref[:, where] = jnp.zeros((s.features, LANES), BF16)
            if count:
                size = count * s.lo_length
                start = pl.multiple_of(begin * s.lo_length, s.lo_length)
                out_ref[:, tile * LANES : tile * LANES + size] = nt(eye, cot_lo_ref[pl.ds(start, size), :]).astype(BF16)


def stage(s, member, keep_lo, keep_hi, mask_lo, mask_hi, cot_lo, cot_hi):
    args = (keep_lo, keep_hi, mask_lo, mask_hi, cot_lo, cot_hi)
    return pl.pallas_call(
        functools.partial(stage_kernel, s),
        grid_spec=pltpu.PrefetchScalarGridSpec(
            num_scalar_prefetch=1,
            grid=(1,),
            in_specs=[whole(a) for a in args],
            out_specs=[fixed(s.groups, s.tiles, LANES), fixed(s.tiles, LANES)]
            + [fixed(s.features, s.rows)] * s.groups,
        ),
        out_shape=[shape((s.groups, s.tiles, LANES), jnp.int32), shape((s.tiles, LANES), F32)]
        + [shape((s.features, s.rows), BF16)] * s.groups,
        compiler_params=params(24),
        cost_estimate=cost(1e8, 4e6),
    )(member, *args)


def chosen_rows(s, keep_ref, tile, patches, wanted_hi):
    row = keep_ref[pl.ds(tile, 1), :]
    is_hi = tile < s.hi_each
    row = jnp.where(is_hi if wanted_hi else jnp.logical_not(is_hi), row, -1)
    return jnp.where(iota((patches, LANES), 0) == row, 1.0, 0.0).astype(BF16)


def pair_masks():
    lane = iota((1, LANES), 1)
    low = jnp.where(lane < LANES // 2, 1.0, 0.0).astype(BF16)
    high = jnp.where(lane < LANES // 2, 0.0, 1.0).astype(BF16)
    return low, high


def doubled(block, masks):
    return jnp.concatenate([block * masks[0], block * masks[1]], axis=0)


def allowed(s, seen_ref, tile):
    bits = jnp.where(tile < s.hi_each, s.hi_length.bit_length() - 1, s.lo_length.bit_length() - 1)
    same = (iota((LANES, LANES), 0) >> bits) == (iota((LANES, LANES), 1) >> bits)
    open_to = jnp.logical_and(same, seen_ref[pl.ds(tile, 1), :] > 0)
    return jnp.concatenate([open_to, open_to], axis=0)


def forward_kernel(s, heads, keep_ref, seen_ref, p0, p1, p2, p3, w0, w1, w2, w3, pos_lo_ref, pos_hi_ref, gain1_ref, wqkv_ref, gain2_ref, wout_ref, x0_ref, a_ref, qkv_ref, probs_ref, mixed_ref, x1_ref, b_ref):
    step = pl.program_id(0)
    per = ROWS // LANES
    width = s.width
    picked = jnp.concatenate([p[...] for p in (p0, p1, p2, p3)], axis=0)
    embed = jnp.concatenate([w[: s.features, :] for w in (w0, w1, w2, w3)], axis=0)
    hot_hi = jnp.concatenate([chosen_rows(s, keep_ref, step * per + j, s.hi_patches, True) for j in range(per)], axis=1)
    hot_lo = jnp.concatenate([chosen_rows(s, keep_ref, step * per + j, s.lo_patches, False) for j in range(per)], axis=1)
    start = tn(picked, embed) + (tn(hot_hi, pos_hi_ref[...]) + tn(hot_lo, pos_lo_ref[...]))
    x0_ref[...] = start
    normed, _ = normalize(start)
    normed = (normed * gain1_ref[...]).astype(BF16)
    a_ref[...] = normed
    for c in range(3):
        part = slice(c * width, (c + 1) * width)
        qkv_ref[:, part] = nn(normed, wqkv_ref[:, part]).astype(BF16)
    masks = pair_masks()
    scale = 1.0 / math.sqrt(width // heads)
    for j in range(per):
        rows = slice(j * LANES, (j + 1) * LANES)
        ok = allowed(s, seen_ref, step * per + j)
        for h in range(width // LANES):
            at = h * LANES
            q = qkv_ref[rows, at : at + LANES]
            k = qkv_ref[rows, width + at : width + at + LANES]
            v = qkv_ref[rows, 2 * width + at : 2 * width + at + LANES]
            scores = nt(doubled(q, masks), k) * scale
            scores = jnp.where(ok, scores, MASKED)
            raised = jnp.exp(scores - jnp.max(scores, axis=-1, keepdims=True))
            probs = raised / jnp.sum(raised, axis=-1, keepdims=True)
            probs_ref[j, h] = probs
            rounded = probs.astype(BF16)
            wide = jnp.concatenate([rounded[:LANES], rounded[LANES:]], axis=1)
            mixed_ref[rows, at : at + LANES] = nn(wide, doubled(v, masks)).astype(BF16)
    middle = start + nn(mixed_ref[...], wout_ref[...])
    x1_ref[...] = middle
    normed, _ = normalize(middle)
    b_ref[...] = (normed * gain2_ref[...]).astype(BF16)


def forward(s, heads, keep, seen, picked, weights, pos_lo, pos_hi, gain1, wqkv, gain2, wout):
    width, rows = s.width, s.rows
    per, pairs = ROWS // LANES, width // LANES
    return pl.pallas_call(
        functools.partial(forward_kernel, s, heads),
        grid=(rows // ROWS,),
        in_specs=[whole(keep), whole(seen)]
        + [along(s.features, ROWS)] * 4
        + [whole(w) for w in weights]
        + [whole(a) for a in (pos_lo, pos_hi, gain1, wqkv, gain2, wout)],
        out_specs=[
            across(ROWS, width),
            across(ROWS, width),
            across(ROWS, 3 * width),
            pl.BlockSpec((per, pairs, 2 * LANES, LANES), lambda i: (i, 0, 0, 0)),
            across(ROWS, width),
            across(ROWS, width),
            across(ROWS, width),
        ],
        out_shape=[
            shape((rows, width), F32),
            shape((rows, width), BF16),
            shape((rows, 3 * width), BF16),
            shape((s.tiles, pairs, 2 * LANES, LANES), F32),
            shape((rows, width), BF16),
            shape((rows, width), F32),
            shape((rows, width), BF16),
        ],
        compiler_params=params(40),
        cost_estimate=cost(1.5e10, 3e7),
    )(keep, seen, *picked, *weights, pos_lo, pos_hi, gain1, wqkv, gain2, wout)


def upstream_kernel(s, seen_ref, c0, c1, c2, c3, w0, w1, w2, w3, gpred_ref, gm_ref, gb2_ref):
    step = pl.program_id(0)
    per = ROWS // LANES
    seen = jnp.concatenate([seen_ref[pl.ds(step * per + j, 1), :] for j in range(per)], axis=1).astype(BF16)
    grads = jnp.concatenate([c[...] for c in (c0, c1, c2, c3)], axis=0) * seen
    gpred_ref[...] = grads
    head = jnp.concatenate([w[s.features :, :] for w in (w0, w1, w2, w3)], axis=0)
    rounded = tn(grads, head).astype(BF16)
    gm_ref[...] = rounded
    accumulate(gb2_ref, step == 0, jnp.sum(rounded.astype(F32), axis=0, keepdims=True))


def upstream(s, seen, cots, weights):
    rows, width = s.rows, s.width
    high = s.groups * s.features
    return pl.pallas_call(
        functools.partial(upstream_kernel, s),
        grid=(rows // ROWS,),
        in_specs=[whole(seen)] + [along(s.features, ROWS)] * 4 + [whole(w) for w in weights],
        out_specs=[along(high, ROWS), across(ROWS, width), fixed(1, width)],
        out_shape=[shape((high, rows), BF16), shape((rows, width), BF16), shape((1, width), F32)],
        compiler_params=params(16),
        cost_estimate=cost(1e9, 4e6),
    )(seen, *cots, *weights)


def hidden_kernel(sub, b_ref, gm_ref, w1_ref, b1_ref, w2_ref, z_ref, gu_ref, gb1_ref):
    w1, w2, bias = w1_ref[...], w2_ref[...], b1_ref[...]
    total = None
    for i in range(b_ref.shape[0] // sub):
        rows = slice(i * sub, (i + 1) * sub)
        u = nn(b_ref[rows, :], w1) + bias
        upward = nt(gm_ref[rows, :], w2)
        z, slope = gelu_parts(u)
        z_ref[rows, :] = z.astype(BF16)
        gu = (upward * slope).astype(BF16)
        gu_ref[rows, :] = gu
        part = jnp.sum(gu.astype(F32), axis=0, keepdims=True)
        total = part if total is None else total + part
    gb1_ref[...] = total


def hidden(b, gm, w1, b1, w2, columns=768, sub=256):
    rows, width = b.shape
    inner = w1.shape[1]
    return pl.pallas_call(
        functools.partial(hidden_kernel, sub),
        grid=(inner // columns,),
        in_specs=[
            whole(b),
            whole(gm),
            along(width, columns),
            along(1, columns),
            across(columns, width),
        ],
        out_specs=[along(rows, columns), along(rows, columns), along(1, columns)],
        out_shape=[shape((rows, inner), BF16), shape((rows, inner), BF16), shape((1, inner), F32)],
        compiler_params=params(40),
        cost_estimate=cost(2e10, 2.5e7),
    )(b, gm, w1, b1, w2)


def weight_kernel(left_ref, right_ref, out_ref):
    out_ref[...] = tn(left_ref[...], right_ref[...]).astype(BF16)


def weight_grad(left, right, tall, broad):
    rows = left.shape[0]
    m, n = left.shape[1], right.shape[1]
    return pl.pallas_call(
        weight_kernel,
        grid=(m // tall, n // broad),
        in_specs=[
            pl.BlockSpec((rows, tall), lambda i, j: (0, i)),
            pl.BlockSpec((rows, broad), lambda i, j: (0, j)),
        ],
        out_specs=pl.BlockSpec((tall, broad), lambda i, j: (i, j)),
        out_shape=shape((m, n), BF16),
        compiler_params=params(32),
        cost_estimate=cost(2 * rows * m * n, 2 * (rows * (m + n) + m * n)),
    )(left, right)


def middle_kernel(s, seen_ref, x1_ref, z_ref, gu_ref, gm_ref, gpred_ref, mixed_ref, w1_ref, w2_ref, b2_ref, gain2_ref, wout_ref, h0, h1, h2, h3, o0, o1, o2, o3, g1_ref, go_ref, ghead_ref, gln2_ref, gout_ref):
    step = pl.program_id(0)
    per = ROWS // LANES
    first = step == 0
    middle = x1_ref[...]
    final = (middle + (nn(z_ref[...], w2_ref[...]) + b2_ref[...])).astype(BF16)
    seen = jnp.concatenate([seen_ref[pl.ds(step * per + j, 1), :] for j in range(per)], axis=1)
    for head, out in zip((h0, h1, h2, h3), (o0, o1, o2, o3)):
        out[...] = (nt(head[s.features :, :], final) * seen).astype(BF16)
    accumulate(ghead_ref, first, nn(gpred_ref[...], final))
    upward = nt(gu_ref[...], w1_ref[...])
    normed, inverse = normalize(middle)
    accumulate(gln2_ref, first, jnp.sum(upward * normed, axis=0, keepdims=True))
    grad = gm_ref[...].astype(F32) + normalize_back(upward, normed, inverse, gain2_ref[...])
    g1_ref[...] = grad
    rounded = grad.astype(BF16)
    go_ref[...] = nt(rounded, wout_ref[...]).astype(BF16)
    accumulate(gout_ref, first, tn(mixed_ref[...], rounded))


def middle(s, seen, x1, z, gu, gm, gpred, mixed, w1, w2, b2, gain2, wout, weights):
    rows, width = s.rows, s.width
    inner = w1.shape[1]
    high = s.groups * s.features
    return pl.pallas_call(
        functools.partial(middle_kernel, s),
        grid=(rows // ROWS,),
        in_specs=[
            whole(seen),
            across(ROWS, width),
            across(ROWS, inner),
            across(ROWS, inner),
            across(ROWS, width),
            along(high, ROWS),
            across(ROWS, width),
        ]
        + [whole(a) for a in (w1, w2, b2, gain2, wout, *weights)],
        out_specs=[along(s.features, ROWS)] * 4
        + [
            across(ROWS, width),
            across(ROWS, width),
            fixed(high, width),
            fixed(1, width),
            fixed(width, width),
        ],
        out_shape=[shape((s.features, rows), BF16)] * 4
        + [
            shape((rows, width), F32),
            shape((rows, width), BF16),
            shape((high, width), F32),
            shape((1, width), F32),
            shape((width, width), F32),
        ],
        compiler_params=params(44),
        cost_estimate=cost(1.5e10, 3e7),
    )(seen, x1, z, gu, gm, gpred, mixed, w1, w2, b2, gain2, wout, *weights)


def backward_kernel(s, heads, keep_ref, qkv_ref, probs_ref, go_ref, x0_ref, g1_ref, p0, p1, p2, p3, wqkv_ref, gain1_ref, w0, w1, w2, w3, gqkv_ref, o0, o1, o2, o3, gln1_ref, glo_ref, ghi_ref, gembed_ref):
    step = pl.program_id(0)
    per = ROWS // LANES
    width = s.width
    first = step == 0
    masks = pair_masks()
    scale = 1.0 / math.sqrt(width // heads)
    for j in range(per):
        rows = slice(j * LANES, (j + 1) * LANES)
        for h in range(width // LANES):
            at = h * LANES
            q = doubled(qkv_ref[rows, at : at + LANES], masks)
            k = doubled(qkv_ref[rows, width + at : width + at + LANES], masks)
            v = qkv_ref[rows, 2 * width + at : 2 * width + at + LANES]
            out = doubled(go_ref[rows, at : at + LANES], masks)
            probs = probs_ref[j, h]
            upward = nt(out, v)
            centred = upward - jnp.sum(probs * upward, axis=-1, keepdims=True)
            grads = (probs * centred).astype(BF16)
            wide = jnp.concatenate([grads[:LANES], grads[LANES:]], axis=1)
            gqkv_ref[rows, at : at + LANES] = (nn(wide, k) * scale).astype(BF16)
            gqkv_ref[rows, width + at : width + at + LANES] = (tn(grads, q) * scale).astype(BF16)
            gqkv_ref[rows, 2 * width + at : 2 * width + at + LANES] = tn(probs.astype(BF16), out).astype(BF16)
    upward = nt(gqkv_ref[...], wqkv_ref[...])
    normed, inverse = normalize(x0_ref[...])
    accumulate(gln1_ref, first, jnp.sum(upward * normed, axis=0, keepdims=True))
    grad = (g1_ref[...] + normalize_back(upward, normed, inverse, gain1_ref[...])).astype(BF16)
    for weight, out in zip((w0, w1, w2, w3), (o0, o1, o2, o3)):
        out[...] = nt(weight[: s.features, :], grad).astype(BF16)
    hot_hi = jnp.concatenate([chosen_rows(s, keep_ref, step * per + j, s.hi_patches, True) for j in range(per)], axis=1)
    hot_lo = jnp.concatenate([chosen_rows(s, keep_ref, step * per + j, s.lo_patches, False) for j in range(per)], axis=1)
    accumulate(ghi_ref, first, nn(hot_hi, grad))
    accumulate(glo_ref, first, nn(hot_lo, grad))
    picked = jnp.concatenate([p[...] for p in (p0, p1, p2, p3)], axis=0)
    accumulate(gembed_ref, first, nn(picked, grad))


def backward(s, heads, keep, qkv, probs, go, x0, g1, picked, wqkv, gain1, weights):
    rows, width = s.rows, s.width
    per, pairs = ROWS // LANES, width // LANES
    high = s.groups * s.features
    return pl.pallas_call(
        functools.partial(backward_kernel, s, heads),
        grid=(rows // ROWS,),
        in_specs=[
            whole(keep),
            across(ROWS, 3 * width),
            pl.BlockSpec((per, pairs, 2 * LANES, LANES), lambda i: (i, 0, 0, 0)),
            across(ROWS, width),
            across(ROWS, width),
            across(ROWS, width),
        ]
        + [along(s.features, ROWS)] * 4
        + [whole(a) for a in (wqkv, gain1, *weights)],
        out_specs=[across(ROWS, 3 * width)]
        + [along(s.features, ROWS)] * 4
        + [
            fixed(1, width),
            fixed(s.lo_patches, width),
            fixed(s.hi_patches, width),
            fixed(high, width),
        ],
        out_shape=[shape((rows, 3 * width), BF16)]
        + [shape((s.features, rows), BF16)] * 4
        + [
            shape((1, width), F32),
            shape((s.lo_patches, width), F32),
            shape((s.hi_patches, width), F32),
            shape((high, width), F32),
        ],
        compiler_params=params(44),
        cost_estimate=cost(1.5e10, 3e7),
    )(keep, qkv, probs, go, x0, g1, *picked, wqkv, gain1, *weights)


def place_kernel(s, member_ref, keep_ref, r0, r1, r2, r3, lo_ref, hi_ref):
    lane_sample = iota((1, LANES), 1) // s.lo_length
    for k, got_ref in enumerate((r0, r1, r2, r3)):
        other = member_ref[0] ^ k
        for i in range(s.hi_each):
            chosen = iota((s.hi_patches, LANES), 0) == keep_ref[k, i : i + 1, :]
            hot = jnp.where(chosen, 1.0, 0.0).astype(BF16)
            hi_ref[other * s.hi_each + i] = nt(got_ref[:, i * LANES : (i + 1) * LANES], hot).astype(BF16)
        for tile, first, count in sample_tiles(s):
            got = got_ref[:, tile * LANES : (tile + 1) * LANES]
            for j in range(count):
                row = jnp.where(lane_sample == j, keep_ref[k, tile : tile + 1, :], -1)
                hot = jnp.where(iota((s.lo_patches, LANES), 0) == row, 1.0, 0.0).astype(BF16)
                lo_ref[other * s.lo_each + first + j] = nt(got, hot).astype(BF16)


def place(s, member, keep, blocks):
    lo = s.groups * s.lo_each
    hi = s.groups * s.hi_each
    return pl.pallas_call(
        functools.partial(place_kernel, s),
        grid_spec=pltpu.PrefetchScalarGridSpec(
            num_scalar_prefetch=1,
            grid=(1,),
            in_specs=[whole(keep)] + [whole(b) for b in blocks],
            out_specs=[fixed(lo, s.features, s.lo_patches), fixed(hi, s.features, s.hi_patches)],
        ),
        out_shape=[
            shape((lo, s.features, s.lo_patches), BF16),
            shape((hi, s.features, s.hi_patches), BF16),
        ],
        compiler_params=params(24),
        cost_estimate=cost(2e9, 4e6),
    )(member, keep, *blocks)


def predict_kernel(s, member_ref, r0, r1, r2, r3, lo_ref, hi_ref):
    eye = jnp.where(iota((s.features, s.features), 0) == iota((s.features, s.features), 1), 1.0, 0.0).astype(BF16)
    for k, got_ref in enumerate((r0, r1, r2, r3)):
        other = member_ref[0] ^ k
        for i in range(s.hi_each):
            hi_ref[other * s.hi_each + i] = got_ref[:, i * LANES : (i + 1) * LANES]
        for tile, first, count in sample_tiles(s):
            if count:
                size = count * s.lo_length
                turned = tn(got_ref[:, tile * LANES : (tile + 1) * LANES], eye).astype(BF16)
                start = pl.multiple_of((other * s.lo_each + first) * s.lo_length, s.lo_length)
                lo_ref[pl.ds(start, size), :] = turned[:size]


def predict(s, member, blocks):
    lo = s.groups * s.lo_each * s.lo_length
    hi = s.groups * s.hi_each
    return pl.pallas_call(
        functools.partial(predict_kernel, s),
        grid_spec=pltpu.PrefetchScalarGridSpec(
            num_scalar_prefetch=1,
            grid=(1,),
            in_specs=[whole(b) for b in blocks],
            out_specs=[fixed(lo, s.features), fixed(hi, s.features, s.hi_length)],
        ),
        out_shape=[shape((lo, s.features), BF16), shape((hi, s.features, s.hi_length), BF16)],
        compiler_params=params(16),
        cost_estimate=cost(1e8, 3e6),
    )(member, *blocks)


def swap(value, data_bit, var_bit):
    dp, var = lax.axis_size("dp"), lax.axis_size("var")
    pairs = [
        (d * var + v, (d ^ data_bit) * var + (v ^ var_bit)) for d in range(dp) for v in range(var)
    ]
    return lax.ppermute(value, AXES, pairs)


def add_rounded(left, right):
    return (left.astype(F32) + right.astype(F32)).astype(BF16)


def stages(order):
    dp, var = lax.axis_size("dp"), lax.axis_size("var")
    data = [("d", 1 << i) for i in range(dp.bit_length() - 1)]
    core = [("v", 1 << i) for i in range(var.bit_length() - 1)]
    if order == 0:
        return core + data
    return core[:1] + data[:1] + core[1:] + data[1:]


def reduce_scatter(full, order):
    dp, var = lax.axis_size("dp"), lax.axis_size("var")
    places = [("d", 1 << i) for i in reversed(range(dp.bit_length() - 1))]
    places += [("v", 1 << i) for i in reversed(range(var.bit_length() - 1))]
    rows = full.shape[0] // (dp * var)
    value = full.astype(BF16).reshape((2,) * len(places) + (rows,) + full.shape[1:])
    d, v = lax.axis_index("dp"), lax.axis_index("var")
    for stage_of in stages(order):
        axis = places.index(stage_of)
        kind, bit = stage_of
        mine = ((d if kind == "d" else v) // bit) % 2
        keep = lax.dynamic_index_in_dim(value, mine, axis, keepdims=False)
        send = lax.dynamic_index_in_dim(value, 1 - mine, axis, keepdims=False)
        got = swap(send, bit if kind == "d" else 0, bit if kind == "v" else 0)
        value = add_rounded(keep, got)
        places.remove(stage_of)
    return value.astype(F32)


def reduce_relative(blocks):
    var, dp = lax.axis_size("var"), lax.axis_size("dp")
    value = blocks
    bit = 1
    while bit < var:
        value = value.reshape((value.shape[0] // 2, 2) + value.shape[1:])
        value = add_rounded(value[:, 0], swap(value[:, 1], 0, bit))
        bit *= 2
    value = value[0]
    bit = 1
    while bit < dp:
        value = add_rounded(value, swap(value, bit, 0))
        bit *= 2
    return value.astype(F32)


def exchange_relative(blocks):
    return [blocks[0]] + [swap(blocks[k], 0, k) for k in range(1, len(blocks))]


def body(
    img_lo,
    img_hi,
    keep_lo,
    keep_hi,
    mask_lo,
    mask_hi,
    w_embed,
    pos_lo,
    pos_hi,
    ln1_gain,
    w_qkv,
    w_out,
    ln2_gain,
    w_fc1,
    b_fc1,
    w_fc2,
    b_fc2,
    w_head,
    cot_lo,
    cot_hi,
):
    groups = lax.axis_size("var")
    devices = lax.axis_size("dp") * groups
    member = lax.axis_index("var").astype(jnp.int32).reshape(1)
    s = Sizes(keep_lo.shape, keep_hi.shape, w_embed.shape, img_lo.shape, img_hi.shape, groups)
    features, width = s.features, s.width
    gain1, gain2 = ln1_gain.reshape(1, -1), ln2_gain.reshape(1, -1)
    img_lo_t, img_hi_t = img_lo.transpose(0, 2, 1), img_hi.transpose(0, 2, 1)

    own = jnp.concatenate([w_embed, w_head.T], axis=0)
    crossed = swap(own, 0, 2)
    weights = [own, swap(own, 0, 1), crossed, swap(crossed, 0, 1)]
    sent = pick(s, (1, 2, 3), member, keep_lo, keep_hi, img_lo_t, img_hi_t)
    picked = [swap(value, 0, k + 1) for k, value in enumerate(sent)]
    picked = [*pick(s, (0,), member, keep_lo, keep_hi, img_lo_t, img_hi_t), *picked]
    keep, seen, *cots = stage(
        s,
        member,
        keep_lo,
        keep_hi,
        mask_lo,
        mask_hi,
        cot_lo.reshape(-1, features),
        cot_hi.transpose(0, 2, 1),
    )
    cots = exchange_relative(cots)
    own_keep = keep[0]
    x0, a, qkv, probs, mixed, x1, b = forward(
        s, HEADS, own_keep, seen, picked, weights, pos_lo, pos_hi, gain1, w_qkv, gain2, w_out
    )
    gpred, gm, grad_b2 = upstream(s, seen, cots, weights)
    z, gu, grad_b1 = hidden(b, gm, w_fc1, b_fc1.reshape(1, -1), w_fc2)
    grad_fc2 = reduce_scatter(weight_grad(z, gm, 768, width), 0)
    grad_fc1 = reduce_scatter(weight_grad(b, gu, width, 1024), 1)
    *preds, g1, go, grad_head, grad_ln2, grad_out = middle(
        s,
        seen,
        x1,
        z,
        gu,
        gm,
        gpred,
        mixed,
        w_fc1,
        w_fc2,
        b_fc2.reshape(1, -1),
        gain2,
        w_out,
        weights,
    )
    pred_lo, pred_hi = predict(s, member, exchange_relative(preds))
    gqkv, *blocks, grad_ln1, grad_pos_lo, grad_pos_hi, grad_embed = backward(
        s, HEADS, own_keep, qkv, probs, go, x0, g1, picked, w_qkv, gain1, weights
    )
    grad_qkv = reduce_scatter(weight_grad(a, gqkv, width, 768), 0)
    grad_img_lo, grad_img_hi = place(s, member, keep, exchange_relative(blocks))

    pieces = [
        value.reshape((devices, -1, width)) for value in (grad_out, grad_pos_lo, grad_pos_hi)
    ]
    sides = [value.reshape(devices, -1) for value in (grad_ln1, grad_ln2, grad_b1, grad_b2)]
    length = sum(side.shape[1] for side in sides)
    side_rows = -(-length // width)
    sides = jnp.pad(jnp.concatenate(sides, axis=1), ((0, 0), (0, side_rows * width - length)))
    pieces.append(sides.reshape(devices, side_rows, width))
    counts = [piece.shape[1] for piece in pieces]
    total = sum(counts)
    rest = reduce_scatter(
        jnp.concatenate([p.astype(BF16) for p in pieces], axis=1).reshape(-1, width), 1
    )
    grad_out = rest[: counts[0]]
    grad_pos_lo = rest[counts[0] : counts[0] + counts[1]]
    grad_pos_hi = rest[counts[0] + counts[1] : counts[0] + counts[1] + counts[2]]
    sides = rest[total - side_rows :].reshape(-1)
    n1 = width // devices
    nf = w_fc1.shape[1] // devices
    grad_ln1 = sides[:n1]
    grad_ln2 = sides[n1 : 2 * n1]
    grad_b1 = sides[2 * n1 : 2 * n1 + nf]
    grad_b2 = sides[2 * n1 + nf : 3 * n1 + nf]

    both = reduce_relative(
        jnp.concatenate(
            [
                grad_embed.astype(BF16).reshape(groups, features, width),
                grad_head.astype(BF16).reshape(groups, features, width),
            ],
            axis=1,
        )
    )
    grad_embed = both[:features]
    grad_head = both[features:].T
    return (
        pred_lo.reshape(cot_lo.shape),
        pred_hi.transpose(0, 2, 1),
        grad_img_lo.transpose(0, 2, 1),
        grad_img_hi.transpose(0, 2, 1),
        grad_embed,
        grad_pos_lo,
        grad_pos_hi,
        grad_ln1,
        grad_qkv,
        grad_out,
        grad_ln2,
        grad_fc1,
        grad_b1,
        grad_fc2,
        grad_b2,
        grad_head,
    )


def solution(mesh):
    placed = (
        P("dp", None, "var"),
        P("dp", None, "var"),
        P("dp", None),
        P("dp", None),
        P("dp", None),
        P("dp", None),
        P("var", None),
        P(),
        P(),
        P(),
        P(),
        P(),
        P(),
        P(),
        P(),
        P(),
        P(),
        P(None, "var"),
        P("dp", None, "var"),
        P("dp", None, "var"),
    )
    return jax.shard_map(
        body,
        mesh=mesh,
        in_specs=placed,
        out_specs=(
            P("dp", None, "var"),
            P("dp", None, "var"),
            P("dp", None, "var"),
            P("dp", None, "var"),
            P("var", None),
            P(("dp", "var"), None),
            P(("dp", "var"), None),
            P(("dp", "var")),
            P(("dp", "var"), None),
            P(("dp", "var"), None),
            P(("dp", "var")),
            P(("dp", "var"), None),
            P(("dp", "var")),
            P(("dp", "var"), None),
            P(("dp", "var")),
            P(None, "var"),
        ),
        check_vma=False,
    )
```

```python
import functools
import math

import jax
import jax.numpy as jnp
from jax import lax
from jax.experimental import pallas as pl
from jax.experimental.pallas import tpu as pltpu
from jax.sharding import PartitionSpec as P

HEADS = 12
EPSILON = 1e-06
AXES = ("dp", "var")
BF16 = jnp.bfloat16
F32 = jnp.float32
LANES = 128
ROWS = 256
MASKED = -1000000000.0


def dot(left, right, dims):
    return lax.dot_general(left, right, (dims, ((), ())), preferred_element_type=F32)


def nn(left, right):
    return dot(left, right, ((1,), (0,)))


def nt(left, right):
    return dot(left, right, ((1,), (1,)))


def tn(left, right):
    return dot(left, right, ((0,), (0,)))


def shape(dims, dtype):
    return jax.ShapeDtypeStruct(dims, dtype)


def whole(array):
    zeros = (0,) * array.ndim
    return pl.BlockSpec(array.shape, lambda *_: zeros, pipeline_mode=pl.Buffered(1))


def across(rows, width):
    return pl.BlockSpec((rows, width), lambda i, *_: (i, 0))


def along(height, columns):
    return pl.BlockSpec((height, columns), lambda i, *_: (0, i))


def fixed(*dims):
    zeros = (0,) * len(dims)
    return pl.BlockSpec(dims, lambda *_: zeros)


def params(mebibytes):
    return pltpu.CompilerParams(vmem_limit_bytes=mebibytes << 20)


def cost(flops, nbytes):
    return pl.CostEstimate(flops=int(flops), bytes_accessed=int(nbytes), transcendentals=0)


def iota(dims, axis):
    return lax.broadcasted_iota(jnp.int32, dims, axis)


def accumulate(ref, first, value):
    @pl.when(first)
    def _():
        ref[...] = value

    @pl.when(jnp.logical_not(first))
    def _():
        ref[...] += value


def normalize(values):
    center = values - jnp.mean(values, axis=-1, keepdims=True)
    inverse = lax.rsqrt(jnp.mean(center * center, axis=-1, keepdims=True) + EPSILON)
    return center * inverse, inverse


def normalize_back(upstream, normed, inverse, gains):
    scaled = upstream * gains
    mean_plain = jnp.mean(scaled, axis=-1, keepdims=True)
    mean_mixed = jnp.mean(scaled * normed, axis=-1, keepdims=True)
    return inverse * (scaled - mean_plain - normed * mean_mixed)


def gelu_parts(u):
    ratio = 1.0 / (1.0 + (0.3275911 * math.sqrt(0.5)) * jnp.abs(u))
    bell = jnp.exp(-0.5 * u * u)
    series = 0.5 * 1.061405429
    for factor in (-1.453152027, 1.421413741, -0.284496736, 0.254829592):
        series = series * ratio + 0.5 * factor
    tail = series * ratio * bell
    below = jnp.where(u < 0, tail, 1.0 - tail)
    return u * below, below + u * (bell * (1.0 / math.sqrt(2.0 * math.pi)))


class Sizes:
    def __init__(self, keep_lo, keep_hi, w_embed, img_lo, img_hi, groups):
        self.lo_each, self.hi_each = keep_lo[0] // groups, keep_hi[0] // groups
        self.lo_length, self.hi_length = keep_lo[1], keep_hi[1]
        self.features, self.width = w_embed
        self.lo_patches, self.hi_patches = img_lo[1], img_hi[1]
        self.groups = groups
        self.pack = LANES // self.lo_length
        self.lo_tiles = -(-self.lo_each // self.pack)
        self.hi_rows = self.hi_each * self.hi_length
        tiles = self.hi_each + self.lo_tiles
        self.tiles = tiles + tiles % 2
        self.rows = self.tiles * LANES


def sample_tiles(s):
    out = []
    for t in range(s.tiles - s.hi_each):
        first = t * s.pack
        out.append((s.hi_each + t, first, max(0, min(s.pack, s.lo_each - first))))
    return out


def slots(rows, fill, s):
    missing = s.pack - len(rows)
    if missing:
        rows = rows + [jnp.full((1, missing * s.lo_length), fill, rows[0].dtype if rows else jnp.int32)]
    return rows[0] if len(rows) == 1 else jnp.concatenate(rows, axis=1)


def pick_kernel(s, members, member_ref, keep_lo_ref, keep_hi_ref, img_lo_ref, img_hi_ref, *out_refs):
    for k, out_ref in zip(members, out_refs):
        other = member_ref[0] ^ k
        for i in range(s.hi_each):
            at = other * s.hi_each + i
            chosen = iota((s.hi_patches, LANES), 0) == keep_hi_ref[pl.ds(at, 1), :]
            got = nn(img_hi_ref[at], jnp.where(chosen, 1.0, 0.0).astype(BF16))
            out_ref[:, i * LANES : (i + 1) * LANES] = got.astype(BF16)
        for tile, first, count in sample_tiles(s):
            parts = []
            for j in range(count):
                at = other * s.lo_each + first + j
                chosen = iota((s.lo_patches, s.lo_length), 0) == keep_lo_ref[pl.ds(at, 1), :]
                parts.append(nn(img_lo_ref[at], jnp.where(chosen, 1.0, 0.0).astype(BF16)))
            if count < s.pack:
                parts.append(jnp.zeros((s.features, (s.pack - count) * s.lo_length), F32))
            joined = jnp.concatenate(parts, axis=1) if len(parts) > 1 else parts[0]
            out_ref[:, tile * LANES : (tile + 1) * LANES] = joined.astype(BF16)


def pick(s, members, member, keep_lo, keep_hi, img_lo, img_hi):
    args = (keep_lo, keep_hi, img_lo, img_hi)
    return pl.pallas_call(
        functools.partial(pick_kernel, s, members),
        grid_spec=pltpu.PrefetchScalarGridSpec(
            num_scalar_prefetch=1,
            grid=(1,),
            in_specs=[whole(a) for a in args],
            out_specs=[fixed(s.features, s.rows)] * len(members),
        ),
        out_shape=[shape((s.features, s.rows), BF16)] * len(members),
        compiler_params=params(60),
        cost_estimate=cost(2e9, 4e6),
    )(member, *args)


def stage_kernel(s, member_ref, keep_lo_ref, keep_hi_ref, mask_lo_ref, mask_hi_ref, cot_lo_ref, cot_hi_ref, keep_ref, seen_ref, *out_refs):
    eye = jnp.where(iota((s.features, s.features), 0) == iota((s.features, s.features), 1), 1.0, 0.0).astype(BF16)
    first_hi = (iota((1, s.hi_length), 1) == 0).astype(jnp.int32)
    first_lo = (iota((1, s.lo_length), 1) == 0).astype(jnp.int32)
    for k, out_ref in enumerate(out_refs):
        other = member_ref[0] ^ k
        for i in range(s.hi_each):
            at = other * s.hi_each + i
            keep_ref[k, i : i + 1, :] = keep_hi_ref[pl.ds(at, 1), :]
            out_ref[:, i * LANES : (i + 1) * LANES] = cot_hi_ref[at]
            if k == 0:
                seen_ref[i : i + 1, :] = jnp.maximum(mask_hi_ref[pl.ds(at, 1), :], first_hi).astype(F32)
        for tile, first, count in sample_tiles(s):
            begin = other * s.lo_each + first
            keep_ref[k, tile : tile + 1, :] = slots([keep_lo_ref[pl.ds(begin + j, 1), :] for j in range(count)], -1, s)
            if k == 0:
                seen = [jnp.maximum(mask_lo_ref[pl.ds(begin + j, 1), :], first_lo) for j in range(count)]
                seen_ref[tile : tile + 1, :] = slots(seen, 0, s).astype(F32)
            where = slice(tile * LANES, (tile + 1) * LANES)
            if count < s.pack:
                out_ref[:, where] = jnp.zeros((s.features, LANES), BF16)
            if count:
                size = count * s.lo_length
                start = pl.multiple_of(begin * s.lo_length, s.lo_length)
                out_ref[:, tile * LANES : tile * LANES + size] = nt(eye, cot_lo_ref[pl.ds(start, size), :]).astype(BF16)


def stage(s, member, keep_lo, keep_hi, mask_lo, mask_hi, cot_lo, cot_hi):
    args = (keep_lo, keep_hi, mask_lo, mask_hi, cot_lo, cot_hi)
    return pl.pallas_call(
        functools.partial(stage_kernel, s),
        grid_spec=pltpu.PrefetchScalarGridSpec(
            num_scalar_prefetch=1,
            grid=(1,),
            in_specs=[whole(a) for a in args],
            out_specs=[fixed(s.groups, s.tiles, LANES), fixed(s.tiles, LANES)]
            + [fixed(s.features, s.rows)] * s.groups,
        ),
        out_shape=[shape((s.groups, s.tiles, LANES), jnp.int32), shape((s.tiles, LANES), F32)]
        + [shape((s.features, s.rows), BF16)] * s.groups,
        compiler_params=params(60),
        cost_estimate=cost(1e8, 4e6),
    )(member, *args)


def chosen_rows(s, keep_ref, tile, patches, wanted_hi):
    row = keep_ref[pl.ds(tile, 1), :]
    is_hi = tile < s.hi_each
    row = jnp.where(is_hi if wanted_hi else jnp.logical_not(is_hi), row, -1)
    return jnp.where(iota((patches, LANES), 0) == row, 1.0, 0.0).astype(BF16)


def pair_masks():
    lane = iota((1, LANES), 1)
    low = jnp.where(lane < LANES // 2, 1.0, 0.0).astype(BF16)
    high = jnp.where(lane < LANES // 2, 0.0, 1.0).astype(BF16)
    return low, high


def doubled(block, masks):
    return jnp.concatenate([block * masks[0], block * masks[1]], axis=0)


def allowed(s, seen_ref, tile):
    bits = jnp.where(tile < s.hi_each, s.hi_length.bit_length() - 1, s.lo_length.bit_length() - 1)
    same = (iota((LANES, LANES), 0) >> bits) == (iota((LANES, LANES), 1) >> bits)
    open_to = jnp.logical_and(same, seen_ref[pl.ds(tile, 1), :] > 0)
    return jnp.concatenate([open_to, open_to], axis=0)


def forward_kernel(s, heads, keep_ref, seen_ref, p0, p1, p2, p3, w0, w1, w2, w3, pos_lo_ref, pos_hi_ref, gain1_ref, wqkv_ref, gain2_ref, wout_ref, x0_ref, a_ref, qkv_ref, probs_ref, mixed_ref, x1_ref, b_ref):
    step = pl.program_id(0)
    per = ROWS // LANES
    width = s.width
    picked = jnp.concatenate([p[...] for p in (p0, p1, p2, p3)], axis=0)
    embed = jnp.concatenate([w[: s.features, :] for w in (w0, w1, w2, w3)], axis=0)
    hot_hi = jnp.concatenate([chosen_rows(s, keep_ref, step * per + j, s.hi_patches, True) for j in range(per)], axis=1)
    hot_lo = jnp.concatenate([chosen_rows(s, keep_ref, step * per + j, s.lo_patches, False) for j in range(per)], axis=1)
    start = tn(picked, embed) + (tn(hot_hi, pos_hi_ref[...]) + tn(hot_lo, pos_lo_ref[...]))
    x0_ref[...] = start
    normed, _ = normalize(start)
    normed = (normed * gain1_ref[...]).astype(BF16)
    a_ref[...] = normed
    for c in range(3):
        part = slice(c * width, (c + 1) * width)
        qkv_ref[:, part] = nn(normed, wqkv_ref[:, part]).astype(BF16)
    masks = pair_masks()
    scale = 1.0 / math.sqrt(width // heads)
    for j in range(per):
        rows = slice(j * LANES, (j + 1) * LANES)
        ok = allowed(s, seen_ref, step * per + j)
        for h in range(width // LANES):
            at = h * LANES
            q = qkv_ref[rows, at : at + LANES]
            k = qkv_ref[rows, width + at : width + at + LANES]
            v = qkv_ref[rows, 2 * width + at : 2 * width + at + LANES]
            scores = nt(doubled(q, masks), k) * scale
            scores = jnp.where(ok, scores, MASKED)
            raised = jnp.exp(scores - jnp.max(scores, axis=-1, keepdims=True))
            probs = raised / jnp.sum(raised, axis=-1, keepdims=True)
            probs_ref[j, h] = probs
            rounded = probs.astype(BF16)
            wide = jnp.concatenate([rounded[:LANES], rounded[LANES:]], axis=1)
            mixed_ref[rows, at : at + LANES] = nn(wide, doubled(v, masks)).astype(BF16)
    middle = start + nn(mixed_ref[...], wout_ref[...])
    x1_ref[...] = middle
    normed, _ = normalize(middle)
    b_ref[...] = (normed * gain2_ref[...]).astype(BF16)


def forward(s, heads, keep, seen, picked, weights, pos_lo, pos_hi, gain1, wqkv, gain2, wout):
    width, rows = s.width, s.rows
    per, pairs = ROWS // LANES, width // LANES
    return pl.pallas_call(
        functools.partial(forward_kernel, s, heads),
        grid=(rows // ROWS,),
        in_specs=[whole(keep), whole(seen)]
        + [along(s.features, ROWS)] * 4
        + [whole(w) for w in weights]
        + [whole(a) for a in (pos_lo, pos_hi, gain1, wqkv, gain2, wout)],
        out_specs=[
            across(ROWS, width),
            across(ROWS, width),
            across(ROWS, 3 * width),
            pl.BlockSpec((per, pairs, 2 * LANES, LANES), lambda i: (i, 0, 0, 0)),
            across(ROWS, width),
            across(ROWS, width),
            across(ROWS, width),
        ],
        out_shape=[
            shape((rows, width), F32),
            shape((rows, width), BF16),
            shape((rows, 3 * width), BF16),
            shape((s.tiles, pairs, 2 * LANES, LANES), F32),
            shape((rows, width), BF16),
            shape((rows, width), F32),
            shape((rows, width), BF16),
        ],
        compiler_params=params(60),
        cost_estimate=cost(1.5e10, 3e7),
    )(keep, seen, *picked, *weights, pos_lo, pos_hi, gain1, wqkv, gain2, wout)


def upstream_kernel(s, seen_ref, c0, c1, c2, c3, w0, w1, w2, w3, gpred_ref, gm_ref, gb2_ref):
    step = pl.program_id(0)
    per = ROWS // LANES
    seen = jnp.concatenate([seen_ref[pl.ds(step * per + j, 1), :] for j in range(per)], axis=1).astype(BF16)
    grads = jnp.concatenate([c[...] for c in (c0, c1, c2, c3)], axis=0) * seen
    gpred_ref[...] = grads
    head = jnp.concatenate([w[s.features :, :] for w in (w0, w1, w2, w3)], axis=0)
    rounded = tn(grads, head).astype(BF16)
    gm_ref[...] = rounded
    accumulate(gb2_ref, step == 0, jnp.sum(rounded.astype(F32), axis=0, keepdims=True))


def upstream(s, seen, cots, weights):
    rows, width = s.rows, s.width
    high = s.groups * s.features
    return pl.pallas_call(
        functools.partial(upstream_kernel, s),
        grid=(rows // ROWS,),
        in_specs=[whole(seen)] + [along(s.features, ROWS)] * 4 + [whole(w) for w in weights],
        out_specs=[along(high, ROWS), across(ROWS, width), fixed(1, width)],
        out_shape=[shape((high, rows), BF16), shape((rows, width), BF16), shape((1, width), F32)],
        compiler_params=params(60),
        cost_estimate=cost(1e9, 4e6),
    )(seen, *cots, *weights)


def hidden_kernel(sub, b_ref, gm_ref, w1_ref, b1_ref, w2_ref, z_ref, gu_ref, gb1_ref):
    w1, w2, bias = w1_ref[...], w2_ref[...], b1_ref[...]
    total = None
    for i in range(b_ref.shape[0] // sub):
        rows = slice(i * sub, (i + 1) * sub)
        u = nn(b_ref[rows, :], w1) + bias
        upward = nt(gm_ref[rows, :], w2)
        z, slope = gelu_parts(u)
        z_ref[rows, :] = z.astype(BF16)
        gu = (upward * slope).astype(BF16)
        gu_ref[rows, :] = gu
        part = jnp.sum(gu.astype(F32), axis=0, keepdims=True)
        total = part if total is None else total + part
    gb1_ref[...] = total


def hidden(b, gm, w1, b1, w2, columns=768, sub=256):
    rows, width = b.shape
    inner = w1.shape[1]
    return pl.pallas_call(
        functools.partial(hidden_kernel, sub),
        grid=(inner // columns,),
        in_specs=[
            whole(b),
            whole(gm),
            along(width, columns),
            along(1, columns),
            across(columns, width),
        ],
        out_specs=[along(rows, columns), along(rows, columns), along(1, columns)],
        out_shape=[shape((rows, inner), BF16), shape((rows, inner), BF16), shape((1, inner), F32)],
        compiler_params=params(60),
        cost_estimate=cost(2e10, 2.5e7),
    )(b, gm, w1, b1, w2)


def weight_kernel(left_ref, right_ref, out_ref):
    out_ref[...] = tn(left_ref[...], right_ref[...]).astype(BF16)


def weight_grad(left, right, tall, broad):
    rows = left.shape[0]
    m, n = left.shape[1], right.shape[1]
    return pl.pallas_call(
        weight_kernel,
        grid=(m // tall, n // broad),
        in_specs=[
            pl.BlockSpec((rows, tall), lambda i, j: (0, i)),
            pl.BlockSpec((rows, broad), lambda i, j: (0, j)),
        ],
        out_specs=pl.BlockSpec((tall, broad), lambda i, j: (i, j)),
        out_shape=shape((m, n), BF16),
        compiler_params=params(60),
        cost_estimate=cost(2 * rows * m * n, 2 * (rows * (m + n) + m * n)),
    )(left, right)


def relative(ids_ref, x, y, z, c):
    return ids_ref[0] ^ (2 * z + y), ids_ref[1] ^ (2 * x + c)


def high_rows_kernel(far, block, ids_ref, left_ref, right_ref, o0_ref, o1_ref, acc_ref):
    acc_ref[...] = tn(left_ref[...], right_ref[...])
    for x in range(2):
        for y in range(2):
            for c, out_ref in enumerate((o0_ref, o1_ref)):
                d, v = relative(ids_ref, x, y, 0, c)
                start = pl.multiple_of(((d & 1) * 4 + v) * block, 8)
                out_ref[x, y, 0] = acc_ref[pl.ds(start, block), :].astype(BF16)


def high_rows(ids, far, left, right):
    rows, width = right.shape
    block = left.shape[1] // (8 * far)
    out = pl.BlockSpec((2, 2, 1, block, width), lambda i, ids: (0, 0, i, 0, 0))
    return pl.pallas_call(
        functools.partial(high_rows_kernel, far, block),
        grid_spec=pltpu.PrefetchScalarGridSpec(
            num_scalar_prefetch=1,
            grid=(far,),
            in_specs=[
                pl.BlockSpec((rows, 8 * block), lambda i, ids: (0, (ids[0] >> 1) ^ i)),
                whole(right),
            ],
            out_specs=[out, out],
            scratch_shapes=[pltpu.VMEM((8 * block, width), F32)],
        ),
        out_shape=[shape((2, 2, far, block, width), BF16)] * 2,
        compiler_params=params(60),
        cost_estimate=cost(2 * rows * left.shape[1] * width, 1.3e7),
    )(ids, left, right)


def spread(ids_ref, far, acc_ref, outs, block, extra=None):
    for x in range(2):
        for y in range(2):
            for z in range(far):
                for c, out_ref in enumerate(outs):
                    d, v = relative(ids_ref, x, y, z, c)
                    start = pl.multiple_of((d * 4 + v) * block, 8)
                    out_ref[x, y, z, :block, :] = acc_ref[pl.ds(start, block), :].astype(BF16)
                    if extra is not None:
                        out_ref[x, y, z, block:, :] = extra


def low_rows_kernel(far, block, ids_ref, left_ref, right_ref, o0_ref, o1_ref, turned_ref, acc_ref):
    @pl.when(pl.program_id(0) == 0)
    def _():
        turned_ref[...] = left_ref[...].T

    acc_ref[...] = nn(turned_ref[...], right_ref[...])
    spread(ids_ref, far, acc_ref, (o0_ref, o1_ref), block)


def low_rows(ids, far, left, right):
    rows, width = left.shape
    chunks = right.shape[1] // width
    block = width // (8 * far)
    out = pl.BlockSpec((2, 2, far, block, width), lambda i, ids: (0, 0, 0, i, 0))
    return pl.pallas_call(
        functools.partial(low_rows_kernel, far, block),
        grid_spec=pltpu.PrefetchScalarGridSpec(
            num_scalar_prefetch=1,
            grid=(chunks,),
            in_specs=[whole(left), pl.BlockSpec((rows, width), lambda i, ids: (0, i))],
            out_specs=[out, out],
            scratch_shapes=[pltpu.VMEM((width, rows), BF16), pltpu.VMEM((width, width), F32)],
        ),
        out_shape=[shape((2, 2, far, chunks * block, width), BF16)] * 2,
        compiler_params=params(60),
        cost_estimate=cost(2 * rows * width * right.shape[1], 1.3e7),
    )(ids, left, right)


def part_rows(width, offset):
    return pl.BlockSpec((ROWS, width), lambda i, *_: (i + offset, 0))


def middle_kernel(x1_ref, z_ref, gu_ref, gm_ref, w1_ref, w2_ref, b2_ref, gain2_ref, wout_ref, final_ref, ga_ref, g1_ref, go_ref, gln2_ref):
    middle = x1_ref[...]
    final_ref[...] = (middle + (nn(z_ref[...], w2_ref[...]) + b2_ref[...])).astype(BF16)
    upward = nt(gu_ref[...], w1_ref[...])
    normed, inverse = normalize(middle)
    accumulate(gln2_ref, pl.program_id(0) == 0, jnp.sum(upward * normed, axis=0, keepdims=True))
    grad = gm_ref[...].astype(F32) + normalize_back(upward, normed, inverse, gain2_ref[...])
    g1_ref[...] = grad
    rounded = grad.astype(BF16)
    ga_ref[...] = rounded
    go_ref[...] = nt(rounded, wout_ref[...]).astype(BF16)


def middle(part, parts, x1, z, gu, gm, w1, w2, b2, gain2, wout):
    rows, width = x1.shape
    inner = w1.shape[1]
    steps = rows // ROWS // parts
    at = part * steps
    size = steps * ROWS
    return pl.pallas_call(
        middle_kernel,
        grid=(steps,),
        in_specs=[
            part_rows(width, at),
            part_rows(inner, at),
            part_rows(inner, at),
            part_rows(width, at),
        ]
        + [whole(a) for a in (w1, w2, b2, gain2, wout)],
        out_specs=[across(ROWS, width)] * 4 + [fixed(1, width)],
        out_shape=[
            shape((size, width), BF16),
            shape((size, width), BF16),
            shape((size, width), F32),
            shape((size, width), BF16),
            shape((1, width), F32),
        ],
        compiler_params=params(60),
        cost_estimate=cost(2e10 / parts, 3e7 / parts),
    )(x1, z, gu, gm, w1, w2, b2, gain2, wout)


def head_kernel(s, seen_ref, f0, f1, weights, out_refs):
    final = jnp.concatenate([f0[...], f1[...]], axis=0)
    seen = jnp.concatenate([seen_ref[t : t + 1, :] for t in range(s.tiles)], axis=1)
    for head, out in zip(weights, out_refs):
        out[...] = (nt(head[s.features :, :], final) * seen).astype(BF16)
    return final


def output_kernel(s, far, block, ids_ref, seen_ref, f0, f1, ga0, ga1, mixed_ref, gpred_ref, la, lb, gb1_ref, gb2_ref, h0, h1, h2, h3, p0, p1, p2, p3, o0_ref, o1_ref, n0_ref, n1_ref, acc_ref):
    final = head_kernel(s, seen_ref, f0, f1, (h0, h1, h2, h3), (p0, p1, p2, p3))
    ghead = nn(gpred_ref[...], final).astype(BF16)
    for k in range(4):
        (n0_ref, n1_ref)[k % 2][k // 2] = ghead[k * s.features : (k + 1) * s.features]
    half = ga0.shape[0]
    acc_ref[...] = tn(mixed_ref[:half, :], ga0[...]) + tn(mixed_ref[half:, :], ga1[...])
    inner = gb1_ref.shape[1] // s.width
    sides = [la[...] + lb[...], gb2_ref[...]]
    sides += [gb1_ref[:, i * s.width : (i + 1) * s.width] for i in range(inner)]
    sides.append(jnp.zeros((-len(sides) % 8, s.width), F32))
    extra = jnp.concatenate(sides, axis=0).astype(BF16)
    spread(ids_ref, far, acc_ref, (o0_ref, o1_ref), block, extra)


def output_grads(s, ids, far, seen, finals, gas, mixed, gpred, gln2s, gb1, gb2, weights):
    width, rows = s.width, s.rows
    block = width // (8 * far)
    tall = block + 8 * (-(-(2 + gb1.shape[1] // width) // 8))
    args = [seen, *finals, *gas, mixed, gpred, *gln2s, gb1, gb2, *weights]
    outs = (
        [((s.features, rows), BF16)] * 4
        + [((2, 2, far, tall, width), BF16)] * 2
        + [((2, s.features, width), BF16)] * 2
    )
    return pl.pallas_call(
        functools.partial(output_kernel, s, far, block),
        grid_spec=pltpu.PrefetchScalarGridSpec(
            num_scalar_prefetch=1,
            grid=(1,),
            in_specs=[whole(a) for a in args],
            out_specs=[fixed(*dims) for dims, _ in outs],
            scratch_shapes=[pltpu.VMEM((width, width), F32)],
        ),
        out_shape=[shape(*out) for out in outs],
        compiler_params=params(60),
        cost_estimate=cost(4e9, 1e7),
    )(ids, *args)


def backward_kernel(s, heads, qkv_ref, probs_ref, go_ref, x0_ref, g1_ref, wqkv_ref, gain1_ref, gqkv_ref, g0_ref, gln1_ref):
    per = ROWS // LANES
    width = s.width
    masks = pair_masks()
    scale = 1.0 / math.sqrt(width // heads)
    for j in range(per):
        rows = slice(j * LANES, (j + 1) * LANES)
        for h in range(width // LANES):
            at = h * LANES
            q = doubled(qkv_ref[rows, at : at + LANES], masks)
            k = doubled(qkv_ref[rows, width + at : width + at + LANES], masks)
            v = qkv_ref[rows, 2 * width + at : 2 * width + at + LANES]
            out = doubled(go_ref[rows, at : at + LANES], masks)
            probs = probs_ref[j, h]
            upward = nt(out, v)
            centred = upward - jnp.sum(probs * upward, axis=-1, keepdims=True)
            grads = (probs * centred).astype(BF16)
            wide = jnp.concatenate([grads[:LANES], grads[LANES:]], axis=1)
            gqkv_ref[rows, at : at + LANES] = (nn(wide, k) * scale).astype(BF16)
            gqkv_ref[rows, width + at : width + at + LANES] = (tn(grads, q) * scale).astype(BF16)
            gqkv_ref[rows, 2 * width + at : 2 * width + at + LANES] = tn(probs.astype(BF16), out).astype(BF16)
    upward = nt(gqkv_ref[...], wqkv_ref[...])
    normed, inverse = normalize(x0_ref[...])
    accumulate(gln1_ref, pl.program_id(0) == 0, jnp.sum(upward * normed, axis=0, keepdims=True))
    g0_ref[...] = (g1_ref[...] + normalize_back(upward, normed, inverse, gain1_ref[...])).astype(BF16)


def backward(s, heads, part, parts, qkv, probs, go, x0, g1, wqkv, gain1):
    rows, width = s.rows, s.width
    per, pairs = ROWS // LANES, width // LANES
    steps = rows // ROWS // parts
    at = part * steps
    size = steps * ROWS
    return pl.pallas_call(
        functools.partial(backward_kernel, s, heads),
        grid=(steps,),
        in_specs=[
            part_rows(3 * width, at),
            pl.BlockSpec((per, pairs, 2 * LANES, LANES), lambda i: (i + at, 0, 0, 0)),
            across(ROWS, width),
            part_rows(width, at),
            across(ROWS, width),
            whole(wqkv),
            whole(gain1),
        ],
        out_specs=[across(ROWS, 3 * width), across(ROWS, width), fixed(1, width)],
        out_shape=[shape((size, 3 * width), BF16), shape((size, width), BF16), shape((1, width), F32)],
        compiler_params=params(60),
        cost_estimate=cost(2.5e10 / parts, 3e7 / parts),
    )(qkv, probs, go, x0, g1, wqkv, gain1)


def image_kernel(s, keep_ref, a_ref, b_ref, w0, w1, w2, w3, o0, o1, o2, o3):
    half = a_ref.shape[0]
    for weight, out in zip((w0, w1, w2, w3), (o0, o1, o2, o3)):
        out[:, :half] = nt(weight[: s.features, :], a_ref[...]).astype(BF16)
        out[:, half:] = nt(weight[: s.features, :], b_ref[...]).astype(BF16)


def image_grads(s, keep, g0s, weights):
    args = [keep, *g0s, *weights]
    return pl.pallas_call(
        functools.partial(image_kernel, s),
        grid=(1,),
        in_specs=[whole(a) for a in args],
        out_specs=[fixed(s.features, s.rows)] * 4,
        out_shape=[shape((s.features, s.rows), BF16)] * 4,
        compiler_params=params(60),
        cost_estimate=cost(1e9, 3e6),
    )(*args)


def position_grads(s, keep_ref, g0, picked):
    hot_hi, hot_lo = [], []
    for t in range(s.tiles):
        row = keep_ref[t : t + 1, :]
        patches = s.hi_patches if t < s.hi_each else s.lo_patches
        hot = jnp.where(iota((patches, LANES), 0) == row, 1.0, 0.0).astype(BF16)
        (hot_hi if t < s.hi_each else hot_lo).append(hot)
    hi_rows = s.hi_each * LANES
    hi = nn(jnp.concatenate(hot_hi, axis=1), g0[:hi_rows])
    lo = nn(jnp.concatenate(hot_lo, axis=1), g0[hi_rows:])
    return lo, hi, nn(jnp.concatenate(picked, axis=0), g0)


def first_kernel(s, far, block, chunks, ids_ref, keep_ref, a_ref, r0_ref, r1_ref, g0a, g0b, la, lb, p0, p1, p2, p3, o0_ref, o1_ref, e0_ref, e1_ref, turned_ref, acc_ref, lo_ref, hi_ref):
    step = pl.program_id(0)
    half = r0_ref.shape[0]
    width = s.width
    outs = (o0_ref, o1_ref)

    @pl.when(step == 0)
    def _():
        turned_ref[...] = a_ref[...].T

    @pl.when(step < chunks)
    def _():
        acc_ref[...] = nn(turned_ref[:, :half], r0_ref[...]) + nn(turned_ref[:, half:], r1_ref[...])
        spread(ids_ref, far, acc_ref, outs, block)

    @pl.when(step == chunks)
    def _():
        g0 = jnp.concatenate([g0a[...], g0b[...]], axis=0)
        lo, hi, embed = position_grads(s, keep_ref, g0, [p[...] for p in (p0, p1, p2, p3)])
        lo_ref[...] = lo
        hi_ref[...] = hi
        embed = embed.astype(BF16)
        for k in range(4):
            (e0_ref, e1_ref)[k % 2][k // 2] = embed[k * s.features : (k + 1) * s.features]
        hi_block = s.hi_patches // (8 * far)
        lo_block = s.lo_patches // (8 * far)
        gln1 = la[...] + lb[...]
        pad = jnp.zeros((block - hi_block - lo_block - 1, width), F32)
        for x in range(2):
            for y in range(2):
                for z in range(far):
                    for c in range(2):
                        d, v = relative(ids_ref, x, y, z, c)
                        at = d * 4 + v
                        mine = hi_ref[pl.ds(pl.multiple_of(at * hi_block, 8), hi_block), :]
                        both = lo_ref[pl.ds(pl.multiple_of((at >> 1) * 8, 8), 8), :]
                        less = jnp.where((at & 1) == 1, both[lo_block:], both[:lo_block])
                        outs[c][x, y, z] = jnp.concatenate([mine, less, gln1, pad], axis=0).astype(BF16)


def first_grads(s, ids, far, keep, a, gqkvs, g0s, gln1s, picked):
    width, rows = s.width, s.rows
    block = width // (8 * far)
    chunks = gqkvs[0].shape[1] // width
    half = gqkvs[0].shape[0]
    out = pl.BlockSpec((2, 2, far, block, width), lambda i, ids: (0, 0, 0, i, 0))
    right = pl.BlockSpec((half, width), lambda i, ids: (0, jnp.minimum(i, chunks - 1)))
    rest = [*g0s, *gln1s, *picked]
    return pl.pallas_call(
        functools.partial(first_kernel, s, far, block, chunks),
        grid_spec=pltpu.PrefetchScalarGridSpec(
            num_scalar_prefetch=1,
            grid=(chunks + 1,),
            in_specs=[whole(keep), whole(a), right, right] + [whole(r) for r in rest],
            out_specs=[out, out, fixed(2, s.features, width), fixed(2, s.features, width)],
            scratch_shapes=[
                pltpu.VMEM((width, rows), BF16),
                pltpu.VMEM((width, width), F32),
                pltpu.VMEM((s.lo_patches, width), F32),
                pltpu.VMEM((s.hi_patches, width), F32),
            ],
        ),
        out_shape=[shape((2, 2, far, (chunks + 1) * block, width), BF16)] * 2
        + [shape((2, s.features, width), BF16)] * 2,
        compiler_params=params(60),
        cost_estimate=cost(7e9, 1.2e7),
    )(ids, keep, a, *gqkvs, *rest)


def place_kernel(s, member_ref, keep_ref, r0, r1, r2, r3, lo_ref, hi_ref):
    lane_sample = iota((1, LANES), 1) // s.lo_length
    for k, got_ref in enumerate((r0, r1, r2, r3)):
        other = member_ref[0] ^ k
        for i in range(s.hi_each):
            chosen = iota((s.hi_patches, LANES), 0) == keep_ref[k, i : i + 1, :]
            hot = jnp.where(chosen, 1.0, 0.0).astype(BF16)
            hi_ref[other * s.hi_each + i] = nt(got_ref[:, i * LANES : (i + 1) * LANES], hot).astype(BF16)
        for tile, first, count in sample_tiles(s):
            got = got_ref[:, tile * LANES : (tile + 1) * LANES]
            for j in range(count):
                row = jnp.where(lane_sample == j, keep_ref[k, tile : tile + 1, :], -1)
                hot = jnp.where(iota((s.lo_patches, LANES), 0) == row, 1.0, 0.0).astype(BF16)
                lo_ref[other * s.lo_each + first + j] = nt(got, hot).astype(BF16)


def place(s, member, keep, blocks):
    lo = s.groups * s.lo_each
    hi = s.groups * s.hi_each
    return pl.pallas_call(
        functools.partial(place_kernel, s),
        grid_spec=pltpu.PrefetchScalarGridSpec(
            num_scalar_prefetch=1,
            grid=(1,),
            in_specs=[whole(keep)] + [whole(b) for b in blocks],
            out_specs=[fixed(lo, s.features, s.lo_patches), fixed(hi, s.features, s.hi_patches)],
        ),
        out_shape=[
            shape((lo, s.features, s.lo_patches), BF16),
            shape((hi, s.features, s.hi_patches), BF16),
        ],
        compiler_params=params(60),
        cost_estimate=cost(2e9, 4e6),
    )(member, keep, *blocks)


def predict_kernel(s, member_ref, r0, r1, r2, r3, lo_ref, hi_ref):
    eye = jnp.where(iota((s.features, s.features), 0) == iota((s.features, s.features), 1), 1.0, 0.0).astype(BF16)
    for k, got_ref in enumerate((r0, r1, r2, r3)):
        other = member_ref[0] ^ k
        for i in range(s.hi_each):
            hi_ref[other * s.hi_each + i] = got_ref[:, i * LANES : (i + 1) * LANES]
        for tile, first, count in sample_tiles(s):
            if count:
                size = count * s.lo_length
                turned = tn(got_ref[:, tile * LANES : (tile + 1) * LANES], eye).astype(BF16)
                start = pl.multiple_of((other * s.lo_each + first) * s.lo_length, s.lo_length)
                lo_ref[pl.ds(start, size), :] = turned[:size]


def predict(s, member, blocks):
    lo = s.groups * s.lo_each * s.lo_length
    hi = s.groups * s.hi_each
    return pl.pallas_call(
        functools.partial(predict_kernel, s),
        grid_spec=pltpu.PrefetchScalarGridSpec(
            num_scalar_prefetch=1,
            grid=(1,),
            in_specs=[whole(b) for b in blocks],
            out_specs=[fixed(lo, s.features), fixed(hi, s.features, s.hi_length)],
        ),
        out_shape=[shape((lo, s.features), BF16), shape((hi, s.features, s.hi_length), BF16)],
        compiler_params=params(60),
        cost_estimate=cost(1e8, 3e6),
    )(member, *blocks)


def swap(value, data_bit, var_bit):
    dp, var = lax.axis_size("dp"), lax.axis_size("var")
    pairs = [
        (d * var + v, (d ^ data_bit) * var + (v ^ var_bit)) for d in range(dp) for v in range(var)
    ]
    return lax.ppermute(value, AXES, pairs)


def add_rounded(left, right):
    return (left.astype(F32) + right.astype(F32)).astype(BF16)


def added(*values):
    values = [value.astype(F32) for value in values]
    while len(values) > 1:
        values = [values[i] + values[i + 1] for i in range(0, len(values), 2)]
    return values[0]


def tie(value, *tokens):
    return lax.optimization_barrier((value, tokens))[0]


PARTNERS = {"core": (0, 1), "x": (0, 2), "y": (1, 0), "z0": (2, 0), "z1": (4, 0)}


class Chain:
    def __init__(self, near, sent):
        self.near, self.sent = near, sent
        self.repeats = near.ndim == 3
        self.names = ["x"] if self.repeats else ["x", "y", "z1", "z0"]
        self.held = self.got = None

    def outgoing(self, name):
        if name == "core":
            self.held = self.near
            return self.sent
        if name not in self.names:
            self.held = add_rounded(self.held, self.got)
            return self.held
        axis = self.names.index(name)
        self.names.remove(name)
        kept, sent = (
            [lax.index_in_dim(value, side, axis, keepdims=False) for value in (self.held, self.got)]
            for side in range(2)
        )
        self.held = add_rounded(*kept)
        return add_rounded(*sent)

    def hold(self, *tokens):
        self.held, self.got = tie((self.held, self.got), *tokens)

    def final(self):
        return added(self.held, self.got) if self.got is not None else added(*self.fanned)


def send_rows(values, bits):
    if len(values) == 1:
        return [swap(values[0], *bits)]
    width = values[0].shape[-1]
    flat = [value.reshape(-1, width) for value in values]
    got = swap(jnp.concatenate(flat, axis=0), *bits)
    out, start = [], 0
    for value, rows in zip(values, flat):
        out.append(got[start : start + rows.shape[0]].reshape(value.shape))
        start += rows.shape[0]
    return out


def trade(name, *chains):
    got = send_rows([chain.outgoing(name) for chain in chains], PARTNERS[name])
    for chain, value in zip(chains, got):
        chain.got = value
    return got[0]


def trade_line(*chains):
    values = [add_rounded(chain.held, chain.got) for chain in chains]
    split = [
        [value] * 4 if chain.repeats else list(value.reshape((4,) + value.shape[2:]))
        for chain, value in zip(chains, values)
    ]
    for chain, value in zip(chains, split):
        chain.fanned, chain.got = [value[0]], None
    for z in range(1, 4):
        for chain, got in zip(chains, send_rows([value[z] for value in split], (2 * z, 0))):
            chain.fanned.append(got)
    return chains[0].fanned[1:]


def natural(near, sent):
    both = jnp.stack([near, sent]).transpose(3, 2, 1, 0, 4, 5)
    return both.reshape((-1,) + near.shape[3:])


def scattered(full):
    return lax.psum_scatter(full, AXES, scatter_dimension=0, tiled=True).astype(F32)


def joined(blocks, chunks):
    count, rows, width = blocks.shape
    split = blocks.reshape(count, chunks, rows // chunks, width).transpose(0, 2, 1, 3)
    return split.reshape(count * (rows // chunks), chunks * width)


def plain_sum(near, sent):
    if near.ndim == 6:
        near, sent = (value.reshape((2, 2, 4) + value.shape[4:]) for value in (near, sent))
        return natural(near, sent)
    value = jnp.stack([near, sent], axis=1)
    value = value.reshape((-1,) + value.shape[2:])
    bit = 1
    while value.shape[0] > 1:
        value = value.reshape((value.shape[0] // 2, 2) + value.shape[1:])
        value = add_rounded(value[:, 0], swap(value[:, 1], 0, bit))
        bit *= 2
    return lax.psum(value[0], "dp").astype(F32)


def exchange_relative(blocks):
    return [blocks[0]] + [swap(blocks[k], 0, k) for k in range(1, len(blocks))]


def body(
    img_lo,
    img_hi,
    keep_lo,
    keep_hi,
    mask_lo,
    mask_hi,
    w_embed,
    pos_lo,
    pos_hi,
    ln1_gain,
    w_qkv,
    w_out,
    ln2_gain,
    w_fc1,
    b_fc1,
    w_fc2,
    b_fc2,
    w_head,
    cot_lo,
    cot_hi,
):
    groups = lax.axis_size("var")
    devices = lax.axis_size("dp") * groups
    member = lax.axis_index("var").astype(jnp.int32).reshape(1)
    s = Sizes(keep_lo.shape, keep_hi.shape, w_embed.shape, img_lo.shape, img_hi.shape, groups)
    features, width = s.features, s.width
    gain1, gain2 = ln1_gain.reshape(1, -1), ln2_gain.reshape(1, -1)
    img_lo_t, img_hi_t = img_lo.transpose(0, 2, 1), img_hi.transpose(0, 2, 1)

    own = jnp.concatenate([w_embed, w_head.T], axis=0)
    crossed = swap(own, 0, 2)
    weights = [own, swap(own, 0, 1), crossed, swap(crossed, 0, 1)]
    sent = pick(s, (1, 2, 3), member, keep_lo, keep_hi, img_lo_t, img_hi_t)
    picked = [swap(value, 0, k + 1) for k, value in enumerate(sent)]
    picked = [*pick(s, (0,), member, keep_lo, keep_hi, img_lo_t, img_hi_t), *picked]
    keep, seen, *cots = stage(
        s,
        tie(member, sent[0]),
        keep_lo,
        keep_hi,
        mask_lo,
        mask_hi,
        cot_lo.reshape(-1, features),
        cot_hi.transpose(0, 2, 1),
    )
    cots = exchange_relative(cots)
    own_keep = keep[0]
    x0, a, qkv, probs, mixed, x1, b = forward(
        s, HEADS, own_keep, seen, picked, weights, pos_lo, pos_hi, gain1, w_qkv, gain2, w_out
    )
    gpred, gm, grad_b2 = upstream(s, tie(seen, b), cots, weights)
    z, gu, grad_b1 = hidden(b, gm, w_fc1, b_fc1.reshape(1, -1), w_fc2)
    far = 4
    cube = lax.axis_size("dp") == 2 * far
    place_of = lax.axis_index("dp") * groups + lax.axis_index("var")
    ids = jnp.stack([lax.axis_index("dp"), lax.axis_index("var")]).astype(jnp.int32)
    if not cube:
        ids = jnp.zeros_like(ids)

    def chain_of(near, sent):
        if near.ndim == 5:
            near, sent = (
                value.reshape((2, 2, 2, 2) + value.shape[3:]) for value in (near, sent)
            )
        return Chain(near, sent)

    def step(name, *chains):
        return trade(name, *chains) if cube else ()

    def halves_of(chain):
        out = []
        for side in range(2):
            piece = Chain(chain.near, chain.sent)
            rows = chain.near.shape[4] // 2
            piece.held, piece.got = (
                lax.slice_in_dim(value, side * rows, (side + 1) * rows, axis=4)
                for value in (chain.held, chain.got)
            )
            out.append(piece)
        return out

    bias2 = b_fc2.reshape(1, -1)

    def middle_part(part, *tokens):
        return middle(part, 2, x1, z, gu, gm, w_fc1, w_fc2, tie(bias2, *tokens), gain2, w_out)

    two = chain_of(*high_rows(ids, far, z, gm))
    token = step("core", two)
    one = chain_of(*low_rows(tie(ids, two.near), far, b, gu))
    halves = [middle_part(0, token, one.near)]
    two_x = step("x", two)
    halves.append(middle_part(1, step("core", one), halves[0][0]))
    one_y = step("y", one)
    finals, gas, g1s, gos, gln2s = zip(*halves)
    *preds, near, sent, near_head, sent_head = output_grads(
        s,
        tie(ids, two_x, *finals),
        far,
        seen,
        finals,
        gas,
        mixed,
        gpred,
        gln2s,
        grad_b1,
        grad_b2,
        weights,
    )
    out, head = chain_of(near, sent), chain_of(near_head, sent_head)

    def backward_part(part, *tokens):
        return backward(
            s, HEADS, part, 2, qkv, probs, gos[part], x0, g1s[part], w_qkv, tie(gain1, *tokens)
        )

    tokens = [step("y", two), step("core", out), step("core", head)]
    halves = [backward_part(0, near, one_y)]
    tokens += [step("x", one)]
    tokens += exchange_relative(preds)
    got_preds = tokens[-groups:]
    halves.append(backward_part(1, halves[0][0], *tokens))
    tokens = [step("z0", two), step("x", out, head), step("z0", one)]
    gqkvs, g0s, gln1s = zip(*halves)
    near, sent, near_embed, sent_embed = first_grads(
        s, tie(ids, *tokens), far, own_keep, a, gqkvs, g0s, gln1s, picked
    )
    first, embed = chain_of(near, sent), chain_of(near_embed, sent_embed)
    tokens = [step("core", first), step("core", embed)]
    blocks = image_grads(s, tie(own_keep, near), g0s, weights)
    pred_lo, pred_hi = predict(s, tie(member, blocks[0]), got_preds)
    if cube:
        for chain in (out, head, two, one):
            chain.hold(*tokens)
        one_half, other_half = halves_of(first)
        tokens = [trade("x", one_half), trade("y", other_half), trade("z0", embed)]
        early = [trade("y", out, head), trade("z1", two), trade("z1", one)]
        for chain in (out, head):
            chain.hold(*tokens)
        for chain in (one_half, other_half, embed):
            chain.hold(*early)
        tokens = [trade("y", one_half), trade("x", other_half), trade("z1", embed)]
        early = [trade("z0", out, head)]
        for chain in (out, head):
            chain.hold(*tokens)
        for chain in (one_half, other_half, embed):
            chain.hold(*early)
        blocks = [tie(block_of, *tokens) for block_of in blocks]
        trade("x", embed)
        trade("z1", out, head)
        trade_line(one_half, other_half)
        trade("y", embed)
        grad_fc2, grad_fc1, rest, grad_head, grad_embed = (
            chain.final() for chain in (two, one, out, head, embed)
        )
        first = jnp.concatenate([one_half.final(), other_half.final()], axis=0)
    else:
        grad_fc2, grad_fc1, rest, grad_head, grad_embed, first = (
            plain_sum(chain.near, chain.sent) for chain in (two, one, out, head, embed, first)
        )
    grad_img_lo, grad_img_hi = place(s, member, keep, exchange_relative(blocks))
    grad_head = grad_head.T

    block = width // devices
    inner = w_fc1.shape[1] // width

    hi_block = s.hi_patches // devices
    lo_block = s.lo_patches // devices

    def own_part(row):
        return lax.dynamic_slice_in_dim(row, place_of * block, block)

    if cube:
        grad_fc1 = joined(grad_fc1[None], inner)
        grad_qkv = joined(first[None, : 3 * block], 3)
        grad_out, sides = rest[:block], rest[block:]
        extra = first[3 * block :]
        grad_pos_hi = extra[:hi_block]
        grad_pos_lo = extra[hi_block : hi_block + lo_block]
        first_side = extra[hi_block + lo_block]
    else:
        tall = width // 32
        hi_tall, lo_tall = s.hi_patches // 32, s.lo_patches // 32
        grad_fc2 = scattered(grad_fc2.reshape(-1, width))
        grad_fc1 = scattered(joined(grad_fc1, inner))
        grad_qkv = scattered(joined(first[:, : 3 * tall], 3))
        grad_out, sides = scattered(rest[:, :tall].reshape(-1, width)), rest[0, tall:]
        extra = first[:, 3 * tall :]
        grad_pos_hi = scattered(extra[:, :hi_tall].reshape(-1, width))
        grad_pos_lo = scattered(extra[:, hi_tall : hi_tall + lo_tall].reshape(-1, width))
        sides = lax.psum(jnp.concatenate([sides, extra[0, hi_tall + lo_tall :]]), AXES).astype(F32)
        first_side = sides[rest.shape[1] - tall]
    grad_ln1 = own_part(first_side)
    grad_ln2 = own_part(sides[0])
    grad_b2 = own_part(sides[1])
    grad_b1 = lax.dynamic_slice_in_dim(
        sides[2 : 2 + inner].reshape(-1), place_of * inner * block, inner * block
    )
    return (
        pred_lo.reshape(cot_lo.shape),
        pred_hi.transpose(0, 2, 1),
        grad_img_lo.transpose(0, 2, 1),
        grad_img_hi.transpose(0, 2, 1),
        grad_embed,
        grad_pos_lo,
        grad_pos_hi,
        grad_ln1,
        grad_qkv,
        grad_out,
        grad_ln2,
        grad_fc1,
        grad_b1,
        grad_fc2,
        grad_b2,
        grad_head,
    )


def solution(mesh):
    placed = (
        P("dp", None, "var"),
        P("dp", None, "var"),
        P("dp", None),
        P("dp", None),
        P("dp", None),
        P("dp", None),
        P("var", None),
        P(),
        P(),
        P(),
        P(),
        P(),
        P(),
        P(),
        P(),
        P(),
        P(),
        P(None, "var"),
        P("dp", None, "var"),
        P("dp", None, "var"),
    )
    return jax.shard_map(
        body,
        mesh=mesh,
        in_specs=placed,
        out_specs=(
            P("dp", None, "var"),
            P("dp", None, "var"),
            P("dp", None, "var"),
            P("dp", None, "var"),
            P("var", None),
            P(("dp", "var"), None),
            P(("dp", "var"), None),
            P(("dp", "var")),
            P(("dp", "var"), None),
            P(("dp", "var"), None),
            P(("dp", "var")),
            P(("dp", "var"), None),
            P(("dp", "var")),
            P(("dp", "var"), None),
            P(("dp", "var")),
            P(None, "var"),
        ),
        check_vma=False,
    )
```

```python
import functools
import math

import jax
import jax.numpy as jnp
from jax import lax
from jax.experimental import pallas as pl
from jax.experimental.pallas import tpu as pltpu
from jax.sharding import PartitionSpec as P

HEADS = 12
EPSILON = 1e-06
AXES = ("dp", "var")
BF16 = jnp.bfloat16
F32 = jnp.float32
LANES = 128
ROWS = 256
MASKED = -1000000000.0
SHARE = 0.5


def dot(left, right, dims):
    return lax.dot_general(left, right, (dims, ((), ())), preferred_element_type=F32)


def nn(left, right):
    return dot(left, right, ((1,), (0,)))


def nt(left, right):
    return dot(left, right, ((1,), (1,)))


def tn(left, right):
    return dot(left, right, ((0,), (0,)))


def shape(dims, dtype):
    return jax.ShapeDtypeStruct(dims, dtype)


def whole(array):
    zeros = (0,) * array.ndim
    return pl.BlockSpec(array.shape, lambda *_: zeros, pipeline_mode=pl.Buffered(1))


def across(rows, width):
    return pl.BlockSpec((rows, width), lambda i, *_: (i, 0))


def along(height, columns):
    return pl.BlockSpec((height, columns), lambda i, *_: (0, i))


def fixed(*dims):
    zeros = (0,) * len(dims)
    return pl.BlockSpec(dims, lambda *_: zeros)


def params(mebibytes):
    return pltpu.CompilerParams(vmem_limit_bytes=mebibytes << 20)


def cost(flops, nbytes):
    return pl.CostEstimate(flops=int(flops * SHARE), bytes_accessed=int(nbytes * SHARE), transcendentals=0)


def iota(dims, axis):
    return lax.broadcasted_iota(jnp.int32, dims, axis)


def accumulate(ref, first, value):
    @pl.when(first)
    def _():
        ref[...] = value

    @pl.when(jnp.logical_not(first))
    def _():
        ref[...] += value


def normalize(values):
    center = values - jnp.mean(values, axis=-1, keepdims=True)
    inverse = lax.rsqrt(jnp.mean(center * center, axis=-1, keepdims=True) + EPSILON)
    return center * inverse, inverse


def normalize_back(upstream, normed, inverse, gains):
    scaled = upstream * gains
    mean_plain = jnp.mean(scaled, axis=-1, keepdims=True)
    mean_mixed = jnp.mean(scaled * normed, axis=-1, keepdims=True)
    return inverse * (scaled - mean_plain - normed * mean_mixed)


def gelu_parts(u):
    ratio = 1.0 / (1.0 + (0.3275911 * math.sqrt(0.5)) * jnp.abs(u))
    bell = jnp.exp(-0.5 * u * u)
    series = 0.5 * 1.061405429
    for factor in (-1.453152027, 1.421413741, -0.284496736, 0.254829592):
        series = series * ratio + 0.5 * factor
    tail = series * ratio * bell
    below = jnp.where(u < 0, tail, 1.0 - tail)
    return u * below, below + u * (bell * (1.0 / math.sqrt(2.0 * math.pi)))


class Sizes:
    def __init__(self, keep_lo, keep_hi, w_embed, img_lo, img_hi, groups):
        self.lo_each, self.hi_each = keep_lo[0] // groups, keep_hi[0] // groups
        self.lo_length, self.hi_length = keep_lo[1], keep_hi[1]
        self.features, self.width = w_embed
        self.lo_patches, self.hi_patches = img_lo[1], img_hi[1]
        self.groups = groups
        self.pack = LANES // self.lo_length
        self.lo_tiles = -(-self.lo_each // self.pack)
        self.hi_rows = self.hi_each * self.hi_length
        tiles = self.hi_each + self.lo_tiles
        self.tiles = tiles + tiles % 2
        self.rows = self.tiles * LANES


def sample_tiles(s):
    out = []
    for t in range(s.tiles - s.hi_each):
        first = t * s.pack
        out.append((s.hi_each + t, first, max(0, min(s.pack, s.lo_each - first))))
    return out


def slots(rows, fill, s):
    missing = s.pack - len(rows)
    if missing:
        rows = rows + [jnp.full((1, missing * s.lo_length), fill, rows[0].dtype if rows else jnp.int32)]
    return rows[0] if len(rows) == 1 else jnp.concatenate(rows, axis=1)


def pick_kernel(s, members, member_ref, keep_lo_ref, keep_hi_ref, img_lo_ref, img_hi_ref, *out_refs):
    for k, out_ref in zip(members, out_refs):
        other = member_ref[0] ^ k
        for i in range(s.hi_each):
            at = other * s.hi_each + i
            chosen = iota((s.hi_patches, LANES), 0) == keep_hi_ref[pl.ds(at, 1), :]
            got = nn(img_hi_ref[at], jnp.where(chosen, 1.0, 0.0).astype(BF16))
            out_ref[:, i * LANES : (i + 1) * LANES] = got.astype(BF16)
        for tile, first, count in sample_tiles(s):
            parts = []
            for j in range(count):
                at = other * s.lo_each + first + j
                chosen = iota((s.lo_patches, s.lo_length), 0) == keep_lo_ref[pl.ds(at, 1), :]
                parts.append(nn(img_lo_ref[at], jnp.where(chosen, 1.0, 0.0).astype(BF16)))
            if count < s.pack:
                parts.append(jnp.zeros((s.features, (s.pack - count) * s.lo_length), F32))
            joined = jnp.concatenate(parts, axis=1) if len(parts) > 1 else parts[0]
            out_ref[:, tile * LANES : (tile + 1) * LANES] = joined.astype(BF16)


def pick(s, members, member, keep_lo, keep_hi, img_lo, img_hi):
    args = (keep_lo, keep_hi, img_lo, img_hi)
    return pl.pallas_call(
        functools.partial(pick_kernel, s, members),
        grid_spec=pltpu.PrefetchScalarGridSpec(
            num_scalar_prefetch=1,
            grid=(1,),
            in_specs=[whole(a) for a in args],
            out_specs=[fixed(s.features, s.rows)] * len(members),
        ),
        out_shape=[shape((s.features, s.rows), BF16)] * len(members),
        compiler_params=params(60),
        cost_estimate=cost(2e9, 4e6),
    )(member, *args)


def stage_kernel(s, member_ref, keep_lo_ref, keep_hi_ref, mask_lo_ref, mask_hi_ref, cot_lo_ref, cot_hi_ref, keep_ref, seen_ref, *out_refs):
    eye = jnp.where(iota((s.features, s.features), 0) == iota((s.features, s.features), 1), 1.0, 0.0).astype(BF16)
    first_hi = (iota((1, s.hi_length), 1) == 0).astype(jnp.int32)
    first_lo = (iota((1, s.lo_length), 1) == 0).astype(jnp.int32)
    for k, out_ref in enumerate(out_refs):
        other = member_ref[0] ^ k
        for i in range(s.hi_each):
            at = other * s.hi_each + i
            keep_ref[k, i : i + 1, :] = keep_hi_ref[pl.ds(at, 1), :]
            out_ref[:, i * LANES : (i + 1) * LANES] = cot_hi_ref[at]
            if k == 0:
                seen_ref[i : i + 1, :] = jnp.maximum(mask_hi_ref[pl.ds(at, 1), :], first_hi).astype(F32)
        for tile, first, count in sample_tiles(s):
            begin = other * s.lo_each + first
            keep_ref[k, tile : tile + 1, :] = slots([keep_lo_ref[pl.ds(begin + j, 1), :] for j in range(count)], -1, s)
            if k == 0:
                seen = [jnp.maximum(mask_lo_ref[pl.ds(begin + j, 1), :], first_lo) for j in range(count)]
                seen_ref[tile : tile + 1, :] = slots(seen, 0, s).astype(F32)
            where = slice(tile * LANES, (tile + 1) * LANES)
            if count < s.pack:
                out_ref[:, where] = jnp.zeros((s.features, LANES), BF16)
            if count:
                size = count * s.lo_length
                start = pl.multiple_of(begin * s.lo_length, s.lo_length)
                out_ref[:, tile * LANES : tile * LANES + size] = nt(eye, cot_lo_ref[pl.ds(start, size), :]).astype(BF16)


def stage(s, member, keep_lo, keep_hi, mask_lo, mask_hi, cot_lo, cot_hi):
    args = (keep_lo, keep_hi, mask_lo, mask_hi, cot_lo, cot_hi)
    return pl.pallas_call(
        functools.partial(stage_kernel, s),
        grid_spec=pltpu.PrefetchScalarGridSpec(
            num_scalar_prefetch=1,
            grid=(1,),
            in_specs=[whole(a) for a in args],
            out_specs=[fixed(s.groups, s.tiles, LANES), fixed(s.tiles, LANES)]
            + [fixed(s.features, s.rows)] * s.groups,
        ),
        out_shape=[shape((s.groups, s.tiles, LANES), jnp.int32), shape((s.tiles, LANES), F32)]
        + [shape((s.features, s.rows), BF16)] * s.groups,
        compiler_params=params(60),
        cost_estimate=cost(1e8, 4e6),
    )(member, *args)


def chosen_columns(s, keep_ref, tile, patches, wanted_hi):
    row = keep_ref[pl.ds(tile, 1), :]
    is_hi = tile < s.hi_each
    row = jnp.where(is_hi if wanted_hi else jnp.logical_not(is_hi), row, -1)
    column = jnp.broadcast_to(row.astype(F32), (LANES, LANES)).T.astype(jnp.int32)
    parts = [jnp.where(iota((LANES, LANES), 1) + at == column, 1.0, 0.0) for at in range(0, patches, LANES)]
    return jnp.concatenate(parts, axis=1).astype(BF16)


def pair_masks():
    lane = iota((1, LANES), 1)
    low = jnp.where(lane < LANES // 2, 1.0, 0.0).astype(BF16)
    high = jnp.where(lane < LANES // 2, 0.0, 1.0).astype(BF16)
    return low, high


def doubled(block, masks):
    return jnp.concatenate([block * masks[0], block * masks[1]], axis=0)


def allowed(s, seen_ref, tile):
    bits = jnp.where(tile < s.hi_each, s.hi_length.bit_length() - 1, s.lo_length.bit_length() - 1)
    same = (iota((LANES, LANES), 0) >> bits) == (iota((LANES, LANES), 1) >> bits)
    open_to = jnp.logical_and(same, seen_ref[pl.ds(tile, 1), :] > 0)
    return jnp.concatenate([open_to, open_to], axis=0)


def forward_kernel(s, heads, keep_ref, seen_ref, p0, p1, p2, p3, w0, w1, w2, w3, pos_lo_ref, pos_hi_ref, gain1_ref, wqkv_ref, wout_ref, x0_ref, a_ref, qkv_ref, probs_ref, mixed_ref, x1_ref):
    step = pl.program_id(0)
    per = ROWS // LANES
    width = s.width
    picked = jnp.concatenate([p[...] for p in (p0, p1, p2, p3)], axis=0)
    embed = jnp.concatenate([w[: s.features, :] for w in (w0, w1, w2, w3)], axis=0)
    hot_hi = jnp.concatenate([chosen_columns(s, keep_ref, step * per + j, s.hi_patches, True) for j in range(per)], axis=0)
    hot_lo = jnp.concatenate([chosen_columns(s, keep_ref, step * per + j, s.lo_patches, False) for j in range(per)], axis=0)
    start = tn(picked, embed) + (nn(hot_hi, pos_hi_ref[...]) + nn(hot_lo, pos_lo_ref[...]))
    x0_ref[...] = start.astype(BF16)
    normed, _ = normalize(start)
    normed = (normed * gain1_ref[...]).astype(BF16)
    a_ref[...] = normed
    for c in range(3):
        part = slice(c * width, (c + 1) * width)
        qkv_ref[:, part] = nn(normed, wqkv_ref[:, part]).astype(BF16)
    masks = pair_masks()
    scale = 1.0 / math.sqrt(width // heads)
    for j in range(per):
        rows = slice(j * LANES, (j + 1) * LANES)
        ok = allowed(s, seen_ref, step * per + j)
        for h in range(width // LANES):
            at = h * LANES
            q = qkv_ref[rows, at : at + LANES]
            k = qkv_ref[rows, width + at : width + at + LANES]
            v = qkv_ref[rows, 2 * width + at : 2 * width + at + LANES]
            scores = nt(doubled(q, masks), k) * scale
            scores = jnp.where(ok, scores, MASKED)
            raised = jnp.exp(scores - jnp.max(scores, axis=-1, keepdims=True))
            probs = raised / jnp.sum(raised, axis=-1, keepdims=True)
            rounded = probs.astype(BF16)
            probs_ref[j, h] = rounded
            wide = jnp.concatenate([rounded[:LANES], rounded[LANES:]], axis=1)
            mixed_ref[rows, at : at + LANES] = nn(wide, doubled(v, masks)).astype(BF16)
    middle = start + nn(mixed_ref[...], wout_ref[...])
    x1_ref[...] = middle


def forward(s, heads, keep, seen, picked, weights, pos_lo, pos_hi, gain1, wqkv, wout):
    width, rows = s.width, s.rows
    per, pairs = ROWS // LANES, width // LANES
    return pl.pallas_call(
        functools.partial(forward_kernel, s, heads),
        grid=(rows // ROWS,),
        in_specs=[whole(keep), whole(seen)]
        + [along(s.features, ROWS)] * 4
        + [whole(w) for w in weights]
        + [whole(a) for a in (pos_lo, pos_hi, gain1, wqkv, wout)],
        out_specs=[
            across(ROWS, width),
            across(ROWS, width),
            across(ROWS, 3 * width),
            pl.BlockSpec((per, pairs, 2 * LANES, LANES), lambda i: (i, 0, 0, 0)),
            across(ROWS, width),
            across(ROWS, width),
        ],
        out_shape=[
            shape((rows, width), BF16),
            shape((rows, width), BF16),
            shape((rows, 3 * width), BF16),
            shape((s.tiles, pairs, 2 * LANES, LANES), BF16),
            shape((rows, width), BF16),
            shape((rows, width), F32),
        ],
        compiler_params=params(60),
        cost_estimate=cost(1.5e10, 3e7),
    )(keep, seen, *picked, *weights, pos_lo, pos_hi, gain1, wqkv, wout)


def part_rows(width, offset):
    return pl.BlockSpec((ROWS, width), lambda i, *_: (i + offset, 0))


def relative(ids_ref, x, y, z, c):
    return ids_ref[0] ^ (2 * z + y), ids_ref[1] ^ (2 * x + c)


def places(ids_ref, far):
    out = []
    for c in range(2):
        for x in range(2):
            for y in range(2):
                for z in range(far):
                    d, v = relative(ids_ref, x, y, z, c)
                    out.append(d * 4 + v)
    return out


def turn_relative(ids_ref, far, block, source_ref, turned_ref, acc_ref):
    order = places(ids_ref, far)
    rows = source_ref.shape[0]
    for begin in range(0, rows, rows // 2):
        span = slice(begin, begin + rows // 2)
        acc_ref[:, : rows // 2] = source_ref[span, :].astype(F32).T
        for p in range(0, len(order), 2):
            pair = [
                acc_ref[pl.ds(pl.multiple_of(at * block, 8), block), : rows // 2]
                for at in order[p : p + 2]
            ]
            turned_ref[p * block : (p + 2) * block, span] = jnp.concatenate(pair, axis=0).astype(BF16)


def spread(ids_ref, far, acc_ref, outs, block, extra):
    for x in range(2):
        for y in range(2):
            for z in range(far):
                for c, out_ref in enumerate(outs):
                    d, v = relative(ids_ref, x, y, z, c)
                    start = pl.multiple_of((d * 4 + v) * block, 8)
                    out_ref[x, y, z, :block, :] = acc_ref[pl.ds(start, block), :].astype(BF16)
                    out_ref[x, y, z, block:, :] = extra


def spread_features(s, ids_ref, acc_ref, outs):
    half = s.features // 2
    for k in range(4):
        for y in range(2):
            start = k * s.features + ((ids_ref[0] & 1) ^ y) * half
            rows = acc_ref[pl.ds(pl.multiple_of(start, 8), half), :]
            outs[k % 2][k // 2, y] = rows.astype(BF16)


def hidden_kernel(s, far, chunks, ids_ref, seen_ref, c0, c1, c2, c3, h0, h1, h2, h3, x1_ref, mixed_ref, w1_ref, b1_ref, w2_ref, b2_ref, gain2_ref, wout_ref, two0_ref, two1_ref, one0_ref, one1_ref, p0, p1, p2, p3, out0_ref, out1_ref, n0_ref, n1_ref, go_ref, ga_ref, b_ref, turned_ref, gm_ref, gpred_ref, forth_ref, back_ref, z_ref, gu_ref, acc_ref, side_ref):
    step = pl.program_id(0)
    width = s.width
    block = width // (8 * far)
    subs = [slice(begin, begin + ROWS) for begin in range(0, s.rows, ROWS)]
    seen = jnp.concatenate([seen_ref[t : t + 1, :] for t in range(s.tiles)], axis=1)

    @pl.when(step == 0)
    def _():
        gpred_ref[...] = jnp.concatenate([c[...] for c in (c0, c1, c2, c3)], axis=0) * seen.astype(BF16)
        head = jnp.concatenate([h[s.features :, :] for h in (h0, h1, h2, h3)], axis=0)
        total = None
        for rows in subs:
            values = x1_ref[rows, :]
            normed, _ = normalize(values)
            b_ref[rows, :] = (normed * gain2_ref[...]).astype(BF16)
            forth_ref[rows, :] = values + b2_ref[...]
            back_ref[rows, :] = jnp.zeros((ROWS, width), F32)
            upward = tn(gpred_ref[:, rows], head).astype(BF16)
            gm_ref[rows, :] = upward
            part = jnp.sum(upward.astype(F32), axis=0, keepdims=True)
            total = part if total is None else total + part
        side_ref[1:2, :] = total
        turn_relative(ids_ref, far, block, b_ref, turned_ref, acc_ref)

    @pl.when(step < chunks)
    def _():
        w1, w2, bias = w1_ref[...], w2_ref[...], b1_ref[...]
        total = None
        ahead = [(nn(b_ref[subs[0], :], w1), nt(gm_ref[subs[0], :], w2))]
        for at, rows in enumerate(subs):
            if at + 1 < len(subs):
                later = subs[at + 1]
                ahead.append((nn(b_ref[later, :], w1), nt(gm_ref[later, :], w2)))
            u, upward = ahead[at]
            z, slope = gelu_parts(u + bias)
            z = z.astype(BF16)
            gu = (upward * slope).astype(BF16)
            z_ref[rows, :] = z
            gu_ref[rows, :] = gu
            part = jnp.sum(gu.astype(F32), axis=0, keepdims=True)
            total = part if total is None else total + part
            forth_ref[rows, :] += nn(z, w2)
            back_ref[rows, :] += nt(gu, w1)
        side_ref[pl.ds(2 + ((ids_ref[0] >> 1) ^ step), 1), :] = total
        ones = nn(turned_ref[...], gu_ref[...])
        one0_ref[0] = ones[: width // 2].astype(BF16)
        one1_ref[0] = ones[width // 2 :].astype(BF16)
        acc_ref[...] = tn(z_ref[...], gm_ref[...])
        tall = width // 8
        for x in range(2):
            for y in range(2):
                for c, out_ref in enumerate((two0_ref, two1_ref)):
                    d, v = relative(ids_ref, x, y, 0, c)
                    start = pl.multiple_of(((d & 1) * 4 + v) * tall, 8)
                    out_ref[x, y, 0] = acc_ref[pl.ds(start, tall), :].astype(BF16)

    @pl.when(step == chunks)
    def _():
        total = None
        for rows in subs:
            z_ref[rows, :] = forth_ref[rows, :].astype(BF16)
            upward = back_ref[rows, :]
            normed, inverse = normalize(x1_ref[rows, :])
            part = jnp.sum(upward * normed, axis=0, keepdims=True)
            total = part if total is None else total + part
            grad = gm_ref[rows, :].astype(F32) + normalize_back(upward, normed, inverse, gain2_ref[...])
            grad = grad.astype(BF16)
            ga_ref[rows, :] = grad
            go_ref[rows, :] = nt(grad, wout_ref[...]).astype(BF16)
        side_ref[0:1, :] = total
        final = z_ref[...]
        for head, out in zip((h0, h1, h2, h3), (p0, p1, p2, p3)):
            out[...] = (nt(head[s.features :, :], final) * seen).astype(BF16)
        acc_ref[: s.groups * s.features, :] = nn(gpred_ref[...], final)
        spread_features(s, ids_ref, acc_ref, (n0_ref, n1_ref))
        acc_ref[...] = tn(mixed_ref[...], ga_ref[...])
        spread(ids_ref, far, acc_ref, (out0_ref, out1_ref), block, side_ref[...].astype(BF16))


def hidden(s, ids, far, seen, cots, weights, x1, mixed, w1, b1, w2, b2, gain2, wout):
    rows, width = s.rows, s.width
    chunks = w1.shape[1] // width
    block = width // (8 * far)
    high = s.groups * s.features
    sides = 8 * -(-(2 + chunks) // 8)
    last = chunks - 1

    def chunk(i, ids):
        return (ids[0] >> 1) ^ jnp.minimum(i, last)

    first = [seen, *cots, *weights, x1, mixed]
    rest = [b2, gain2, wout]
    outs = (
        [((2, 2, far, width // 8, width), BF16)] * 2
        + [((chunks, width // 2, width), BF16)] * 2
        + [((s.features, rows), BF16)] * 4
        + [((2, 2, far, block + sides, width), BF16)] * 2
        + [((2, 2, s.features // 2, width), BF16)] * 2
        + [((rows, width), BF16)] * 2
    )
    specs = [
        pl.BlockSpec((2, 2, 1, width // 8, width), lambda i, ids: (0, 0, jnp.minimum(i, last), 0, 0))
    ] * 2
    specs += [pl.BlockSpec((1, width // 2, width), lambda i, ids: (chunk(i, ids), 0, 0))] * 2
    specs += [fixed(*dims) for dims, _ in outs[4:]]
    return pl.pallas_call(
        functools.partial(hidden_kernel, s, far, chunks),
        grid_spec=pltpu.PrefetchScalarGridSpec(
            num_scalar_prefetch=1,
            grid=(chunks + 1,),
            in_specs=[whole(a) for a in first]
            + [
                pl.BlockSpec((width, width), lambda i, ids: (0, chunk(i, ids))),
                pl.BlockSpec((1, width), lambda i, ids: (0, chunk(i, ids))),
                pl.BlockSpec((width, width), lambda i, ids: (chunk(i, ids), 0)),
            ]
            + [whole(a) for a in rest],
            out_specs=specs,
            scratch_shapes=[
                pltpu.VMEM((rows, width), BF16),
                pltpu.VMEM((width, rows), BF16),
                pltpu.VMEM((rows, width), BF16),
                pltpu.VMEM((high, rows), BF16),
                pltpu.VMEM((rows, width), F32),
                pltpu.VMEM((rows, width), F32),
                pltpu.VMEM((rows, width), BF16),
                pltpu.VMEM((rows, width), BF16),
                pltpu.VMEM((width, width), F32),
                pltpu.VMEM((sides, width), F32),
            ],
        ),
        out_shape=[shape(*out) for out in outs],
        compiler_params=params(60),
        cost_estimate=cost(3.4e10, 4e7),
    )(ids, *first, w1, b1, w2, *rest)


def attention_back(s, heads, qkv_ref, probs_ref, go_ref, gqkv_ref):
    per = ROWS // LANES
    width = s.width
    masks = pair_masks()
    scale = 1.0 / math.sqrt(width // heads)
    for j in range(per):
        rows = slice(j * LANES, (j + 1) * LANES)
        for h in range(width // LANES):
            at = h * LANES
            q = doubled(qkv_ref[rows, at : at + LANES], masks)
            k = doubled(qkv_ref[rows, width + at : width + at + LANES], masks)
            v = qkv_ref[rows, 2 * width + at : 2 * width + at + LANES]
            out = doubled(go_ref[rows, at : at + LANES], masks)
            rounded = probs_ref[j, h]
            probs = rounded.astype(F32)
            upward = nt(out, v)
            centred = upward - jnp.sum(probs * upward, axis=-1, keepdims=True)
            grads = (probs * centred).astype(BF16)
            wide = jnp.concatenate([grads[:LANES], grads[LANES:]], axis=1)
            gqkv_ref[rows, at : at + LANES] = (nn(wide, k) * scale).astype(BF16)
            gqkv_ref[rows, width + at : width + at + LANES] = (tn(grads, q) * scale).astype(BF16)
            gqkv_ref[rows, 2 * width + at : 2 * width + at + LANES] = tn(rounded, out).astype(BF16)


def first_norm_back(gqkv, x0_ref, ga_ref, wqkv_ref, gain1_ref):
    upward = nt(gqkv, wqkv_ref[...])
    normed, inverse = normalize(x0_ref[...].astype(F32))
    grad = ga_ref[...].astype(F32) + normalize_back(upward, normed, inverse, gain1_ref[...])
    return grad.astype(BF16), jnp.sum(upward * normed, axis=0, keepdims=True)


def backward_kernel(s, heads, qkv_ref, probs_ref, go_ref, x0_ref, ga_ref, wqkv_ref, gain1_ref, gqkv_ref, g0_ref, gln1_ref):
    attention_back(s, heads, qkv_ref, probs_ref, go_ref, gqkv_ref)
    g0_ref[...], gain_part = first_norm_back(gqkv_ref[...], x0_ref, ga_ref, wqkv_ref, gain1_ref)
    accumulate(gln1_ref, pl.program_id(0) == 0, gain_part)


def row_inputs(s, offset):
    width = s.width
    return [
        part_rows(3 * width, offset),
        pl.BlockSpec((ROWS // LANES, width // LANES, 2 * LANES, LANES), lambda i, *_: (i + offset, 0, 0, 0)),
        part_rows(width, offset),
        part_rows(width, offset),
        part_rows(width, offset),
    ]


def backward(s, heads, offset, steps, qkv, probs, go, x0, ga, wqkv, gain1):
    width = s.width
    size = steps * ROWS
    return pl.pallas_call(
        functools.partial(backward_kernel, s, heads),
        grid=(steps,),
        in_specs=row_inputs(s, offset) + [whole(wqkv), whole(gain1)],
        out_specs=[across(ROWS, 3 * width), across(ROWS, width), fixed(1, width)],
        out_shape=[shape((size, 3 * width), BF16), shape((size, width), BF16), shape((1, width), F32)],
        compiler_params=params(60),
        cost_estimate=cost(8e9 * steps, 6e6 * steps),
    )(qkv, probs, go, x0, ga, wqkv, gain1)


def position_grads(s, keep_ref, g0, picked):
    hot_hi, hot_lo = [], []
    for t in range(s.tiles):
        row = keep_ref[t : t + 1, :]
        patches = s.hi_patches if t < s.hi_each else s.lo_patches
        hot = jnp.where(iota((patches, LANES), 0) == row, 1.0, 0.0).astype(BF16)
        (hot_hi if t < s.hi_each else hot_lo).append(hot)
    hi_rows = s.hi_each * LANES
    hi = nn(jnp.concatenate(hot_hi, axis=1), g0[:hi_rows])
    lo = nn(jnp.concatenate(hot_lo, axis=1), g0[hi_rows:])
    return lo, hi, nn(jnp.concatenate(picked, axis=0), g0)


def finish_kernel(s, far, chunks, ids_ref, keep_ref, a_ref, r0_ref, r1_ref, ga_ref, gb_ref, la_ref, lb_ref, p0, p1, p2, p3, w0, w1, w2, w3, o0_ref, o1_ref, e0_ref, e1_ref, i0, i1, i2, i3, turned_ref, acc_ref, lo_ref, hi_ref):
    step = pl.program_id(0)
    width = s.width
    block = width // (8 * far)
    half = width // 2
    done = r0_ref.shape[0]

    @pl.when(step == 0)
    def _():
        turn_relative(ids_ref, far, block, a_ref, turned_ref, acc_ref)

    @pl.when(step < chunks)
    def _():
        value = nn(turned_ref[:, :done], r0_ref[...]) + nn(turned_ref[:, done:], r1_ref[...])
        o0_ref[0] = value[:half].astype(BF16)
        o1_ref[0] = value[half:].astype(BF16)

    @pl.when(step == chunks)
    def _():
        g0 = jnp.concatenate([ga_ref[...], gb_ref[...]], axis=0)
        lo, hi, embed = position_grads(s, keep_ref, g0, [p[...] for p in (p0, p1, p2, p3)])
        lo_ref[...] = lo
        hi_ref[...] = hi
        acc_ref[: s.groups * s.features, :] = embed
        spread_features(s, ids_ref, acc_ref, (e0_ref, e1_ref))
        for weight, out in zip((w0, w1, w2, w3), (i0, i1, i2, i3)):
            out[...] = nt(weight[: s.features, :], g0).astype(BF16)
        hi_block = s.hi_patches // (8 * far)
        lo_block = s.lo_patches // (8 * far)
        gain = la_ref[...] + lb_ref[...]
        pad = jnp.zeros((block - hi_block - lo_block - 1, width), F32)
        order = places(ids_ref, far)
        for p in range(0, len(order), 2):
            pair = []
            for at in order[p : p + 2]:
                both = lo_ref[pl.ds(pl.multiple_of((at >> 1) * 8, 8), 8), :]
                pair += [
                    hi_ref[pl.ds(pl.multiple_of(at * hi_block, 8), hi_block), :],
                    jnp.where((at & 1) == 1, both[lo_block:], both[:lo_block]),
                    gain,
                    pad,
                ]
            row = (p % (len(order) // 2)) * block
            (o0_ref, o1_ref)[p // (len(order) // 2)][0, row : row + 2 * block, :] = jnp.concatenate(pair, axis=0).astype(BF16)


def finish(s, ids, far, keep, a, gqkvs, g0s, gains, picked, weights):
    width, rows = s.width, s.rows
    chunks = gqkvs[0].shape[1] // width
    rest = [*g0s, *gains, *picked, *weights]
    out = pl.BlockSpec((1, width // 2, width), lambda i, ids: (i, 0, 0))
    return pl.pallas_call(
        functools.partial(finish_kernel, s, far, chunks),
        grid_spec=pltpu.PrefetchScalarGridSpec(
            num_scalar_prefetch=1,
            grid=(chunks + 1,),
            in_specs=[whole(keep), whole(a)]
            + [
                pl.BlockSpec((g.shape[0], width), lambda i, ids: (0, jnp.minimum(i, chunks - 1)))
                for g in gqkvs
            ]
            + [whole(r) for r in rest],
            out_specs=[out, out]
            + [fixed(2, 2, s.features // 2, width)] * 2
            + [fixed(s.features, rows)] * 4,
            scratch_shapes=[
                pltpu.VMEM((width, rows), BF16),
                pltpu.VMEM((width, width), F32),
                pltpu.VMEM((s.lo_patches, width), F32),
                pltpu.VMEM((s.hi_patches, width), F32),
            ],
        ),
        out_shape=[shape((chunks + 1, width // 2, width), BF16)] * 2
        + [shape((2, 2, s.features // 2, width), BF16)] * 2
        + [shape((s.features, rows), BF16)] * 4,
        compiler_params=params(60),
        cost_estimate=cost(7e9, 1.2e7),
    )(ids, keep, a, *gqkvs, *rest)


def combine_kernel(held_ref, got_ref, keep_ref, send_ref):
    send_ref[...] = (held_ref[:, 1].astype(F32) + got_ref[:, 1].astype(F32)).astype(BF16)
    keep_ref[...] = (held_ref[:, 0].astype(F32) + got_ref[:, 0].astype(F32)).astype(BF16)


def combine(held, got, axis):
    dims = held.shape
    width = dims[-1]
    outer = math.prod(dims[:axis])
    inner = math.prod(dims[axis + 1 : -1])
    grid = (outer // 4, 1) if outer > 4 else (1, 2)
    broad, tall = outer // grid[0], inner // grid[1]
    half = shape((outer, inner, width), BF16)
    spec = pl.BlockSpec((broad, 2, tall, width), lambda i, j: (i, 0, j, 0))
    out = pl.BlockSpec((broad, tall, width), lambda i, j: (i, j, 0))
    keep, send = pl.pallas_call(
        combine_kernel,
        grid=grid,
        in_specs=[spec, spec],
        out_specs=[out, out],
        out_shape=[half, half],
        compiler_params=params(60),
        cost_estimate=cost(1e6, 6 * outer * inner * width),
    )(*(value.reshape(outer, 2, inner, width) for value in (held, got)))
    left = dims[:axis] + dims[axis + 1 :]
    return keep.reshape(left), send.reshape(left)


def place_kernel(s, member_ref, keep_ref, r0, r1, r2, r3, lo_ref, hi_ref):
    lane_sample = iota((1, LANES), 1) // s.lo_length
    for k, got_ref in enumerate((r0, r1, r2, r3)):
        other = member_ref[0] ^ k
        for i in range(s.hi_each):
            chosen = iota((s.hi_patches, LANES), 0) == keep_ref[k, i : i + 1, :]
            hot = jnp.where(chosen, 1.0, 0.0).astype(BF16)
            hi_ref[other * s.hi_each + i] = nt(got_ref[:, i * LANES : (i + 1) * LANES], hot).astype(BF16)
        for tile, first, count in sample_tiles(s):
            got = got_ref[:, tile * LANES : (tile + 1) * LANES]
            for j in range(count):
                row = jnp.where(lane_sample == j, keep_ref[k, tile : tile + 1, :], -1)
                hot = jnp.where(iota((s.lo_patches, LANES), 0) == row, 1.0, 0.0).astype(BF16)
                lo_ref[other * s.lo_each + first + j] = nt(got, hot).astype(BF16)


def place(s, member, keep, blocks):
    lo = s.groups * s.lo_each
    hi = s.groups * s.hi_each
    return pl.pallas_call(
        functools.partial(place_kernel, s),
        grid_spec=pltpu.PrefetchScalarGridSpec(
            num_scalar_prefetch=1,
            grid=(1,),
            in_specs=[whole(keep)] + [whole(b) for b in blocks],
            out_specs=[fixed(lo, s.features, s.lo_patches), fixed(hi, s.features, s.hi_patches)],
        ),
        out_shape=[
            shape((lo, s.features, s.lo_patches), BF16),
            shape((hi, s.features, s.hi_patches), BF16),
        ],
        compiler_params=params(60),
        cost_estimate=cost(2e9, 4e6),
    )(member, keep, *blocks)


def predict_kernel(s, member_ref, r0, r1, r2, r3, lo_ref, hi_ref):
    eye = jnp.where(iota((s.features, s.features), 0) == iota((s.features, s.features), 1), 1.0, 0.0).astype(BF16)
    for k, got_ref in enumerate((r0, r1, r2, r3)):
        other = member_ref[0] ^ k
        for i in range(s.hi_each):
            hi_ref[other * s.hi_each + i] = got_ref[:, i * LANES : (i + 1) * LANES]
        for tile, first, count in sample_tiles(s):
            if count:
                size = count * s.lo_length
                turned = tn(got_ref[:, tile * LANES : (tile + 1) * LANES], eye).astype(BF16)
                start = pl.multiple_of((other * s.lo_each + first) * s.lo_length, s.lo_length)
                lo_ref[pl.ds(start, size), :] = turned[:size]


def predict(s, member, blocks):
    lo = s.groups * s.lo_each * s.lo_length
    hi = s.groups * s.hi_each
    return pl.pallas_call(
        functools.partial(predict_kernel, s),
        grid_spec=pltpu.PrefetchScalarGridSpec(
            num_scalar_prefetch=1,
            grid=(1,),
            in_specs=[whole(b) for b in blocks],
            out_specs=[fixed(lo, s.features), fixed(hi, s.features, s.hi_length)],
        ),
        out_shape=[shape((lo, s.features), BF16), shape((hi, s.features, s.hi_length), BF16)],
        compiler_params=params(60),
        cost_estimate=cost(1e8, 3e6),
    )(member, *blocks)


def swap(value, data_bit, var_bit):
    dp, var = lax.axis_size("dp"), lax.axis_size("var")
    pairs = [
        (d * var + v, (d ^ data_bit) * var + (v ^ var_bit)) for d in range(dp) for v in range(var)
    ]
    return lax.ppermute(value, AXES, pairs)


def add_rounded(left, right):
    return (left.astype(F32) + right.astype(F32)).astype(BF16)


def added(*values):
    values = [value.astype(F32) for value in values]
    while len(values) > 1:
        values = [values[i] + values[i + 1] for i in range(0, len(values), 2)]
    return values[0]


def tie(value, *tokens):
    return lax.optimization_barrier((value, tokens))[0]


PARTNERS = {"core": (0, 1), "x": (0, 2), "y": (1, 0), "z0": (2, 0), "z1": (4, 0)}


class Chain:
    def __init__(self, near, sent):
        self.near, self.sent = near, sent
        self.repeats = near.ndim == 4
        self.names = ["x", "y"] if self.repeats else ["chunk", "x", "y", "z1", "z0"][7 - near.ndim :]
        self.held = self.got = None

    def outgoing(self, name):
        if name == "core":
            self.held = self.near
            return self.sent
        if name not in self.names:
            self.held = add_rounded(self.held, self.got)
            return self.held
        axis = self.names.index(name)
        self.names.remove(name)
        if math.prod(self.held.shape) >= 1 << 20:
            self.held, sent = combine(self.held, self.got, axis)
            return sent
        kept, sent = (
            [lax.index_in_dim(value, side, axis, keepdims=False) for value in (self.held, self.got)]
            for side in range(2)
        )
        self.held = add_rounded(*kept)
        return add_rounded(*sent)

    def hold(self, *tokens):
        self.held, self.got = tie((self.held, self.got), *tokens)

    def final(self):
        return added(self.held, self.got)


def send_rows(values, bits):
    if len(values) == 1:
        return [swap(values[0], *bits)]
    width = values[0].shape[-1]
    flat = [value.reshape(-1, width) for value in values]
    got = swap(jnp.concatenate(flat, axis=0), *bits)
    out, start = [], 0
    for value, rows in zip(values, flat):
        out.append(got[start : start + rows.shape[0]].reshape(value.shape))
        start += rows.shape[0]
    return out


def trade(name, *chains):
    got = send_rows([chain.outgoing(name) for chain in chains], PARTNERS[name])
    for chain, value in zip(chains, got):
        chain.got = value
    return got[0]


def both_halves(value):
    value = value.astype(BF16)
    other = swap(value, 1, 0)
    second = lax.axis_index("dp") % 2 == 1
    return jnp.concatenate(
        [jnp.where(second, other, value), jnp.where(second, value, other)], axis=0
    ).astype(F32)


def natural(near, sent):
    rows, width = near.shape[-2:]
    both = jnp.stack([near, sent]).reshape((2, -1, 2, 2, 4, rows, width))
    return both.transpose(4, 3, 2, 0, 1, 5, 6).reshape(32, -1, width)


def scattered(full):
    return lax.psum_scatter(full, AXES, scatter_dimension=0, tiled=True).astype(F32)


def joined(blocks, chunks):
    count, rows, width = blocks.shape
    split = blocks.reshape(count, chunks, rows // chunks, width).transpose(0, 2, 1, 3)
    return split.reshape(count * (rows // chunks), chunks * width)


def plain_sum(near, sent):
    if near.ndim >= 6:
        return natural(near, sent)
    value = jnp.stack([near, sent], axis=1)
    value = value.reshape((4, -1, near.shape[-1]))
    bit = 1
    while value.shape[0] > 1:
        value = value.reshape((value.shape[0] // 2, 2) + value.shape[1:])
        value = add_rounded(value[:, 0], swap(value[:, 1], 0, bit))
        bit *= 2
    return lax.psum(value[0], "dp").astype(F32)


def exchange_relative(blocks):
    return [blocks[0]] + [swap(blocks[k], 0, k) for k in range(1, len(blocks))]


def body(
    img_lo,
    img_hi,
    keep_lo,
    keep_hi,
    mask_lo,
    mask_hi,
    w_embed,
    pos_lo,
    pos_hi,
    ln1_gain,
    w_qkv,
    w_out,
    ln2_gain,
    w_fc1,
    b_fc1,
    w_fc2,
    b_fc2,
    w_head,
    cot_lo,
    cot_hi,
):
    groups = lax.axis_size("var")
    devices = lax.axis_size("dp") * groups
    member = lax.axis_index("var").astype(jnp.int32).reshape(1)
    s = Sizes(keep_lo.shape, keep_hi.shape, w_embed.shape, img_lo.shape, img_hi.shape, groups)
    features, width = s.features, s.width
    gain1, gain2 = ln1_gain.reshape(1, -1), ln2_gain.reshape(1, -1)
    img_lo_t, img_hi_t = img_lo.transpose(0, 2, 1), img_hi.transpose(0, 2, 1)

    own = jnp.concatenate([w_embed, w_head.T], axis=0)
    crossed = swap(own, 0, 2)
    weights = [own, swap(own, 0, 1), crossed, swap(crossed, 0, 1)]
    sent = pick(s, (1, 2, 3), member, keep_lo, keep_hi, img_lo_t, img_hi_t)
    picked = [swap(value, 0, k + 1) for k, value in enumerate(sent)]
    picked = [*pick(s, (0,), member, keep_lo, keep_hi, img_lo_t, img_hi_t), *picked]
    keep, seen, *cots = stage(
        s,
        tie(member, sent[0]),
        keep_lo,
        keep_hi,
        mask_lo,
        mask_hi,
        cot_lo.reshape(-1, features),
        cot_hi.transpose(0, 2, 1),
    )
    cots = exchange_relative(cots)
    own_keep = keep[0]
    x0, a, qkv, probs, mixed, x1 = forward(
        s, HEADS, own_keep, seen, picked, weights, pos_lo, pos_hi, gain1, w_qkv, w_out
    )
    far = 4
    cube = lax.axis_size("dp") == 2 * far
    place_of = lax.axis_index("dp") * groups + lax.axis_index("var")
    ids = jnp.stack([lax.axis_index("dp"), lax.axis_index("var")]).astype(jnp.int32)
    if not cube:
        ids = jnp.zeros_like(ids)

    def chain_of(near, sent):
        if near.ndim == 5:
            near, sent = (
                value.reshape((2, 2, 2, 2) + value.shape[3:]) for value in (near, sent)
            )
        elif near.ndim == 3:
            near, sent = (
                value.reshape((-1, 2, 2, 2, 2, width // 32, width)) for value in (near, sent)
            )
        return Chain(near, sent)

    def step(name, *chains):
        return trade(name, *chains) if cube else ()

    def halves_of(chain):
        out = []
        for side in range(2):
            piece = Chain(chain.near, chain.sent)
            count = chain.near.shape[0] // 2
            piece.held, piece.got = (
                lax.slice_in_dim(value, side * count, (side + 1) * count, axis=0)
                for value in (chain.held, chain.got)
            )
            out.append(piece)
        return out

    two0, two1, one0, one1, *rest = hidden(
        s,
        ids,
        far,
        tie(seen, x1),
        cots,
        weights,
        x1,
        mixed,
        w_fc1,
        b_fc1.reshape(1, -1),
        w_fc2,
        b_fc2.reshape(1, -1),
        gain2,
        w_out,
    )
    preds, (out0, out1, head0, head1, go, ga) = rest[:groups], rest[groups:]
    two, one = chain_of(two0, two1), chain_of(one0, one1)
    out, head = chain_of(out0, out1), chain_of(head0, head1)
    tokens = [step("core", chain) for chain in (two, one, out, head)]

    def back(offset, steps, *ready):
        return backward(
            s, HEADS, offset, steps, qkv, probs, go, x0, ga, w_qkv, tie(gain1, *ready)
        )

    parts = [back(0, 1, go)]
    if cube:
        for chain in (two, one, out, head):
            chain.hold(parts[0][0])
    near_tokens = [step("x", two, out, head), step("y", one)]
    parts.append(back(1, s.rows // ROWS - 1, parts[0][0], two.held, one.held, *tokens))
    got_preds = exchange_relative(preds)
    if cube:
        for chain in (two, one, out, head):
            chain.hold(parts[1][0])
    tokens = [step("y", two, out, head), step("x", one)]
    gqkvs, g0s, gains = zip(*parts)
    near, sent, near_embed, sent_embed, *blocks = finish(
        s,
        tie(ids, two.held, one.held, *near_tokens, *got_preds),
        far,
        own_keep,
        a,
        gqkvs,
        g0s,
        gains,
        picked,
        weights,
    )
    sent, sent_embed = tie((sent, sent_embed), *tokens)
    first, embed = chain_of(near, sent), chain_of(near_embed, sent_embed)
    tokens += [step("core", first), step("core", embed)]
    pred_lo, pred_hi = predict(s, tie(member, near), got_preds)
    if cube:
        old = (two, one, out, head)
        for chain in old:
            chain.hold(first.got)
        one_half, other_half = halves_of(first)
        tokens = [trade("x", one_half, embed), trade("y", other_half)]
        trade("z0", *old)
        for chain in old:
            chain.hold(*tokens)
        tokens = [trade("y", one_half, embed), trade("x", other_half)]
        trade("z1", *old)
        blocks = [tie(block_of, *tokens) for block_of in blocks]
        trade("z0", one_half, other_half, embed)
        trade("z1", one_half, other_half, embed)
        grad_fc2, grad_fc1, rest, grad_head, grad_embed = (
            chain.final() for chain in (two, one, out, head, embed)
        )
        grad_head, grad_embed = both_halves(grad_head), both_halves(grad_embed)
        first = jnp.concatenate([one_half.final(), other_half.final()], axis=0).reshape(-1, width)
        grad_fc1 = grad_fc1.reshape(-1, width)
    else:
        grad_fc2, grad_fc1, rest, grad_head, grad_embed, first = (
            plain_sum(chain.near, chain.sent) for chain in (two, one, out, head, embed, first)
        )
    grad_img_lo, grad_img_hi = place(s, member, keep, exchange_relative(blocks))
    grad_head = grad_head.T

    block = width // devices
    inner = w_fc1.shape[1] // width

    hi_block = s.hi_patches // devices
    lo_block = s.lo_patches // devices

    def own_part(row):
        return lax.dynamic_slice_in_dim(row, place_of * block, block)

    if cube:
        grad_fc1 = joined(grad_fc1[None], inner)
        grad_qkv = joined(first[None, : 3 * block], 3)
        grad_out, sides = rest[:block], rest[block:]
        extra = first[3 * block :]
        grad_pos_hi = extra[:hi_block]
        grad_pos_lo = extra[hi_block : hi_block + lo_block]
        first_side = extra[hi_block + lo_block]
    else:
        tall = width // 32
        hi_tall, lo_tall = s.hi_patches // 32, s.lo_patches // 32
        grad_fc2 = scattered(grad_fc2.reshape(-1, width))
        grad_fc1 = scattered(joined(grad_fc1, inner))
        grad_qkv = scattered(joined(first[:, : 3 * tall], 3))
        grad_out, sides = scattered(rest[:, :tall].reshape(-1, width)), rest[0, tall:]
        extra = first[:, 3 * tall :]
        grad_pos_hi = scattered(extra[:, :hi_tall].reshape(-1, width))
        grad_pos_lo = scattered(extra[:, hi_tall : hi_tall + lo_tall].reshape(-1, width))
        sides = lax.psum(jnp.concatenate([sides, extra[0, hi_tall + lo_tall :]]), AXES).astype(F32)
        first_side = sides[rest.shape[1] - tall]
    grad_ln1 = own_part(first_side)
    grad_ln2 = own_part(sides[0])
    grad_b2 = own_part(sides[1])
    grad_b1 = lax.dynamic_slice_in_dim(
        sides[2 : 2 + inner].reshape(-1), place_of * inner * block, inner * block
    )
    return (
        pred_lo.reshape(cot_lo.shape),
        pred_hi.transpose(0, 2, 1),
        grad_img_lo.transpose(0, 2, 1),
        grad_img_hi.transpose(0, 2, 1),
        grad_embed,
        grad_pos_lo,
        grad_pos_hi,
        grad_ln1,
        grad_qkv,
        grad_out,
        grad_ln2,
        grad_fc1,
        grad_b1,
        grad_fc2,
        grad_b2,
        grad_head,
    )


def solution(mesh):
    placed = (
        P("dp", None, "var"),
        P("dp", None, "var"),
        P("dp", None),
        P("dp", None),
        P("dp", None),
        P("dp", None),
        P("var", None),
        P(),
        P(),
        P(),
        P(),
        P(),
        P(),
        P(),
        P(),
        P(),
        P(),
        P(None, "var"),
        P("dp", None, "var"),
        P("dp", None, "var"),
    )
    return jax.shard_map(
        body,
        mesh=mesh,
        in_specs=placed,
        out_specs=(
            P("dp", None, "var"),
            P("dp", None, "var"),
            P("dp", None, "var"),
            P("dp", None, "var"),
            P("var", None),
            P(("dp", "var"), None),
            P(("dp", "var"), None),
            P(("dp", "var")),
            P(("dp", "var"), None),
            P(("dp", "var"), None),
            P(("dp", "var")),
            P(("dp", "var"), None),
            P(("dp", "var")),
            P(("dp", "var"), None),
            P(("dp", "var")),
            P(None, "var"),
        ),
        check_vma=False,
    )
```

```python
import functools
import math

import jax
import jax.numpy as jnp
from jax import lax
from jax.experimental import pallas as pl
from jax.experimental.pallas import tpu as pltpu
from jax.sharding import PartitionSpec as P

HEADS = 12
EPSILON = 1e-06
AXES = ("dp", "var")
BF16 = jnp.bfloat16
F32 = jnp.float32
LANES = 128
ROWS = 256
MASKED = -1000000000.0
SHARE = 0.5


def dot(left, right, dims):
    return lax.dot_general(left, right, (dims, ((), ())), preferred_element_type=F32)


def nn(left, right):
    return dot(left, right, ((1,), (0,)))


def nt(left, right):
    return dot(left, right, ((1,), (1,)))


def tn(left, right):
    return dot(left, right, ((0,), (0,)))


def shape(dims, dtype):
    return jax.ShapeDtypeStruct(dims, dtype)


def whole(array):
    zeros = (0,) * array.ndim
    return pl.BlockSpec(array.shape, lambda *_: zeros, pipeline_mode=pl.Buffered(1))


def across(rows, width):
    return pl.BlockSpec((rows, width), lambda i, *_: (i, 0))


def along(height, columns):
    return pl.BlockSpec((height, columns), lambda i, *_: (0, i))


def fixed(*dims):
    zeros = (0,) * len(dims)
    return pl.BlockSpec(dims, lambda *_: zeros)


def params(mebibytes):
    return pltpu.CompilerParams(vmem_limit_bytes=mebibytes << 20)


def cost(flops, nbytes):
    return pl.CostEstimate(flops=int(flops * SHARE), bytes_accessed=int(nbytes * SHARE), transcendentals=0)


def iota(dims, axis):
    return lax.broadcasted_iota(jnp.int32, dims, axis)


def accumulate(ref, first, value):
    @pl.when(first)
    def _():
        ref[...] = value

    @pl.when(jnp.logical_not(first))
    def _():
        ref[...] += value


def normalize(values):
    center = values - jnp.mean(values, axis=-1, keepdims=True)
    inverse = lax.rsqrt(jnp.mean(center * center, axis=-1, keepdims=True) + EPSILON)
    return center * inverse, inverse


def normalize_back(upstream, normed, inverse, gains):
    scaled = upstream * gains
    mean_plain = jnp.mean(scaled, axis=-1, keepdims=True)
    mean_mixed = jnp.mean(scaled * normed, axis=-1, keepdims=True)
    return inverse * (scaled - mean_plain - normed * mean_mixed)


def gelu_parts(u):
    ratio = 1.0 / (1.0 + (0.3275911 * math.sqrt(0.5)) * jnp.abs(u))
    bell = jnp.exp(-0.5 * u * u)
    series = 0.5 * 1.061405429
    for factor in (-1.453152027, 1.421413741, -0.284496736, 0.254829592):
        series = series * ratio + 0.5 * factor
    tail = series * ratio * bell
    below = jnp.where(u < 0, tail, 1.0 - tail)
    return u * below, below + u * (bell * (1.0 / math.sqrt(2.0 * math.pi)))


class Sizes:
    def __init__(self, keep_lo, keep_hi, w_embed, img_lo, img_hi, groups):
        self.lo_each, self.hi_each = keep_lo[0] // groups, keep_hi[0] // groups
        self.lo_length, self.hi_length = keep_lo[1], keep_hi[1]
        self.features, self.width = w_embed
        self.lo_patches, self.hi_patches = img_lo[1], img_hi[1]
        self.groups = groups
        self.pack = LANES // self.lo_length
        self.lo_tiles = -(-self.lo_each // self.pack)
        self.hi_rows = self.hi_each * self.hi_length
        tiles = self.hi_each + self.lo_tiles
        self.tiles = tiles + tiles % 2
        self.rows = self.tiles * LANES


def sample_tiles(s):
    out = []
    for t in range(s.tiles - s.hi_each):
        first = t * s.pack
        out.append((s.hi_each + t, first, max(0, min(s.pack, s.lo_each - first))))
    return out


def slots(rows, fill, s):
    missing = s.pack - len(rows)
    if missing:
        rows = rows + [jnp.full((1, missing * s.lo_length), fill, rows[0].dtype if rows else jnp.int32)]
    return rows[0] if len(rows) == 1 else jnp.concatenate(rows, axis=1)


def pick_kernel(s, members, member_ref, keep_lo_ref, keep_hi_ref, img_lo_ref, img_hi_ref, *out_refs):
    for k, out_ref in zip(members, out_refs):
        other = member_ref[0] ^ k
        for i in range(s.hi_each):
            at = other * s.hi_each + i
            chosen = iota((s.hi_patches, LANES), 0) == keep_hi_ref[pl.ds(at, 1), :]
            got = nn(img_hi_ref[at], jnp.where(chosen, 1.0, 0.0).astype(BF16))
            out_ref[:, i * LANES : (i + 1) * LANES] = got.astype(BF16)
        for tile, first, count in sample_tiles(s):
            parts = []
            for j in range(count):
                at = other * s.lo_each + first + j
                chosen = iota((s.lo_patches, s.lo_length), 0) == keep_lo_ref[pl.ds(at, 1), :]
                parts.append(nn(img_lo_ref[at], jnp.where(chosen, 1.0, 0.0).astype(BF16)))
            if count < s.pack:
                parts.append(jnp.zeros((s.features, (s.pack - count) * s.lo_length), F32))
            joined = jnp.concatenate(parts, axis=1) if len(parts) > 1 else parts[0]
            out_ref[:, tile * LANES : (tile + 1) * LANES] = joined.astype(BF16)


def pick(s, members, member, keep_lo, keep_hi, img_lo, img_hi):
    args = (keep_lo, keep_hi, img_lo, img_hi)
    return pl.pallas_call(
        functools.partial(pick_kernel, s, members),
        grid_spec=pltpu.PrefetchScalarGridSpec(
            num_scalar_prefetch=1,
            grid=(1,),
            in_specs=[whole(a) for a in args],
            out_specs=[fixed(s.features, s.rows)] * len(members),
        ),
        out_shape=[shape((s.features, s.rows), BF16)] * len(members),
        compiler_params=params(60),
        cost_estimate=cost(2e9, 4e6),
    )(member, *args)


def stage_kernel(s, member_ref, keep_lo_ref, keep_hi_ref, mask_lo_ref, mask_hi_ref, cot_lo_ref, cot_hi_ref, keep_ref, seen_ref, *out_refs):
    eye = jnp.where(iota((s.features, s.features), 0) == iota((s.features, s.features), 1), 1.0, 0.0).astype(BF16)
    first_hi = (iota((1, s.hi_length), 1) == 0).astype(jnp.int32)
    first_lo = (iota((1, s.lo_length), 1) == 0).astype(jnp.int32)
    for k, out_ref in enumerate(out_refs):
        other = member_ref[0] ^ k
        for i in range(s.hi_each):
            at = other * s.hi_each + i
            keep_ref[k, i : i + 1, :] = keep_hi_ref[pl.ds(at, 1), :]
            out_ref[:, i * LANES : (i + 1) * LANES] = cot_hi_ref[at]
            if k == 0:
                seen_ref[i : i + 1, :] = jnp.maximum(mask_hi_ref[pl.ds(at, 1), :], first_hi).astype(F32)
        for tile, first, count in sample_tiles(s):
            begin = other * s.lo_each + first
            keep_ref[k, tile : tile + 1, :] = slots([keep_lo_ref[pl.ds(begin + j, 1), :] for j in range(count)], -1, s)
            if k == 0:
                seen = [jnp.maximum(mask_lo_ref[pl.ds(begin + j, 1), :], first_lo) for j in range(count)]
                seen_ref[tile : tile + 1, :] = slots(seen, 0, s).astype(F32)
            where = slice(tile * LANES, (tile + 1) * LANES)
            if count < s.pack:
                out_ref[:, where] = jnp.zeros((s.features, LANES), BF16)
            if count:
                size = count * s.lo_length
                start = pl.multiple_of(begin * s.lo_length, s.lo_length)
                out_ref[:, tile * LANES : tile * LANES + size] = nt(eye, cot_lo_ref[pl.ds(start, size), :]).astype(BF16)


def stage(s, member, keep_lo, keep_hi, mask_lo, mask_hi, cot_lo, cot_hi):
    args = (keep_lo, keep_hi, mask_lo, mask_hi, cot_lo, cot_hi)
    return pl.pallas_call(
        functools.partial(stage_kernel, s),
        grid_spec=pltpu.PrefetchScalarGridSpec(
            num_scalar_prefetch=1,
            grid=(1,),
            in_specs=[whole(a) for a in args],
            out_specs=[fixed(s.groups, s.tiles, LANES), fixed(s.tiles, LANES)]
            + [fixed(s.features, s.rows)] * s.groups,
        ),
        out_shape=[shape((s.groups, s.tiles, LANES), jnp.int32), shape((s.tiles, LANES), F32)]
        + [shape((s.features, s.rows), BF16)] * s.groups,
        compiler_params=params(60),
        cost_estimate=cost(1e8, 4e6),
    )(member, *args)


def chosen_columns(s, keep_ref, tile, patches, wanted_hi):
    row = keep_ref[pl.ds(tile, 1), :]
    is_hi = tile < s.hi_each
    row = jnp.where(is_hi if wanted_hi else jnp.logical_not(is_hi), row, -1)
    column = jnp.broadcast_to(row.astype(F32), (LANES, LANES)).T.astype(jnp.int32)
    parts = [jnp.where(iota((LANES, LANES), 1) + at == column, 1.0, 0.0) for at in range(0, patches, LANES)]
    return jnp.concatenate(parts, axis=1).astype(BF16)


def pair_masks():
    lane = iota((1, LANES), 1)
    low = jnp.where(lane < LANES // 2, 1.0, 0.0).astype(BF16)
    high = jnp.where(lane < LANES // 2, 0.0, 1.0).astype(BF16)
    return low, high


def doubled(block, masks):
    return jnp.concatenate([block * masks[0], block * masks[1]], axis=0)


def allowed(s, seen_ref, tile):
    bits = jnp.where(tile < s.hi_each, s.hi_length.bit_length() - 1, s.lo_length.bit_length() - 1)
    same = (iota((LANES, LANES), 0) >> bits) == (iota((LANES, LANES), 1) >> bits)
    open_to = jnp.logical_and(same, seen_ref[pl.ds(tile, 1), :] > 0)
    return jnp.concatenate([open_to, open_to], axis=0)


def forward_kernel(s, heads, keep_ref, seen_ref, p0, p1, p2, p3, w0, w1, w2, w3, pos_lo_ref, pos_hi_ref, gain1_ref, wqkv_ref, wout_ref, x0_ref, a_ref, qkv_ref, probs_ref, mixed_ref, x1_ref):
    step = pl.program_id(0)
    per = ROWS // LANES
    width = s.width
    picked = jnp.concatenate([p[...] for p in (p0, p1, p2, p3)], axis=0)
    embed = jnp.concatenate([w[: s.features, :] for w in (w0, w1, w2, w3)], axis=0)
    hot_hi = jnp.concatenate([chosen_columns(s, keep_ref, step * per + j, s.hi_patches, True) for j in range(per)], axis=0)
    hot_lo = jnp.concatenate([chosen_columns(s, keep_ref, step * per + j, s.lo_patches, False) for j in range(per)], axis=0)
    start = tn(picked, embed) + (nn(hot_hi, pos_hi_ref[...]) + nn(hot_lo, pos_lo_ref[...]))
    x0_ref[...] = start.astype(BF16)
    normed, _ = normalize(start)
    normed = (normed * gain1_ref[...]).astype(BF16)
    a_ref[...] = normed
    for c in range(3):
        part = slice(c * width, (c + 1) * width)
        qkv_ref[:, part] = nn(normed, wqkv_ref[:, part]).astype(BF16)
    masks = pair_masks()
    scale = 1.0 / math.sqrt(width // heads)
    for j in range(per):
        rows = slice(j * LANES, (j + 1) * LANES)
        ok = allowed(s, seen_ref, step * per + j)
        for h in range(width // LANES):
            at = h * LANES
            q = qkv_ref[rows, at : at + LANES]
            k = qkv_ref[rows, width + at : width + at + LANES]
            v = qkv_ref[rows, 2 * width + at : 2 * width + at + LANES]
            scores = nt(doubled(q, masks), k) * scale
            scores = jnp.where(ok, scores, MASKED)
            raised = jnp.exp(scores - jnp.max(scores, axis=-1, keepdims=True))
            probs = raised / jnp.sum(raised, axis=-1, keepdims=True)
            rounded = probs.astype(BF16)
            probs_ref[j, h] = rounded
            wide = jnp.concatenate([rounded[:LANES], rounded[LANES:]], axis=1)
            mixed_ref[rows, at : at + LANES] = nn(wide, doubled(v, masks)).astype(BF16)
    middle = start + nn(mixed_ref[...], wout_ref[...])
    x1_ref[...] = middle


def forward(s, heads, keep, seen, picked, weights, pos_lo, pos_hi, gain1, wqkv, wout):
    width, rows = s.width, s.rows
    per, pairs = ROWS // LANES, width // LANES
    return pl.pallas_call(
        functools.partial(forward_kernel, s, heads),
        grid=(rows // ROWS,),
        in_specs=[whole(keep), whole(seen)]
        + [along(s.features, ROWS)] * 4
        + [whole(w) for w in weights]
        + [whole(a) for a in (pos_lo, pos_hi, gain1, wqkv, wout)],
        out_specs=[
            across(ROWS, width),
            across(ROWS, width),
            across(ROWS, 3 * width),
            pl.BlockSpec((per, pairs, 2 * LANES, LANES), lambda i: (i, 0, 0, 0)),
            across(ROWS, width),
            across(ROWS, width),
        ],
        out_shape=[
            shape((rows, width), BF16),
            shape((rows, width), BF16),
            shape((rows, 3 * width), BF16),
            shape((s.tiles, pairs, 2 * LANES, LANES), BF16),
            shape((rows, width), BF16),
            shape((rows, width), F32),
        ],
        compiler_params=params(60),
        cost_estimate=cost(1.5e10, 3e7),
    )(keep, seen, *picked, *weights, pos_lo, pos_hi, gain1, wqkv, wout)


def part_rows(width, offset):
    return pl.BlockSpec((ROWS, width), lambda i, *_: (i + offset, 0))


def relative(ids_ref, x, y, z, c):
    return ids_ref[0] ^ (2 * z + y), ids_ref[1] ^ (2 * x + c)


def places(ids_ref, far):
    out = []
    for c in range(2):
        for x in range(2):
            for y in range(2):
                for z in range(far):
                    d, v = relative(ids_ref, x, y, z, c)
                    out.append(d * 4 + v)
    return out


def turn_relative(ids_ref, far, block, source_ref, turned_ref, acc_ref):
    order = places(ids_ref, far)
    rows = source_ref.shape[0]
    for begin in range(0, rows, rows // 2):
        span = slice(begin, begin + rows // 2)
        acc_ref[:, : rows // 2] = source_ref[span, :].astype(F32).T
        for p in range(0, len(order), 2):
            pair = [
                acc_ref[pl.ds(pl.multiple_of(at * block, 8), block), : rows // 2]
                for at in order[p : p + 2]
            ]
            turned_ref[p * block : (p + 2) * block, span] = jnp.concatenate(pair, axis=0).astype(BF16)


def spread(ids_ref, far, acc_ref, outs, block, extra):
    for x in range(2):
        for y in range(2):
            for z in range(far):
                for c, out_ref in enumerate(outs):
                    d, v = relative(ids_ref, x, y, z, c)
                    start = pl.multiple_of((d * 4 + v) * block, 8)
                    out_ref[x, y, z, :block, :] = acc_ref[pl.ds(start, block), :].astype(BF16)
                    out_ref[x, y, z, block:, :] = extra


def spread_features(s, ids_ref, acc_ref, outs):
    half = s.features // 2
    for k in range(4):
        for y in range(2):
            start = k * s.features + ((ids_ref[0] & 1) ^ y) * half
            rows = acc_ref[pl.ds(pl.multiple_of(start, 8), half), :]
            outs[k % 2][k // 2, y] = rows.astype(BF16)


def hidden_kernel(s, far, chunks, ids_ref, seen_ref, c0, c1, c2, c3, h0, h1, h2, h3, x1_ref, mixed_ref, w1_ref, b1_ref, w2_ref, b2_ref, gain2_ref, wout_ref, two0_ref, two1_ref, one0_ref, one1_ref, p0, p1, p2, p3, out0_ref, out1_ref, n0_ref, n1_ref, go_ref, ga_ref, b_ref, turned_ref, gm_ref, gpred_ref, forth_ref, back_ref, z_ref, gu_ref, acc_ref, side_ref):
    step = pl.program_id(0)
    width = s.width
    block = width // (8 * far)
    subs = [slice(begin, begin + ROWS) for begin in range(0, s.rows, ROWS)]
    seen = jnp.concatenate([seen_ref[t : t + 1, :] for t in range(s.tiles)], axis=1)

    @pl.when(step == 0)
    def _():
        gpred_ref[...] = jnp.concatenate([c[...] for c in (c0, c1, c2, c3)], axis=0) * seen.astype(BF16)
        head = jnp.concatenate([h[s.features :, :] for h in (h0, h1, h2, h3)], axis=0)
        total = None
        for rows in subs:
            values = x1_ref[rows, :]
            normed, _ = normalize(values)
            b_ref[rows, :] = (normed * gain2_ref[...]).astype(BF16)
            forth_ref[rows, :] = values + b2_ref[...]
            back_ref[rows, :] = jnp.zeros((ROWS, width), F32)
            upward = tn(gpred_ref[:, rows], head).astype(BF16)
            gm_ref[rows, :] = upward
            part = jnp.sum(upward.astype(F32), axis=0, keepdims=True)
            total = part if total is None else total + part
        side_ref[1:2, :] = total
        turn_relative(ids_ref, far, block, b_ref, turned_ref, acc_ref)

    @pl.when(step < chunks)
    def _():
        w1, w2, bias = w1_ref[...], w2_ref[...], b1_ref[...]
        total = None
        for rows in subs:
            u = nn(b_ref[rows, :], w1)
            upward = nt(gm_ref[rows, :], w2)
            z, slope = gelu_parts(u + bias)
            z = z.astype(BF16)
            gu = (upward * slope).astype(BF16)
            z_ref[rows, :] = z
            gu_ref[rows, :] = gu
            part = jnp.sum(gu.astype(F32), axis=0, keepdims=True)
            total = part if total is None else total + part
        side_ref[pl.ds(2 + ((ids_ref[0] >> 1) ^ step), 1), :] = total
        forth_ref[...] += nn(z_ref[...], w2)
        back_ref[...] += nt(gu_ref[...], w1)
        ones = nn(turned_ref[...], gu_ref[...])
        one0_ref[0] = ones[: width // 2].astype(BF16)
        one1_ref[0] = ones[width // 2 :].astype(BF16)
        acc_ref[...] = tn(z_ref[...], gm_ref[...])
        tall = width // 8
        for x in range(2):
            for y in range(2):
                for c, out_ref in enumerate((two0_ref, two1_ref)):
                    d, v = relative(ids_ref, x, y, 0, c)
                    start = pl.multiple_of(((d & 1) * 4 + v) * tall, 8)
                    out_ref[x, y, 0] = acc_ref[pl.ds(start, tall), :].astype(BF16)

    @pl.when(step == chunks)
    def _():
        total = None
        for rows in subs:
            z_ref[rows, :] = forth_ref[rows, :].astype(BF16)
            upward = back_ref[rows, :]
            normed, inverse = normalize(x1_ref[rows, :])
            part = jnp.sum(upward * normed, axis=0, keepdims=True)
            total = part if total is None else total + part
            grad = gm_ref[rows, :].astype(F32) + normalize_back(upward, normed, inverse, gain2_ref[...])
            grad = grad.astype(BF16)
            ga_ref[rows, :] = grad
            go_ref[rows, :] = nt(grad, wout_ref[...]).astype(BF16)
        side_ref[0:1, :] = total
        final = z_ref[...]
        for head, out in zip((h0, h1, h2, h3), (p0, p1, p2, p3)):
            out[...] = (nt(head[s.features :, :], final) * seen).astype(BF16)
        acc_ref[: s.groups * s.features, :] = nn(gpred_ref[...], final)
        spread_features(s, ids_ref, acc_ref, (n0_ref, n1_ref))
        acc_ref[...] = tn(mixed_ref[...], ga_ref[...])
        spread(ids_ref, far, acc_ref, (out0_ref, out1_ref), block, side_ref[...].astype(BF16))


def hidden(s, ids, far, seen, cots, weights, x1, mixed, w1, b1, w2, b2, gain2, wout):
    rows, width = s.rows, s.width
    chunks = w1.shape[1] // width
    block = width // (8 * far)
    high = s.groups * s.features
    sides = 8 * -(-(2 + chunks) // 8)
    last = chunks - 1

    def chunk(i, ids):
        return (ids[0] >> 1) ^ jnp.minimum(i, last)

    first = [seen, *cots, *weights, x1, mixed]
    rest = [b2, gain2, wout]
    outs = (
        [((2, 2, far, width // 8, width), BF16)] * 2
        + [((chunks, width // 2, width), BF16)] * 2
        + [((s.features, rows), BF16)] * 4
        + [((2, 2, far, block + sides, width), BF16)] * 2
        + [((2, 2, s.features // 2, width), BF16)] * 2
        + [((rows, width), BF16)] * 2
    )
    specs = [
        pl.BlockSpec((2, 2, 1, width // 8, width), lambda i, ids: (0, 0, jnp.minimum(i, last), 0, 0))
    ] * 2
    specs += [pl.BlockSpec((1, width // 2, width), lambda i, ids: (chunk(i, ids), 0, 0))] * 2
    specs += [fixed(*dims) for dims, _ in outs[4:]]
    return pl.pallas_call(
        functools.partial(hidden_kernel, s, far, chunks),
        grid_spec=pltpu.PrefetchScalarGridSpec(
            num_scalar_prefetch=1,
            grid=(chunks + 1,),
            in_specs=[whole(a) for a in first]
            + [
                pl.BlockSpec((width, width), lambda i, ids: (0, chunk(i, ids))),
                pl.BlockSpec((1, width), lambda i, ids: (0, chunk(i, ids))),
                pl.BlockSpec((width, width), lambda i, ids: (chunk(i, ids), 0)),
            ]
            + [whole(a) for a in rest],
            out_specs=specs,
            scratch_shapes=[
                pltpu.VMEM((rows, width), BF16),
                pltpu.VMEM((width, rows), BF16),
                pltpu.VMEM((rows, width), BF16),
                pltpu.VMEM((high, rows), BF16),
                pltpu.VMEM((rows, width), F32),
                pltpu.VMEM((rows, width), F32),
                pltpu.VMEM((rows, width), BF16),
                pltpu.VMEM((rows, width), BF16),
                pltpu.VMEM((width, width), F32),
                pltpu.VMEM((sides, width), F32),
            ],
        ),
        out_shape=[shape(*out) for out in outs],
        compiler_params=params(60),
        cost_estimate=cost(3.4e10, 4e7),
    )(ids, *first, w1, b1, w2, *rest)


def attention_back(s, heads, qkv_ref, probs_ref, go_ref, gqkv_ref):
    per = ROWS // LANES
    width = s.width
    masks = pair_masks()
    scale = 1.0 / math.sqrt(width // heads)
    for j in range(per):
        rows = slice(j * LANES, (j + 1) * LANES)
        for h in range(width // LANES):
            at = h * LANES
            q = doubled(qkv_ref[rows, at : at + LANES], masks)
            k = doubled(qkv_ref[rows, width + at : width + at + LANES], masks)
            v = qkv_ref[rows, 2 * width + at : 2 * width + at + LANES]
            out = doubled(go_ref[rows, at : at + LANES], masks)
            rounded = probs_ref[j, h]
            probs = rounded.astype(F32)
            upward = nt(out, v)
            centred = upward - jnp.sum(probs * upward, axis=-1, keepdims=True)
            grads = (probs * centred).astype(BF16)
            wide = jnp.concatenate([grads[:LANES], grads[LANES:]], axis=1)
            gqkv_ref[rows, at : at + LANES] = (nn(wide, k) * scale).astype(BF16)
            gqkv_ref[rows, width + at : width + at + LANES] = (tn(grads, q) * scale).astype(BF16)
            gqkv_ref[rows, 2 * width + at : 2 * width + at + LANES] = tn(rounded, out).astype(BF16)


def first_norm_back(gqkv, x0_ref, ga_ref, wqkv_ref, gain1_ref):
    upward = nt(gqkv, wqkv_ref[...])
    normed, inverse = normalize(x0_ref[...].astype(F32))
    grad = ga_ref[...].astype(F32) + normalize_back(upward, normed, inverse, gain1_ref[...])
    return grad.astype(BF16), jnp.sum(upward * normed, axis=0, keepdims=True)


def backward_kernel(s, heads, qkv_ref, probs_ref, go_ref, x0_ref, ga_ref, wqkv_ref, gain1_ref, gqkv_ref, g0_ref, gln1_ref):
    attention_back(s, heads, qkv_ref, probs_ref, go_ref, gqkv_ref)
    g0_ref[...], gain_part = first_norm_back(gqkv_ref[...], x0_ref, ga_ref, wqkv_ref, gain1_ref)
    accumulate(gln1_ref, pl.program_id(0) == 0, gain_part)


def row_inputs(s, offset):
    width = s.width
    return [
        part_rows(3 * width, offset),
        pl.BlockSpec((ROWS // LANES, width // LANES, 2 * LANES, LANES), lambda i, *_: (i + offset, 0, 0, 0)),
        part_rows(width, offset),
        part_rows(width, offset),
        part_rows(width, offset),
    ]


def backward(s, heads, offset, steps, qkv, probs, go, x0, ga, wqkv, gain1):
    width = s.width
    size = steps * ROWS
    return pl.pallas_call(
        functools.partial(backward_kernel, s, heads),
        grid=(steps,),
        in_specs=row_inputs(s, offset) + [whole(wqkv), whole(gain1)],
        out_specs=[across(ROWS, 3 * width), across(ROWS, width), fixed(1, width)],
        out_shape=[shape((size, 3 * width), BF16), shape((size, width), BF16), shape((1, width), F32)],
        compiler_params=params(60),
        cost_estimate=cost(8e9 * steps, 6e6 * steps),
    )(qkv, probs, go, x0, ga, wqkv, gain1)


def position_grads(s, keep_ref, g0, picked):
    hot_hi, hot_lo = [], []
    for t in range(s.tiles):
        row = keep_ref[t : t + 1, :]
        patches = s.hi_patches if t < s.hi_each else s.lo_patches
        hot = jnp.where(iota((patches, LANES), 0) == row, 1.0, 0.0).astype(BF16)
        (hot_hi if t < s.hi_each else hot_lo).append(hot)
    hi_rows = s.hi_each * LANES
    hi = nn(jnp.concatenate(hot_hi, axis=1), g0[:hi_rows])
    lo = nn(jnp.concatenate(hot_lo, axis=1), g0[hi_rows:])
    return lo, hi, nn(jnp.concatenate(picked, axis=0), g0)


def finish_kernel(s, far, chunks, ids_ref, keep_ref, a_ref, r0_ref, r1_ref, ga_ref, gb_ref, la_ref, lb_ref, p0, p1, p2, p3, w0, w1, w2, w3, q0, q1, q2, q3, o0_ref, o1_ref, e0_ref, e1_ref, i0, i1, i2, i3, turned_ref, acc_ref, lo_ref, hi_ref):
    step = pl.program_id(0)
    width = s.width
    block = width // (8 * far)
    half = width // 2
    done = r0_ref.shape[0]

    @pl.when(step == 0)
    def _():
        turn_relative(ids_ref, far, block, a_ref, turned_ref, acc_ref)

    @pl.when(step < chunks)
    def _():
        value = nn(turned_ref[:, :done], r0_ref[...]) + nn(turned_ref[:, done:], r1_ref[...])
        o0_ref[0] = value[:half].astype(BF16)
        o1_ref[0] = value[half:].astype(BF16)

    @pl.when(step == chunks)
    def _():
        g0 = jnp.concatenate([ga_ref[...], gb_ref[...]], axis=0)
        lo, hi, embed = position_grads(s, keep_ref, g0, [p[...] for p in (p0, p1, p2, p3)])
        lo_ref[...] = lo
        hi_ref[...] = hi
        acc_ref[: s.groups * s.features, :] = embed
        spread_features(s, ids_ref, acc_ref, (e0_ref, e1_ref))
        for weight, pred, out in zip((w0, w1, w2, w3), (q0, q1, q2, q3), (i0, i1, i2, i3)):
            out[: s.features, :] = nt(weight[: s.features, :], g0).astype(BF16)
            out[s.features :, :] = pred[...]
        hi_block = s.hi_patches // (8 * far)
        lo_block = s.lo_patches // (8 * far)
        gain = la_ref[...] + lb_ref[...]
        pad = jnp.zeros((block - hi_block - lo_block - 1, width), F32)
        order = places(ids_ref, far)
        for p in range(0, len(order), 2):
            pair = []
            for at in order[p : p + 2]:
                both = lo_ref[pl.ds(pl.multiple_of((at >> 1) * 8, 8), 8), :]
                pair += [
                    hi_ref[pl.ds(pl.multiple_of(at * hi_block, 8), hi_block), :],
                    jnp.where((at & 1) == 1, both[lo_block:], both[:lo_block]),
                    gain,
                    pad,
                ]
            row = (p % (len(order) // 2)) * block
            (o0_ref, o1_ref)[p // (len(order) // 2)][0, row : row + 2 * block, :] = jnp.concatenate(pair, axis=0).astype(BF16)


def finish(s, ids, far, keep, a, gqkvs, g0s, gains, picked, weights, preds):
    width, rows = s.width, s.rows
    chunks = gqkvs[0].shape[1] // width
    rest = [*g0s, *gains, *picked, *weights, *preds]
    out = pl.BlockSpec((1, width // 2, width), lambda i, ids: (i, 0, 0))
    return pl.pallas_call(
        functools.partial(finish_kernel, s, far, chunks),
        grid_spec=pltpu.PrefetchScalarGridSpec(
            num_scalar_prefetch=1,
            grid=(chunks + 1,),
            in_specs=[whole(keep), whole(a)]
            + [
                pl.BlockSpec((g.shape[0], width), lambda i, ids: (0, jnp.minimum(i, chunks - 1)))
                for g in gqkvs
            ]
            + [whole(r) for r in rest],
            out_specs=[out, out]
            + [fixed(2, 2, s.features // 2, width)] * 2
            + [fixed(2 * s.features, rows)] * 4,
            scratch_shapes=[
                pltpu.VMEM((width, rows), BF16),
                pltpu.VMEM((width, width), F32),
                pltpu.VMEM((s.lo_patches, width), F32),
                pltpu.VMEM((s.hi_patches, width), F32),
            ],
        ),
        out_shape=[shape((chunks + 1, width // 2, width), BF16)] * 2
        + [shape((2, 2, s.features // 2, width), BF16)] * 2
        + [shape((2 * s.features, rows), BF16)] * 4,
        compiler_params=params(60),
        cost_estimate=cost(7e9, 1.2e7),
    )(ids, keep, a, *gqkvs, *rest)


def combine_kernel(held_ref, got_ref, keep_ref, send_ref):
    send_ref[...] = (held_ref[:, 1].astype(F32) + got_ref[:, 1].astype(F32)).astype(BF16)
    keep_ref[...] = (held_ref[:, 0].astype(F32) + got_ref[:, 0].astype(F32)).astype(BF16)


def combine(held, got, axis):
    dims = held.shape
    width = dims[-1]
    outer = math.prod(dims[:axis])
    inner = math.prod(dims[axis + 1 : -1])
    grid = (outer // 4, 1) if outer > 4 else (1, 2)
    broad, tall = outer // grid[0], inner // grid[1]
    half = shape((outer, inner, width), BF16)
    spec = pl.BlockSpec((broad, 2, tall, width), lambda i, j: (i, 0, j, 0))
    out = pl.BlockSpec((broad, tall, width), lambda i, j: (i, j, 0))
    keep, send = pl.pallas_call(
        combine_kernel,
        grid=grid,
        in_specs=[spec, spec],
        out_specs=[out, out],
        out_shape=[half, half],
        compiler_params=params(60),
        cost_estimate=cost(1e6, 6 * outer * inner * width),
    )(*(value.reshape(outer, 2, inner, width) for value in (held, got)))
    left = dims[:axis] + dims[axis + 1 :]
    return keep.reshape(left), send.reshape(left)


def place_kernel(s, member_ref, keep_ref, r0, r1, r2, r3, lo_ref, hi_ref, pred_lo_ref, pred_hi_ref):
    lane_sample = iota((1, LANES), 1) // s.lo_length
    eye = jnp.where(iota((s.features, s.features), 0) == iota((s.features, s.features), 1), 1.0, 0.0).astype(BF16)
    for k, got_ref in enumerate((r0, r1, r2, r3)):
        other = member_ref[0] ^ k
        for i in range(s.hi_each):
            chosen = iota((s.hi_patches, LANES), 0) == keep_ref[k, i : i + 1, :]
            hot = jnp.where(chosen, 1.0, 0.0).astype(BF16)
            lanes = slice(i * LANES, (i + 1) * LANES)
            hi_ref[other * s.hi_each + i] = nt(got_ref[: s.features, lanes], hot).astype(BF16)
            pred_hi_ref[other * s.hi_each + i] = got_ref[s.features :, lanes]
        for tile, first, count in sample_tiles(s):
            lanes = slice(tile * LANES, (tile + 1) * LANES)
            got = got_ref[: s.features, lanes]
            for j in range(count):
                row = jnp.where(lane_sample == j, keep_ref[k, tile : tile + 1, :], -1)
                hot = jnp.where(iota((s.lo_patches, LANES), 0) == row, 1.0, 0.0).astype(BF16)
                lo_ref[other * s.lo_each + first + j] = nt(got, hot).astype(BF16)
            if count:
                size = count * s.lo_length
                turned = tn(got_ref[s.features :, lanes], eye).astype(BF16)
                start = pl.multiple_of((other * s.lo_each + first) * s.lo_length, s.lo_length)
                pred_lo_ref[pl.ds(start, size), :] = turned[:size]


def place(s, member, keep, blocks):
    lo = s.groups * s.lo_each
    hi = s.groups * s.hi_each
    outs = [
        (lo, s.features, s.lo_patches),
        (hi, s.features, s.hi_patches),
        (lo * s.lo_length, s.features),
        (hi, s.features, s.hi_length),
    ]
    return pl.pallas_call(
        functools.partial(place_kernel, s),
        grid_spec=pltpu.PrefetchScalarGridSpec(
            num_scalar_prefetch=1,
            grid=(1,),
            in_specs=[whole(keep)] + [whole(b) for b in blocks],
            out_specs=[fixed(*dims) for dims in outs],
        ),
        out_shape=[shape(dims, BF16) for dims in outs],
        compiler_params=params(60),
        cost_estimate=cost(2e9, 8e6),
    )(member, keep, *blocks)


def swap(value, data_bit, var_bit):
    dp, var = lax.axis_size("dp"), lax.axis_size("var")
    pairs = [
        (d * var + v, (d ^ data_bit) * var + (v ^ var_bit)) for d in range(dp) for v in range(var)
    ]
    return lax.ppermute(value, AXES, pairs)


def add_rounded(left, right):
    return (left.astype(F32) + right.astype(F32)).astype(BF16)


def added(*values):
    values = [value.astype(F32) for value in values]
    while len(values) > 1:
        values = [values[i] + values[i + 1] for i in range(0, len(values), 2)]
    return values[0]


def tie(value, *tokens):
    return lax.optimization_barrier((value, tokens))[0]


PARTNERS = {"core": (0, 1), "x": (0, 2), "y": (1, 0), "z0": (2, 0), "z1": (4, 0)}


class Chain:
    def __init__(self, near, sent):
        self.near, self.sent = near, sent
        self.repeats = near.ndim == 4
        self.names = ["x", "y"] if self.repeats else ["chunk", "x", "y", "z1", "z0"][7 - near.ndim :]
        self.held = self.got = None

    def outgoing(self, name):
        if name == "core":
            self.held = self.near
            return self.sent
        if name not in self.names:
            self.held = add_rounded(self.held, self.got)
            return self.held
        axis = self.names.index(name)
        self.names.remove(name)
        if math.prod(self.held.shape) >= 1 << 20:
            self.held, sent = combine(self.held, self.got, axis)
            return sent
        kept, sent = (
            [lax.index_in_dim(value, side, axis, keepdims=False) for value in (self.held, self.got)]
            for side in range(2)
        )
        self.held = add_rounded(*kept)
        return add_rounded(*sent)

    def hold(self, *tokens):
        self.held, self.got = tie((self.held, self.got), *tokens)

    def final(self):
        return added(self.held, self.got)


def send_rows(values, bits):
    width = values[0].shape[-1]
    if len(values) == 1:
        return [swap(values[0].reshape(-1, width), *bits).reshape(values[0].shape)]
    flat = [value.reshape(-1, width) for value in values]
    got = swap(jnp.concatenate(flat, axis=0), *bits)
    out, start = [], 0
    for value, rows in zip(values, flat):
        out.append(got[start : start + rows.shape[0]].reshape(value.shape))
        start += rows.shape[0]
    return out


def trade(name, *chains):
    got = send_rows([chain.outgoing(name) for chain in chains], PARTNERS[name])
    for chain, value in zip(chains, got):
        chain.got = value
    return got[0]


def both_halves(value):
    value = value.astype(BF16)
    other = swap(value, 1, 0)
    second = lax.axis_index("dp") % 2 == 1
    return jnp.concatenate(
        [jnp.where(second, other, value), jnp.where(second, value, other)], axis=0
    ).astype(F32)


def natural(near, sent):
    rows, width = near.shape[-2:]
    both = jnp.stack([near, sent]).reshape((2, -1, 2, 2, 4, rows, width))
    return both.transpose(4, 3, 2, 0, 1, 5, 6).reshape(32, -1, width)


def scattered(full):
    return lax.psum_scatter(full, AXES, scatter_dimension=0, tiled=True).astype(F32)


def joined(blocks, chunks):
    count, rows, width = blocks.shape
    split = blocks.reshape(count, chunks, rows // chunks, width).transpose(0, 2, 1, 3)
    return split.reshape(count * (rows // chunks), chunks * width)


def plain_sum(near, sent):
    if near.ndim >= 6:
        return natural(near, sent)
    value = jnp.stack([near, sent], axis=1)
    value = value.reshape((4, -1, near.shape[-1]))
    bit = 1
    while value.shape[0] > 1:
        value = value.reshape((value.shape[0] // 2, 2) + value.shape[1:])
        value = add_rounded(value[:, 0], swap(value[:, 1], 0, bit))
        bit *= 2
    return lax.psum(value[0], "dp").astype(F32)


def exchange_relative(blocks):
    return [blocks[0]] + [swap(blocks[k], 0, k) for k in range(1, len(blocks))]


def body(
    img_lo,
    img_hi,
    keep_lo,
    keep_hi,
    mask_lo,
    mask_hi,
    w_embed,
    pos_lo,
    pos_hi,
    ln1_gain,
    w_qkv,
    w_out,
    ln2_gain,
    w_fc1,
    b_fc1,
    w_fc2,
    b_fc2,
    w_head,
    cot_lo,
    cot_hi,
):
    groups = lax.axis_size("var")
    devices = lax.axis_size("dp") * groups
    member = lax.axis_index("var").astype(jnp.int32).reshape(1)
    s = Sizes(keep_lo.shape, keep_hi.shape, w_embed.shape, img_lo.shape, img_hi.shape, groups)
    features, width = s.features, s.width
    gain1, gain2 = ln1_gain.reshape(1, -1), ln2_gain.reshape(1, -1)
    img_lo_t, img_hi_t = img_lo.transpose(0, 2, 1), img_hi.transpose(0, 2, 1)

    own = jnp.concatenate([w_embed, w_head.T], axis=0)
    crossed = swap(own, 0, 2)
    weights = [own, swap(own, 0, 1), crossed, swap(crossed, 0, 1)]
    sent = pick(s, (1, 2, 3), member, keep_lo, keep_hi, img_lo_t, img_hi_t)
    picked = [swap(value, 0, k + 1) for k, value in enumerate(sent)]
    picked = [*pick(s, (0,), member, keep_lo, keep_hi, img_lo_t, img_hi_t), *picked]
    keep, seen, *cots = stage(
        s,
        tie(member, sent[0]),
        keep_lo,
        keep_hi,
        mask_lo,
        mask_hi,
        cot_lo.reshape(-1, features),
        cot_hi.transpose(0, 2, 1),
    )
    cots = exchange_relative(cots)
    own_keep = keep[0]
    x0, a, qkv, probs, mixed, x1 = forward(
        s, HEADS, own_keep, seen, picked, weights, pos_lo, pos_hi, gain1, w_qkv, w_out
    )
    far = 4
    cube = lax.axis_size("dp") == 2 * far
    place_of = lax.axis_index("dp") * groups + lax.axis_index("var")
    ids = jnp.stack([lax.axis_index("dp"), lax.axis_index("var")]).astype(jnp.int32)
    if not cube:
        ids = jnp.zeros_like(ids)

    def chain_of(near, sent):
        if near.ndim == 5:
            near, sent = (
                value.reshape((2, 2, 2, 2) + value.shape[3:]) for value in (near, sent)
            )
        elif near.ndim == 3:
            near, sent = (
                value.reshape((-1, 2, 2, 2, 2, width // 32, width)) for value in (near, sent)
            )
        return Chain(near, sent)

    def step(name, *chains):
        return trade(name, *chains) if cube else ()

    def halves_of(chain):
        out = []
        for side in range(2):
            piece = Chain(chain.near, chain.sent)
            count = chain.near.shape[0] // 2
            piece.held, piece.got = (
                lax.slice_in_dim(value, side * count, (side + 1) * count, axis=0)
                for value in (chain.held, chain.got)
            )
            out.append(piece)
        return out

    two0, two1, one0, one1, *rest = hidden(
        s,
        ids,
        far,
        tie(seen, x1),
        cots,
        weights,
        x1,
        mixed,
        w_fc1,
        b_fc1.reshape(1, -1),
        w_fc2,
        b_fc2.reshape(1, -1),
        gain2,
        w_out,
    )
    preds, (out0, out1, head0, head1, go, ga) = rest[:groups], rest[groups:]
    two, one = chain_of(two0, two1), chain_of(one0, one1)
    out, head = chain_of(out0, out1), chain_of(head0, head1)
    tokens = [step("core", chain) for chain in (two, one, out, head)]

    def back(offset, steps, *ready):
        return backward(
            s, HEADS, offset, steps, qkv, probs, go, x0, ga, w_qkv, tie(gain1, *ready)
        )

    parts = [back(0, 1, go)]
    if cube:
        for chain in (two, one, out, head):
            chain.hold(parts[0][0])
    near_tokens = [step("x", two, out, head), step("y", one)]
    parts.append(back(1, s.rows // ROWS - 1, parts[0][0], two.held, one.held, *tokens))
    if cube:
        for chain in (two, one, out, head):
            chain.hold(parts[1][0])
    tokens = [step("y", two, out, head), step("x", one)]
    gqkvs, g0s, gains = zip(*parts)
    near, sent, near_embed, sent_embed, *blocks = finish(
        s,
        tie(ids, two.held, one.held, *near_tokens),
        far,
        own_keep,
        a,
        gqkvs,
        g0s,
        gains,
        picked,
        weights,
        preds,
    )
    sent, sent_embed = tie((sent, sent_embed), *tokens)
    first, embed = chain_of(near, sent), chain_of(near_embed, sent_embed)
    tokens += [step("core", first), step("core", embed)]
    if cube:
        old = (two, one, out, head)
        for chain in old:
            chain.hold(first.got)
        one_half, other_half = halves_of(first)
        tokens = [trade("x", one_half, embed), trade("y", other_half)]
        trade("z0", *old)
        for chain in old:
            chain.hold(*tokens)
        tokens = [trade("y", one_half, embed), trade("x", other_half)]
        trade("z1", *old)
        blocks = [tie(block_of, *tokens) for block_of in blocks]
        trade("z0", one_half, other_half, embed)
        token = trade("z1", one_half, other_half, embed)
        for chain in old:
            chain.hold(token)
        last_member = tie(member, token)
        grad_fc2, grad_fc1, rest, grad_head, grad_embed = (
            chain.final() for chain in (two, one, out, head, embed)
        )
        grad_head, grad_embed = both_halves(grad_head), both_halves(grad_embed)
        first = jnp.concatenate([one_half.final(), other_half.final()], axis=0).reshape(-1, width)
        grad_fc1 = grad_fc1.reshape(-1, width)
    else:
        grad_fc2, grad_fc1, rest, grad_head, grad_embed, first = (
            plain_sum(chain.near, chain.sent) for chain in (two, one, out, head, embed, first)
        )
        last_member = member
    grad_img_lo, grad_img_hi, pred_lo, pred_hi = place(s, last_member, keep, exchange_relative(blocks))
    grad_head = grad_head.T

    block = width // devices
    inner = w_fc1.shape[1] // width

    hi_block = s.hi_patches // devices
    lo_block = s.lo_patches // devices

    def own_part(row):
        return lax.dynamic_slice_in_dim(row, place_of * block, block)

    if cube:
        grad_fc1 = joined(grad_fc1[None], inner)
        grad_qkv = joined(first[None, : 3 * block], 3)
        grad_out, sides = rest[:block], rest[block:]
        extra = first[3 * block :]
        grad_pos_hi = extra[:hi_block]
        grad_pos_lo = extra[hi_block : hi_block + lo_block]
        first_side = extra[hi_block + lo_block]
    else:
        tall = width // 32
        hi_tall, lo_tall = s.hi_patches // 32, s.lo_patches // 32
        grad_fc2 = scattered(grad_fc2.reshape(-1, width))
        grad_fc1 = scattered(joined(grad_fc1, inner))
        grad_qkv = scattered(joined(first[:, : 3 * tall], 3))
        grad_out, sides = scattered(rest[:, :tall].reshape(-1, width)), rest[0, tall:]
        extra = first[:, 3 * tall :]
        grad_pos_hi = scattered(extra[:, :hi_tall].reshape(-1, width))
        grad_pos_lo = scattered(extra[:, hi_tall : hi_tall + lo_tall].reshape(-1, width))
        sides = lax.psum(jnp.concatenate([sides, extra[0, hi_tall + lo_tall :]]), AXES).astype(F32)
        first_side = sides[rest.shape[1] - tall]
    grad_ln1 = own_part(first_side)
    grad_ln2 = own_part(sides[0])
    grad_b2 = own_part(sides[1])
    grad_b1 = lax.dynamic_slice_in_dim(
        sides[2 : 2 + inner].reshape(-1), place_of * inner * block, inner * block
    )
    return (
        pred_lo.reshape(cot_lo.shape),
        pred_hi.transpose(0, 2, 1),
        grad_img_lo.transpose(0, 2, 1),
        grad_img_hi.transpose(0, 2, 1),
        grad_embed,
        grad_pos_lo,
        grad_pos_hi,
        grad_ln1,
        grad_qkv,
        grad_out,
        grad_ln2,
        grad_fc1,
        grad_b1,
        grad_fc2,
        grad_b2,
        grad_head,
    )


def solution(mesh):
    placed = (
        P("dp", None, "var"),
        P("dp", None, "var"),
        P("dp", None),
        P("dp", None),
        P("dp", None),
        P("dp", None),
        P("var", None),
        P(),
        P(),
        P(),
        P(),
        P(),
        P(),
        P(),
        P(),
        P(),
        P(),
        P(None, "var"),
        P("dp", None, "var"),
        P("dp", None, "var"),
    )
    return jax.shard_map(
        body,
        mesh=mesh,
        in_specs=placed,
        out_specs=(
            P("dp", None, "var"),
            P("dp", None, "var"),
            P("dp", None, "var"),
            P("dp", None, "var"),
            P("var", None),
            P(("dp", "var"), None),
            P(("dp", "var"), None),
            P(("dp", "var")),
            P(("dp", "var"), None),
            P(("dp", "var"), None),
            P(("dp", "var")),
            P(("dp", "var"), None),
            P(("dp", "var")),
            P(("dp", "var"), None),
            P(("dp", "var")),
            P(None, "var"),
        ),
        check_vma=False,
    )
```

```python
import functools
import math

import jax
import jax.numpy as jnp
from jax import lax
from jax.experimental import pallas as pl
from jax.experimental.pallas import tpu as pltpu
from jax.sharding import PartitionSpec as P

HEADS = 12
EPSILON = 1e-06
AXES = ("dp", "var")
BF16 = jnp.bfloat16
F32 = jnp.float32
LANES = 128
ROWS = 256
MASKED = -1000000000.0
SHARE = 0.5


def dot(left, right, dims):
    return lax.dot_general(left, right, (dims, ((), ())), preferred_element_type=F32)


def nn(left, right):
    return dot(left, right, ((1,), (0,)))


def nt(left, right):
    return dot(left, right, ((1,), (1,)))


def tn(left, right):
    return dot(left, right, ((0,), (0,)))


def shape(dims, dtype):
    return jax.ShapeDtypeStruct(dims, dtype)


def whole(array):
    zeros = (0,) * array.ndim
    return pl.BlockSpec(array.shape, lambda *_: zeros, pipeline_mode=pl.Buffered(1))


def across(rows, width):
    return pl.BlockSpec((rows, width), lambda i, *_: (i, 0))


def along(height, columns):
    return pl.BlockSpec((height, columns), lambda i, *_: (0, i))


def fixed(*dims):
    zeros = (0,) * len(dims)
    return pl.BlockSpec(dims, lambda *_: zeros)


def params(mebibytes):
    return pltpu.CompilerParams(vmem_limit_bytes=mebibytes << 20)


def cost(flops, nbytes):
    return pl.CostEstimate(flops=int(flops * SHARE), bytes_accessed=int(nbytes * SHARE), transcendentals=0)


def iota(dims, axis):
    return lax.broadcasted_iota(jnp.int32, dims, axis)


def accumulate(ref, first, value):
    @pl.when(first)
    def _():
        ref[...] = value

    @pl.when(jnp.logical_not(first))
    def _():
        ref[...] += value


def normalize(values):
    center = values - jnp.mean(values, axis=-1, keepdims=True)
    inverse = lax.rsqrt(jnp.mean(center * center, axis=-1, keepdims=True) + EPSILON)
    return center * inverse, inverse


def normalize_back(upstream, normed, inverse, gains):
    scaled = upstream * gains
    mean_plain = jnp.mean(scaled, axis=-1, keepdims=True)
    mean_mixed = jnp.mean(scaled * normed, axis=-1, keepdims=True)
    return inverse * (scaled - mean_plain - normed * mean_mixed)


def gelu_parts(u):
    ratio = 1.0 / (1.0 + (0.3275911 * math.sqrt(0.5)) * jnp.abs(u))
    bell = jnp.exp(-0.5 * u * u)
    series = 0.5 * 1.061405429
    for factor in (-1.453152027, 1.421413741, -0.284496736, 0.254829592):
        series = series * ratio + 0.5 * factor
    tail = series * ratio * bell
    below = jnp.where(u < 0, tail, 1.0 - tail)
    return u * below, below + u * (bell * (1.0 / math.sqrt(2.0 * math.pi)))


class Sizes:
    def __init__(self, keep_lo, keep_hi, w_embed, img_lo, img_hi, groups):
        self.lo_each, self.hi_each = keep_lo[0] // groups, keep_hi[0] // groups
        self.lo_length, self.hi_length = keep_lo[1], keep_hi[1]
        self.features, self.width = w_embed
        self.lo_patches, self.hi_patches = img_lo[1], img_hi[1]
        self.groups = groups
        self.pack = LANES // self.lo_length
        self.lo_tiles = -(-self.lo_each // self.pack)
        self.hi_rows = self.hi_each * self.hi_length
        tiles = self.hi_each + self.lo_tiles
        self.tiles = tiles + tiles % 2
        self.rows = self.tiles * LANES


def sample_tiles(s):
    out = []
    for t in range(s.tiles - s.hi_each):
        first = t * s.pack
        out.append((s.hi_each + t, first, max(0, min(s.pack, s.lo_each - first))))
    return out


def slots(rows, fill, s):
    missing = s.pack - len(rows)
    if missing:
        rows = rows + [jnp.full((1, missing * s.lo_length), fill, rows[0].dtype if rows else jnp.int32)]
    return rows[0] if len(rows) == 1 else jnp.concatenate(rows, axis=1)


def pick_kernel(s, members, member_ref, keep_lo_ref, keep_hi_ref, img_lo_ref, img_hi_ref, *out_refs):
    for k, out_ref in zip(members, out_refs):
        other = member_ref[0] ^ k
        for i in range(s.hi_each):
            at = other * s.hi_each + i
            chosen = iota((s.hi_patches, LANES), 0) == keep_hi_ref[pl.ds(at, 1), :]
            got = nn(img_hi_ref[at], jnp.where(chosen, 1.0, 0.0).astype(BF16))
            out_ref[:, i * LANES : (i + 1) * LANES] = got.astype(BF16)
        for tile, first, count in sample_tiles(s):
            parts = []
            for j in range(count):
                at = other * s.lo_each + first + j
                chosen = iota((s.lo_patches, s.lo_length), 0) == keep_lo_ref[pl.ds(at, 1), :]
                parts.append(nn(img_lo_ref[at], jnp.where(chosen, 1.0, 0.0).astype(BF16)))
            if count < s.pack:
                parts.append(jnp.zeros((s.features, (s.pack - count) * s.lo_length), F32))
            joined = jnp.concatenate(parts, axis=1) if len(parts) > 1 else parts[0]
            out_ref[:, tile * LANES : (tile + 1) * LANES] = joined.astype(BF16)


def pick(s, members, member, keep_lo, keep_hi, img_lo, img_hi):
    args = (keep_lo, keep_hi, img_lo, img_hi)
    return pl.pallas_call(
        functools.partial(pick_kernel, s, members),
        grid_spec=pltpu.PrefetchScalarGridSpec(
            num_scalar_prefetch=1,
            grid=(1,),
            in_specs=[whole(a) for a in args],
            out_specs=[fixed(s.features, s.rows)] * len(members),
        ),
        out_shape=[shape((s.features, s.rows), BF16)] * len(members),
        compiler_params=params(60),
        cost_estimate=cost(2e9, 4e6),
    )(member, *args)


def stage_kernel(s, member_ref, keep_lo_ref, keep_hi_ref, mask_lo_ref, mask_hi_ref, cot_lo_ref, cot_hi_ref, keep_ref, seen_ref, *out_refs):
    eye = jnp.where(iota((s.features, s.features), 0) == iota((s.features, s.features), 1), 1.0, 0.0).astype(BF16)
    first_hi = (iota((1, s.hi_length), 1) == 0).astype(jnp.int32)
    first_lo = (iota((1, s.lo_length), 1) == 0).astype(jnp.int32)
    for k, out_ref in enumerate(out_refs):
        other = member_ref[0] ^ k
        for i in range(s.hi_each):
            at = other * s.hi_each + i
            keep_ref[k, i : i + 1, :] = keep_hi_ref[pl.ds(at, 1), :]
            out_ref[:, i * LANES : (i + 1) * LANES] = cot_hi_ref[at]
            if k == 0:
                seen_ref[i : i + 1, :] = jnp.maximum(mask_hi_ref[pl.ds(at, 1), :], first_hi).astype(F32)
        for tile, first, count in sample_tiles(s):
            begin = other * s.lo_each + first
            keep_ref[k, tile : tile + 1, :] = slots([keep_lo_ref[pl.ds(begin + j, 1), :] for j in range(count)], -1, s)
            if k == 0:
                seen = [jnp.maximum(mask_lo_ref[pl.ds(begin + j, 1), :], first_lo) for j in range(count)]
                seen_ref[tile : tile + 1, :] = slots(seen, 0, s).astype(F32)
            where = slice(tile * LANES, (tile + 1) * LANES)
            if count < s.pack:
                out_ref[:, where] = jnp.zeros((s.features, LANES), BF16)
            if count:
                size = count * s.lo_length
                start = pl.multiple_of(begin * s.lo_length, s.lo_length)
                out_ref[:, tile * LANES : tile * LANES + size] = nt(eye, cot_lo_ref[pl.ds(start, size), :]).astype(BF16)


def stage(s, member, keep_lo, keep_hi, mask_lo, mask_hi, cot_lo, cot_hi):
    args = (keep_lo, keep_hi, mask_lo, mask_hi, cot_lo, cot_hi)
    return pl.pallas_call(
        functools.partial(stage_kernel, s),
        grid_spec=pltpu.PrefetchScalarGridSpec(
            num_scalar_prefetch=1,
            grid=(1,),
            in_specs=[whole(a) for a in args],
            out_specs=[fixed(s.groups, s.tiles, LANES), fixed(s.tiles, LANES)]
            + [fixed(s.features, s.rows)] * s.groups,
        ),
        out_shape=[shape((s.groups, s.tiles, LANES), jnp.int32), shape((s.tiles, LANES), F32)]
        + [shape((s.features, s.rows), BF16)] * s.groups,
        compiler_params=params(60),
        cost_estimate=cost(1e8, 4e6),
    )(member, *args)


def chosen_columns(s, keep_ref, tile, patches, wanted_hi):
    row = keep_ref[0, pl.ds(tile, 1), :]
    is_hi = tile < s.hi_each
    row = jnp.where(is_hi if wanted_hi else jnp.logical_not(is_hi), row, -1)
    column = jnp.broadcast_to(row.astype(F32), (LANES, LANES)).T.astype(jnp.int32)
    parts = [jnp.where(iota((LANES, LANES), 1) + at == column, 1.0, 0.0) for at in range(0, patches, LANES)]
    return jnp.concatenate(parts, axis=1).astype(BF16)


def pair_masks():
    lane = iota((1, LANES), 1)
    low = jnp.where(lane < LANES // 2, 1.0, 0.0).astype(BF16)
    high = jnp.where(lane < LANES // 2, 0.0, 1.0).astype(BF16)
    return low, high


def doubled(block, masks):
    return jnp.concatenate([block * masks[0], block * masks[1]], axis=0)


def allowed(s, seen_ref, tile):
    bits = jnp.where(tile < s.hi_each, s.hi_length.bit_length() - 1, s.lo_length.bit_length() - 1)
    same = (iota((LANES, LANES), 0) >> bits) == (iota((LANES, LANES), 1) >> bits)
    open_to = jnp.logical_and(same, seen_ref[pl.ds(tile, 1), :] > 0)
    return jnp.concatenate([open_to, open_to], axis=0)


def forward_kernel(s, heads, keep_ref, seen_ref, p0, p1, p2, p3, w0, w1, w2, w3, pos_lo_ref, pos_hi_ref, gain1_ref, wqkv_ref, wout_ref, x0_ref, a_ref, qkv_ref, probs_ref, mixed_ref, x1_ref):
    step = pl.program_id(0)
    per = ROWS // LANES
    width = s.width
    picked = jnp.concatenate([p[...] for p in (p0, p1, p2, p3)], axis=0)
    embed = jnp.concatenate([w[: s.features, :] for w in (w0, w1, w2, w3)], axis=0)
    hot_hi = jnp.concatenate([chosen_columns(s, keep_ref, step * per + j, s.hi_patches, True) for j in range(per)], axis=0)
    hot_lo = jnp.concatenate([chosen_columns(s, keep_ref, step * per + j, s.lo_patches, False) for j in range(per)], axis=0)
    start = tn(picked, embed) + (nn(hot_hi, pos_hi_ref[...]) + nn(hot_lo, pos_lo_ref[...]))
    x0_ref[...] = start.astype(BF16)
    normed, _ = normalize(start)
    normed = (normed * gain1_ref[0:1, :]).astype(BF16)
    a_ref[...] = normed
    for c in range(3):
        part = slice(c * width, (c + 1) * width)
        qkv_ref[:, part] = nn(normed, wqkv_ref[:, part]).astype(BF16)
    masks = pair_masks()
    scale = 1.0 / math.sqrt(width // heads)
    for j in range(per):
        rows = slice(j * LANES, (j + 1) * LANES)
        ok = allowed(s, seen_ref, step * per + j)
        for h in range(width // LANES):
            at = h * LANES
            q = qkv_ref[rows, at : at + LANES]
            k = qkv_ref[rows, width + at : width + at + LANES]
            v = qkv_ref[rows, 2 * width + at : 2 * width + at + LANES]
            scores = nt(doubled(q, masks), k) * scale
            scores = jnp.where(ok, scores, MASKED)
            raised = jnp.exp(scores - jnp.max(scores, axis=-1, keepdims=True))
            probs = raised / jnp.sum(raised, axis=-1, keepdims=True)
            rounded = probs.astype(BF16)
            probs_ref[j, h] = rounded
            wide = jnp.concatenate([rounded[:LANES], rounded[LANES:]], axis=1)
            mixed_ref[rows, at : at + LANES] = nn(wide, doubled(v, masks)).astype(BF16)
    middle = start + nn(mixed_ref[...], wout_ref[...])
    x1_ref[...] = middle


def forward(s, heads, keep, seen, picked, weights, pos_lo, pos_hi, gain1, wqkv, wout):
    width, rows = s.width, s.rows
    per, pairs = ROWS // LANES, width // LANES
    return pl.pallas_call(
        functools.partial(forward_kernel, s, heads),
        grid=(rows // ROWS,),
        in_specs=[whole(keep), whole(seen)]
        + [along(s.features, ROWS)] * 4
        + [whole(w) for w in weights]
        + [whole(a) for a in (pos_lo, pos_hi, gain1, wqkv, wout)],
        out_specs=[
            across(ROWS, width),
            across(ROWS, width),
            across(ROWS, 3 * width),
            pl.BlockSpec((per, pairs, 2 * LANES, LANES), lambda i: (i, 0, 0, 0)),
            across(ROWS, width),
            across(ROWS, width),
        ],
        out_shape=[
            shape((rows, width), BF16),
            shape((rows, width), BF16),
            shape((rows, 3 * width), BF16),
            shape((s.tiles, pairs, 2 * LANES, LANES), BF16),
            shape((rows, width), BF16),
            shape((rows, width), F32),
        ],
        compiler_params=params(60),
        cost_estimate=cost(1.5e10, 3e7),
    )(keep, seen, *picked, *weights, pos_lo, pos_hi, gain1, wqkv, wout)


def part_rows(width, offset):
    return pl.BlockSpec((ROWS, width), lambda i, *_: (i + offset, 0))


def relative(ids_ref, x, y, z, c):
    return ids_ref[0] ^ (2 * z + y), ids_ref[1] ^ (2 * x + c)


def places(ids_ref, far):
    out = []
    for c in range(2):
        for x in range(2):
            for y in range(2):
                for z in range(far):
                    d, v = relative(ids_ref, x, y, z, c)
                    out.append(d * 4 + v)
    return out


def turn_relative(ids_ref, far, block, source_ref, turned_ref, acc_ref):
    order = places(ids_ref, far)
    rows = source_ref.shape[0]
    for begin in range(0, rows, rows // 2):
        span = slice(begin, begin + rows // 2)
        acc_ref[:, : rows // 2] = source_ref[span, :].astype(F32).T
        for p in range(0, len(order), 2):
            pair = [
                acc_ref[pl.ds(pl.multiple_of(at * block, 8), block), : rows // 2]
                for at in order[p : p + 2]
            ]
            turned_ref[p * block : (p + 2) * block, span] = jnp.concatenate(pair, axis=0).astype(BF16)


def spread(ids_ref, far, acc_ref, outs, block, extra):
    for x in range(2):
        for y in range(2):
            for z in range(far):
                for c, out_ref in enumerate(outs):
                    d, v = relative(ids_ref, x, y, z, c)
                    start = pl.multiple_of((d * 4 + v) * block, 8)
                    out_ref[x, y, z, :block, :] = acc_ref[pl.ds(start, block), :].astype(BF16)
                    out_ref[x, y, z, block:, :] = extra


def spread_features(s, ids_ref, acc_ref, outs):
    half = s.features // 2
    for k in range(4):
        for y in range(2):
            start = k * s.features + ((ids_ref[0] & 1) ^ y) * half
            rows = acc_ref[pl.ds(pl.multiple_of(start, 8), half), :]
            outs[k % 2][k // 2, y] = rows.astype(BF16)


def hidden_kernel(s, far, chunks, ids_ref, seen_ref, c0, c1, c2, c3, h0, h1, h2, h3, x1_ref, mixed_ref, w1_ref, b1_ref, w2_ref, b2_ref, gain2_ref, wout_ref, two0_ref, two1_ref, one0_ref, one1_ref, p0, p1, p2, p3, out0_ref, out1_ref, n0_ref, n1_ref, go_ref, ga_ref, b_ref, turned_ref, gm_ref, gpred_ref, forth_ref, back_ref, z_ref, gu_ref, acc_ref, side_ref):
    step = pl.program_id(0)
    width = s.width
    block = width // (8 * far)
    subs = [slice(begin, begin + ROWS) for begin in range(0, s.rows, ROWS)]
    seen = jnp.concatenate([seen_ref[t : t + 1, :] for t in range(s.tiles)], axis=1)

    @pl.when(step == 0)
    def _():
        gpred_ref[...] = jnp.concatenate([c[...] for c in (c0, c1, c2, c3)], axis=0) * seen.astype(BF16)
        head = jnp.concatenate([h[s.features :, :] for h in (h0, h1, h2, h3)], axis=0)
        total = None
        for rows in subs:
            values = x1_ref[rows, :]
            normed, _ = normalize(values)
            b_ref[rows, :] = (normed * gain2_ref[1:2, :]).astype(BF16)
            forth_ref[rows, :] = values + b2_ref[2:3, :]
            back_ref[rows, :] = jnp.zeros((ROWS, width), F32)
            upward = tn(gpred_ref[:, rows], head).astype(BF16)
            gm_ref[rows, :] = upward
            part = jnp.sum(upward.astype(F32), axis=0, keepdims=True)
            total = part if total is None else total + part
        side_ref[1:2, :] = total
        turn_relative(ids_ref, far, block, b_ref, turned_ref, acc_ref)

    @pl.when(step < chunks)
    def _():
        w1, w2, bias = w1_ref[...], w2_ref[...], b1_ref[...]
        total = None
        for rows in subs:
            u = nn(b_ref[rows, :], w1)
            upward = nt(gm_ref[rows, :], w2)
            z, slope = gelu_parts(u + bias)
            z = z.astype(BF16)
            gu = (upward * slope).astype(BF16)
            z_ref[rows, :] = z
            gu_ref[rows, :] = gu
            part = jnp.sum(gu.astype(F32), axis=0, keepdims=True)
            total = part if total is None else total + part
        side_ref[pl.ds(2 + ((ids_ref[0] >> 1) ^ step), 1), :] = total
        forth_ref[...] += nn(z_ref[...], w2)
        back_ref[...] += nt(gu_ref[...], w1)
        ones = nn(turned_ref[...], gu_ref[...])
        one0_ref[0] = ones[: width // 2].astype(BF16)
        one1_ref[0] = ones[width // 2 :].astype(BF16)
        acc_ref[...] = tn(z_ref[...], gm_ref[...])
        tall = width // 8
        for x in range(2):
            for y in range(2):
                for c, out_ref in enumerate((two0_ref, two1_ref)):
                    d, v = relative(ids_ref, x, y, 0, c)
                    start = pl.multiple_of(((d & 1) * 4 + v) * tall, 8)
                    out_ref[x, y, 0] = acc_ref[pl.ds(start, tall), :].astype(BF16)

    @pl.when(step == chunks)
    def _():
        total = None
        for rows in subs:
            z_ref[rows, :] = forth_ref[rows, :].astype(BF16)
            upward = back_ref[rows, :]
            normed, inverse = normalize(x1_ref[rows, :])
            part = jnp.sum(upward * normed, axis=0, keepdims=True)
            total = part if total is None else total + part
            grad = gm_ref[rows, :].astype(F32) + normalize_back(upward, normed, inverse, gain2_ref[1:2, :])
            grad = grad.astype(BF16)
            ga_ref[rows, :] = grad
            go_ref[rows, :] = nt(grad, wout_ref[...]).astype(BF16)
        side_ref[0:1, :] = total
        final = z_ref[...]
        for head, out in zip((h0, h1, h2, h3), (p0, p1, p2, p3)):
            out[...] = (nt(head[s.features :, :], final) * seen).astype(BF16)
        acc_ref[: s.groups * s.features, :] = nn(gpred_ref[...], final)
        spread_features(s, ids_ref, acc_ref, (n0_ref, n1_ref))
        acc_ref[...] = tn(mixed_ref[...], ga_ref[...])
        spread(ids_ref, far, acc_ref, (out0_ref, out1_ref), block, side_ref[...].astype(BF16))


def hidden(s, ids, far, seen, cots, weights, x1, mixed, w1, b1, w2, b2, gain2, wout):
    rows, width = s.rows, s.width
    chunks = w1.shape[1] // width
    block = width // (8 * far)
    high = s.groups * s.features
    sides = 8 * -(-(2 + chunks) // 8)
    last = chunks - 1

    def chunk(i, ids):
        return (ids[0] >> 1) ^ jnp.minimum(i, last)

    first = [seen, *cots, *weights, x1, mixed]
    rest = [b2, gain2, wout]
    outs = (
        [((2, 2, far, width // 8, width), BF16)] * 2
        + [((chunks, width // 2, width), BF16)] * 2
        + [((s.features, rows), BF16)] * 4
        + [((2, 2, far, block + sides, width), BF16)] * 2
        + [((2, 2, s.features // 2, width), BF16)] * 2
        + [((rows, width), BF16)] * 2
    )
    specs = [
        pl.BlockSpec((2, 2, 1, width // 8, width), lambda i, ids: (0, 0, jnp.minimum(i, last), 0, 0))
    ] * 2
    specs += [pl.BlockSpec((1, width // 2, width), lambda i, ids: (chunk(i, ids), 0, 0))] * 2
    specs += [fixed(*dims) for dims, _ in outs[4:]]
    return pl.pallas_call(
        functools.partial(hidden_kernel, s, far, chunks),
        grid_spec=pltpu.PrefetchScalarGridSpec(
            num_scalar_prefetch=1,
            grid=(chunks + 1,),
            in_specs=[whole(a) for a in first]
            + [
                pl.BlockSpec((width, width), lambda i, ids: (0, chunk(i, ids))),
                pl.BlockSpec((1, width), lambda i, ids: (0, chunk(i, ids))),
                pl.BlockSpec((width, width), lambda i, ids: (chunk(i, ids), 0)),
            ]
            + [whole(a) for a in rest],
            out_specs=specs,
            scratch_shapes=[
                pltpu.VMEM((rows, width), BF16),
                pltpu.VMEM((width, rows), BF16),
                pltpu.VMEM((rows, width), BF16),
                pltpu.VMEM((high, rows), BF16),
                pltpu.VMEM((rows, width), F32),
                pltpu.VMEM((rows, width), F32),
                pltpu.VMEM((rows, width), BF16),
                pltpu.VMEM((rows, width), BF16),
                pltpu.VMEM((width, width), F32),
                pltpu.VMEM((sides, width), F32),
            ],
        ),
        out_shape=[shape(*out) for out in outs],
        compiler_params=params(60),
        cost_estimate=cost(3.4e10, 4e7),
    )(ids, *first, w1, b1, w2, *rest)


def attention_back(s, heads, qkv_ref, probs_ref, go_ref, gqkv_ref):
    per = ROWS // LANES
    width = s.width
    masks = pair_masks()
    scale = 1.0 / math.sqrt(width // heads)
    for j in range(per):
        rows = slice(j * LANES, (j + 1) * LANES)
        for h in range(width // LANES):
            at = h * LANES
            q = doubled(qkv_ref[rows, at : at + LANES], masks)
            k = doubled(qkv_ref[rows, width + at : width + at + LANES], masks)
            v = qkv_ref[rows, 2 * width + at : 2 * width + at + LANES]
            out = doubled(go_ref[rows, at : at + LANES], masks)
            rounded = probs_ref[j, h]
            probs = rounded.astype(F32)
            upward = nt(out, v)
            centred = upward - jnp.sum(probs * upward, axis=-1, keepdims=True)
            grads = (probs * centred).astype(BF16)
            wide = jnp.concatenate([grads[:LANES], grads[LANES:]], axis=1)
            gqkv_ref[rows, at : at + LANES] = (nn(wide, k) * scale).astype(BF16)
            gqkv_ref[rows, width + at : width + at + LANES] = (tn(grads, q) * scale).astype(BF16)
            gqkv_ref[rows, 2 * width + at : 2 * width + at + LANES] = tn(rounded, out).astype(BF16)


def first_norm_back(gqkv, x0_ref, ga_ref, wqkv_ref, gain1_ref):
    upward = nt(gqkv, wqkv_ref[...])
    normed, inverse = normalize(x0_ref[...].astype(F32))
    grad = ga_ref[...].astype(F32) + normalize_back(upward, normed, inverse, gain1_ref[0:1, :])
    return grad.astype(BF16), jnp.sum(upward * normed, axis=0, keepdims=True)


def backward_kernel(s, heads, qkv_ref, probs_ref, go_ref, x0_ref, ga_ref, wqkv_ref, gain1_ref, gqkv_ref, g0_ref, gln1_ref):
    attention_back(s, heads, qkv_ref, probs_ref, go_ref, gqkv_ref)
    g0_ref[...], gain_part = first_norm_back(gqkv_ref[...], x0_ref, ga_ref, wqkv_ref, gain1_ref)
    accumulate(gln1_ref, pl.program_id(0) == 0, gain_part)


def row_inputs(s, offset):
    width = s.width
    return [
        part_rows(3 * width, offset),
        pl.BlockSpec((ROWS // LANES, width // LANES, 2 * LANES, LANES), lambda i, *_: (i + offset, 0, 0, 0)),
        part_rows(width, offset),
        part_rows(width, offset),
        part_rows(width, offset),
    ]


def backward(s, heads, offset, steps, qkv, probs, go, x0, ga, wqkv, gain1):
    width = s.width
    size = steps * ROWS
    return pl.pallas_call(
        functools.partial(backward_kernel, s, heads),
        grid=(steps,),
        in_specs=row_inputs(s, offset) + [whole(wqkv), whole(gain1)],
        out_specs=[across(ROWS, 3 * width), across(ROWS, width), fixed(1, width)],
        out_shape=[shape((size, 3 * width), BF16), shape((size, width), BF16), shape((1, width), F32)],
        compiler_params=params(60),
        cost_estimate=cost(8e9 * steps, 6e6 * steps),
    )(qkv, probs, go, x0, ga, wqkv, gain1)


def position_grads(s, keep_ref, g0, picked):
    hot_hi, hot_lo = [], []
    for t in range(s.tiles):
        row = keep_ref[0, t : t + 1, :]
        patches = s.hi_patches if t < s.hi_each else s.lo_patches
        hot = jnp.where(iota((patches, LANES), 0) == row, 1.0, 0.0).astype(BF16)
        (hot_hi if t < s.hi_each else hot_lo).append(hot)
    hi_rows = s.hi_each * LANES
    hi = nn(jnp.concatenate(hot_hi, axis=1), g0[:hi_rows])
    lo = nn(jnp.concatenate(hot_lo, axis=1), g0[hi_rows:])
    return lo, hi, nn(jnp.concatenate(picked, axis=0), g0)


def finish_kernel(s, far, chunks, ids_ref, keep_ref, a_ref, r0_ref, r1_ref, ga_ref, gb_ref, la_ref, lb_ref, p0, p1, p2, p3, w0, w1, w2, w3, q0, q1, q2, q3, o0_ref, o1_ref, e0_ref, e1_ref, i0, i1, i2, i3, turned_ref, acc_ref, lo_ref, hi_ref):
    step = pl.program_id(0)
    width = s.width
    block = width // (8 * far)
    half = width // 2
    done = r0_ref.shape[0]

    @pl.when(step == 0)
    def _():
        turn_relative(ids_ref, far, block, a_ref, turned_ref, acc_ref)

    @pl.when(step < chunks)
    def _():
        value = nn(turned_ref[:, :done], r0_ref[...]) + nn(turned_ref[:, done:], r1_ref[...])
        o0_ref[0] = value[:half].astype(BF16)
        o1_ref[0] = value[half:].astype(BF16)

    @pl.when(step == chunks)
    def _():
        g0 = jnp.concatenate([ga_ref[...], gb_ref[...]], axis=0)
        lo, hi, embed = position_grads(s, keep_ref, g0, [p[...] for p in (p0, p1, p2, p3)])
        lo_ref[...] = lo
        hi_ref[...] = hi
        acc_ref[: s.groups * s.features, :] = embed
        spread_features(s, ids_ref, acc_ref, (e0_ref, e1_ref))
        for weight, pred, out in zip((w0, w1, w2, w3), (q0, q1, q2, q3), (i0, i1, i2, i3)):
            out[: s.features, :] = nt(weight[: s.features, :], g0).astype(BF16)
            out[s.features :, :] = pred[...]
        hi_block = s.hi_patches // (8 * far)
        lo_block = s.lo_patches // (8 * far)
        gain = la_ref[...] + lb_ref[...]
        pad = jnp.zeros((block - hi_block - lo_block - 1, width), F32)
        order = places(ids_ref, far)
        for p in range(0, len(order), 2):
            pair = []
            for at in order[p : p + 2]:
                both = lo_ref[pl.ds(pl.multiple_of((at >> 1) * 8, 8), 8), :]
                pair += [
                    hi_ref[pl.ds(pl.multiple_of(at * hi_block, 8), hi_block), :],
                    jnp.where((at & 1) == 1, both[lo_block:], both[:lo_block]),
                    gain,
                    pad,
                ]
            row = (p % (len(order) // 2)) * block
            (o0_ref, o1_ref)[p // (len(order) // 2)][0, row : row + 2 * block, :] = jnp.concatenate(pair, axis=0).astype(BF16)


def finish(s, ids, far, keep, a, gqkvs, g0s, gains, picked, weights, preds):
    width, rows = s.width, s.rows
    chunks = gqkvs[0].shape[1] // width
    rest = [*g0s, *gains, *picked, *weights, *preds]
    out = pl.BlockSpec((1, width // 2, width), lambda i, ids: (i, 0, 0))
    return pl.pallas_call(
        functools.partial(finish_kernel, s, far, chunks),
        grid_spec=pltpu.PrefetchScalarGridSpec(
            num_scalar_prefetch=1,
            grid=(chunks + 1,),
            in_specs=[whole(keep), whole(a)]
            + [
                pl.BlockSpec((g.shape[0], width), lambda i, ids: (0, jnp.minimum(i, chunks - 1)))
                for g in gqkvs
            ]
            + [whole(r) for r in rest],
            out_specs=[out, out]
            + [fixed(2, 2, s.features // 2, width)] * 2
            + [fixed(2 * s.features, rows)] * 4,
            scratch_shapes=[
                pltpu.VMEM((width, rows), BF16),
                pltpu.VMEM((width, width), F32),
                pltpu.VMEM((s.lo_patches, width), F32),
                pltpu.VMEM((s.hi_patches, width), F32),
            ],
        ),
        out_shape=[shape((chunks + 1, width // 2, width), BF16)] * 2
        + [shape((2, 2, s.features // 2, width), BF16)] * 2
        + [shape((2 * s.features, rows), BF16)] * 4,
        compiler_params=params(60),
        cost_estimate=cost(7e9, 1.2e7),
    )(ids, keep, a, *gqkvs, *rest)


def combine_kernel(held_ref, got_ref, keep_ref, send_ref):
    send_ref[...] = (held_ref[:, 1].astype(F32) + got_ref[:, 1].astype(F32)).astype(BF16)
    keep_ref[...] = (held_ref[:, 0].astype(F32) + got_ref[:, 0].astype(F32)).astype(BF16)


def combine(held, got, axis):
    dims = held.shape
    width = dims[-1]
    outer = math.prod(dims[:axis])
    inner = math.prod(dims[axis + 1 : -1])
    grid = (outer // 4, 1) if outer > 4 else (1, 2)
    broad, tall = outer // grid[0], inner // grid[1]
    half = shape((outer, inner, width), BF16)
    spec = pl.BlockSpec((broad, 2, tall, width), lambda i, j: (i, 0, j, 0))
    out = pl.BlockSpec((broad, tall, width), lambda i, j: (i, j, 0))
    keep, send = pl.pallas_call(
        combine_kernel,
        grid=grid,
        in_specs=[spec, spec],
        out_specs=[out, out],
        out_shape=[half, half],
        compiler_params=params(60),
        cost_estimate=cost(1e6, 6 * outer * inner * width),
    )(*(value.reshape(outer, 2, inner, width) for value in (held, got)))
    left = dims[:axis] + dims[axis + 1 :]
    return keep.reshape(left), send.reshape(left)


def place_kernel(s, member_ref, keep_ref, r0, r1, r2, r3, lo_ref, hi_ref, pred_lo_ref, pred_hi_ref):
    lane_sample = iota((1, LANES), 1) // s.lo_length
    eye = jnp.where(iota((s.features, s.features), 0) == iota((s.features, s.features), 1), 1.0, 0.0).astype(BF16)
    for k, got_ref in enumerate((r0, r1, r2, r3)):
        other = member_ref[0] ^ k
        for i in range(s.hi_each):
            chosen = iota((s.hi_patches, LANES), 0) == keep_ref[k, i : i + 1, :]
            hot = jnp.where(chosen, 1.0, 0.0).astype(BF16)
            lanes = slice(i * LANES, (i + 1) * LANES)
            hi_ref[other * s.hi_each + i] = nt(got_ref[: s.features, lanes], hot).astype(BF16)
            pred_hi_ref[other * s.hi_each + i] = got_ref[s.features :, lanes]
        for tile, first, count in sample_tiles(s):
            lanes = slice(tile * LANES, (tile + 1) * LANES)
            got = got_ref[: s.features, lanes]
            for j in range(count):
                row = jnp.where(lane_sample == j, keep_ref[k, tile : tile + 1, :], -1)
                hot = jnp.where(iota((s.lo_patches, LANES), 0) == row, 1.0, 0.0).astype(BF16)
                lo_ref[other * s.lo_each + first + j] = nt(got, hot).astype(BF16)
            if count:
                size = count * s.lo_length
                turned = tn(got_ref[s.features :, lanes], eye).astype(BF16)
                start = pl.multiple_of((other * s.lo_each + first) * s.lo_length, s.lo_length)
                pred_lo_ref[pl.ds(start, size), :] = turned[:size]


def place(s, member, keep, blocks):
    lo = s.groups * s.lo_each
    hi = s.groups * s.hi_each
    outs = [
        (lo, s.features, s.lo_patches),
        (hi, s.features, s.hi_patches),
        (lo * s.lo_length, s.features),
        (hi, s.features, s.hi_length),
    ]
    return pl.pallas_call(
        functools.partial(place_kernel, s),
        grid_spec=pltpu.PrefetchScalarGridSpec(
            num_scalar_prefetch=1,
            grid=(1,),
            in_specs=[whole(keep)] + [whole(b) for b in blocks],
            out_specs=[fixed(*dims) for dims in outs],
        ),
        out_shape=[shape(dims, BF16) for dims in outs],
        compiler_params=params(60),
        cost_estimate=cost(2e9, 8e6),
    )(member, keep, *blocks)


def swap(value, data_bit, var_bit):
    dp, var = lax.axis_size("dp"), lax.axis_size("var")
    pairs = [
        (d * var + v, (d ^ data_bit) * var + (v ^ var_bit)) for d in range(dp) for v in range(var)
    ]
    return lax.ppermute(value, AXES, pairs)


def add_rounded(left, right):
    return (left.astype(F32) + right.astype(F32)).astype(BF16)


def added(*values):
    values = [value.astype(F32) for value in values]
    while len(values) > 1:
        values = [values[i] + values[i + 1] for i in range(0, len(values), 2)]
    return values[0]


def tie(value, *tokens):
    return lax.optimization_barrier((value, tokens))[0]


PARTNERS = {"core": (0, 1), "x": (0, 2), "y": (1, 0), "z0": (2, 0), "z1": (4, 0)}


class Chain:
    def __init__(self, near, sent):
        self.near, self.sent = near, sent
        self.repeats = near.ndim == 4
        self.names = ["x", "y"] if self.repeats else ["chunk", "x", "y", "z1", "z0"][7 - near.ndim :]
        self.held = self.got = None

    def outgoing(self, name):
        if name == "core":
            self.held = self.near
            return self.sent
        if name not in self.names:
            self.held = add_rounded(self.held, self.got)
            return self.held
        axis = self.names.index(name)
        self.names.remove(name)
        if math.prod(self.held.shape) >= 1 << 20:
            self.held, sent = combine(self.held, self.got, axis)
            return sent
        kept, sent = (
            [lax.index_in_dim(value, side, axis, keepdims=False) for value in (self.held, self.got)]
            for side in range(2)
        )
        self.held = add_rounded(*kept)
        return add_rounded(*sent)

    def hold(self, *tokens):
        self.held, self.got = tie((self.held, self.got), *tokens)

    def final(self):
        return added(self.held, self.got)


def send_rows(values, bits):
    width = values[0].shape[-1]
    if len(values) == 1:
        return [swap(values[0].reshape(-1, width), *bits).reshape(values[0].shape)]
    flat = [value.reshape(-1, width) for value in values]
    got = swap(jnp.concatenate(flat, axis=0), *bits)
    out, start = [], 0
    for value, rows in zip(values, flat):
        out.append(got[start : start + rows.shape[0]].reshape(value.shape))
        start += rows.shape[0]
    return out


def trade(name, *chains):
    got = send_rows([chain.outgoing(name) for chain in chains], PARTNERS[name])
    for chain, value in zip(chains, got):
        chain.got = value
    return got[0]


def both_halves(value):
    value = value.astype(BF16)
    other = swap(value, 1, 0)
    second = lax.axis_index("dp") % 2 == 1
    return jnp.concatenate(
        [jnp.where(second, other, value), jnp.where(second, value, other)], axis=0
    ).astype(F32)


def natural(near, sent):
    rows, width = near.shape[-2:]
    both = jnp.stack([near, sent]).reshape((2, -1, 2, 2, 4, rows, width))
    return both.transpose(4, 3, 2, 0, 1, 5, 6).reshape(32, -1, width)


def scattered(full):
    return lax.psum_scatter(full, AXES, scatter_dimension=0, tiled=True).astype(F32)


def joined(blocks, chunks):
    count, rows, width = blocks.shape
    split = blocks.reshape(count, chunks, rows // chunks, width).transpose(0, 2, 1, 3)
    return split.reshape(count * (rows // chunks), chunks * width)


def plain_sum(near, sent):
    if near.ndim >= 6:
        return natural(near, sent)
    value = jnp.stack([near, sent], axis=1)
    value = value.reshape((4, -1, near.shape[-1]))
    bit = 1
    while value.shape[0] > 1:
        value = value.reshape((value.shape[0] // 2, 2) + value.shape[1:])
        value = add_rounded(value[:, 0], swap(value[:, 1], 0, bit))
        bit *= 2
    return lax.psum(value[0], "dp").astype(F32)


def exchange_relative(blocks):
    return [blocks[0]] + [swap(blocks[k], 0, k) for k in range(1, len(blocks))]


def body(
    img_lo,
    img_hi,
    keep_lo,
    keep_hi,
    mask_lo,
    mask_hi,
    w_embed,
    pos_lo,
    pos_hi,
    ln1_gain,
    w_qkv,
    w_out,
    ln2_gain,
    w_fc1,
    b_fc1,
    w_fc2,
    b_fc2,
    w_head,
    cot_lo,
    cot_hi,
):
    groups = lax.axis_size("var")
    devices = lax.axis_size("dp") * groups
    member = lax.axis_index("var").astype(jnp.int32).reshape(1)
    s = Sizes(keep_lo.shape, keep_hi.shape, w_embed.shape, img_lo.shape, img_hi.shape, groups)
    features, width = s.features, s.width
    gain1 = gain2 = vectors = jnp.stack([ln1_gain, ln2_gain, b_fc2])
    img_lo_t, img_hi_t = img_lo.transpose(0, 2, 1), img_hi.transpose(0, 2, 1)

    own = jnp.concatenate([w_embed, w_head.T], axis=0)
    crossed = swap(own, 0, 2)
    beside = swap(own, 0, 1)
    sent = pick(s, (2, 3, 1, 0), member, keep_lo, keep_hi, img_lo_t, img_hi_t)
    crossed = tie(crossed, sent[0])
    weights = [own, beside, crossed, swap(crossed, 0, 1)]
    picked = [sent[3], swap(sent[2], 0, 1), swap(sent[0], 0, 2), swap(sent[1], 0, 3)]
    keep, seen, *cots = stage(
        s,
        tie(member, sent[0]),
        keep_lo,
        keep_hi,
        mask_lo,
        mask_hi,
        cot_lo.reshape(-1, features),
        cot_hi.transpose(0, 2, 1),
    )
    cots = exchange_relative(cots)
    own_keep = keep
    x0, a, qkv, probs, mixed, x1 = forward(
        s, HEADS, own_keep, seen, picked, weights, pos_lo, pos_hi, gain1, w_qkv, w_out
    )
    far = 4
    cube = lax.axis_size("dp") == 2 * far
    place_of = lax.axis_index("dp") * groups + lax.axis_index("var")
    ids = jnp.stack([lax.axis_index("dp"), lax.axis_index("var")]).astype(jnp.int32)
    if not cube:
        ids = jnp.zeros_like(ids)

    def chain_of(near, sent):
        if near.ndim == 5:
            near, sent = (
                value.reshape((2, 2, 2, 2) + value.shape[3:]) for value in (near, sent)
            )
        elif near.ndim == 3:
            near, sent = (
                value.reshape((-1, 2, 2, 2, 2, width // 32, width)) for value in (near, sent)
            )
        return Chain(near, sent)

    def step(name, *chains):
        return trade(name, *chains) if cube else ()

    def halves_of(chain):
        out = []
        for side in range(2):
            piece = Chain(chain.near, chain.sent)
            count = chain.near.shape[0] // 2
            piece.held, piece.got = (
                lax.slice_in_dim(value, side * count, (side + 1) * count, axis=0)
                for value in (chain.held, chain.got)
            )
            out.append(piece)
        return out

    two0, two1, one0, one1, *rest = hidden(
        s,
        ids,
        far,
        tie(seen, x1),
        cots,
        weights,
        x1,
        mixed,
        w_fc1,
        b_fc1.reshape(1, -1),
        w_fc2,
        vectors,
        gain2,
        w_out,
    )
    preds, (out0, out1, head0, head1, go, ga) = rest[:groups], rest[groups:]
    two, one = chain_of(two0, two1), chain_of(one0, one1)
    out, head = chain_of(out0, out1), chain_of(head0, head1)
    tokens = [step("core", chain) for chain in (two, one, out, head)]

    def back(offset, steps, *ready):
        return backward(
            s, HEADS, offset, steps, qkv, probs, go, x0, ga, w_qkv, tie(gain1, *ready)
        )

    parts = [back(0, 1, go)]
    if cube:
        for chain in (two, one, out, head):
            chain.hold(parts[0][0])
    near_tokens = [step("x", two), step("y", one)]
    if cube:
        for chain in (out, head):
            chain.hold(two.held, one.held)
    near_tokens.append(step("z0", out, head))
    parts.append(back(1, s.rows // ROWS - 1, parts[0][0], two.held, one.held, *tokens))
    if cube:
        for chain in (two, one, out, head):
            chain.hold(parts[1][0])
    tokens = [step("y", two), step("x", one, out, head)]
    gqkvs, g0s, gains = zip(*parts)
    near, sent, near_embed, sent_embed, *blocks = finish(
        s,
        tie(ids, two.held, one.held, *near_tokens),
        far,
        own_keep,
        a,
        gqkvs,
        g0s,
        gains,
        picked,
        weights,
        preds,
    )
    sent, sent_embed = tie((sent, sent_embed), *tokens)
    first, embed = chain_of(near, sent), chain_of(near_embed, sent_embed)
    tokens += [step("core", first), step("core", embed)]
    if cube:
        old = (two, one, out, head)
        for chain in old:
            chain.hold(first.got)
        one_half, other_half = halves_of(first)
        tokens = [trade("x", one_half, embed), trade("y", other_half, out, head)]
        trade("z0", two, one)
        for chain in old:
            chain.hold(*tokens)
        tokens = [trade("y", one_half, embed), trade("x", other_half)]
        trade("z1", *old)
        blocks = [tie(block_of, *tokens) for block_of in blocks]
        trade("z0", one_half, other_half, embed)
        trade("z1", one_half, other_half, embed)
        head.hold(embed.held)
        grad_head = both_halves(head.final())
        last_member = tie(member, grad_head)
        for chain in (two, one, out):
            chain.hold(grad_head)
        grad_fc2, grad_fc1, rest, grad_embed = (
            chain.final() for chain in (two, one, out, embed)
        )
        grad_embed = both_halves(grad_embed)
        first = jnp.concatenate([one_half.final(), other_half.final()], axis=0).reshape(-1, width)
        grad_fc1 = grad_fc1.reshape(-1, width)
    else:
        grad_fc2, grad_fc1, rest, grad_head, grad_embed, first = (
            plain_sum(chain.near, chain.sent) for chain in (two, one, out, head, embed, first)
        )
        last_member = member
    grad_img_lo, grad_img_hi, pred_lo, pred_hi = place(s, last_member, keep, exchange_relative(blocks))
    grad_head = grad_head.T

    block = width // devices
    inner = w_fc1.shape[1] // width

    hi_block = s.hi_patches // devices
    lo_block = s.lo_patches // devices

    def own_part(row):
        return lax.dynamic_slice_in_dim(row, place_of * block, block)

    if cube:
        grad_fc1 = joined(grad_fc1[None], inner)
        grad_qkv = joined(first[None, : 3 * block], 3)
        grad_out, sides = rest[:block], rest[block:]
        extra = first[3 * block :]
        grad_pos_hi = extra[:hi_block]
        grad_pos_lo = extra[hi_block : hi_block + lo_block]
        first_side = extra[hi_block + lo_block]
    else:
        tall = width // 32
        hi_tall, lo_tall = s.hi_patches // 32, s.lo_patches // 32
        grad_fc2 = scattered(grad_fc2.reshape(-1, width))
        grad_fc1 = scattered(joined(grad_fc1, inner))
        grad_qkv = scattered(joined(first[:, : 3 * tall], 3))
        grad_out, sides = scattered(rest[:, :tall].reshape(-1, width)), rest[0, tall:]
        extra = first[:, 3 * tall :]
        grad_pos_hi = scattered(extra[:, :hi_tall].reshape(-1, width))
        grad_pos_lo = scattered(extra[:, hi_tall : hi_tall + lo_tall].reshape(-1, width))
        sides = lax.psum(jnp.concatenate([sides, extra[0, hi_tall + lo_tall :]]), AXES).astype(F32)
        first_side = sides[rest.shape[1] - tall]
    grad_ln1 = own_part(first_side)
    grad_ln2 = own_part(sides[0])
    grad_b2 = own_part(sides[1])
    grad_b1 = lax.dynamic_slice_in_dim(
        sides[2 : 2 + inner].reshape(-1), place_of * inner * block, inner * block
    )
    return (
        pred_lo.reshape(cot_lo.shape),
        pred_hi.transpose(0, 2, 1),
        grad_img_lo.transpose(0, 2, 1),
        grad_img_hi.transpose(0, 2, 1),
        grad_embed,
        grad_pos_lo,
        grad_pos_hi,
        grad_ln1,
        grad_qkv,
        grad_out,
        grad_ln2,
        grad_fc1,
        grad_b1,
        grad_fc2,
        grad_b2,
        grad_head,
    )


def solution(mesh):
    placed = (
        P("dp", None, "var"),
        P("dp", None, "var"),
        P("dp", None),
        P("dp", None),
        P("dp", None),
        P("dp", None),
        P("var", None),
        P(),
        P(),
        P(),
        P(),
        P(),
        P(),
        P(),
        P(),
        P(),
        P(),
        P(None, "var"),
        P("dp", None, "var"),
        P("dp", None, "var"),
    )
    return jax.shard_map(
        body,
        mesh=mesh,
        in_specs=placed,
        out_specs=(
            P("dp", None, "var"),
            P("dp", None, "var"),
            P("dp", None, "var"),
            P("dp", None, "var"),
            P("var", None),
            P(("dp", "var"), None),
            P(("dp", "var"), None),
            P(("dp", "var")),
            P(("dp", "var"), None),
            P(("dp", "var"), None),
            P(("dp", "var")),
            P(("dp", "var"), None),
            P(("dp", "var")),
            P(("dp", "var"), None),
            P(("dp", "var")),
            P(None, "var"),
        ),
        check_vma=False,
    )
```

```python
import functools
import math

import jax
import jax.numpy as jnp
from jax import lax
from jax.experimental import pallas as pl
from jax.experimental.pallas import tpu as pltpu
from jax.sharding import PartitionSpec as P

HEADS = 12
EPSILON = 1e-06
AXES = ("dp", "var")
BF16 = jnp.bfloat16
F32 = jnp.float32
LANES = 128
ROWS = 256
MASKED = -1000000000.0
SHARE = 0.5


def dot(left, right, dims):
    return lax.dot_general(left, right, (dims, ((), ())), preferred_element_type=F32)


def nn(left, right):
    return dot(left, right, ((1,), (0,)))


def nt(left, right):
    return dot(left, right, ((1,), (1,)))


def tn(left, right):
    return dot(left, right, ((0,), (0,)))


def shape(dims, dtype):
    return jax.ShapeDtypeStruct(dims, dtype)


def whole(array):
    zeros = (0,) * array.ndim
    return pl.BlockSpec(array.shape, lambda *_: zeros, pipeline_mode=pl.Buffered(1))


def across(rows, width):
    return pl.BlockSpec((rows, width), lambda i, *_: (i, 0))


def along(height, columns):
    return pl.BlockSpec((height, columns), lambda i, *_: (0, i))


def fixed(*dims):
    zeros = (0,) * len(dims)
    return pl.BlockSpec(dims, lambda *_: zeros)


def params(mebibytes):
    return pltpu.CompilerParams(vmem_limit_bytes=mebibytes << 20)


def cost(flops, nbytes):
    return pl.CostEstimate(flops=int(flops * SHARE), bytes_accessed=int(nbytes * SHARE), transcendentals=0)


def iota(dims, axis):
    return lax.broadcasted_iota(jnp.int32, dims, axis)


def accumulate(ref, first, value):
    @pl.when(first)
    def _():
        ref[...] = value

    @pl.when(jnp.logical_not(first))
    def _():
        ref[...] += value


def normalize(values):
    center = values - jnp.mean(values, axis=-1, keepdims=True)
    inverse = lax.rsqrt(jnp.mean(center * center, axis=-1, keepdims=True) + EPSILON)
    return center * inverse, inverse


def normalize_back(upstream, normed, inverse, gains):
    scaled = upstream * gains
    mean_plain = jnp.mean(scaled, axis=-1, keepdims=True)
    mean_mixed = jnp.mean(scaled * normed, axis=-1, keepdims=True)
    return inverse * (scaled - mean_plain - normed * mean_mixed)


def gelu_parts(u):
    ratio = 1.0 / (1.0 + (0.3275911 * math.sqrt(0.5)) * jnp.abs(u))
    bell = jnp.exp(-0.5 * u * u)
    series = 0.5 * 1.061405429
    for factor in (-1.453152027, 1.421413741, -0.284496736, 0.254829592):
        series = series * ratio + 0.5 * factor
    tail = series * ratio * bell
    below = jnp.where(u < 0, tail, 1.0 - tail)
    return u * below, below + u * (bell * (1.0 / math.sqrt(2.0 * math.pi)))


class Sizes:
    def __init__(self, keep_lo, keep_hi, w_embed, img_lo, img_hi, groups):
        self.lo_each, self.hi_each = keep_lo[0] // groups, keep_hi[0] // groups
        self.lo_length, self.hi_length = keep_lo[1], keep_hi[1]
        self.features, self.width = w_embed
        self.lo_patches, self.hi_patches = img_lo[1], img_hi[1]
        self.groups = groups
        self.pack = LANES // self.lo_length
        self.lo_tiles = -(-self.lo_each // self.pack)
        self.hi_rows = self.hi_each * self.hi_length
        tiles = self.hi_each + self.lo_tiles
        self.tiles = tiles + tiles % 2
        self.rows = self.tiles * LANES


def sample_tiles(s):
    out = []
    for t in range(s.tiles - s.hi_each):
        first = t * s.pack
        out.append((s.hi_each + t, first, max(0, min(s.pack, s.lo_each - first))))
    return out


def slots(rows, fill, s):
    missing = s.pack - len(rows)
    if missing:
        rows = rows + [jnp.full((1, missing * s.lo_length), fill, rows[0].dtype if rows else jnp.int32)]
    return rows[0] if len(rows) == 1 else jnp.concatenate(rows, axis=1)


def pick_kernel(s, members, member_ref, keep_lo_ref, keep_hi_ref, img_lo_ref, img_hi_ref, *out_refs):
    for k, out_ref in zip(members, out_refs):
        other = member_ref[0] ^ k
        for i in range(s.hi_each):
            at = other * s.hi_each + i
            chosen = iota((s.hi_patches, LANES), 0) == keep_hi_ref[pl.ds(at, 1), :]
            got = nn(img_hi_ref[at], jnp.where(chosen, 1.0, 0.0).astype(BF16))
            out_ref[:, i * LANES : (i + 1) * LANES] = got.astype(BF16)
        for tile, first, count in sample_tiles(s):
            parts = []
            for j in range(count):
                at = other * s.lo_each + first + j
                chosen = iota((s.lo_patches, s.lo_length), 0) == keep_lo_ref[pl.ds(at, 1), :]
                parts.append(nn(img_lo_ref[at], jnp.where(chosen, 1.0, 0.0).astype(BF16)))
            if count < s.pack:
                parts.append(jnp.zeros((s.features, (s.pack - count) * s.lo_length), F32))
            joined = jnp.concatenate(parts, axis=1) if len(parts) > 1 else parts[0]
            out_ref[:, tile * LANES : (tile + 1) * LANES] = joined.astype(BF16)


def pick(s, members, member, keep_lo, keep_hi, img_lo, img_hi):
    args = (keep_lo, keep_hi, img_lo, img_hi)
    return pl.pallas_call(
        functools.partial(pick_kernel, s, members),
        grid_spec=pltpu.PrefetchScalarGridSpec(
            num_scalar_prefetch=1,
            grid=(1,),
            in_specs=[whole(a) for a in args],
            out_specs=[fixed(s.features, s.rows)] * len(members),
        ),
        out_shape=[shape((s.features, s.rows), BF16)] * len(members),
        compiler_params=params(60),
        cost_estimate=cost(2e9, 4e6),
    )(member, *args)


def stage_kernel(s, member_ref, keep_lo_ref, keep_hi_ref, mask_lo_ref, mask_hi_ref, cot_lo_ref, cot_hi_ref, keep_ref, seen_ref, *out_refs):
    eye = jnp.where(iota((s.features, s.features), 0) == iota((s.features, s.features), 1), 1.0, 0.0).astype(BF16)
    first_hi = (iota((1, s.hi_length), 1) == 0).astype(jnp.int32)
    first_lo = (iota((1, s.lo_length), 1) == 0).astype(jnp.int32)
    for k, out_ref in enumerate(out_refs):
        other = member_ref[0] ^ k
        for i in range(s.hi_each):
            at = other * s.hi_each + i
            keep_ref[k, i : i + 1, :] = keep_hi_ref[pl.ds(at, 1), :]
            out_ref[:, i * LANES : (i + 1) * LANES] = cot_hi_ref[at]
            if k == 0:
                seen_ref[i : i + 1, :] = jnp.maximum(mask_hi_ref[pl.ds(at, 1), :], first_hi).astype(F32)
        for tile, first, count in sample_tiles(s):
            begin = other * s.lo_each + first
            keep_ref[k, tile : tile + 1, :] = slots([keep_lo_ref[pl.ds(begin + j, 1), :] for j in range(count)], -1, s)
            if k == 0:
                seen = [jnp.maximum(mask_lo_ref[pl.ds(begin + j, 1), :], first_lo) for j in range(count)]
                seen_ref[tile : tile + 1, :] = slots(seen, 0, s).astype(F32)
            where = slice(tile * LANES, (tile + 1) * LANES)
            if count < s.pack:
                out_ref[:, where] = jnp.zeros((s.features, LANES), BF16)
            if count:
                size = count * s.lo_length
                start = pl.multiple_of(begin * s.lo_length, s.lo_length)
                out_ref[:, tile * LANES : tile * LANES + size] = nt(eye, cot_lo_ref[pl.ds(start, size), :]).astype(BF16)


def stage(s, member, keep_lo, keep_hi, mask_lo, mask_hi, cot_lo, cot_hi):
    args = (keep_lo, keep_hi, mask_lo, mask_hi, cot_lo, cot_hi)
    return pl.pallas_call(
        functools.partial(stage_kernel, s),
        grid_spec=pltpu.PrefetchScalarGridSpec(
            num_scalar_prefetch=1,
            grid=(1,),
            in_specs=[whole(a) for a in args],
            out_specs=[fixed(s.groups, s.tiles, LANES), fixed(s.tiles, LANES)]
            + [fixed(s.features, s.rows)] * s.groups,
        ),
        out_shape=[shape((s.groups, s.tiles, LANES), jnp.int32), shape((s.tiles, LANES), F32)]
        + [shape((s.features, s.rows), BF16)] * s.groups,
        compiler_params=params(60),
        cost_estimate=cost(1e8, 4e6),
    )(member, *args)


def chosen_columns(s, keep_ref, tile, patches, wanted_hi):
    row = keep_ref[0, pl.ds(tile, 1), :]
    is_hi = tile < s.hi_each
    row = jnp.where(is_hi if wanted_hi else jnp.logical_not(is_hi), row, -1)
    column = jnp.broadcast_to(row.astype(F32), (LANES, LANES)).T.astype(jnp.int32)
    parts = [jnp.where(iota((LANES, LANES), 1) + at == column, 1.0, 0.0) for at in range(0, patches, LANES)]
    return jnp.concatenate(parts, axis=1).astype(BF16)


def pair_masks():
    lane = iota((1, LANES), 1)
    low = jnp.where(lane < LANES // 2, 1.0, 0.0).astype(BF16)
    high = jnp.where(lane < LANES // 2, 0.0, 1.0).astype(BF16)
    return low, high


def doubled(block, masks):
    return jnp.concatenate([block * masks[0], block * masks[1]], axis=0)


def allowed(s, seen_ref, tile):
    bits = jnp.where(tile < s.hi_each, s.hi_length.bit_length() - 1, s.lo_length.bit_length() - 1)
    same = (iota((LANES, LANES), 0) >> bits) == (iota((LANES, LANES), 1) >> bits)
    open_to = jnp.logical_and(same, seen_ref[pl.ds(tile, 1), :] > 0)
    return jnp.concatenate([open_to, open_to], axis=0)


def forward_kernel(s, heads, keep_ref, seen_ref, p0, p1, p2, p3, w0, w1, w2, w3, pos_lo_ref, pos_hi_ref, gain1_ref, wqkv_ref, wout_ref, x0_ref, a_ref, qkv_ref, probs_ref, mixed_ref, x1_ref):
    step = pl.program_id(0)
    per = ROWS // LANES
    width = s.width
    picked = jnp.concatenate([p[...] for p in (p0, p1, p2, p3)], axis=0)
    embed = jnp.concatenate([w[: s.features, :] for w in (w0, w1, w2, w3)], axis=0)
    hot_hi = jnp.concatenate([chosen_columns(s, keep_ref, step * per + j, s.hi_patches, True) for j in range(per)], axis=0)
    hot_lo = jnp.concatenate([chosen_columns(s, keep_ref, step * per + j, s.lo_patches, False) for j in range(per)], axis=0)
    start = tn(picked, embed) + (nn(hot_hi, pos_hi_ref[...]) + nn(hot_lo, pos_lo_ref[...]))
    x0_ref[...] = start.astype(BF16)
    normed, _ = normalize(start)
    normed = (normed * gain1_ref[0:1, :]).astype(BF16)
    a_ref[...] = normed
    for c in range(3):
        part = slice(c * width, (c + 1) * width)
        qkv_ref[:, part] = nn(normed, wqkv_ref[:, part]).astype(BF16)
    masks = pair_masks()
    scale = 1.0 / math.sqrt(width // heads)
    for j in range(per):
        rows = slice(j * LANES, (j + 1) * LANES)
        ok = allowed(s, seen_ref, step * per + j)
        for h in range(width // LANES):
            at = h * LANES
            q = qkv_ref[rows, at : at + LANES]
            k = qkv_ref[rows, width + at : width + at + LANES]
            v = qkv_ref[rows, 2 * width + at : 2 * width + at + LANES]
            scores = nt(doubled(q, masks), k) * scale
            scores = jnp.where(ok, scores, MASKED)
            raised = jnp.exp(scores - jnp.max(scores, axis=-1, keepdims=True))
            probs = raised / jnp.sum(raised, axis=-1, keepdims=True)
            rounded = probs.astype(BF16)
            probs_ref[j, h] = rounded
            wide = jnp.concatenate([rounded[:LANES], rounded[LANES:]], axis=1)
            mixed_ref[rows, at : at + LANES] = nn(wide, doubled(v, masks)).astype(BF16)
    middle = start + nn(mixed_ref[...], wout_ref[...])
    x1_ref[...] = middle


def forward(s, heads, keep, seen, picked, weights, pos_lo, pos_hi, gain1, wqkv, wout):
    width, rows = s.width, s.rows
    per, pairs = ROWS // LANES, width // LANES
    return pl.pallas_call(
        functools.partial(forward_kernel, s, heads),
        grid=(rows // ROWS,),
        in_specs=[whole(keep), whole(seen)]
        + [along(s.features, ROWS)] * 4
        + [whole(w) for w in weights]
        + [whole(a) for a in (pos_lo, pos_hi, gain1, wqkv, wout)],
        out_specs=[
            across(ROWS, width),
            across(ROWS, width),
            across(ROWS, 3 * width),
            pl.BlockSpec((per, pairs, 2 * LANES, LANES), lambda i: (i, 0, 0, 0)),
            across(ROWS, width),
            across(ROWS, width),
        ],
        out_shape=[
            shape((rows, width), BF16),
            shape((rows, width), BF16),
            shape((rows, 3 * width), BF16),
            shape((s.tiles, pairs, 2 * LANES, LANES), BF16),
            shape((rows, width), BF16),
            shape((rows, width), F32),
        ],
        compiler_params=params(60),
        cost_estimate=cost(1.5e10, 3e7),
    )(keep, seen, *picked, *weights, pos_lo, pos_hi, gain1, wqkv, wout)


def part_rows(width, offset):
    return pl.BlockSpec((ROWS, width), lambda i, *_: (i + offset, 0))


def relative(ids_ref, x, y, z, c):
    return ids_ref[0] ^ (2 * z + y), ids_ref[1] ^ (2 * x + c)


def places(ids_ref, far):
    out = []
    for c in range(2):
        for x in range(2):
            for y in range(2):
                for z in range(far):
                    d, v = relative(ids_ref, x, y, z, c)
                    out.append(d * 4 + v)
    return out


def turn_relative(ids_ref, far, block, source_ref, turned_ref, acc_ref):
    order = places(ids_ref, far)
    rows = source_ref.shape[0]
    for begin in range(0, rows, rows // 2):
        span = slice(begin, begin + rows // 2)
        acc_ref[:, : rows // 2] = source_ref[span, :].astype(F32).T
        for p in range(0, len(order), 2):
            pair = [
                acc_ref[pl.ds(pl.multiple_of(at * block, 8), block), : rows // 2]
                for at in order[p : p + 2]
            ]
            turned_ref[p * block : (p + 2) * block, span] = jnp.concatenate(pair, axis=0).astype(BF16)


def spread(ids_ref, far, acc_ref, outs, block, extra):
    for x in range(2):
        for y in range(2):
            for z in range(far):
                for c, out_ref in enumerate(outs):
                    d, v = relative(ids_ref, x, y, z, c)
                    start = pl.multiple_of((d * 4 + v) * block, 8)
                    out_ref[x, y, z, :block, :] = acc_ref[pl.ds(start, block), :].astype(BF16)
                    out_ref[x, y, z, block:, :] = extra


def spread_features(s, ids_ref, acc_ref, outs):
    half = s.features // 2
    for k in range(4):
        for y in range(2):
            start = k * s.features + ((ids_ref[0] & 1) ^ y) * half
            rows = acc_ref[pl.ds(pl.multiple_of(start, 8), half), :]
            outs[k % 2][k // 2, y] = rows.astype(BF16)


def late_copy(source_ref, held_ref, sem_ref, needed=0):
    @pl.when(pl.program_id(0) == 0)
    def _():
        pltpu.make_async_copy(source_ref, held_ref, sem_ref).start()

    def ready():
        @pl.when(pl.program_id(0) == needed)
        def _():
            pltpu.make_async_copy(source_ref, held_ref, sem_ref).wait()

    return ready


LATE = pl.BlockSpec(memory_space=pl.ANY)


def late_scratch(array):
    return [pltpu.VMEM(array.shape, array.dtype), pltpu.SemaphoreType.DMA(())]


def hidden_kernel(s, far, chunks, ids_ref, seen_ref, c0, c1, c2, c3, h0, h1, h2, h3, x1_ref, mixed_hbm, w1_ref, b1_ref, w2_ref, b2_ref, gain2_ref, wout_hbm, two0_ref, two1_ref, one0_ref, one1_ref, p0, p1, p2, p3, out0_ref, out1_ref, n0_ref, n1_ref, go_ref, ga_ref, b_ref, turned_ref, gm_ref, gpred_ref, forth_ref, back_ref, z_ref, gu_ref, acc_ref, side_ref, mixed_ref, mixed_sem, wout_ref, wout_sem):
    step = pl.program_id(0)
    mixed_ready = late_copy(mixed_hbm, mixed_ref, mixed_sem, chunks)
    wout_ready = late_copy(wout_hbm, wout_ref, wout_sem, chunks)
    width = s.width
    block = width // (8 * far)
    subs = [slice(begin, begin + ROWS) for begin in range(0, s.rows, ROWS)]
    seen = jnp.concatenate([seen_ref[t : t + 1, :] for t in range(s.tiles)], axis=1)

    @pl.when(step == 0)
    def _():
        gpred_ref[...] = jnp.concatenate([c[...] for c in (c0, c1, c2, c3)], axis=0) * seen.astype(BF16)
        head = jnp.concatenate([h[s.features :, :] for h in (h0, h1, h2, h3)], axis=0)
        total = None
        for rows in subs:
            values = x1_ref[rows, :]
            normed, _ = normalize(values)
            b_ref[rows, :] = (normed * gain2_ref[1:2, :]).astype(BF16)
            forth_ref[rows, :] = values + b2_ref[2:3, :]
            back_ref[rows, :] = jnp.zeros((ROWS, width), F32)
            upward = tn(gpred_ref[:, rows], head).astype(BF16)
            gm_ref[rows, :] = upward
            part = jnp.sum(upward.astype(F32), axis=0, keepdims=True)
            total = part if total is None else total + part
        side_ref[1:2, :] = total
        turn_relative(ids_ref, far, block, b_ref, turned_ref, acc_ref)

    @pl.when(step < chunks)
    def _():
        w1, w2, bias = w1_ref[...], w2_ref[...], b1_ref[...]
        total = None
        for rows in subs:
            u = nn(b_ref[rows, :], w1)
            upward = nt(gm_ref[rows, :], w2)
            z, slope = gelu_parts(u + bias)
            z = z.astype(BF16)
            gu = (upward * slope).astype(BF16)
            z_ref[rows, :] = z
            gu_ref[rows, :] = gu
            part = jnp.sum(gu.astype(F32), axis=0, keepdims=True)
            total = part if total is None else total + part
        side_ref[pl.ds(2 + ((ids_ref[0] >> 1) ^ step), 1), :] = total
        forth_ref[...] += nn(z_ref[...], w2)
        back_ref[...] += nt(gu_ref[...], w1)
        ones = nn(turned_ref[...], gu_ref[...])
        one0_ref[0] = ones[: width // 2].astype(BF16)
        one1_ref[0] = ones[width // 2 :].astype(BF16)
        acc_ref[...] = tn(z_ref[...], gm_ref[...])
        tall = width // 8
        for x in range(2):
            for y in range(2):
                for c, out_ref in enumerate((two0_ref, two1_ref)):
                    d, v = relative(ids_ref, x, y, 0, c)
                    start = pl.multiple_of(((d & 1) * 4 + v) * tall, 8)
                    out_ref[x, y, 0] = acc_ref[pl.ds(start, tall), :].astype(BF16)

    mixed_ready()
    wout_ready()

    @pl.when(step == chunks)
    def _():
        total = None
        for rows in subs:
            z_ref[rows, :] = forth_ref[rows, :].astype(BF16)
            upward = back_ref[rows, :]
            normed, inverse = normalize(x1_ref[rows, :])
            part = jnp.sum(upward * normed, axis=0, keepdims=True)
            total = part if total is None else total + part
            grad = gm_ref[rows, :].astype(F32) + normalize_back(upward, normed, inverse, gain2_ref[1:2, :])
            grad = grad.astype(BF16)
            ga_ref[rows, :] = grad
            go_ref[rows, :] = nt(grad, wout_ref[...]).astype(BF16)
        side_ref[0:1, :] = total
        final = z_ref[...]
        for head, out in zip((h0, h1, h2, h3), (p0, p1, p2, p3)):
            out[...] = (nt(head[s.features :, :], final) * seen).astype(BF16)
        acc_ref[: s.groups * s.features, :] = nn(gpred_ref[...], final)
        spread_features(s, ids_ref, acc_ref, (n0_ref, n1_ref))
        acc_ref[...] = tn(mixed_ref[...], ga_ref[...])
        spread(ids_ref, far, acc_ref, (out0_ref, out1_ref), block, side_ref[...].astype(BF16))


def hidden(s, ids, far, seen, cots, weights, x1, mixed, w1, b1, w2, b2, gain2, wout):
    rows, width = s.rows, s.width
    chunks = w1.shape[1] // width
    block = width // (8 * far)
    high = s.groups * s.features
    sides = 8 * -(-(2 + chunks) // 8)
    last = chunks - 1

    def chunk(i, ids):
        return (ids[0] >> 1) ^ jnp.minimum(i, last)

    first = [seen, *cots, *weights, x1]
    rest = [b2, gain2]
    outs = (
        [((2, 2, far, width // 8, width), BF16)] * 2
        + [((chunks, width // 2, width), BF16)] * 2
        + [((s.features, rows), BF16)] * 4
        + [((2, 2, far, block + sides, width), BF16)] * 2
        + [((2, 2, s.features // 2, width), BF16)] * 2
        + [((rows, width), BF16)] * 2
    )
    specs = [
        pl.BlockSpec((2, 2, 1, width // 8, width), lambda i, ids: (0, 0, jnp.minimum(i, last), 0, 0))
    ] * 2
    specs += [pl.BlockSpec((1, width // 2, width), lambda i, ids: (chunk(i, ids), 0, 0))] * 2
    specs += [fixed(*dims) for dims, _ in outs[4:]]
    return pl.pallas_call(
        functools.partial(hidden_kernel, s, far, chunks),
        grid_spec=pltpu.PrefetchScalarGridSpec(
            num_scalar_prefetch=1,
            grid=(chunks + 1,),
            in_specs=[whole(a) for a in first]
            + [
                LATE,
                pl.BlockSpec((width, width), lambda i, ids: (0, chunk(i, ids))),
                pl.BlockSpec((1, width), lambda i, ids: (0, chunk(i, ids))),
                pl.BlockSpec((width, width), lambda i, ids: (chunk(i, ids), 0)),
            ]
            + [whole(a) for a in rest]
            + [LATE],
            out_specs=specs,
            scratch_shapes=[
                pltpu.VMEM((rows, width), BF16),
                pltpu.VMEM((width, rows), BF16),
                pltpu.VMEM((rows, width), BF16),
                pltpu.VMEM((high, rows), BF16),
                pltpu.VMEM((rows, width), F32),
                pltpu.VMEM((rows, width), F32),
                pltpu.VMEM((rows, width), BF16),
                pltpu.VMEM((rows, width), BF16),
                pltpu.VMEM((width, width), F32),
                pltpu.VMEM((sides, width), F32),
                *late_scratch(mixed),
                *late_scratch(wout),
            ],
        ),
        out_shape=[shape(*out) for out in outs],
        compiler_params=params(60),
        cost_estimate=cost(3.4e10, 4e7),
    )(ids, *first, mixed, w1, b1, w2, *rest, wout)


def attention_back(s, heads, qkv_ref, probs_ref, go_ref, gqkv_ref):
    per = ROWS // LANES
    width = s.width
    masks = pair_masks()
    scale = 1.0 / math.sqrt(width // heads)
    for j in range(per):
        rows = slice(j * LANES, (j + 1) * LANES)
        for h in range(width // LANES):
            at = h * LANES
            q = doubled(qkv_ref[rows, at : at + LANES], masks)
            k = doubled(qkv_ref[rows, width + at : width + at + LANES], masks)
            v = qkv_ref[rows, 2 * width + at : 2 * width + at + LANES]
            out = doubled(go_ref[rows, at : at + LANES], masks)
            rounded = probs_ref[j, h]
            probs = rounded.astype(F32)
            upward = nt(out, v)
            centred = upward - jnp.sum(probs * upward, axis=-1, keepdims=True)
            grads = (probs * centred).astype(BF16)
            wide = jnp.concatenate([grads[:LANES], grads[LANES:]], axis=1)
            gqkv_ref[rows, at : at + LANES] = (nn(wide, k) * scale).astype(BF16)
            gqkv_ref[rows, width + at : width + at + LANES] = (tn(grads, q) * scale).astype(BF16)
            gqkv_ref[rows, 2 * width + at : 2 * width + at + LANES] = tn(rounded, out).astype(BF16)


def first_norm_back(gqkv, x0_ref, ga_ref, wqkv_ref, gain1_ref):
    upward = nt(gqkv, wqkv_ref[...])
    normed, inverse = normalize(x0_ref[...].astype(F32))
    grad = ga_ref[...].astype(F32) + normalize_back(upward, normed, inverse, gain1_ref[0:1, :])
    return grad.astype(BF16), jnp.sum(upward * normed, axis=0, keepdims=True)


def backward_kernel(s, heads, qkv_ref, probs_ref, go_ref, x0_ref, ga_ref, wqkv_hbm, gain1_ref, gqkv_ref, g0_ref, gln1_ref, wqkv_ref, sem_ref):
    ready = late_copy(wqkv_hbm, wqkv_ref, sem_ref)
    attention_back(s, heads, qkv_ref, probs_ref, go_ref, gqkv_ref)
    ready()
    g0_ref[...], gain_part = first_norm_back(gqkv_ref[...], x0_ref, ga_ref, wqkv_ref, gain1_ref)
    accumulate(gln1_ref, pl.program_id(0) == 0, gain_part)


def row_inputs(s, offset):
    width = s.width
    return [
        part_rows(3 * width, offset),
        pl.BlockSpec((ROWS // LANES, width // LANES, 2 * LANES, LANES), lambda i, *_: (i + offset, 0, 0, 0)),
        part_rows(width, offset),
        part_rows(width, offset),
        part_rows(width, offset),
    ]


def backward(s, heads, offset, steps, qkv, probs, go, x0, ga, wqkv, gain1):
    width = s.width
    size = steps * ROWS
    return pl.pallas_call(
        functools.partial(backward_kernel, s, heads),
        grid=(steps,),
        in_specs=row_inputs(s, offset) + [LATE, whole(gain1)],
        scratch_shapes=late_scratch(wqkv),
        out_specs=[across(ROWS, 3 * width), across(ROWS, width), fixed(1, width)],
        out_shape=[shape((size, 3 * width), BF16), shape((size, width), BF16), shape((1, width), F32)],
        compiler_params=params(60),
        cost_estimate=cost(8e9 * steps, 6e6 * steps),
    )(qkv, probs, go, x0, ga, wqkv, gain1)


def position_grads(s, keep_ref, g0, picked):
    hot_hi, hot_lo = [], []
    for t in range(s.tiles):
        row = keep_ref[0, t : t + 1, :]
        patches = s.hi_patches if t < s.hi_each else s.lo_patches
        hot = jnp.where(iota((patches, LANES), 0) == row, 1.0, 0.0).astype(BF16)
        (hot_hi if t < s.hi_each else hot_lo).append(hot)
    hi_rows = s.hi_each * LANES
    hi = nn(jnp.concatenate(hot_hi, axis=1), g0[:hi_rows])
    lo = nn(jnp.concatenate(hot_lo, axis=1), g0[hi_rows:])
    return lo, hi, nn(jnp.concatenate(picked, axis=0), g0)


def finish_kernel(s, far, chunks, ids_ref, keep_ref, a_ref, r0_ref, r1_ref, ga_hbm, gb_hbm, la_ref, lb_ref, p0, p1, p2, p3, w0, w1, w2, w3, q0, q1, q2, q3, o0_ref, o1_ref, e0_ref, e1_ref, i0, i1, i2, i3, turned_ref, acc_ref, lo_ref, hi_ref, ga_ref, ga_sem, gb_ref, gb_sem):
    ga_ready = late_copy(ga_hbm, ga_ref, ga_sem, chunks)
    gb_ready = late_copy(gb_hbm, gb_ref, gb_sem, chunks)
    step = pl.program_id(0)
    width = s.width
    block = width // (8 * far)
    half = width // 2
    done = r0_ref.shape[0]

    @pl.when(step == 0)
    def _():
        turn_relative(ids_ref, far, block, a_ref, turned_ref, acc_ref)

    @pl.when(step < chunks)
    def _():
        value = nn(turned_ref[:, :done], r0_ref[...]) + nn(turned_ref[:, done:], r1_ref[...])
        o0_ref[0] = value[:half].astype(BF16)
        o1_ref[0] = value[half:].astype(BF16)

    ga_ready()
    gb_ready()

    @pl.when(step == chunks)
    def _():
        g0 = jnp.concatenate([ga_ref[...], gb_ref[...]], axis=0)
        lo, hi, embed = position_grads(s, keep_ref, g0, [p[...] for p in (p0, p1, p2, p3)])
        lo_ref[...] = lo
        hi_ref[...] = hi
        acc_ref[: s.groups * s.features, :] = embed
        spread_features(s, ids_ref, acc_ref, (e0_ref, e1_ref))
        for weight, pred, out in zip((w0, w1, w2, w3), (q0, q1, q2, q3), (i0, i1, i2, i3)):
            out[: s.features, :] = nt(weight[: s.features, :], g0).astype(BF16)
            out[s.features :, :] = pred[...]
        hi_block = s.hi_patches // (8 * far)
        lo_block = s.lo_patches // (8 * far)
        gain = la_ref[...] + lb_ref[...]
        pad = jnp.zeros((block - hi_block - lo_block - 1, width), F32)
        order = places(ids_ref, far)
        for p in range(0, len(order), 2):
            pair = []
            for at in order[p : p + 2]:
                both = lo_ref[pl.ds(pl.multiple_of((at >> 1) * 8, 8), 8), :]
                pair += [
                    hi_ref[pl.ds(pl.multiple_of(at * hi_block, 8), hi_block), :],
                    jnp.where((at & 1) == 1, both[lo_block:], both[:lo_block]),
                    gain,
                    pad,
                ]
            row = (p % (len(order) // 2)) * block
            (o0_ref, o1_ref)[p // (len(order) // 2)][0, row : row + 2 * block, :] = jnp.concatenate(pair, axis=0).astype(BF16)


def finish(s, ids, far, keep, a, gqkvs, g0s, gains, picked, weights, preds):
    width, rows = s.width, s.rows
    chunks = gqkvs[0].shape[1] // width
    rest = [*gains, *picked, *weights, *preds]
    out = pl.BlockSpec((1, width // 2, width), lambda i, ids: (i, 0, 0))
    return pl.pallas_call(
        functools.partial(finish_kernel, s, far, chunks),
        grid_spec=pltpu.PrefetchScalarGridSpec(
            num_scalar_prefetch=1,
            grid=(chunks + 1,),
            in_specs=[whole(keep), whole(a)]
            + [
                pl.BlockSpec((g.shape[0], width), lambda i, ids: (0, jnp.minimum(i, chunks - 1)))
                for g in gqkvs
            ]
            + [LATE, LATE]
            + [whole(r) for r in rest],
            out_specs=[out, out]
            + [fixed(2, 2, s.features // 2, width)] * 2
            + [fixed(2 * s.features, rows)] * 4,
            scratch_shapes=[
                pltpu.VMEM((width, rows), BF16),
                pltpu.VMEM((width, width), F32),
                pltpu.VMEM((s.lo_patches, width), F32),
                pltpu.VMEM((s.hi_patches, width), F32),
                *late_scratch(g0s[0]),
                *late_scratch(g0s[1]),
            ],
        ),
        out_shape=[shape((chunks + 1, width // 2, width), BF16)] * 2
        + [shape((2, 2, s.features // 2, width), BF16)] * 2
        + [shape((2 * s.features, rows), BF16)] * 4,
        compiler_params=params(60),
        cost_estimate=cost(7e9, 1.2e7),
    )(ids, keep, a, *gqkvs, *g0s, *rest)


def combine_kernel(held_ref, got_ref, keep_ref, send_ref):
    send_ref[...] = (held_ref[:, 1].astype(F32) + got_ref[:, 1].astype(F32)).astype(BF16)
    keep_ref[...] = (held_ref[:, 0].astype(F32) + got_ref[:, 0].astype(F32)).astype(BF16)


def combine(held, got, axis):
    dims = held.shape
    width = dims[-1]
    outer = math.prod(dims[:axis])
    inner = math.prod(dims[axis + 1 : -1])
    grid = (outer // 4, 1) if outer > 4 else (1, 2)
    broad, tall = outer // grid[0], inner // grid[1]
    half = shape((outer, inner, width), BF16)
    spec = pl.BlockSpec((broad, 2, tall, width), lambda i, j: (i, 0, j, 0))
    out = pl.BlockSpec((broad, tall, width), lambda i, j: (i, j, 0))
    keep, send = pl.pallas_call(
        combine_kernel,
        grid=grid,
        in_specs=[spec, spec],
        out_specs=[out, out],
        out_shape=[half, half],
        compiler_params=params(60),
        cost_estimate=cost(1e6, 6 * outer * inner * width),
    )(*(value.reshape(outer, 2, inner, width) for value in (held, got)))
    left = dims[:axis] + dims[axis + 1 :]
    return keep.reshape(left), send.reshape(left)


def place_kernel(s, member_ref, keep_ref, r0, r1, r2, r3, lo_ref, hi_ref, pred_lo_ref, pred_hi_ref):
    lane_sample = iota((1, LANES), 1) // s.lo_length
    eye = jnp.where(iota((s.features, s.features), 0) == iota((s.features, s.features), 1), 1.0, 0.0).astype(BF16)
    for k, got_ref in enumerate((r0, r1, r2, r3)):
        other = member_ref[0] ^ k
        for i in range(s.hi_each):
            chosen = iota((s.hi_patches, LANES), 0) == keep_ref[k, i : i + 1, :]
            hot = jnp.where(chosen, 1.0, 0.0).astype(BF16)
            lanes = slice(i * LANES, (i + 1) * LANES)
            hi_ref[other * s.hi_each + i] = nt(got_ref[: s.features, lanes], hot).astype(BF16)
            pred_hi_ref[other * s.hi_each + i] = got_ref[s.features :, lanes]
        for tile, first, count in sample_tiles(s):
            lanes = slice(tile * LANES, (tile + 1) * LANES)
            got = got_ref[: s.features, lanes]
            for j in range(count):
                row = jnp.where(lane_sample == j, keep_ref[k, tile : tile + 1, :], -1)
                hot = jnp.where(iota((s.lo_patches, LANES), 0) == row, 1.0, 0.0).astype(BF16)
                lo_ref[other * s.lo_each + first + j] = nt(got, hot).astype(BF16)
            if count:
                size = count * s.lo_length
                turned = tn(got_ref[s.features :, lanes], eye).astype(BF16)
                start = pl.multiple_of((other * s.lo_each + first) * s.lo_length, s.lo_length)
                pred_lo_ref[pl.ds(start, size), :] = turned[:size]


def place(s, member, keep, blocks):
    lo = s.groups * s.lo_each
    hi = s.groups * s.hi_each
    outs = [
        (lo, s.features, s.lo_patches),
        (hi, s.features, s.hi_patches),
        (lo * s.lo_length, s.features),
        (hi, s.features, s.hi_length),
    ]
    return pl.pallas_call(
        functools.partial(place_kernel, s),
        grid_spec=pltpu.PrefetchScalarGridSpec(
            num_scalar_prefetch=1,
            grid=(1,),
            in_specs=[whole(keep)] + [whole(b) for b in blocks],
            out_specs=[fixed(*dims) for dims in outs],
        ),
        out_shape=[shape(dims, BF16) for dims in outs],
        compiler_params=params(60),
        cost_estimate=cost(2e9, 8e6),
    )(member, keep, *blocks)


def swap(value, data_bit, var_bit):
    dp, var = lax.axis_size("dp"), lax.axis_size("var")
    pairs = [
        (d * var + v, (d ^ data_bit) * var + (v ^ var_bit)) for d in range(dp) for v in range(var)
    ]
    return lax.ppermute(value, AXES, pairs)


def add_rounded(left, right):
    return (left.astype(F32) + right.astype(F32)).astype(BF16)


def added(*values):
    values = [value.astype(F32) for value in values]
    while len(values) > 1:
        values = [values[i] + values[i + 1] for i in range(0, len(values), 2)]
    return values[0]


def tie(value, *tokens):
    return lax.optimization_barrier((value, tokens))[0]


PARTNERS = {"core": (0, 1), "x": (0, 2), "y": (1, 0), "z0": (2, 0), "z1": (4, 0)}


class Chain:
    def __init__(self, near, sent):
        self.near, self.sent = near, sent
        self.repeats = near.ndim == 4
        self.names = ["x", "y"] if self.repeats else ["chunk", "x", "y", "z1", "z0"][7 - near.ndim :]
        self.held = self.got = None

    def outgoing(self, name):
        if name == "core":
            self.held = self.near
            return self.sent
        if name not in self.names:
            self.held = add_rounded(self.held, self.got)
            return self.held
        axis = self.names.index(name)
        self.names.remove(name)
        if math.prod(self.held.shape) >= 1 << 20:
            self.held, sent = combine(self.held, self.got, axis)
            return sent
        kept, sent = (
            [lax.index_in_dim(value, side, axis, keepdims=False) for value in (self.held, self.got)]
            for side in range(2)
        )
        self.held = add_rounded(*kept)
        return add_rounded(*sent)

    def hold(self, *tokens):
        self.held, self.got = tie((self.held, self.got), *tokens)

    def final(self):
        return added(self.held, self.got)


def send_rows(values, bits):
    width = values[0].shape[-1]
    if len(values) == 1:
        return [swap(values[0].reshape(-1, width), *bits).reshape(values[0].shape)]
    flat = [value.reshape(-1, width) for value in values]
    got = swap(jnp.concatenate(flat, axis=0), *bits)
    out, start = [], 0
    for value, rows in zip(values, flat):
        out.append(got[start : start + rows.shape[0]].reshape(value.shape))
        start += rows.shape[0]
    return out


def trade(name, *chains):
    got = send_rows([chain.outgoing(name) for chain in chains], PARTNERS[name])
    for chain, value in zip(chains, got):
        chain.got = value
    return got[0]


def both_halves(value):
    value = value.astype(BF16)
    other = swap(value, 1, 0)
    second = lax.axis_index("dp") % 2 == 1
    return jnp.concatenate(
        [jnp.where(second, other, value), jnp.where(second, value, other)], axis=0
    ).astype(F32)


def natural(near, sent):
    rows, width = near.shape[-2:]
    both = jnp.stack([near, sent]).reshape((2, -1, 2, 2, 4, rows, width))
    return both.transpose(4, 3, 2, 0, 1, 5, 6).reshape(32, -1, width)


def scattered(full):
    return lax.psum_scatter(full, AXES, scatter_dimension=0, tiled=True).astype(F32)


def joined(blocks, chunks):
    count, rows, width = blocks.shape
    split = blocks.reshape(count, chunks, rows // chunks, width).transpose(0, 2, 1, 3)
    return split.reshape(count * (rows // chunks), chunks * width)


def plain_sum(near, sent):
    if near.ndim >= 6:
        return natural(near, sent)
    value = jnp.stack([near, sent], axis=1)
    value = value.reshape((4, -1, near.shape[-1]))
    bit = 1
    while value.shape[0] > 1:
        value = value.reshape((value.shape[0] // 2, 2) + value.shape[1:])
        value = add_rounded(value[:, 0], swap(value[:, 1], 0, bit))
        bit *= 2
    return lax.psum(value[0], "dp").astype(F32)


def exchange_relative(blocks):
    return [blocks[0]] + [swap(blocks[k], 0, k) for k in range(1, len(blocks))]


def body(
    img_lo,
    img_hi,
    keep_lo,
    keep_hi,
    mask_lo,
    mask_hi,
    w_embed,
    pos_lo,
    pos_hi,
    ln1_gain,
    w_qkv,
    w_out,
    ln2_gain,
    w_fc1,
    b_fc1,
    w_fc2,
    b_fc2,
    w_head,
    cot_lo,
    cot_hi,
):
    groups = lax.axis_size("var")
    devices = lax.axis_size("dp") * groups
    member = lax.axis_index("var").astype(jnp.int32).reshape(1)
    s = Sizes(keep_lo.shape, keep_hi.shape, w_embed.shape, img_lo.shape, img_hi.shape, groups)
    features, width = s.features, s.width
    gain1 = gain2 = vectors = jnp.stack([ln1_gain, ln2_gain, b_fc2])
    img_lo_t, img_hi_t = img_lo.transpose(0, 2, 1), img_hi.transpose(0, 2, 1)

    own = jnp.concatenate([w_embed, w_head.T], axis=0)
    crossed = swap(own, 0, 2)
    beside = swap(own, 0, 1)
    sent = pick(s, (2, 3, 1, 0), member, keep_lo, keep_hi, img_lo_t, img_hi_t)
    crossed = tie(crossed, sent[0])
    weights = [own, beside, crossed, swap(crossed, 0, 1)]
    picked = [sent[3], swap(sent[2], 0, 1), swap(sent[0], 0, 2), swap(sent[1], 0, 3)]
    keep, seen, *cots = stage(
        s,
        tie(member, sent[0]),
        keep_lo,
        keep_hi,
        mask_lo,
        mask_hi,
        cot_lo.reshape(-1, features),
        cot_hi.transpose(0, 2, 1),
    )
    cots = exchange_relative(cots)
    own_keep = keep
    x0, a, qkv, probs, mixed, x1 = forward(
        s, HEADS, own_keep, seen, picked, weights, pos_lo, pos_hi, gain1, w_qkv, w_out
    )
    far = 4
    cube = lax.axis_size("dp") == 2 * far
    place_of = lax.axis_index("dp") * groups + lax.axis_index("var")
    ids = jnp.stack([lax.axis_index("dp"), lax.axis_index("var")]).astype(jnp.int32)
    if not cube:
        ids = jnp.zeros_like(ids)

    def chain_of(near, sent):
        if near.ndim == 5:
            near, sent = (
                value.reshape((2, 2, 2, 2) + value.shape[3:]) for value in (near, sent)
            )
        elif near.ndim == 3:
            near, sent = (
                value.reshape((-1, 2, 2, 2, 2, width // 32, width)) for value in (near, sent)
            )
        return Chain(near, sent)

    def step(name, *chains):
        return trade(name, *chains) if cube else ()

    def halves_of(chain):
        out = []
        for side in range(2):
            piece = Chain(chain.near, chain.sent)
            count = chain.near.shape[0] // 2
            piece.held, piece.got = (
                lax.slice_in_dim(value, side * count, (side + 1) * count, axis=0)
                for value in (chain.held, chain.got)
            )
            out.append(piece)
        return out

    two0, two1, one0, one1, *rest = hidden(
        s,
        ids,
        far,
        tie(seen, x1),
        cots,
        weights,
        x1,
        mixed,
        w_fc1,
        b_fc1.reshape(1, -1),
        w_fc2,
        vectors,
        gain2,
        w_out,
    )
    preds, (out0, out1, head0, head1, go, ga) = rest[:groups], rest[groups:]
    two, one = chain_of(two0, two1), chain_of(one0, one1)
    out, head = chain_of(out0, out1), chain_of(head0, head1)
    tokens = [step("core", chain) for chain in (two, one, out, head)]

    def back(offset, steps, *ready):
        return backward(
            s, HEADS, offset, steps, qkv, probs, go, x0, ga, w_qkv, tie(gain1, *ready)
        )

    parts = [back(0, 1, go)]
    if cube:
        for chain in (two, one, out, head):
            chain.hold(parts[0][0])
    near_tokens = [step("x", two), step("y", one)]
    if cube:
        for chain in (out, head):
            chain.hold(two.held, one.held)
    near_tokens.append(step("z0", out, head))
    parts.append(back(1, s.rows // ROWS - 1, parts[0][0], two.held, one.held, *tokens))
    if cube:
        for chain in (two, one, out, head):
            chain.hold(parts[1][0])
    tokens = [step("y", two), step("x", one, out, head)]
    gqkvs, g0s, gains = zip(*parts)
    near, sent, near_embed, sent_embed, *blocks = finish(
        s,
        tie(ids, two.held, one.held, *near_tokens),
        far,
        own_keep,
        a,
        gqkvs,
        g0s,
        gains,
        picked,
        weights,
        preds,
    )
    sent, sent_embed = tie((sent, sent_embed), *tokens)
    first, embed = chain_of(near, sent), chain_of(near_embed, sent_embed)
    tokens += [step("core", first), step("core", embed)]
    if cube:
        old = (two, one, out, head)
        for chain in old:
            chain.hold(first.got)
        one_half, other_half = halves_of(first)
        tokens = [trade("x", one_half, embed), trade("y", other_half, out, head)]
        trade("z0", two, one)
        for chain in old:
            chain.hold(*tokens)
        tokens = [trade("y", one_half, embed), trade("x", other_half)]
        trade("z1", *old)
        blocks = [tie(block_of, *tokens) for block_of in blocks]
        trade("z0", one_half, other_half, embed)
        trade("z1", one_half, other_half, embed)
        head.hold(embed.held)
        grad_head = both_halves(head.final())
        last_member = tie(member, grad_head)
        for chain in (two, one, out):
            chain.hold(grad_head)
        grad_fc2, grad_fc1, rest, grad_embed = (
            chain.final() for chain in (two, one, out, embed)
        )
        grad_embed = both_halves(grad_embed)
        first = jnp.concatenate([one_half.final(), other_half.final()], axis=0).reshape(-1, width)
        grad_fc1 = grad_fc1.reshape(-1, width)
    else:
        grad_fc2, grad_fc1, rest, grad_head, grad_embed, first = (
            plain_sum(chain.near, chain.sent) for chain in (two, one, out, head, embed, first)
        )
        last_member = member
    grad_img_lo, grad_img_hi, pred_lo, pred_hi = place(s, last_member, keep, exchange_relative(blocks))
    grad_head = grad_head.T

    block = width // devices
    inner = w_fc1.shape[1] // width

    hi_block = s.hi_patches // devices
    lo_block = s.lo_patches // devices

    def own_part(row):
        return lax.dynamic_slice_in_dim(row, place_of * block, block)

    if cube:
        grad_fc1 = joined(grad_fc1[None], inner)
        grad_qkv = joined(first[None, : 3 * block], 3)
        grad_out, sides = rest[:block], rest[block:]
        extra = first[3 * block :]
        grad_pos_hi = extra[:hi_block]
        grad_pos_lo = extra[hi_block : hi_block + lo_block]
        first_side = extra[hi_block + lo_block]
    else:
        tall = width // 32
        hi_tall, lo_tall = s.hi_patches // 32, s.lo_patches // 32
        grad_fc2 = scattered(grad_fc2.reshape(-1, width))
        grad_fc1 = scattered(joined(grad_fc1, inner))
        grad_qkv = scattered(joined(first[:, : 3 * tall], 3))
        grad_out, sides = scattered(rest[:, :tall].reshape(-1, width)), rest[0, tall:]
        extra = first[:, 3 * tall :]
        grad_pos_hi = scattered(extra[:, :hi_tall].reshape(-1, width))
        grad_pos_lo = scattered(extra[:, hi_tall : hi_tall + lo_tall].reshape(-1, width))
        sides = lax.psum(jnp.concatenate([sides, extra[0, hi_tall + lo_tall :]]), AXES).astype(F32)
        first_side = sides[rest.shape[1] - tall]
    grad_ln1 = own_part(first_side)
    grad_ln2 = own_part(sides[0])
    grad_b2 = own_part(sides[1])
    grad_b1 = lax.dynamic_slice_in_dim(
        sides[2 : 2 + inner].reshape(-1), place_of * inner * block, inner * block
    )
    return (
        pred_lo.reshape(cot_lo.shape),
        pred_hi.transpose(0, 2, 1),
        grad_img_lo.transpose(0, 2, 1),
        grad_img_hi.transpose(0, 2, 1),
        grad_embed,
        grad_pos_lo,
        grad_pos_hi,
        grad_ln1,
        grad_qkv,
        grad_out,
        grad_ln2,
        grad_fc1,
        grad_b1,
        grad_fc2,
        grad_b2,
        grad_head,
    )


def solution(mesh):
    placed = (
        P("dp", None, "var"),
        P("dp", None, "var"),
        P("dp", None),
        P("dp", None),
        P("dp", None),
        P("dp", None),
        P("var", None),
        P(),
        P(),
        P(),
        P(),
        P(),
        P(),
        P(),
        P(),
        P(),
        P(),
        P(None, "var"),
        P("dp", None, "var"),
        P("dp", None, "var"),
    )
    return jax.shard_map(
        body,
        mesh=mesh,
        in_specs=placed,
        out_specs=(
            P("dp", None, "var"),
            P("dp", None, "var"),
            P("dp", None, "var"),
            P("dp", None, "var"),
            P("var", None),
            P(("dp", "var"), None),
            P(("dp", "var"), None),
            P(("dp", "var")),
            P(("dp", "var"), None),
            P(("dp", "var"), None),
            P(("dp", "var")),
            P(("dp", "var"), None),
            P(("dp", "var")),
            P(("dp", "var"), None),
            P(("dp", "var")),
            P(None, "var"),
        ),
        check_vma=False,
    )
```

```python
import functools
import math

import jax
import jax.numpy as jnp
from jax import lax
from jax.experimental import pallas as pl
from jax.experimental.pallas import tpu as pltpu
from jax.sharding import PartitionSpec as P

HEADS = 12
EPSILON = 1e-06
AXES = ("dp", "var")
BF16 = jnp.bfloat16
F32 = jnp.float32
LANES = 128
ROWS = 256
MASKED = -1000000000.0
SHARE = 0.5


def dot(left, right, dims):
    return lax.dot_general(left, right, (dims, ((), ())), preferred_element_type=F32)


def nn(left, right):
    return dot(left, right, ((1,), (0,)))


def nt(left, right):
    return dot(left, right, ((1,), (1,)))


def tn(left, right):
    return dot(left, right, ((0,), (0,)))


def shape(dims, dtype):
    return jax.ShapeDtypeStruct(dims, dtype)


def whole(array):
    zeros = (0,) * array.ndim
    return pl.BlockSpec(array.shape, lambda *_: zeros, pipeline_mode=pl.Buffered(1))


def across(rows, width):
    return pl.BlockSpec((rows, width), lambda i, *_: (i, 0))


def along(height, columns):
    return pl.BlockSpec((height, columns), lambda i, *_: (0, i))


def fixed(*dims):
    zeros = (0,) * len(dims)
    return pl.BlockSpec(dims, lambda *_: zeros)


def params(mebibytes):
    return pltpu.CompilerParams(vmem_limit_bytes=mebibytes << 20)


def cost(flops, nbytes):
    return pl.CostEstimate(flops=int(flops * SHARE), bytes_accessed=int(nbytes * SHARE), transcendentals=0)


def iota(dims, axis):
    return lax.broadcasted_iota(jnp.int32, dims, axis)


def accumulate(ref, first, value):
    @pl.when(first)
    def _():
        ref[...] = value

    @pl.when(jnp.logical_not(first))
    def _():
        ref[...] += value


def normalize(values):
    center = values - jnp.mean(values, axis=-1, keepdims=True)
    inverse = lax.rsqrt(jnp.mean(center * center, axis=-1, keepdims=True) + EPSILON)
    return center * inverse, inverse


def normalize_back(upstream, normed, inverse, gains):
    scaled = upstream * gains
    mean_plain = jnp.mean(scaled, axis=-1, keepdims=True)
    mean_mixed = jnp.mean(scaled * normed, axis=-1, keepdims=True)
    return inverse * (scaled - mean_plain - normed * mean_mixed)


def gelu_parts(u):
    ratio = 1.0 / (1.0 + (0.3275911 * math.sqrt(0.5)) * jnp.abs(u))
    bell = jnp.exp(-0.5 * u * u)
    series = 0.5 * 1.061405429
    for factor in (-1.453152027, 1.421413741, -0.284496736, 0.254829592):
        series = series * ratio + 0.5 * factor
    tail = series * ratio * bell
    below = jnp.where(u < 0, tail, 1.0 - tail)
    return u * below, below + u * (bell * (1.0 / math.sqrt(2.0 * math.pi)))


class Sizes:
    def __init__(self, keep_lo, keep_hi, w_embed, img_lo, img_hi, groups):
        self.lo_each, self.hi_each = keep_lo[0] // groups, keep_hi[0] // groups
        self.lo_length, self.hi_length = keep_lo[1], keep_hi[1]
        self.features, self.width = w_embed
        self.lo_patches, self.hi_patches = img_lo[1], img_hi[1]
        self.groups = groups
        self.pack = LANES // self.lo_length
        self.lo_tiles = -(-self.lo_each // self.pack)
        self.hi_rows = self.hi_each * self.hi_length
        tiles = self.hi_each + self.lo_tiles
        self.tiles = tiles + tiles % 2
        self.rows = self.tiles * LANES


def sample_tiles(s):
    out = []
    for t in range(s.tiles - s.hi_each):
        first = t * s.pack
        out.append((s.hi_each + t, first, max(0, min(s.pack, s.lo_each - first))))
    return out


def slots(rows, fill, s):
    missing = s.pack - len(rows)
    if missing:
        rows = rows + [jnp.full((1, missing * s.lo_length), fill, rows[0].dtype if rows else jnp.int32)]
    return rows[0] if len(rows) == 1 else jnp.concatenate(rows, axis=1)


def pick_kernel(s, members, member_ref, keep_lo_ref, keep_hi_ref, img_lo_ref, img_hi_ref, *out_refs):
    for k, out_ref in zip(members, out_refs):
        other = member_ref[0] ^ k
        for i in range(s.hi_each):
            at = other * s.hi_each + i
            chosen = iota((s.hi_patches, LANES), 0) == keep_hi_ref[pl.ds(at, 1), :]
            got = nn(img_hi_ref[at], jnp.where(chosen, 1.0, 0.0).astype(BF16))
            out_ref[:, i * LANES : (i + 1) * LANES] = got.astype(BF16)
        for tile, first, count in sample_tiles(s):
            parts = []
            for j in range(count):
                at = other * s.lo_each + first + j
                chosen = iota((s.lo_patches, s.lo_length), 0) == keep_lo_ref[pl.ds(at, 1), :]
                parts.append(nn(img_lo_ref[at], jnp.where(chosen, 1.0, 0.0).astype(BF16)))
            if count < s.pack:
                parts.append(jnp.zeros((s.features, (s.pack - count) * s.lo_length), F32))
            joined = jnp.concatenate(parts, axis=1) if len(parts) > 1 else parts[0]
            out_ref[:, tile * LANES : (tile + 1) * LANES] = joined.astype(BF16)


def pick(s, members, member, keep_lo, keep_hi, img_lo, img_hi):
    args = (keep_lo, keep_hi, img_lo, img_hi)
    return pl.pallas_call(
        functools.partial(pick_kernel, s, members),
        grid_spec=pltpu.PrefetchScalarGridSpec(
            num_scalar_prefetch=1,
            grid=(1,),
            in_specs=[whole(a) for a in args],
            out_specs=[fixed(s.features, s.rows)] * len(members),
        ),
        out_shape=[shape((s.features, s.rows), BF16)] * len(members),
        compiler_params=params(60),
        cost_estimate=cost(2e9, 4e6),
    )(member, *args)


def stage_kernel(s, member_ref, keep_lo_ref, keep_hi_ref, mask_lo_ref, mask_hi_ref, cot_lo_ref, cot_hi_ref, keep_ref, seen_ref, *out_refs):
    eye = jnp.where(iota((s.features, s.features), 0) == iota((s.features, s.features), 1), 1.0, 0.0).astype(BF16)
    first_hi = (iota((1, s.hi_length), 1) == 0).astype(jnp.int32)
    first_lo = (iota((1, s.lo_length), 1) == 0).astype(jnp.int32)
    for k, out_ref in enumerate(out_refs):
        other = member_ref[0] ^ k
        for i in range(s.hi_each):
            at = other * s.hi_each + i
            keep_ref[k, i : i + 1, :] = keep_hi_ref[pl.ds(at, 1), :]
            out_ref[:, i * LANES : (i + 1) * LANES] = cot_hi_ref[at]
            if k == 0:
                seen_ref[i : i + 1, :] = jnp.maximum(mask_hi_ref[pl.ds(at, 1), :], first_hi).astype(F32)
        for tile, first, count in sample_tiles(s):
            begin = other * s.lo_each + first
            keep_ref[k, tile : tile + 1, :] = slots([keep_lo_ref[pl.ds(begin + j, 1), :] for j in range(count)], -1, s)
            if k == 0:
                seen = [jnp.maximum(mask_lo_ref[pl.ds(begin + j, 1), :], first_lo) for j in range(count)]
                seen_ref[tile : tile + 1, :] = slots(seen, 0, s).astype(F32)
            where = slice(tile * LANES, (tile + 1) * LANES)
            if count < s.pack:
                out_ref[:, where] = jnp.zeros((s.features, LANES), BF16)
            if count:
                size = count * s.lo_length
                start = pl.multiple_of(begin * s.lo_length, s.lo_length)
                out_ref[:, tile * LANES : tile * LANES + size] = nt(eye, cot_lo_ref[pl.ds(start, size), :]).astype(BF16)


def stage(s, member, keep_lo, keep_hi, mask_lo, mask_hi, cot_lo, cot_hi):
    args = (keep_lo, keep_hi, mask_lo, mask_hi, cot_lo, cot_hi)
    return pl.pallas_call(
        functools.partial(stage_kernel, s),
        grid_spec=pltpu.PrefetchScalarGridSpec(
            num_scalar_prefetch=1,
            grid=(1,),
            in_specs=[whole(a) for a in args],
            out_specs=[fixed(s.groups, s.tiles, LANES), fixed(s.tiles, LANES)]
            + [fixed(s.features, s.rows)] * s.groups,
        ),
        out_shape=[shape((s.groups, s.tiles, LANES), jnp.int32), shape((s.tiles, LANES), F32)]
        + [shape((s.features, s.rows), BF16)] * s.groups,
        compiler_params=params(60),
        cost_estimate=cost(1e8, 4e6),
    )(member, *args)


def chosen_columns(s, keep_ref, tile, patches, wanted_hi):
    row = keep_ref[0, pl.ds(tile, 1), :]
    is_hi = tile < s.hi_each
    row = jnp.where(is_hi if wanted_hi else jnp.logical_not(is_hi), row, -1)
    column = jnp.broadcast_to(row.astype(F32), (LANES, LANES)).T.astype(jnp.int32)
    parts = [jnp.where(iota((LANES, LANES), 1) + at == column, 1.0, 0.0) for at in range(0, patches, LANES)]
    return jnp.concatenate(parts, axis=1).astype(BF16)


def pair_masks():
    lane = iota((1, LANES), 1)
    low = jnp.where(lane < LANES // 2, 1.0, 0.0).astype(BF16)
    high = jnp.where(lane < LANES // 2, 0.0, 1.0).astype(BF16)
    return low, high


def doubled(block, masks):
    return jnp.concatenate([block * masks[0], block * masks[1]], axis=0)


def allowed(s, seen_ref, tile):
    bits = jnp.where(tile < s.hi_each, s.hi_length.bit_length() - 1, s.lo_length.bit_length() - 1)
    same = (iota((LANES, LANES), 0) >> bits) == (iota((LANES, LANES), 1) >> bits)
    open_to = jnp.logical_and(same, seen_ref[pl.ds(tile, 1), :] > 0)
    return jnp.concatenate([open_to, open_to], axis=0)


def forward_kernel(s, heads, keep_ref, seen_ref, p0, p1, p2, p3, w0, w1, w2, w3, pos_lo_ref, pos_hi_ref, gain1_ref, wqkv_ref, wout_ref, x0_ref, a_ref, qkv_ref, probs_ref, mixed_ref, x1_ref):
    step = pl.program_id(0)
    per = ROWS // LANES
    width = s.width
    picked = jnp.concatenate([p[...] for p in (p0, p1, p2, p3)], axis=0)
    embed = jnp.concatenate([w[: s.features, :] for w in (w0, w1, w2, w3)], axis=0)
    hot_hi = jnp.concatenate([chosen_columns(s, keep_ref, step * per + j, s.hi_patches, True) for j in range(per)], axis=0)
    hot_lo = jnp.concatenate([chosen_columns(s, keep_ref, step * per + j, s.lo_patches, False) for j in range(per)], axis=0)
    start = tn(picked, embed) + (nn(hot_hi, pos_hi_ref[...]) + nn(hot_lo, pos_lo_ref[...]))
    x0_ref[...] = start.astype(BF16)
    normed, _ = normalize(start)
    normed = (normed * gain1_ref[0:1, :]).astype(BF16)
    a_ref[...] = normed
    for c in range(3):
        part = slice(c * width, (c + 1) * width)
        qkv_ref[:, part] = nn(normed, wqkv_ref[:, part]).astype(BF16)
    masks = pair_masks()
    scale = 1.0 / math.sqrt(width // heads)
    for j in range(per):
        rows = slice(j * LANES, (j + 1) * LANES)
        ok = allowed(s, seen_ref, step * per + j)
        for h in range(width // LANES):
            at = h * LANES
            q = qkv_ref[rows, at : at + LANES]
            k = qkv_ref[rows, width + at : width + at + LANES]
            v = qkv_ref[rows, 2 * width + at : 2 * width + at + LANES]
            scores = nt(doubled(q, masks), k) * scale
            scores = jnp.where(ok, scores, MASKED)
            raised = jnp.exp(scores - jnp.max(scores, axis=-1, keepdims=True))
            probs = raised / jnp.sum(raised, axis=-1, keepdims=True)
            rounded = probs.astype(BF16)
            probs_ref[j, h] = rounded
            wide = jnp.concatenate([rounded[:LANES], rounded[LANES:]], axis=1)
            mixed_ref[rows, at : at + LANES] = nn(wide, doubled(v, masks)).astype(BF16)
    middle = start + nn(mixed_ref[...], wout_ref[...])
    x1_ref[...] = middle


def forward(s, heads, keep, seen, picked, weights, pos_lo, pos_hi, gain1, wqkv, wout):
    width, rows = s.width, s.rows
    per, pairs = ROWS // LANES, width // LANES
    return pl.pallas_call(
        functools.partial(forward_kernel, s, heads),
        grid=(rows // ROWS,),
        in_specs=[whole(keep), whole(seen)]
        + [along(s.features, ROWS)] * 4
        + [whole(w) for w in weights]
        + [whole(a) for a in (pos_lo, pos_hi, gain1, wqkv, wout)],
        out_specs=[
            across(ROWS, width),
            across(ROWS, width),
            across(ROWS, 3 * width),
            pl.BlockSpec((per, pairs, 2 * LANES, LANES), lambda i: (i, 0, 0, 0)),
            across(ROWS, width),
            across(ROWS, width),
        ],
        out_shape=[
            shape((rows, width), BF16),
            shape((rows, width), BF16),
            shape((rows, 3 * width), BF16),
            shape((s.tiles, pairs, 2 * LANES, LANES), BF16),
            shape((rows, width), BF16),
            shape((rows, width), F32),
        ],
        compiler_params=params(60),
        cost_estimate=cost(1.5e10, 3e7),
    )(keep, seen, *picked, *weights, pos_lo, pos_hi, gain1, wqkv, wout)


def part_rows(width, offset):
    return pl.BlockSpec((ROWS, width), lambda i, *_: (i + offset, 0))


def relative(ids_ref, x, y, z, c):
    return ids_ref[0] ^ (2 * z + y), ids_ref[1] ^ (2 * x + c)


def places(ids_ref, far):
    out = []
    for c in range(2):
        for x in range(2):
            for y in range(2):
                for z in range(far):
                    d, v = relative(ids_ref, x, y, z, c)
                    out.append(d * 4 + v)
    return out


def turn_relative(ids_ref, far, block, source_ref, turned_ref, acc_ref):
    order = places(ids_ref, far)
    rows = source_ref.shape[0]
    for begin in range(0, rows, rows // 2):
        span = slice(begin, begin + rows // 2)
        acc_ref[:, : rows // 2] = source_ref[span, :].astype(F32).T
        for p in range(0, len(order), 2):
            pair = [
                acc_ref[pl.ds(pl.multiple_of(at * block, 8), block), : rows // 2]
                for at in order[p : p + 2]
            ]
            turned_ref[p * block : (p + 2) * block, span] = jnp.concatenate(pair, axis=0).astype(BF16)


def spread(ids_ref, far, acc_ref, outs, block, extra):
    for x in range(2):
        for y in range(2):
            for z in range(far):
                for c, out_ref in enumerate(outs):
                    d, v = relative(ids_ref, x, y, z, c)
                    start = pl.multiple_of((d * 4 + v) * block, 8)
                    out_ref[x, y, z, :block, :] = acc_ref[pl.ds(start, block), :].astype(BF16)
                    out_ref[x, y, z, block:, :] = extra


def spread_features(s, ids_ref, acc_ref, outs):
    half = s.features // 2
    for k in range(4):
        for y in range(2):
            start = k * s.features + ((ids_ref[0] & 1) ^ y) * half
            rows = acc_ref[pl.ds(pl.multiple_of(start, 8), half), :]
            outs[k % 2][k // 2, y] = rows.astype(BF16)


def late_copy(source_ref, held_ref, sem_ref, needed=0):
    @pl.when(pl.program_id(0) == 0)
    def _():
        pltpu.make_async_copy(source_ref, held_ref, sem_ref).start()

    def ready():
        @pl.when(pl.program_id(0) == needed)
        def _():
            pltpu.make_async_copy(source_ref, held_ref, sem_ref).wait()

    return ready


LATE = pl.BlockSpec(memory_space=pl.ANY)


def late_scratch(array):
    return [pltpu.VMEM(array.shape, array.dtype), pltpu.SemaphoreType.DMA(())]


def hidden_kernel(s, far, chunks, ids_ref, seen_ref, c0, c1, c2, c3, h0, h1, h2, h3, x1_ref, mixed_hbm, w1_ref, b1_ref, w2_ref, b2_ref, gain2_ref, wout_hbm, two0_ref, two1_ref, one0_ref, one1_ref, p0, p1, p2, p3, out0_ref, out1_ref, n0_ref, n1_ref, go_ref, ga_ref, b_ref, turned_ref, gm_ref, gpred_ref, forth_ref, back_ref, z_ref, gu_ref, acc_ref, side_ref, mixed_ref, mixed_sem, wout_ref, wout_sem):
    step = pl.program_id(0)
    mixed_ready = late_copy(mixed_hbm, mixed_ref, mixed_sem, chunks)
    wout_ready = late_copy(wout_hbm, wout_ref, wout_sem, chunks)
    width = s.width
    block = width // (8 * far)
    zero = jnp.zeros((1, width), F32)

    def each_part(part):
        def one_part(i, total):
            return total + part(pl.ds(pl.multiple_of(i * ROWS, ROWS), ROWS))

        return lax.fori_loop(0, s.rows // ROWS, one_part, zero)

    seen = jnp.concatenate([seen_ref[t : t + 1, :] for t in range(s.tiles)], axis=1)

    @pl.when(step == 0)
    def _():
        gpred_ref[...] = jnp.concatenate([c[...] for c in (c0, c1, c2, c3)], axis=0) * seen.astype(BF16)
        head = jnp.concatenate([h[s.features :, :] for h in (h0, h1, h2, h3)], axis=0)

        def begin(rows):
            values = x1_ref[rows, :]
            normed, _ = normalize(values)
            b_ref[rows, :] = (normed * gain2_ref[1:2, :]).astype(BF16)
            forth_ref[rows, :] = values + b2_ref[2:3, :]
            back_ref[rows, :] = jnp.zeros((ROWS, width), F32)
            upward = tn(gpred_ref[:, rows], head).astype(BF16)
            gm_ref[rows, :] = upward
            return jnp.sum(upward.astype(F32), axis=0, keepdims=True)

        side_ref[1:2, :] = each_part(begin)
        turn_relative(ids_ref, far, block, b_ref, turned_ref, acc_ref)

    @pl.when(step < chunks)
    def _():
        w1, w2, bias = w1_ref[...], w2_ref[...], b1_ref[...]

        total = None
        subs = [slice(q, q + ROWS) for q in range(0, s.rows, ROWS)]
        for rows in subs:
            u = nn(b_ref[rows, :], w1)
            upward = nt(gm_ref[rows, :], w2)
            z, slope = gelu_parts(u + bias)
            z = z.astype(BF16)
            gu = (upward * slope).astype(BF16)
            z_ref[rows, :] = z
            gu_ref[rows, :] = gu
            part = jnp.sum(gu.astype(F32), axis=0, keepdims=True)
            total = part if total is None else total + part
        side_ref[pl.ds(2 + ((ids_ref[0] >> 1) ^ step), 1), :] = total
        forth_ref[...] += nn(z_ref[...], w2)
        back_ref[...] += nt(gu_ref[...], w1)
        ones = nn(turned_ref[...], gu_ref[...])
        one0_ref[0] = ones[: width // 2].astype(BF16)
        one1_ref[0] = ones[width // 2 :].astype(BF16)
        acc_ref[...] = tn(z_ref[...], gm_ref[...])
        tall = width // 8
        for x in range(2):
            for y in range(2):
                for c, out_ref in enumerate((two0_ref, two1_ref)):
                    d, v = relative(ids_ref, x, y, 0, c)
                    start = pl.multiple_of(((d & 1) * 4 + v) * tall, 8)
                    out_ref[x, y, 0] = acc_ref[pl.ds(start, tall), :].astype(BF16)

    mixed_ready()
    wout_ready()

    @pl.when(step == chunks)
    def _():

        def end(rows):
            z_ref[rows, :] = forth_ref[rows, :].astype(BF16)
            upward = back_ref[rows, :]
            normed, inverse = normalize(x1_ref[rows, :])
            grad = gm_ref[rows, :].astype(F32) + normalize_back(upward, normed, inverse, gain2_ref[1:2, :])
            grad = grad.astype(BF16)
            ga_ref[rows, :] = grad
            go_ref[rows, :] = nt(grad, wout_ref[...]).astype(BF16)
            return jnp.sum(upward * normed, axis=0, keepdims=True)

        side_ref[0:1, :] = each_part(end)
        final = z_ref[...]
        for head, out in zip((h0, h1, h2, h3), (p0, p1, p2, p3)):
            out[...] = (nt(head[s.features :, :], final) * seen).astype(BF16)
        acc_ref[: s.groups * s.features, :] = nn(gpred_ref[...], final)
        spread_features(s, ids_ref, acc_ref, (n0_ref, n1_ref))
        acc_ref[...] = tn(mixed_ref[...], ga_ref[...])
        spread(ids_ref, far, acc_ref, (out0_ref, out1_ref), block, side_ref[...].astype(BF16))


def hidden(s, ids, far, seen, cots, weights, x1, mixed, w1, b1, w2, b2, gain2, wout):
    rows, width = s.rows, s.width
    chunks = w1.shape[1] // width
    block = width // (8 * far)
    high = s.groups * s.features
    sides = 8 * -(-(2 + chunks) // 8)
    last = chunks - 1

    def chunk(i, ids):
        return (ids[0] >> 1) ^ jnp.minimum(i, last)

    first = [seen, *cots, *weights, x1]
    rest = [b2, gain2]
    outs = (
        [((2, 2, far, width // 8, width), BF16)] * 2
        + [((chunks, width // 2, width), BF16)] * 2
        + [((s.features, rows), BF16)] * 4
        + [((2, 2, far, block + sides, width), BF16)] * 2
        + [((2, 2, s.features // 2, width), BF16)] * 2
        + [((rows, width), BF16)] * 2
    )
    specs = [
        pl.BlockSpec((2, 2, 1, width // 8, width), lambda i, ids: (0, 0, jnp.minimum(i, last), 0, 0))
    ] * 2
    specs += [pl.BlockSpec((1, width // 2, width), lambda i, ids: (chunk(i, ids), 0, 0))] * 2
    specs += [fixed(*dims) for dims, _ in outs[4:]]
    return pl.pallas_call(
        functools.partial(hidden_kernel, s, far, chunks),
        grid_spec=pltpu.PrefetchScalarGridSpec(
            num_scalar_prefetch=1,
            grid=(chunks + 1,),
            in_specs=[whole(a) for a in first]
            + [
                LATE,
                pl.BlockSpec((width, width), lambda i, ids: (0, chunk(i, ids))),
                pl.BlockSpec((1, width), lambda i, ids: (0, chunk(i, ids))),
                pl.BlockSpec((width, width), lambda i, ids: (chunk(i, ids), 0)),
            ]
            + [whole(a) for a in rest]
            + [LATE],
            out_specs=specs,
            scratch_shapes=[
                pltpu.VMEM((rows, width), BF16),
                pltpu.VMEM((width, rows), BF16),
                pltpu.VMEM((rows, width), BF16),
                pltpu.VMEM((high, rows), BF16),
                pltpu.VMEM((rows, width), F32),
                pltpu.VMEM((rows, width), F32),
                pltpu.VMEM((rows, width), BF16),
                pltpu.VMEM((rows, width), BF16),
                pltpu.VMEM((width, width), F32),
                pltpu.VMEM((sides, width), F32),
                *late_scratch(mixed),
                *late_scratch(wout),
            ],
        ),
        out_shape=[shape(*out) for out in outs],
        compiler_params=params(60),
        cost_estimate=cost(3.4e10, 4e7),
    )(ids, *first, mixed, w1, b1, w2, *rest, wout)


def attention_back(s, heads, qkv_ref, probs_ref, go_ref, gqkv_ref):
    per = ROWS // LANES
    width = s.width
    masks = pair_masks()
    scale = 1.0 / math.sqrt(width // heads)
    def tile(j, carry):
        rows = pl.ds(pl.multiple_of(j * LANES, LANES), LANES)
        for h in range(width // LANES):
            at = h * LANES
            q = doubled(qkv_ref[rows, at : at + LANES], masks)
            k = doubled(qkv_ref[rows, width + at : width + at + LANES], masks)
            v = qkv_ref[rows, 2 * width + at : 2 * width + at + LANES]
            out = doubled(go_ref[rows, at : at + LANES], masks)
            rounded = probs_ref[j, h]
            probs = rounded.astype(F32)
            upward = nt(out, v)
            centred = upward - jnp.sum(probs * upward, axis=-1, keepdims=True)
            grads = (probs * centred).astype(BF16)
            wide = jnp.concatenate([grads[:LANES], grads[LANES:]], axis=1)
            gqkv_ref[rows, at : at + LANES] = (nn(wide, k) * scale).astype(BF16)
            gqkv_ref[rows, width + at : width + at + LANES] = (tn(grads, q) * scale).astype(BF16)
            gqkv_ref[rows, 2 * width + at : 2 * width + at + LANES] = tn(rounded, out).astype(BF16)
        return carry

    lax.fori_loop(0, per, tile, 0)


def first_norm_back(gqkv, x0_ref, ga_ref, wqkv_ref, gain1_ref):
    upward = nt(gqkv, wqkv_ref[...])
    normed, inverse = normalize(x0_ref[...].astype(F32))
    grad = ga_ref[...].astype(F32) + normalize_back(upward, normed, inverse, gain1_ref[0:1, :])
    return grad.astype(BF16), jnp.sum(upward * normed, axis=0, keepdims=True)


def backward_kernel(s, heads, qkv_ref, probs_ref, go_ref, x0_ref, ga_ref, wqkv_hbm, gain1_ref, gqkv_ref, g0_ref, gln1_ref, wqkv_ref, sem_ref):
    ready = late_copy(wqkv_hbm, wqkv_ref, sem_ref)
    attention_back(s, heads, qkv_ref, probs_ref, go_ref, gqkv_ref)
    ready()
    g0_ref[...], gain_part = first_norm_back(gqkv_ref[...], x0_ref, ga_ref, wqkv_ref, gain1_ref)
    accumulate(gln1_ref, pl.program_id(0) == 0, gain_part)


def row_inputs(s, offset):
    width = s.width
    return [
        part_rows(3 * width, offset),
        pl.BlockSpec((ROWS // LANES, width // LANES, 2 * LANES, LANES), lambda i, *_: (i + offset, 0, 0, 0)),
        part_rows(width, offset),
        part_rows(width, offset),
        part_rows(width, offset),
    ]


def backward(s, heads, offset, steps, qkv, probs, go, x0, ga, wqkv, gain1):
    width = s.width
    size = steps * ROWS
    return pl.pallas_call(
        functools.partial(backward_kernel, s, heads),
        grid=(steps,),
        in_specs=row_inputs(s, offset) + [LATE, whole(gain1)],
        scratch_shapes=late_scratch(wqkv),
        out_specs=[across(ROWS, 3 * width), across(ROWS, width), fixed(1, width)],
        out_shape=[shape((size, 3 * width), BF16), shape((size, width), BF16), shape((1, width), F32)],
        compiler_params=params(60),
        cost_estimate=cost(8e9 * steps, 6e6 * steps),
    )(qkv, probs, go, x0, ga, wqkv, gain1)


def position_grads(s, keep_ref, g0, picked):
    hot_hi, hot_lo = [], []
    for t in range(s.tiles):
        row = keep_ref[0, t : t + 1, :]
        patches = s.hi_patches if t < s.hi_each else s.lo_patches
        hot = jnp.where(iota((patches, LANES), 0) == row, 1.0, 0.0).astype(BF16)
        (hot_hi if t < s.hi_each else hot_lo).append(hot)
    hi_rows = s.hi_each * LANES
    hi = nn(jnp.concatenate(hot_hi, axis=1), g0[:hi_rows])
    lo = nn(jnp.concatenate(hot_lo, axis=1), g0[hi_rows:])
    return lo, hi, nn(jnp.concatenate(picked, axis=0), g0)


def finish_kernel(s, far, chunks, ids_ref, keep_ref, a_ref, r0_ref, r1_ref, ga_hbm, gb_hbm, la_ref, lb_ref, p0, p1, p2, p3, w0, w1, w2, w3, q0, q1, q2, q3, o0_ref, o1_ref, e0_ref, e1_ref, i0, i1, i2, i3, turned_ref, acc_ref, lo_ref, hi_ref, ga_ref, ga_sem, gb_ref, gb_sem):
    ga_ready = late_copy(ga_hbm, ga_ref, ga_sem, chunks)
    gb_ready = late_copy(gb_hbm, gb_ref, gb_sem, chunks)
    step = pl.program_id(0)
    width = s.width
    block = width // (8 * far)
    half = width // 2
    done = r0_ref.shape[0]

    @pl.when(step == 0)
    def _():
        turn_relative(ids_ref, far, block, a_ref, turned_ref, acc_ref)

    @pl.when(step < chunks)
    def _():
        value = nn(turned_ref[:, :done], r0_ref[...]) + nn(turned_ref[:, done:], r1_ref[...])
        o0_ref[0] = value[:half].astype(BF16)
        o1_ref[0] = value[half:].astype(BF16)

    ga_ready()
    gb_ready()

    @pl.when(step == chunks)
    def _():
        g0 = jnp.concatenate([ga_ref[...], gb_ref[...]], axis=0)
        lo, hi, embed = position_grads(s, keep_ref, g0, [p[...] for p in (p0, p1, p2, p3)])
        lo_ref[...] = lo
        hi_ref[...] = hi
        acc_ref[: s.groups * s.features, :] = embed
        spread_features(s, ids_ref, acc_ref, (e0_ref, e1_ref))
        for weight, pred, out in zip((w0, w1, w2, w3), (q0, q1, q2, q3), (i0, i1, i2, i3)):
            out[: s.features, :] = nt(weight[: s.features, :], g0).astype(BF16)
            out[s.features :, :] = pred[...]
        hi_block = s.hi_patches // (8 * far)
        lo_block = s.lo_patches // (8 * far)
        gain = la_ref[...] + lb_ref[...]
        pad = jnp.zeros((block - hi_block - lo_block - 1, width), F32)
        order = places(ids_ref, far)
        for p in range(0, len(order), 2):
            pair = []
            for at in order[p : p + 2]:
                both = lo_ref[pl.ds(pl.multiple_of((at >> 1) * 8, 8), 8), :]
                pair += [
                    hi_ref[pl.ds(pl.multiple_of(at * hi_block, 8), hi_block), :],
                    jnp.where((at & 1) == 1, both[lo_block:], both[:lo_block]),
                    gain,
                    pad,
                ]
            row = (p % (len(order) // 2)) * block
            (o0_ref, o1_ref)[p // (len(order) // 2)][0, row : row + 2 * block, :] = jnp.concatenate(pair, axis=0).astype(BF16)


def finish(s, ids, far, keep, a, gqkvs, g0s, gains, picked, weights, preds):
    width, rows = s.width, s.rows
    chunks = gqkvs[0].shape[1] // width
    rest = [*gains, *picked, *weights, *preds]
    out = pl.BlockSpec((1, width // 2, width), lambda i, ids: (i, 0, 0))
    return pl.pallas_call(
        functools.partial(finish_kernel, s, far, chunks),
        grid_spec=pltpu.PrefetchScalarGridSpec(
            num_scalar_prefetch=1,
            grid=(chunks + 1,),
            in_specs=[whole(keep), whole(a)]
            + [
                pl.BlockSpec((g.shape[0], width), lambda i, ids: (0, jnp.minimum(i, chunks - 1)))
                for g in gqkvs
            ]
            + [LATE, LATE]
            + [whole(r) for r in rest],
            out_specs=[out, out]
            + [fixed(2, 2, s.features // 2, width)] * 2
            + [fixed(2 * s.features, rows)] * 4,
            scratch_shapes=[
                pltpu.VMEM((width, rows), BF16),
                pltpu.VMEM((width, width), F32),
                pltpu.VMEM((s.lo_patches, width), F32),
                pltpu.VMEM((s.hi_patches, width), F32),
                *late_scratch(g0s[0]),
                *late_scratch(g0s[1]),
            ],
        ),
        out_shape=[shape((chunks + 1, width // 2, width), BF16)] * 2
        + [shape((2, 2, s.features // 2, width), BF16)] * 2
        + [shape((2 * s.features, rows), BF16)] * 4,
        compiler_params=params(60),
        cost_estimate=cost(7e9, 1.2e7),
    )(ids, keep, a, *gqkvs, *g0s, *rest)


def combine_kernel(held_ref, got_ref, keep_ref, send_ref):
    send_ref[...] = (held_ref[:, 1].astype(F32) + got_ref[:, 1].astype(F32)).astype(BF16)
    keep_ref[...] = (held_ref[:, 0].astype(F32) + got_ref[:, 0].astype(F32)).astype(BF16)


def combine(held, got, axis):
    dims = held.shape
    width = dims[-1]
    outer = math.prod(dims[:axis])
    inner = math.prod(dims[axis + 1 : -1])
    grid = (outer // 4, 1) if outer > 4 else (1, 2)
    broad, tall = outer // grid[0], inner // grid[1]
    half = shape((outer, inner, width), BF16)
    spec = pl.BlockSpec((broad, 2, tall, width), lambda i, j: (i, 0, j, 0))
    out = pl.BlockSpec((broad, tall, width), lambda i, j: (i, j, 0))
    keep, send = pl.pallas_call(
        combine_kernel,
        grid=grid,
        in_specs=[spec, spec],
        out_specs=[out, out],
        out_shape=[half, half],
        compiler_params=params(60),
        cost_estimate=cost(1e6, 6 * outer * inner * width),
    )(*(value.reshape(outer, 2, inner, width) for value in (held, got)))
    left = dims[:axis] + dims[axis + 1 :]
    return keep.reshape(left), send.reshape(left)


def place_kernel(s, member_ref, keep_ref, r0, r1, r2, r3, lo_ref, hi_ref, pred_lo_ref, pred_hi_ref):
    lane_sample = iota((1, LANES), 1) // s.lo_length
    eye = jnp.where(iota((s.features, s.features), 0) == iota((s.features, s.features), 1), 1.0, 0.0).astype(BF16)
    for k, got_ref in enumerate((r0, r1, r2, r3)):
        other = member_ref[0] ^ k
        for i in range(s.hi_each):
            chosen = iota((s.hi_patches, LANES), 0) == keep_ref[k, i : i + 1, :]
            hot = jnp.where(chosen, 1.0, 0.0).astype(BF16)
            lanes = slice(i * LANES, (i + 1) * LANES)
            hi_ref[other * s.hi_each + i] = nt(got_ref[: s.features, lanes], hot).astype(BF16)
            pred_hi_ref[other * s.hi_each + i] = got_ref[s.features :, lanes]
        for tile, first, count in sample_tiles(s):
            lanes = slice(tile * LANES, (tile + 1) * LANES)
            got = got_ref[: s.features, lanes]
            for j in range(count):
                row = jnp.where(lane_sample == j, keep_ref[k, tile : tile + 1, :], -1)
                hot = jnp.where(iota((s.lo_patches, LANES), 0) == row, 1.0, 0.0).astype(BF16)
                lo_ref[other * s.lo_each + first + j] = nt(got, hot).astype(BF16)
            if count:
                size = count * s.lo_length
                turned = tn(got_ref[s.features :, lanes], eye).astype(BF16)
                start = pl.multiple_of((other * s.lo_each + first) * s.lo_length, s.lo_length)
                pred_lo_ref[pl.ds(start, size), :] = turned[:size]


def place(s, member, keep, blocks):
    lo = s.groups * s.lo_each
    hi = s.groups * s.hi_each
    outs = [
        (lo, s.features, s.lo_patches),
        (hi, s.features, s.hi_patches),
        (lo * s.lo_length, s.features),
        (hi, s.features, s.hi_length),
    ]
    return pl.pallas_call(
        functools.partial(place_kernel, s),
        grid_spec=pltpu.PrefetchScalarGridSpec(
            num_scalar_prefetch=1,
            grid=(1,),
            in_specs=[whole(keep)] + [whole(b) for b in blocks],
            out_specs=[fixed(*dims) for dims in outs],
        ),
        out_shape=[shape(dims, BF16) for dims in outs],
        compiler_params=params(60),
        cost_estimate=cost(2e9, 8e6),
    )(member, keep, *blocks)


def swap(value, data_bit, var_bit):
    dp, var = lax.axis_size("dp"), lax.axis_size("var")
    pairs = [
        (d * var + v, (d ^ data_bit) * var + (v ^ var_bit)) for d in range(dp) for v in range(var)
    ]
    return lax.ppermute(value, AXES, pairs)


def add_rounded(left, right):
    return (left.astype(F32) + right.astype(F32)).astype(BF16)


def added(*values):
    values = [value.astype(F32) for value in values]
    while len(values) > 1:
        values = [values[i] + values[i + 1] for i in range(0, len(values), 2)]
    return values[0]


def tie(value, *tokens):
    return lax.optimization_barrier((value, tokens))[0]


PARTNERS = {"core": (0, 1), "x": (0, 2), "y": (1, 0), "z0": (2, 0), "z1": (4, 0)}


class Chain:
    def __init__(self, near, sent):
        self.near, self.sent = near, sent
        self.repeats = near.ndim == 4
        self.names = ["x", "y"] if self.repeats else ["chunk", "x", "y", "z1", "z0"][7 - near.ndim :]
        self.held = self.got = None

    def outgoing(self, name):
        if name == "core":
            self.held = self.near
            return self.sent
        if name not in self.names:
            self.held = add_rounded(self.held, self.got)
            return self.held
        axis = self.names.index(name)
        self.names.remove(name)
        if math.prod(self.held.shape) >= 1 << 20:
            self.held, sent = combine(self.held, self.got, axis)
            return sent
        kept, sent = (
            [lax.index_in_dim(value, side, axis, keepdims=False) for value in (self.held, self.got)]
            for side in range(2)
        )
        self.held = add_rounded(*kept)
        return add_rounded(*sent)

    def hold(self, *tokens):
        self.held, self.got = tie((self.held, self.got), *tokens)

    def final(self):
        return added(self.held, self.got)


def send_rows(values, bits):
    width = values[0].shape[-1]
    if len(values) == 1:
        return [swap(values[0].reshape(-1, width), *bits).reshape(values[0].shape)]
    flat = [value.reshape(-1, width) for value in values]
    got = swap(jnp.concatenate(flat, axis=0), *bits)
    out, start = [], 0
    for value, rows in zip(values, flat):
        out.append(got[start : start + rows.shape[0]].reshape(value.shape))
        start += rows.shape[0]
    return out


def trade(name, *chains):
    got = send_rows([chain.outgoing(name) for chain in chains], PARTNERS[name])
    for chain, value in zip(chains, got):
        chain.got = value
    return got[0]


def both_halves(value):
    value = value.astype(BF16)
    other = swap(value, 1, 0)
    second = lax.axis_index("dp") % 2 == 1
    return jnp.concatenate(
        [jnp.where(second, other, value), jnp.where(second, value, other)], axis=0
    ).astype(F32)


def natural(near, sent):
    rows, width = near.shape[-2:]
    both = jnp.stack([near, sent]).reshape((2, -1, 2, 2, 4, rows, width))
    return both.transpose(4, 3, 2, 0, 1, 5, 6).reshape(32, -1, width)


def scattered(full):
    return lax.psum_scatter(full, AXES, scatter_dimension=0, tiled=True).astype(F32)


def joined(blocks, chunks):
    count, rows, width = blocks.shape
    split = blocks.reshape(count, chunks, rows // chunks, width).transpose(0, 2, 1, 3)
    return split.reshape(count * (rows // chunks), chunks * width)


def plain_sum(near, sent):
    if near.ndim >= 6:
        return natural(near, sent)
    value = jnp.stack([near, sent], axis=1)
    value = value.reshape((4, -1, near.shape[-1]))
    bit = 1
    while value.shape[0] > 1:
        value = value.reshape((value.shape[0] // 2, 2) + value.shape[1:])
        value = add_rounded(value[:, 0], swap(value[:, 1], 0, bit))
        bit *= 2
    return lax.psum(value[0], "dp").astype(F32)


def exchange_relative(blocks):
    return [blocks[0]] + [swap(blocks[k], 0, k) for k in range(1, len(blocks))]


def body(
    img_lo,
    img_hi,
    keep_lo,
    keep_hi,
    mask_lo,
    mask_hi,
    w_embed,
    pos_lo,
    pos_hi,
    ln1_gain,
    w_qkv,
    w_out,
    ln2_gain,
    w_fc1,
    b_fc1,
    w_fc2,
    b_fc2,
    w_head,
    cot_lo,
    cot_hi,
):
    groups = lax.axis_size("var")
    devices = lax.axis_size("dp") * groups
    member = lax.axis_index("var").astype(jnp.int32).reshape(1)
    s = Sizes(keep_lo.shape, keep_hi.shape, w_embed.shape, img_lo.shape, img_hi.shape, groups)
    features, width = s.features, s.width
    gain1 = gain2 = vectors = jnp.stack([ln1_gain, ln2_gain, b_fc2])
    img_lo_t, img_hi_t = img_lo.transpose(0, 2, 1), img_hi.transpose(0, 2, 1)

    own = jnp.concatenate([w_embed, w_head.T], axis=0)
    crossed = swap(own, 0, 2)
    beside = swap(own, 0, 1)
    sent = pick(s, (2, 3, 1, 0), member, keep_lo, keep_hi, img_lo_t, img_hi_t)
    crossed = tie(crossed, sent[0])
    weights = [own, beside, crossed, swap(crossed, 0, 1)]
    picked = [sent[3], swap(sent[2], 0, 1), swap(sent[0], 0, 2), swap(sent[1], 0, 3)]
    keep, seen, *cots = stage(
        s,
        tie(member, sent[0]),
        keep_lo,
        keep_hi,
        mask_lo,
        mask_hi,
        cot_lo.reshape(-1, features),
        cot_hi.transpose(0, 2, 1),
    )
    cots = exchange_relative(cots)
    own_keep = keep
    x0, a, qkv, probs, mixed, x1 = forward(
        s, HEADS, own_keep, seen, picked, weights, pos_lo, pos_hi, gain1, w_qkv, w_out
    )
    far = 4
    cube = lax.axis_size("dp") == 2 * far
    place_of = lax.axis_index("dp") * groups + lax.axis_index("var")
    ids = jnp.stack([lax.axis_index("dp"), lax.axis_index("var")]).astype(jnp.int32)
    if not cube:
        ids = jnp.zeros_like(ids)

    def chain_of(near, sent):
        if near.ndim == 5:
            near, sent = (
                value.reshape((2, 2, 2, 2) + value.shape[3:]) for value in (near, sent)
            )
        elif near.ndim == 3:
            near, sent = (
                value.reshape((-1, 2, 2, 2, 2, width // 32, width)) for value in (near, sent)
            )
        return Chain(near, sent)

    def step(name, *chains):
        return trade(name, *chains) if cube else ()

    def halves_of(chain):
        out = []
        for side in range(2):
            piece = Chain(chain.near, chain.sent)
            count = chain.near.shape[0] // 2
            piece.held, piece.got = (
                lax.slice_in_dim(value, side * count, (side + 1) * count, axis=0)
                for value in (chain.held, chain.got)
            )
            out.append(piece)
        return out

    two0, two1, one0, one1, *rest = hidden(
        s,
        ids,
        far,
        tie(seen, x1),
        cots,
        weights,
        x1,
        mixed,
        w_fc1,
        b_fc1.reshape(1, -1),
        w_fc2,
        vectors,
        gain2,
        w_out,
    )
    preds, (out0, out1, head0, head1, go, ga) = rest[:groups], rest[groups:]
    two, one = chain_of(two0, two1), chain_of(one0, one1)
    out, head = chain_of(out0, out1), chain_of(head0, head1)
    tokens = [step("core", chain) for chain in (two, one, out, head)]

    def back(offset, steps, *ready):
        return backward(
            s, HEADS, offset, steps, qkv, probs, go, x0, ga, w_qkv, tie(gain1, *ready)
        )

    parts = [back(0, 1, go)]
    if cube:
        for chain in (two, one, out, head):
            chain.hold(parts[0][0])
    near_tokens = [step("x", two), step("y", one)]
    if cube:
        for chain in (out, head):
            chain.hold(two.held, one.held)
    near_tokens.append(step("z0", out, head))
    parts.append(back(1, s.rows // ROWS - 1, parts[0][0], two.held, one.held, *tokens))
    if cube:
        for chain in (two, one, out, head):
            chain.hold(parts[1][0])
    tokens = [step("y", two), step("x", one, out, head)]
    gqkvs, g0s, gains = zip(*parts)
    near, sent, near_embed, sent_embed, *blocks = finish(
        s,
        tie(ids, two.held, one.held, *near_tokens),
        far,
        own_keep,
        a,
        gqkvs,
        g0s,
        gains,
        picked,
        weights,
        preds,
    )
    sent, sent_embed = tie((sent, sent_embed), *tokens)
    first, embed = chain_of(near, sent), chain_of(near_embed, sent_embed)
    tokens += [step("core", first), step("core", embed)]
    if cube:
        old = (two, one, out, head)
        for chain in old:
            chain.hold(first.got)
        one_half, other_half = halves_of(first)
        tokens = [trade("x", one_half, embed), trade("y", other_half, out, head)]
        trade("z0", two, one)
        for chain in old:
            chain.hold(*tokens)
        tokens = [trade("y", one_half, embed), trade("x", other_half)]
        trade("z1", *old)
        blocks = [tie(block_of, *tokens) for block_of in blocks]
        trade("z0", one_half, other_half, embed)
        trade("z1", one_half, other_half, embed)
        head.hold(embed.held)
        grad_head = both_halves(head.final())
        last_member = tie(member, grad_head)
        for chain in (two, one, out):
            chain.hold(grad_head)
        grad_fc2, grad_fc1, rest, grad_embed = (
            chain.final() for chain in (two, one, out, embed)
        )
        grad_embed = both_halves(grad_embed)
        first = jnp.concatenate([one_half.final(), other_half.final()], axis=0).reshape(-1, width)
        grad_fc1 = grad_fc1.reshape(-1, width)
    else:
        grad_fc2, grad_fc1, rest, grad_head, grad_embed, first = (
            plain_sum(chain.near, chain.sent) for chain in (two, one, out, head, embed, first)
        )
        last_member = member
    grad_img_lo, grad_img_hi, pred_lo, pred_hi = place(s, last_member, keep, exchange_relative(blocks))
    grad_head = grad_head.T

    block = width // devices
    inner = w_fc1.shape[1] // width

    hi_block = s.hi_patches // devices
    lo_block = s.lo_patches // devices

    def own_part(row):
        return lax.dynamic_slice_in_dim(row, place_of * block, block)

    if cube:
        grad_fc1 = joined(grad_fc1[None], inner)
        grad_qkv = joined(first[None, : 3 * block], 3)
        grad_out, sides = rest[:block], rest[block:]
        extra = first[3 * block :]
        grad_pos_hi = extra[:hi_block]
        grad_pos_lo = extra[hi_block : hi_block + lo_block]
        first_side = extra[hi_block + lo_block]
    else:
        tall = width // 32
        hi_tall, lo_tall = s.hi_patches // 32, s.lo_patches // 32
        grad_fc2 = scattered(grad_fc2.reshape(-1, width))
        grad_fc1 = scattered(joined(grad_fc1, inner))
        grad_qkv = scattered(joined(first[:, : 3 * tall], 3))
        grad_out, sides = scattered(rest[:, :tall].reshape(-1, width)), rest[0, tall:]
        extra = first[:, 3 * tall :]
        grad_pos_hi = scattered(extra[:, :hi_tall].reshape(-1, width))
        grad_pos_lo = scattered(extra[:, hi_tall : hi_tall + lo_tall].reshape(-1, width))
        sides = lax.psum(jnp.concatenate([sides, extra[0, hi_tall + lo_tall :]]), AXES).astype(F32)
        first_side = sides[rest.shape[1] - tall]
    grad_ln1 = own_part(first_side)
    grad_ln2 = own_part(sides[0])
    grad_b2 = own_part(sides[1])
    grad_b1 = lax.dynamic_slice_in_dim(
        sides[2 : 2 + inner].reshape(-1), place_of * inner * block, inner * block
    )
    return (
        pred_lo.reshape(cot_lo.shape),
        pred_hi.transpose(0, 2, 1),
        grad_img_lo.transpose(0, 2, 1),
        grad_img_hi.transpose(0, 2, 1),
        grad_embed,
        grad_pos_lo,
        grad_pos_hi,
        grad_ln1,
        grad_qkv,
        grad_out,
        grad_ln2,
        grad_fc1,
        grad_b1,
        grad_fc2,
        grad_b2,
        grad_head,
    )


def solution(mesh):
    placed = (
        P("dp", None, "var"),
        P("dp", None, "var"),
        P("dp", None),
        P("dp", None),
        P("dp", None),
        P("dp", None),
        P("var", None),
        P(),
        P(),
        P(),
        P(),
        P(),
        P(),
        P(),
        P(),
        P(),
        P(),
        P(None, "var"),
        P("dp", None, "var"),
        P("dp", None, "var"),
    )
    return jax.shard_map(
        body,
        mesh=mesh,
        in_specs=placed,
        out_specs=(
            P("dp", None, "var"),
            P("dp", None, "var"),
            P("dp", None, "var"),
            P("dp", None, "var"),
            P("var", None),
            P(("dp", "var"), None),
            P(("dp", "var"), None),
            P(("dp", "var")),
            P(("dp", "var"), None),
            P(("dp", "var"), None),
            P(("dp", "var")),
            P(("dp", "var"), None),
            P(("dp", "var")),
            P(("dp", "var"), None),
            P(("dp", "var")),
            P(None, "var"),
        ),
        check_vma=False,
    )
```

```python
import functools
import math

import jax
import jax.numpy as jnp
from jax import lax
from jax.experimental import pallas as pl
from jax.experimental.pallas import tpu as pltpu
from jax.sharding import PartitionSpec as P

HEADS = 12
EPSILON = 1e-06
AXES = ("dp", "var")
BF16 = jnp.bfloat16
F32 = jnp.float32
LANES = 128
ROWS = 256
MASKED = -1000000000.0
SHARE = 0.2


def dot(left, right, dims):
    return lax.dot_general(left, right, (dims, ((), ())), preferred_element_type=F32)


def nn(left, right):
    return dot(left, right, ((1,), (0,)))


def nt(left, right):
    return dot(left, right, ((1,), (1,)))


def tn(left, right):
    return dot(left, right, ((0,), (0,)))


def shape(dims, dtype):
    return jax.ShapeDtypeStruct(dims, dtype)


def whole(array):
    zeros = (0,) * array.ndim
    return pl.BlockSpec(array.shape, lambda *_: zeros, pipeline_mode=pl.Buffered(1))


def across(rows, width):
    return pl.BlockSpec((rows, width), lambda i, *_: (i, 0))


def along(height, columns):
    return pl.BlockSpec((height, columns), lambda i, *_: (0, i))


def fixed(*dims):
    zeros = (0,) * len(dims)
    return pl.BlockSpec(dims, lambda *_: zeros)


def params(mebibytes):
    return pltpu.CompilerParams(vmem_limit_bytes=mebibytes << 20)


def cost(flops, nbytes):
    return pl.CostEstimate(flops=int(flops * SHARE), bytes_accessed=int(nbytes * SHARE), transcendentals=0)


def iota(dims, axis):
    return lax.broadcasted_iota(jnp.int32, dims, axis)


def accumulate(ref, first, value):
    @pl.when(first)
    def _():
        ref[...] = value

    @pl.when(jnp.logical_not(first))
    def _():
        ref[...] += value


def normalize(values):
    center = values - jnp.mean(values, axis=-1, keepdims=True)
    inverse = lax.rsqrt(jnp.mean(center * center, axis=-1, keepdims=True) + EPSILON)
    return center * inverse, inverse


def normalize_back(upstream, normed, inverse, gains):
    scaled = upstream * gains
    mean_plain = jnp.mean(scaled, axis=-1, keepdims=True)
    mean_mixed = jnp.mean(scaled * normed, axis=-1, keepdims=True)
    return inverse * (scaled - mean_plain - normed * mean_mixed)


def gelu_parts(u):
    ratio = 1.0 / (1.0 + (0.3275911 * math.sqrt(0.5)) * jnp.abs(u))
    bell = jnp.exp(-0.5 * u * u)
    series = 0.5 * 1.061405429
    for factor in (-1.453152027, 1.421413741, -0.284496736, 0.254829592):
        series = series * ratio + 0.5 * factor
    tail = series * ratio * bell
    below = jnp.where(u < 0, tail, 1.0 - tail)
    return u * below, below + u * (bell * (1.0 / math.sqrt(2.0 * math.pi)))


class Sizes:
    def __init__(self, keep_lo, keep_hi, w_embed, img_lo, img_hi, groups):
        self.lo_each, self.hi_each = keep_lo[0] // groups, keep_hi[0] // groups
        self.lo_length, self.hi_length = keep_lo[1], keep_hi[1]
        self.features, self.width = w_embed
        self.lo_patches, self.hi_patches = img_lo[1], img_hi[1]
        self.groups = groups
        self.pack = LANES // self.lo_length
        self.lo_tiles = -(-self.lo_each // self.pack)
        self.hi_rows = self.hi_each * self.hi_length
        tiles = self.hi_each + self.lo_tiles
        self.tiles = tiles + tiles % 2
        self.rows = self.tiles * LANES


def sample_tiles(s):
    out = []
    for t in range(s.tiles - s.hi_each):
        first = t * s.pack
        out.append((s.hi_each + t, first, max(0, min(s.pack, s.lo_each - first))))
    return out


def slots(rows, fill, s):
    missing = s.pack - len(rows)
    if missing:
        rows = rows + [jnp.full((1, missing * s.lo_length), fill, rows[0].dtype if rows else jnp.int32)]
    return rows[0] if len(rows) == 1 else jnp.concatenate(rows, axis=1)


def pick_kernel(s, members, member_ref, keep_lo_ref, keep_hi_ref, img_lo_ref, img_hi_ref, *out_refs):
    for k, out_ref in zip(members, out_refs):
        other = member_ref[0] ^ k
        for i in range(s.hi_each):
            at = other * s.hi_each + i
            chosen = iota((s.hi_patches, LANES), 0) == keep_hi_ref[pl.ds(at, 1), :]
            got = nn(img_hi_ref[at], jnp.where(chosen, 1.0, 0.0).astype(BF16))
            out_ref[:, i * LANES : (i + 1) * LANES] = got.astype(BF16)
        for tile, first, count in sample_tiles(s):
            parts = []
            for j in range(count):
                at = other * s.lo_each + first + j
                chosen = iota((s.lo_patches, s.lo_length), 0) == keep_lo_ref[pl.ds(at, 1), :]
                parts.append(nn(img_lo_ref[at], jnp.where(chosen, 1.0, 0.0).astype(BF16)))
            if count < s.pack:
                parts.append(jnp.zeros((s.features, (s.pack - count) * s.lo_length), F32))
            joined = jnp.concatenate(parts, axis=1) if len(parts) > 1 else parts[0]
            out_ref[:, tile * LANES : (tile + 1) * LANES] = joined.astype(BF16)


def pick(s, members, member, keep_lo, keep_hi, img_lo, img_hi):
    args = (keep_lo, keep_hi, img_lo, img_hi)
    return pl.pallas_call(
        functools.partial(pick_kernel, s, members),
        grid_spec=pltpu.PrefetchScalarGridSpec(
            num_scalar_prefetch=1,
            grid=(1,),
            in_specs=[whole(a) for a in args],
            out_specs=[fixed(s.features, s.rows)] * len(members),
        ),
        out_shape=[shape((s.features, s.rows), BF16)] * len(members),
        compiler_params=params(60),
        cost_estimate=cost(2e9, 4e6),
    )(member, *args)


def stage_kernel(s, member_ref, keep_lo_ref, keep_hi_ref, mask_lo_ref, mask_hi_ref, cot_lo_ref, cot_hi_ref, keep_ref, seen_ref, *out_refs):
    eye = jnp.where(iota((s.features, s.features), 0) == iota((s.features, s.features), 1), 1.0, 0.0).astype(BF16)
    first_hi = (iota((1, s.hi_length), 1) == 0).astype(jnp.int32)
    first_lo = (iota((1, s.lo_length), 1) == 0).astype(jnp.int32)
    for k, out_ref in enumerate(out_refs):
        other = member_ref[0] ^ k
        for i in range(s.hi_each):
            at = other * s.hi_each + i
            keep_ref[k, i : i + 1, :] = keep_hi_ref[pl.ds(at, 1), :]
            out_ref[:, i * LANES : (i + 1) * LANES] = cot_hi_ref[at]
            if k == 0:
                seen_ref[i : i + 1, :] = jnp.maximum(mask_hi_ref[pl.ds(at, 1), :], first_hi).astype(F32)
        for tile, first, count in sample_tiles(s):
            begin = other * s.lo_each + first
            keep_ref[k, tile : tile + 1, :] = slots([keep_lo_ref[pl.ds(begin + j, 1), :] for j in range(count)], -1, s)
            if k == 0:
                seen = [jnp.maximum(mask_lo_ref[pl.ds(begin + j, 1), :], first_lo) for j in range(count)]
                seen_ref[tile : tile + 1, :] = slots(seen, 0, s).astype(F32)
            where = slice(tile * LANES, (tile + 1) * LANES)
            if count < s.pack:
                out_ref[:, where] = jnp.zeros((s.features, LANES), BF16)
            if count:
                size = count * s.lo_length
                start = pl.multiple_of(begin * s.lo_length, s.lo_length)
                out_ref[:, tile * LANES : tile * LANES + size] = nt(eye, cot_lo_ref[pl.ds(start, size), :]).astype(BF16)


def stage(s, member, keep_lo, keep_hi, mask_lo, mask_hi, cot_lo, cot_hi):
    args = (keep_lo, keep_hi, mask_lo, mask_hi, cot_lo, cot_hi)
    return pl.pallas_call(
        functools.partial(stage_kernel, s),
        grid_spec=pltpu.PrefetchScalarGridSpec(
            num_scalar_prefetch=1,
            grid=(1,),
            in_specs=[whole(a) for a in args],
            out_specs=[fixed(s.groups, s.tiles, LANES), fixed(s.tiles, LANES)]
            + [fixed(s.features, s.rows)] * s.groups,
        ),
        out_shape=[shape((s.groups, s.tiles, LANES), jnp.int32), shape((s.tiles, LANES), F32)]
        + [shape((s.features, s.rows), BF16)] * s.groups,
        compiler_params=params(60),
        cost_estimate=cost(1e8, 4e6),
    )(member, *args)


def chosen_columns(s, keep_ref, tile, patches, wanted_hi):
    row = keep_ref[0, pl.ds(tile, 1), :]
    is_hi = tile < s.hi_each
    row = jnp.where(is_hi if wanted_hi else jnp.logical_not(is_hi), row, -1)
    column = jnp.broadcast_to(row.astype(F32), (LANES, LANES)).T.astype(jnp.int32)
    parts = [jnp.where(iota((LANES, LANES), 1) + at == column, 1.0, 0.0) for at in range(0, patches, LANES)]
    return jnp.concatenate(parts, axis=1).astype(BF16)


def pair_masks():
    lane = iota((1, LANES), 1)
    low = jnp.where(lane < LANES // 2, 1.0, 0.0).astype(BF16)
    high = jnp.where(lane < LANES // 2, 0.0, 1.0).astype(BF16)
    return low, high


def doubled(block, masks):
    return jnp.concatenate([block * masks[0], block * masks[1]], axis=0)


def allowed(s, seen_ref, tile):
    bits = jnp.where(tile < s.hi_each, s.hi_length.bit_length() - 1, s.lo_length.bit_length() - 1)
    same = (iota((LANES, LANES), 0) >> bits) == (iota((LANES, LANES), 1) >> bits)
    open_to = jnp.logical_and(same, seen_ref[pl.ds(tile, 1), :] > 0)
    return jnp.concatenate([open_to, open_to], axis=0)


def forward_kernel(s, heads, keep_ref, seen_ref, p0, p1, p2, p3, w0, w1, w2, w3, pos_lo_ref, pos_hi_ref, gain1_ref, wqkv_ref, wout_ref, x0_ref, a_ref, qkv_ref, probs_ref, mixed_ref, x1_ref):
    step = pl.program_id(0)
    per = ROWS // LANES
    width = s.width
    picked = jnp.concatenate([p[...] for p in (p0, p1, p2, p3)], axis=0)
    embed = jnp.concatenate([w[: s.features, :] for w in (w0, w1, w2, w3)], axis=0)
    hot_hi = jnp.concatenate([chosen_columns(s, keep_ref, step * per + j, s.hi_patches, True) for j in range(per)], axis=0)
    hot_lo = jnp.concatenate([chosen_columns(s, keep_ref, step * per + j, s.lo_patches, False) for j in range(per)], axis=0)
    start = tn(picked, embed) + (nn(hot_hi, pos_hi_ref[...]) + nn(hot_lo, pos_lo_ref[...]))
    x0_ref[...] = start.astype(BF16)
    normed, _ = normalize(start)
    normed = (normed * gain1_ref[0:1, :]).astype(BF16)
    a_ref[...] = normed
    for c in range(3):
        part = slice(c * width, (c + 1) * width)
        qkv_ref[:, part] = nn(normed, wqkv_ref[:, part]).astype(BF16)
    masks = pair_masks()
    scale = 1.0 / math.sqrt(width // heads)
    for j in range(per):
        rows = slice(j * LANES, (j + 1) * LANES)
        ok = allowed(s, seen_ref, step * per + j)
        for h in range(width // LANES):
            at = h * LANES
            q = qkv_ref[rows, at : at + LANES]
            k = qkv_ref[rows, width + at : width + at + LANES]
            v = qkv_ref[rows, 2 * width + at : 2 * width + at + LANES]
            scores = nt(doubled(q, masks), k) * scale
            scores = jnp.where(ok, scores, MASKED)
            raised = jnp.exp(scores - jnp.max(scores, axis=-1, keepdims=True))
            probs = raised / jnp.sum(raised, axis=-1, keepdims=True)
            rounded = probs.astype(BF16)
            probs_ref[j, h] = rounded
            wide = jnp.concatenate([rounded[:LANES], rounded[LANES:]], axis=1)
            mixed_ref[rows, at : at + LANES] = nn(wide, doubled(v, masks)).astype(BF16)
    middle = start + nn(mixed_ref[...], wout_ref[...])
    x1_ref[...] = middle


def forward(s, heads, keep, seen, picked, weights, pos_lo, pos_hi, gain1, wqkv, wout):
    width, rows = s.width, s.rows
    per, pairs = ROWS // LANES, width // LANES
    return pl.pallas_call(
        functools.partial(forward_kernel, s, heads),
        grid=(rows // ROWS,),
        in_specs=[whole(keep), whole(seen)]
        + [along(s.features, ROWS)] * 4
        + [whole(w) for w in weights]
        + [whole(a) for a in (pos_lo, pos_hi, gain1, wqkv, wout)],
        out_specs=[
            across(ROWS, width),
            across(ROWS, width),
            across(ROWS, 3 * width),
            pl.BlockSpec((per, pairs, 2 * LANES, LANES), lambda i: (i, 0, 0, 0)),
            across(ROWS, width),
            across(ROWS, width),
        ],
        out_shape=[
            shape((rows, width), BF16),
            shape((rows, width), BF16),
            shape((rows, 3 * width), BF16),
            shape((s.tiles, pairs, 2 * LANES, LANES), BF16),
            shape((rows, width), BF16),
            shape((rows, width), F32),
        ],
        compiler_params=params(60),
        cost_estimate=cost(1.5e10, 3e7),
    )(keep, seen, *picked, *weights, pos_lo, pos_hi, gain1, wqkv, wout)


def part_rows(width, offset):
    return pl.BlockSpec((ROWS, width), lambda i, *_: (i + offset, 0))


def relative(ids_ref, x, y, z, c):
    return ids_ref[0] ^ (2 * z + y), ids_ref[1] ^ (2 * x + c)


def places(ids_ref, far):
    out = []
    for c in range(2):
        for x in range(2):
            for y in range(2):
                for z in range(far):
                    d, v = relative(ids_ref, x, y, z, c)
                    out.append(d * 4 + v)
    return out


def turn_relative(ids_ref, far, block, source_ref, turned_ref, acc_ref):
    order = places(ids_ref, far)
    rows = source_ref.shape[0]
    for begin in range(0, rows, rows // 2):
        span = slice(begin, begin + rows // 2)
        acc_ref[:, : rows // 2] = source_ref[span, :].astype(F32).T
        for p in range(0, len(order), 2):
            pair = [
                acc_ref[pl.ds(pl.multiple_of(at * block, 8), block), : rows // 2]
                for at in order[p : p + 2]
            ]
            turned_ref[p * block : (p + 2) * block, span] = jnp.concatenate(pair, axis=0).astype(BF16)


def spread(ids_ref, far, acc_ref, outs, block, extra):
    for x in range(2):
        for y in range(2):
            for z in range(far):
                for c, out_ref in enumerate(outs):
                    d, v = relative(ids_ref, x, y, z, c)
                    start = pl.multiple_of((d * 4 + v) * block, 8)
                    out_ref[x, y, z, :block, :] = acc_ref[pl.ds(start, block), :].astype(BF16)
                    out_ref[x, y, z, block:, :] = extra


def spread_features(s, ids_ref, acc_ref, outs):
    half = s.features // 2
    for k in range(4):
        for y in range(2):
            start = k * s.features + ((ids_ref[0] & 1) ^ y) * half
            rows = acc_ref[pl.ds(pl.multiple_of(start, 8), half), :]
            outs[k % 2][k // 2, y] = rows.astype(BF16)


def late_copy(source_ref, held_ref, sem_ref, needed=0):
    @pl.when(pl.program_id(0) == 0)
    def _():
        pltpu.make_async_copy(source_ref, held_ref, sem_ref).start()

    def ready():
        @pl.when(pl.program_id(0) == needed)
        def _():
            pltpu.make_async_copy(source_ref, held_ref, sem_ref).wait()

    return ready


LATE = pl.BlockSpec(memory_space=pl.ANY)


def late_scratch(array):
    return [pltpu.VMEM(array.shape, array.dtype), pltpu.SemaphoreType.DMA(())]


def hidden_kernel(s, far, chunks, ids_ref, seen_ref, c0, c1, c2, c3, h0, h1, h2, h3, x1_ref, mixed_hbm, w1_ref, b1_ref, w2_ref, b2_ref, gain2_ref, wout_hbm, two0_ref, two1_ref, one0_ref, one1_ref, p0, p1, p2, p3, out0_ref, out1_ref, n0_ref, n1_ref, go_ref, ga_ref, b_ref, turned_ref, gm_ref, gpred_ref, forth_ref, back_ref, z_ref, gu_ref, acc_ref, side_ref, mixed_ref, mixed_sem, wout_ref, wout_sem):
    step = pl.program_id(0)
    mixed_ready = late_copy(mixed_hbm, mixed_ref, mixed_sem, chunks)
    wout_ready = late_copy(wout_hbm, wout_ref, wout_sem, chunks)
    width = s.width
    block = width // (8 * far)
    subs = [slice(begin, begin + ROWS) for begin in range(0, s.rows, ROWS)]
    seen = jnp.concatenate([seen_ref[t : t + 1, :] for t in range(s.tiles)], axis=1)

    @pl.when(step == 0)
    def _():
        gpred_ref[...] = jnp.concatenate([c[...] for c in (c0, c1, c2, c3)], axis=0) * seen.astype(BF16)
        head = jnp.concatenate([h[s.features :, :] for h in (h0, h1, h2, h3)], axis=0)
        total = None
        for rows in subs:
            values = x1_ref[rows, :]
            normed, _ = normalize(values)
            b_ref[rows, :] = (normed * gain2_ref[1:2, :]).astype(BF16)
            forth_ref[rows, :] = values + b2_ref[2:3, :]
            back_ref[rows, :] = jnp.zeros((ROWS, width), F32)
            upward = tn(gpred_ref[:, rows], head).astype(BF16)
            gm_ref[rows, :] = upward
            part = jnp.sum(upward.astype(F32), axis=0, keepdims=True)
            total = part if total is None else total + part
        side_ref[1:2, :] = total
        turn_relative(ids_ref, far, block, b_ref, turned_ref, acc_ref)

    @pl.when(step < chunks)
    def _():
        w1, w2, bias = w1_ref[...], w2_ref[...], b1_ref[...]
        total = None
        for rows in subs:
            u = nn(b_ref[rows, :], w1)
            upward = nt(gm_ref[rows, :], w2)
            z, slope = gelu_parts(u + bias)
            z = z.astype(BF16)
            gu = (upward * slope).astype(BF16)
            z_ref[rows, :] = z
            gu_ref[rows, :] = gu
            part = jnp.sum(gu.astype(F32), axis=0, keepdims=True)
            total = part if total is None else total + part
        side_ref[pl.ds(2 + ((ids_ref[0] >> 1) ^ step), 1), :] = total
        forth_ref[...] += nn(z_ref[...], w2)
        back_ref[...] += nt(gu_ref[...], w1)
        ones = nn(turned_ref[...], gu_ref[...])
        one0_ref[0] = ones[: width // 2].astype(BF16)
        one1_ref[0] = ones[width // 2 :].astype(BF16)
        acc_ref[...] = tn(z_ref[...], gm_ref[...])
        tall = width // 8
        for x in range(2):
            for y in range(2):
                for c, out_ref in enumerate((two0_ref, two1_ref)):
                    d, v = relative(ids_ref, x, y, 0, c)
                    start = pl.multiple_of(((d & 1) * 4 + v) * tall, 8)
                    out_ref[x, y, 0] = acc_ref[pl.ds(start, tall), :].astype(BF16)

    mixed_ready()
    wout_ready()

    @pl.when(step == chunks)
    def _():
        total = None
        for rows in subs:
            z_ref[rows, :] = forth_ref[rows, :].astype(BF16)
            upward = back_ref[rows, :]
            normed, inverse = normalize(x1_ref[rows, :])
            part = jnp.sum(upward * normed, axis=0, keepdims=True)
            total = part if total is None else total + part
            grad = gm_ref[rows, :].astype(F32) + normalize_back(upward, normed, inverse, gain2_ref[1:2, :])
            grad = grad.astype(BF16)
            ga_ref[rows, :] = grad
            go_ref[rows, :] = nt(grad, wout_ref[...]).astype(BF16)
        side_ref[0:1, :] = total
        final = z_ref[...]
        for head, out in zip((h0, h1, h2, h3), (p0, p1, p2, p3)):
            out[...] = (nt(head[s.features :, :], final) * seen).astype(BF16)
        acc_ref[: s.groups * s.features, :] = nn(gpred_ref[...], final)
        spread_features(s, ids_ref, acc_ref, (n0_ref, n1_ref))
        acc_ref[...] = tn(mixed_ref[...], ga_ref[...])
        spread(ids_ref, far, acc_ref, (out0_ref, out1_ref), block, side_ref[...].astype(BF16))


def hidden(s, ids, far, seen, cots, weights, x1, mixed, w1, b1, w2, b2, gain2, wout):
    rows, width = s.rows, s.width
    chunks = w1.shape[1] // width
    block = width // (8 * far)
    high = s.groups * s.features
    sides = 8 * -(-(2 + chunks) // 8)
    last = chunks - 1

    def chunk(i, ids):
        return (ids[0] >> 1) ^ jnp.minimum(i, last)

    first = [seen, *cots, *weights, x1]
    rest = [b2, gain2]
    outs = (
        [((2, 2, far, width // 8, width), BF16)] * 2
        + [((chunks, width // 2, width), BF16)] * 2
        + [((s.features, rows), BF16)] * 4
        + [((2, 2, far, block + sides, width), BF16)] * 2
        + [((2, 2, s.features // 2, width), BF16)] * 2
        + [((rows, width), BF16)] * 2
    )
    specs = [
        pl.BlockSpec((2, 2, 1, width // 8, width), lambda i, ids: (0, 0, jnp.minimum(i, last), 0, 0))
    ] * 2
    specs += [pl.BlockSpec((1, width // 2, width), lambda i, ids: (chunk(i, ids), 0, 0))] * 2
    specs += [fixed(*dims) for dims, _ in outs[4:]]
    return pl.pallas_call(
        functools.partial(hidden_kernel, s, far, chunks),
        grid_spec=pltpu.PrefetchScalarGridSpec(
            num_scalar_prefetch=1,
            grid=(chunks + 1,),
            in_specs=[whole(a) for a in first]
            + [
                LATE,
                pl.BlockSpec((width, width), lambda i, ids: (0, chunk(i, ids))),
                pl.BlockSpec((1, width), lambda i, ids: (0, chunk(i, ids))),
                pl.BlockSpec((width, width), lambda i, ids: (chunk(i, ids), 0)),
            ]
            + [whole(a) for a in rest]
            + [LATE],
            out_specs=specs,
            scratch_shapes=[
                pltpu.VMEM((rows, width), BF16),
                pltpu.VMEM((width, rows), BF16),
                pltpu.VMEM((rows, width), BF16),
                pltpu.VMEM((high, rows), BF16),
                pltpu.VMEM((rows, width), F32),
                pltpu.VMEM((rows, width), F32),
                pltpu.VMEM((rows, width), BF16),
                pltpu.VMEM((rows, width), BF16),
                pltpu.VMEM((width, width), F32),
                pltpu.VMEM((sides, width), F32),
                *late_scratch(mixed),
                *late_scratch(wout),
            ],
        ),
        out_shape=[shape(*out) for out in outs],
        compiler_params=params(60),
        cost_estimate=cost(3.4e10, 4e7),
    )(ids, *first, mixed, w1, b1, w2, *rest, wout)


def attention_back(s, heads, qkv_ref, probs_ref, go_ref, gqkv_ref):
    per = ROWS // LANES
    width = s.width
    masks = pair_masks()
    scale = 1.0 / math.sqrt(width // heads)
    for j in range(per):
        rows = slice(j * LANES, (j + 1) * LANES)
        for h in range(width // LANES):
            at = h * LANES
            q = doubled(qkv_ref[rows, at : at + LANES], masks)
            k = doubled(qkv_ref[rows, width + at : width + at + LANES], masks)
            v = qkv_ref[rows, 2 * width + at : 2 * width + at + LANES]
            out = doubled(go_ref[rows, at : at + LANES], masks)
            rounded = probs_ref[j, h]
            probs = rounded.astype(F32)
            upward = nt(out, v)
            centred = upward - jnp.sum(probs * upward, axis=-1, keepdims=True)
            grads = (probs * centred).astype(BF16)
            wide = jnp.concatenate([grads[:LANES], grads[LANES:]], axis=1)
            gqkv_ref[rows, at : at + LANES] = (nn(wide, k) * scale).astype(BF16)
            gqkv_ref[rows, width + at : width + at + LANES] = (tn(grads, q) * scale).astype(BF16)
            gqkv_ref[rows, 2 * width + at : 2 * width + at + LANES] = tn(rounded, out).astype(BF16)


def first_norm_back(gqkv, x0_ref, ga_ref, wqkv_ref, gain1_ref):
    upward = nt(gqkv, wqkv_ref[...])
    normed, inverse = normalize(x0_ref[...].astype(F32))
    grad = ga_ref[...].astype(F32) + normalize_back(upward, normed, inverse, gain1_ref[0:1, :])
    return grad.astype(BF16), jnp.sum(upward * normed, axis=0, keepdims=True)


def backward_kernel(s, heads, qkv_ref, probs_ref, go_ref, x0_ref, ga_ref, wqkv_hbm, gain1_ref, gqkv_ref, g0_ref, gln1_ref, wqkv_ref, sem_ref):
    ready = late_copy(wqkv_hbm, wqkv_ref, sem_ref)
    attention_back(s, heads, qkv_ref, probs_ref, go_ref, gqkv_ref)
    ready()
    g0_ref[...], gain_part = first_norm_back(gqkv_ref[...], x0_ref, ga_ref, wqkv_ref, gain1_ref)
    accumulate(gln1_ref, pl.program_id(0) == 0, gain_part)


def row_inputs(s, offset):
    width = s.width
    return [
        part_rows(3 * width, offset),
        pl.BlockSpec((ROWS // LANES, width // LANES, 2 * LANES, LANES), lambda i, *_: (i + offset, 0, 0, 0)),
        part_rows(width, offset),
        part_rows(width, offset),
        part_rows(width, offset),
    ]


def backward(s, heads, offset, steps, qkv, probs, go, x0, ga, wqkv, gain1):
    width = s.width
    size = steps * ROWS
    return pl.pallas_call(
        functools.partial(backward_kernel, s, heads),
        grid=(steps,),
        in_specs=row_inputs(s, offset) + [LATE, whole(gain1)],
        scratch_shapes=late_scratch(wqkv),
        out_specs=[across(ROWS, 3 * width), across(ROWS, width), fixed(1, width)],
        out_shape=[shape((size, 3 * width), BF16), shape((size, width), BF16), shape((1, width), F32)],
        compiler_params=params(60),
        cost_estimate=cost(8e9 * steps, 6e6 * steps),
    )(qkv, probs, go, x0, ga, wqkv, gain1)


def position_grads(s, keep_ref, g0, picked):
    hot_hi, hot_lo = [], []
    for t in range(s.tiles):
        row = keep_ref[0, t : t + 1, :]
        patches = s.hi_patches if t < s.hi_each else s.lo_patches
        hot = jnp.where(iota((patches, LANES), 0) == row, 1.0, 0.0).astype(BF16)
        (hot_hi if t < s.hi_each else hot_lo).append(hot)
    hi_rows = s.hi_each * LANES
    hi = nn(jnp.concatenate(hot_hi, axis=1), g0[:hi_rows])
    lo = nn(jnp.concatenate(hot_lo, axis=1), g0[hi_rows:])
    return lo, hi, nn(jnp.concatenate(picked, axis=0), g0)


def finish_kernel(s, far, chunks, ids_ref, keep_ref, a_ref, r0_ref, r1_ref, ga_hbm, gb_hbm, la_ref, lb_ref, p0, p1, p2, p3, w0, w1, w2, w3, q0, q1, q2, q3, o0_ref, o1_ref, e0_ref, e1_ref, i0, i1, i2, i3, turned_ref, acc_ref, lo_ref, hi_ref, ga_ref, ga_sem, gb_ref, gb_sem):
    ga_ready = late_copy(ga_hbm, ga_ref, ga_sem, chunks)
    gb_ready = late_copy(gb_hbm, gb_ref, gb_sem, chunks)
    step = pl.program_id(0)
    width = s.width
    block = width // (8 * far)
    half = width // 2
    done = r0_ref.shape[0]

    @pl.when(step == 0)
    def _():
        turn_relative(ids_ref, far, block, a_ref, turned_ref, acc_ref)

    @pl.when(step < chunks)
    def _():
        value = nn(turned_ref[:, :done], r0_ref[...]) + nn(turned_ref[:, done:], r1_ref[...])
        o0_ref[0] = value[:half].astype(BF16)
        o1_ref[0] = value[half:].astype(BF16)

    ga_ready()
    gb_ready()

    @pl.when(step == chunks)
    def _():
        g0 = jnp.concatenate([ga_ref[...], gb_ref[...]], axis=0)
        lo, hi, embed = position_grads(s, keep_ref, g0, [p[...] for p in (p0, p1, p2, p3)])
        lo_ref[...] = lo
        hi_ref[...] = hi
        acc_ref[: s.groups * s.features, :] = embed
        spread_features(s, ids_ref, acc_ref, (e0_ref, e1_ref))
        for weight, pred, out in zip((w0, w1, w2, w3), (q0, q1, q2, q3), (i0, i1, i2, i3)):
            out[: s.features, :] = nt(weight[: s.features, :], g0).astype(BF16)
            out[s.features :, :] = pred[...]
        hi_block = s.hi_patches // (8 * far)
        lo_block = s.lo_patches // (8 * far)
        gain = la_ref[...] + lb_ref[...]
        pad = jnp.zeros((block - hi_block - lo_block - 1, width), F32)
        order = places(ids_ref, far)
        for p in range(0, len(order), 2):
            pair = []
            for at in order[p : p + 2]:
                both = lo_ref[pl.ds(pl.multiple_of((at >> 1) * 8, 8), 8), :]
                pair += [
                    hi_ref[pl.ds(pl.multiple_of(at * hi_block, 8), hi_block), :],
                    jnp.where((at & 1) == 1, both[lo_block:], both[:lo_block]),
                    gain,
                    pad,
                ]
            row = (p % (len(order) // 2)) * block
            (o0_ref, o1_ref)[p // (len(order) // 2)][0, row : row + 2 * block, :] = jnp.concatenate(pair, axis=0).astype(BF16)


def finish(s, ids, far, keep, a, gqkvs, g0s, gains, picked, weights, preds):
    width, rows = s.width, s.rows
    chunks = gqkvs[0].shape[1] // width
    rest = [*gains, *picked, *weights, *preds]
    out = pl.BlockSpec((1, width // 2, width), lambda i, ids: (i, 0, 0))
    return pl.pallas_call(
        functools.partial(finish_kernel, s, far, chunks),
        grid_spec=pltpu.PrefetchScalarGridSpec(
            num_scalar_prefetch=1,
            grid=(chunks + 1,),
            in_specs=[whole(keep), whole(a)]
            + [
                pl.BlockSpec((g.shape[0], width), lambda i, ids: (0, jnp.minimum(i, chunks - 1)))
                for g in gqkvs
            ]
            + [LATE, LATE]
            + [whole(r) for r in rest],
            out_specs=[out, out]
            + [fixed(2, 2, s.features // 2, width)] * 2
            + [fixed(2 * s.features, rows)] * 4,
            scratch_shapes=[
                pltpu.VMEM((width, rows), BF16),
                pltpu.VMEM((width, width), F32),
                pltpu.VMEM((s.lo_patches, width), F32),
                pltpu.VMEM((s.hi_patches, width), F32),
                *late_scratch(g0s[0]),
                *late_scratch(g0s[1]),
            ],
        ),
        out_shape=[shape((chunks + 1, width // 2, width), BF16)] * 2
        + [shape((2, 2, s.features // 2, width), BF16)] * 2
        + [shape((2 * s.features, rows), BF16)] * 4,
        compiler_params=params(60),
        cost_estimate=cost(7e9, 1.2e7),
    )(ids, keep, a, *gqkvs, *g0s, *rest)


def combine_kernel(held_ref, got_ref, keep_ref, send_ref):
    send_ref[...] = (held_ref[:, 1].astype(F32) + got_ref[:, 1].astype(F32)).astype(BF16)
    keep_ref[...] = (held_ref[:, 0].astype(F32) + got_ref[:, 0].astype(F32)).astype(BF16)


def combine(held, got, axis):
    dims = held.shape
    width = dims[-1]
    outer = math.prod(dims[:axis])
    inner = math.prod(dims[axis + 1 : -1])
    grid = (outer // 4, 1) if outer > 4 else (1, 2)
    broad, tall = outer // grid[0], inner // grid[1]
    half = shape((outer, inner, width), BF16)
    spec = pl.BlockSpec((broad, 2, tall, width), lambda i, j: (i, 0, j, 0))
    out = pl.BlockSpec((broad, tall, width), lambda i, j: (i, j, 0))
    keep, send = pl.pallas_call(
        combine_kernel,
        grid=grid,
        in_specs=[spec, spec],
        out_specs=[out, out],
        out_shape=[half, half],
        compiler_params=params(60),
        cost_estimate=cost(1e6, 6 * outer * inner * width),
    )(*(value.reshape(outer, 2, inner, width) for value in (held, got)))
    left = dims[:axis] + dims[axis + 1 :]
    return keep.reshape(left), send.reshape(left)


def place_kernel(s, member_ref, keep_ref, r0, r1, r2, r3, lo_ref, hi_ref, pred_lo_ref, pred_hi_ref):
    lane_sample = iota((1, LANES), 1) // s.lo_length
    eye = jnp.where(iota((s.features, s.features), 0) == iota((s.features, s.features), 1), 1.0, 0.0).astype(BF16)
    for k, got_ref in enumerate((r0, r1, r2, r3)):
        other = member_ref[0] ^ k
        for i in range(s.hi_each):
            chosen = iota((s.hi_patches, LANES), 0) == keep_ref[k, i : i + 1, :]
            hot = jnp.where(chosen, 1.0, 0.0).astype(BF16)
            lanes = slice(i * LANES, (i + 1) * LANES)
            hi_ref[other * s.hi_each + i] = nt(got_ref[: s.features, lanes], hot).astype(BF16)
            pred_hi_ref[other * s.hi_each + i] = got_ref[s.features :, lanes]
        for tile, first, count in sample_tiles(s):
            lanes = slice(tile * LANES, (tile + 1) * LANES)
            got = got_ref[: s.features, lanes]
            for j in range(count):
                row = jnp.where(lane_sample == j, keep_ref[k, tile : tile + 1, :], -1)
                hot = jnp.where(iota((s.lo_patches, LANES), 0) == row, 1.0, 0.0).astype(BF16)
                lo_ref[other * s.lo_each + first + j] = nt(got, hot).astype(BF16)
            if count:
                size = count * s.lo_length
                turned = tn(got_ref[s.features :, lanes], eye).astype(BF16)
                start = pl.multiple_of((other * s.lo_each + first) * s.lo_length, s.lo_length)
                pred_lo_ref[pl.ds(start, size), :] = turned[:size]


def place(s, member, keep, blocks):
    lo = s.groups * s.lo_each
    hi = s.groups * s.hi_each
    outs = [
        (lo, s.features, s.lo_patches),
        (hi, s.features, s.hi_patches),
        (lo * s.lo_length, s.features),
        (hi, s.features, s.hi_length),
    ]
    return pl.pallas_call(
        functools.partial(place_kernel, s),
        grid_spec=pltpu.PrefetchScalarGridSpec(
            num_scalar_prefetch=1,
            grid=(1,),
            in_specs=[whole(keep)] + [whole(b) for b in blocks],
            out_specs=[fixed(*dims) for dims in outs],
        ),
        out_shape=[shape(dims, BF16) for dims in outs],
        compiler_params=params(60),
        cost_estimate=cost(2e9, 8e6),
    )(member, keep, *blocks)


def swap(value, data_bit, var_bit):
    dp, var = lax.axis_size("dp"), lax.axis_size("var")
    pairs = [
        (d * var + v, (d ^ data_bit) * var + (v ^ var_bit)) for d in range(dp) for v in range(var)
    ]
    return lax.ppermute(value, AXES, pairs)


def add_rounded(left, right):
    return (left.astype(F32) + right.astype(F32)).astype(BF16)


def added(*values):
    values = [value.astype(F32) for value in values]
    while len(values) > 1:
        values = [values[i] + values[i + 1] for i in range(0, len(values), 2)]
    return values[0]


def tie(value, *tokens):
    return lax.optimization_barrier((value, tokens))[0]


PARTNERS = {"core": (0, 1), "x": (0, 2), "y": (1, 0), "z0": (2, 0), "z1": (4, 0)}


class Chain:
    def __init__(self, near, sent):
        self.near, self.sent = near, sent
        self.repeats = near.ndim == 4
        self.names = ["x", "y"] if self.repeats else ["chunk", "x", "y", "z1", "z0"][7 - near.ndim :]
        self.held = self.got = None

    def outgoing(self, name):
        if name == "core":
            self.held = self.near
            return self.sent
        if name not in self.names:
            self.held = add_rounded(self.held, self.got)
            return self.held
        axis = self.names.index(name)
        self.names.remove(name)
        if math.prod(self.held.shape) >= 1 << 20:
            self.held, sent = combine(self.held, self.got, axis)
            return sent
        kept, sent = (
            [lax.index_in_dim(value, side, axis, keepdims=False) for value in (self.held, self.got)]
            for side in range(2)
        )
        self.held = add_rounded(*kept)
        return add_rounded(*sent)

    def hold(self, *tokens):
        self.held, self.got = tie((self.held, self.got), *tokens)

    def final(self):
        return added(self.held, self.got)


def send_rows(values, bits):
    width = values[0].shape[-1]
    if len(values) == 1:
        return [swap(values[0].reshape(-1, width), *bits).reshape(values[0].shape)]
    flat = [value.reshape(-1, width) for value in values]
    got = swap(jnp.concatenate(flat, axis=0), *bits)
    out, start = [], 0
    for value, rows in zip(values, flat):
        out.append(got[start : start + rows.shape[0]].reshape(value.shape))
        start += rows.shape[0]
    return out


def trade(name, *chains):
    got = send_rows([chain.outgoing(name) for chain in chains], PARTNERS[name])
    for chain, value in zip(chains, got):
        chain.got = value
    return got[0]


def both_halves(value):
    value = value.astype(BF16)
    other = swap(value, 1, 0)
    second = lax.axis_index("dp") % 2 == 1
    return jnp.concatenate(
        [jnp.where(second, other, value), jnp.where(second, value, other)], axis=0
    ).astype(F32)


def natural(near, sent):
    rows, width = near.shape[-2:]
    both = jnp.stack([near, sent]).reshape((2, -1, 2, 2, 4, rows, width))
    return both.transpose(4, 3, 2, 0, 1, 5, 6).reshape(32, -1, width)


def scattered(full):
    return lax.psum_scatter(full, AXES, scatter_dimension=0, tiled=True).astype(F32)


def joined(blocks, chunks):
    count, rows, width = blocks.shape
    split = blocks.reshape(count, chunks, rows // chunks, width).transpose(0, 2, 1, 3)
    return split.reshape(count * (rows // chunks), chunks * width)


def plain_sum(near, sent):
    if near.ndim >= 6:
        return natural(near, sent)
    value = jnp.stack([near, sent], axis=1)
    value = value.reshape((4, -1, near.shape[-1]))
    bit = 1
    while value.shape[0] > 1:
        value = value.reshape((value.shape[0] // 2, 2) + value.shape[1:])
        value = add_rounded(value[:, 0], swap(value[:, 1], 0, bit))
        bit *= 2
    return lax.psum(value[0], "dp").astype(F32)


def exchange_relative(blocks):
    return [blocks[0]] + [swap(blocks[k], 0, k) for k in range(1, len(blocks))]


def body(
    img_lo,
    img_hi,
    keep_lo,
    keep_hi,
    mask_lo,
    mask_hi,
    w_embed,
    pos_lo,
    pos_hi,
    ln1_gain,
    w_qkv,
    w_out,
    ln2_gain,
    w_fc1,
    b_fc1,
    w_fc2,
    b_fc2,
    w_head,
    cot_lo,
    cot_hi,
):
    groups = lax.axis_size("var")
    devices = lax.axis_size("dp") * groups
    member = lax.axis_index("var").astype(jnp.int32).reshape(1)
    s = Sizes(keep_lo.shape, keep_hi.shape, w_embed.shape, img_lo.shape, img_hi.shape, groups)
    features, width = s.features, s.width
    gain1 = gain2 = vectors = jnp.stack([ln1_gain, ln2_gain, b_fc2])
    img_lo_t, img_hi_t = img_lo.transpose(0, 2, 1), img_hi.transpose(0, 2, 1)

    own = jnp.concatenate([w_embed, w_head.T], axis=0)
    crossed = swap(own, 0, 2)
    beside = swap(own, 0, 1)
    sent = pick(s, (2, 3, 1, 0), member, keep_lo, keep_hi, img_lo_t, img_hi_t)
    crossed = tie(crossed, sent[0])
    weights = [own, beside, crossed, swap(crossed, 0, 1)]
    picked = [sent[3], swap(sent[2], 0, 1), swap(sent[0], 0, 2), swap(sent[1], 0, 3)]
    keep, seen, *cots = stage(
        s,
        tie(member, sent[0]),
        keep_lo,
        keep_hi,
        mask_lo,
        mask_hi,
        cot_lo.reshape(-1, features),
        cot_hi.transpose(0, 2, 1),
    )
    cots = exchange_relative(cots)
    own_keep = keep
    x0, a, qkv, probs, mixed, x1 = forward(
        s, HEADS, own_keep, seen, picked, weights, pos_lo, pos_hi, gain1, w_qkv, w_out
    )
    far = 4
    cube = lax.axis_size("dp") == 2 * far
    place_of = lax.axis_index("dp") * groups + lax.axis_index("var")
    ids = jnp.stack([lax.axis_index("dp"), lax.axis_index("var")]).astype(jnp.int32)
    if not cube:
        ids = jnp.zeros_like(ids)

    def chain_of(near, sent):
        if near.ndim == 5:
            near, sent = (
                value.reshape((2, 2, 2, 2) + value.shape[3:]) for value in (near, sent)
            )
        elif near.ndim == 3:
            near, sent = (
                value.reshape((-1, 2, 2, 2, 2, width // 32, width)) for value in (near, sent)
            )
        return Chain(near, sent)

    def step(name, *chains):
        return trade(name, *chains) if cube else ()

    def halves_of(chain):
        out = []
        for side in range(2):
            piece = Chain(chain.near, chain.sent)
            count = chain.near.shape[0] // 2
            piece.held, piece.got = (
                lax.slice_in_dim(value, side * count, (side + 1) * count, axis=0)
                for value in (chain.held, chain.got)
            )
            out.append(piece)
        return out

    two0, two1, one0, one1, *rest = hidden(
        s,
        ids,
        far,
        tie(seen, x1),
        cots,
        weights,
        x1,
        mixed,
        w_fc1,
        b_fc1.reshape(1, -1),
        w_fc2,
        vectors,
        gain2,
        w_out,
    )
    preds, (out0, out1, head0, head1, go, ga) = rest[:groups], rest[groups:]
    two, one = chain_of(two0, two1), chain_of(one0, one1)
    out, head = chain_of(out0, out1), chain_of(head0, head1)
    tokens = [step("core", chain) for chain in (two, one, out, head)]

    def back(offset, steps, *ready):
        return backward(
            s, HEADS, offset, steps, qkv, probs, go, x0, ga, w_qkv, tie(gain1, *ready)
        )

    parts = [back(0, 1, go)]
    if cube:
        for chain in (two, one, out, head):
            chain.hold(parts[0][0])
    near_tokens = [step("x", two), step("y", one)]
    if cube:
        for chain in (out, head):
            chain.hold(two.held, one.held)
    near_tokens.append(step("z0", out, head))
    parts.append(back(1, s.rows // ROWS - 1, parts[0][0], two.held, one.held, *tokens))
    if cube:
        for chain in (two, one, out, head):
            chain.hold(parts[1][0])
    tokens = [step("y", two), step("x", one, out, head)]
    gqkvs, g0s, gains = zip(*parts)
    near, sent, near_embed, sent_embed, *blocks = finish(
        s,
        tie(ids, two.held, one.held, *near_tokens),
        far,
        own_keep,
        a,
        gqkvs,
        g0s,
        gains,
        picked,
        weights,
        preds,
    )
    sent, sent_embed = tie((sent, sent_embed), *tokens)
    first, embed = chain_of(near, sent), chain_of(near_embed, sent_embed)
    tokens += [step("core", first), step("core", embed)]
    if cube:
        old = (two, one, out, head)
        for chain in old:
            chain.hold(first.got)
        one_half, other_half = halves_of(first)
        tokens = [trade("x", one_half, embed), trade("y", other_half, out, head)]
        trade("z0", two, one)
        for chain in old:
            chain.hold(*tokens)
        tokens = [trade("y", one_half, embed), trade("x", other_half)]
        trade("z1", *old)
        blocks = [tie(block_of, *tokens) for block_of in blocks]
        trade("z0", one_half, other_half, embed)
        trade("z1", one_half, other_half, embed)
        head.hold(embed.held)
        grad_head = both_halves(head.final())
        last_member = tie(member, grad_head)
        for chain in (two, one, out):
            chain.hold(grad_head)
        grad_fc2, grad_fc1, rest, grad_embed = (
            chain.final() for chain in (two, one, out, embed)
        )
        grad_embed = both_halves(grad_embed)
        first = jnp.concatenate([one_half.final(), other_half.final()], axis=0).reshape(-1, width)
        grad_fc1 = grad_fc1.reshape(-1, width)
    else:
        grad_fc2, grad_fc1, rest, grad_head, grad_embed, first = (
            plain_sum(chain.near, chain.sent) for chain in (two, one, out, head, embed, first)
        )
        last_member = member
    grad_img_lo, grad_img_hi, pred_lo, pred_hi = place(s, last_member, keep, exchange_relative(blocks))
    grad_head = grad_head.T

    block = width // devices
    inner = w_fc1.shape[1] // width

    hi_block = s.hi_patches // devices
    lo_block = s.lo_patches // devices

    def own_part(row):
        return lax.dynamic_slice_in_dim(row, place_of * block, block)

    if cube:
        grad_fc1 = joined(grad_fc1[None], inner)
        grad_qkv = joined(first[None, : 3 * block], 3)
        grad_out, sides = rest[:block], rest[block:]
        extra = first[3 * block :]
        grad_pos_hi = extra[:hi_block]
        grad_pos_lo = extra[hi_block : hi_block + lo_block]
        first_side = extra[hi_block + lo_block]
    else:
        tall = width // 32
        hi_tall, lo_tall = s.hi_patches // 32, s.lo_patches // 32
        grad_fc2 = scattered(grad_fc2.reshape(-1, width))
        grad_fc1 = scattered(joined(grad_fc1, inner))
        grad_qkv = scattered(joined(first[:, : 3 * tall], 3))
        grad_out, sides = scattered(rest[:, :tall].reshape(-1, width)), rest[0, tall:]
        extra = first[:, 3 * tall :]
        grad_pos_hi = scattered(extra[:, :hi_tall].reshape(-1, width))
        grad_pos_lo = scattered(extra[:, hi_tall : hi_tall + lo_tall].reshape(-1, width))
        sides = lax.psum(jnp.concatenate([sides, extra[0, hi_tall + lo_tall :]]), AXES).astype(F32)
        first_side = sides[rest.shape[1] - tall]
    grad_ln1 = own_part(first_side)
    grad_ln2 = own_part(sides[0])
    grad_b2 = own_part(sides[1])
    grad_b1 = lax.dynamic_slice_in_dim(
        sides[2 : 2 + inner].reshape(-1), place_of * inner * block, inner * block
    )
    return (
        pred_lo.reshape(cot_lo.shape),
        pred_hi.transpose(0, 2, 1),
        grad_img_lo.transpose(0, 2, 1),
        grad_img_hi.transpose(0, 2, 1),
        grad_embed,
        grad_pos_lo,
        grad_pos_hi,
        grad_ln1,
        grad_qkv,
        grad_out,
        grad_ln2,
        grad_fc1,
        grad_b1,
        grad_fc2,
        grad_b2,
        grad_head,
    )


def solution(mesh):
    placed = (
        P("dp", None, "var"),
        P("dp", None, "var"),
        P("dp", None),
        P("dp", None),
        P("dp", None),
        P("dp", None),
        P("var", None),
        P(),
        P(),
        P(),
        P(),
        P(),
        P(),
        P(),
        P(),
        P(),
        P(),
        P(None, "var"),
        P("dp", None, "var"),
        P("dp", None, "var"),
    )
    return jax.shard_map(
        body,
        mesh=mesh,
        in_specs=placed,
        out_specs=(
            P("dp", None, "var"),
            P("dp", None, "var"),
            P("dp", None, "var"),
            P("dp", None, "var"),
            P("var", None),
            P(("dp", "var"), None),
            P(("dp", "var"), None),
            P(("dp", "var")),
            P(("dp", "var"), None),
            P(("dp", "var"), None),
            P(("dp", "var")),
            P(("dp", "var"), None),
            P(("dp", "var")),
            P(("dp", "var"), None),
            P(("dp", "var")),
            P(None, "var"),
        ),
        check_vma=False,
    )
```
